32 devices in a mesh: fsdp: 8 (over y, x, core), tp: 4 (over z).
Axes of the slice: x: 2, y: 2, z: 4, core: 2. Of those that a mesh axis runs over, the one named last changes fastest.
Arguments:
- layer_input: bfloat16 [24576, 512], P(('fsdp', 'tp')), may hold values from -6 to 6
- segment_ids: int32 [24, 1024], P('fsdp'), may hold values from 0 to 15, never falling along the last dimension, each value on 1 to 512 neighbouring positions
- valid_mask: int32 [24576], P(('fsdp', 'tp')), may hold values from 0 to 1, as said below
- teacher: bfloat16 [24576, 512], P(('fsdp', 'tp')), may hold values from -6 to 6
- cotangent: bfloat16 [24576, 512], P(('fsdp', 'tp')), may hold values from -6 to 6
- ln1_gain: bfloat16 [512], P('fsdp'), may hold values from 0.099609375 to 1.8984375
- ln1_bias: bfloat16 [512], P('fsdp'), may hold values from -1.75 to 1.75
- w_q: bfloat16 [512, 512], P('fsdp', 'tp'), may hold values from -0.25 to 0.25
- w_k: bfloat16 [512, 512], P('fsdp', 'tp'), may hold values from -0.25 to 0.25
- w_v: bfloat16 [512, 512], P('fsdp', 'tp'), may hold values from -0.25 to 0.25
- b_q: bfloat16 [8, 64], P('tp', 'fsdp'), may hold values from -3 to 3
- b_v: bfloat16 [8, 64], P('tp', 'fsdp'), may hold values from -3 to 3
- w_o: bfloat16 [512, 512], P('tp', 'fsdp'), may hold values from -1 to 1
- b_o: bfloat16 [512], P('fsdp'), may hold values from -3 to 3
- ln2_gain: bfloat16 [512], P('fsdp'), may hold values from 0.099609375 to 1.8984375
- ln2_bias: bfloat16 [512], P('fsdp'), may hold values from -1.75 to 1.75
- w_up: bfloat16 [512, 2048], P('fsdp', 'tp'), may hold values from -0.25 to 0.25
- b_up: bfloat16 [32, 64], P('tp', 'fsdp'), may hold values from -3 to 3
- w_down: bfloat16 [2048, 512], P('tp', 'fsdp'), may hold values from -0.25 to 0.25
- b_down: bfloat16 [512], P('fsdp'), may hold values from -3 to 3
Outputs:
- layer_out: bfloat16 [24576, 512], P(('fsdp', 'tp'))
- loss: float32 [], replicated
- grad_layer_input: float32 [24576, 512], P(('fsdp', 'tp'))
- grad_ln1_gain: float32 [512], P('fsdp')
- grad_ln1_bias: float32 [512], P('fsdp')
- grad_w_q: float32 [512, 512], P('fsdp', 'tp')
- grad_w_k: float32 [512, 512], P('fsdp', 'tp')
- grad_w_v: float32 [512, 512], P('fsdp', 'tp')
- grad_b_q: float32 [8, 64], P('tp', 'fsdp')
- grad_b_v: float32 [8, 64], P('tp', 'fsdp')
- grad_w_o: float32 [512, 512], P('tp', 'fsdp')
- grad_b_o: float32 [512], P('fsdp')
- grad_ln2_gain: float32 [512], P('fsdp')
- grad_ln2_bias: float32 [512], P('fsdp')
- grad_w_up: float32 [512, 2048], P('fsdp', 'tp')
- grad_b_up: float32 [32, 64], P('tp', 'fsdp')
- grad_w_down: float32 [2048, 512], P('tp', 'fsdp')
- grad_b_down: float32 [512], P('fsdp')
The draws below stay inside these ranges and needn't reach their ends.
Inputs may be any that keep to these rules, and one draw needn't show every extreme that they name: `segment_ids`: in each sequence the ids never fall, each document holds 1 to 512 positions, and one holds exactly 512. `valid_mask`: the first token of every sequence is 1.
All inputs are finite; a program needn't handle non-finite values.
Results may differ from the reference program's by a relative error of at most 0.014.
Values may be sent and summed in bfloat16 or wider, within the bound.
No kernel may reach another device: no remote copies, remote signals or barrier semaphores. Data moves between devices by JAX's collectives and lax.ppermute only.
A program may use at most 128 MiB of HBM per device.

```python
import math
import jax
import jax.numpy as jnp
import numpy as np
from jax import lax

D = 512
H = 8
HD = 64
FF = 2048
LEN = 1024
SEQUENCES = 24
TOKENS = 24576


def draw_valid_mask(key, part):
    rows_index = jnp.arange(TOKENS, dtype=jnp.int32)
    sequence = rows_index // LEN
    threshold = 250 + sequence * 650 // SEQUENCES
    ticket = jax.random.randint(key, (TOKENS,), 0, 1000, dtype=jnp.int32)
    chosen = (ticket < threshold) | (rows_index % LEN == 0)
    return chosen.astype(jnp.int32)


def block_scale(rng, extent, split, smallest, largest):
    def one(axis_at, blocks):
        heights = jax.random.uniform(jax.random.fold_in(jax.random.fold_in(rng, 6), axis_at), (blocks,), jnp.float32, smallest / len(split), largest / len(split))
        return jnp.repeat(jnp.exp(heights), extent[axis_at] // blocks).reshape((-1,) + (1,) * (len(extent) - axis_at - 1))

    loudness = one(*split[0])
    for cut in split[1:]:
        loudness = loudness * one(*cut)
    return loudness


def split_up(count, total, bound, slope):
    weights = [(1 << 20) // math.isqrt(standing ** slope) + 1 for standing in range(2, count + 1)]
    spare, holding = total - bound - (count - 1), [1] * (count - 1)
    while spare > 0:
        free = [i for i in range(count - 1) if holding[i] < bound]
        mass, budget = sum([weights[i] for i in free]), spare
        for i in free:
            more = min(bound - holding[i], max(1, budget * weights[i] // mass), spare)
            holding[i] = holding[i] + more
            spare = spare - more
    return np.array([bound] + holding)


def uneven(key, amount, total, limit, skew):
    if amount == 2:
        one = jax.random.randint(key, (), max(1, total - limit), min(limit, total - 1) + 1)
        return jnp.stack([one, total - one])
    sizes = jnp.asarray(split_up(amount, total, limit, skew), jnp.int32)
    pairs = (amount - 1) // 2
    giver, sink = sizes[1:1 + 2 * pairs:2], sizes[2:2 + 2 * pairs:2]
    margin = jnp.minimum(giver - 1, limit - sink)
    passed = jax.random.randint(jax.random.fold_in(key, 1), (pairs,), 0, 1 << 20) % (margin + 1)
    sizes = sizes.at[1:1 + 2 * pairs:2].set(giver - passed).at[2:2 + 2 * pairs:2].set(sink + passed)
    return sizes[jax.random.permutation(jax.random.fold_in(key, 2), amount)]


def noise(stream_key, dims, scale, bound, pieces=(), kind=jnp.bfloat16):
    factor_of = block_scale(stream_key, dims, pieces, -0.22, 0.18) if pieces else 1.0
    array = jax.random.normal(stream_key, dims, jnp.float32) * scale * factor_of
    return jnp.minimum(jnp.maximum(array, -bound), bound).astype(kind)


def setup_inputs(seed: int = 0) -> dict:
    key_list = jax.random.split(jax.random.key(seed), 21)
    return {
        "layer_input": noise(key_list[0], (TOKENS, D), 1.0, 6.0, ((0, 32),)),
        "segment_ids": jax.vmap(lambda own: jnp.searchsorted(jnp.cumsum(uneven(own, max(4, LEN // 64), LEN, LEN // 2, 2)), jnp.arange(LEN), side="right"))(jax.random.split(key_list[1], SEQUENCES)).reshape((SEQUENCES, LEN)).astype(jnp.int32),
        "valid_mask": draw_valid_mask(jax.random.fold_in(key_list[20], 71), 0),
        "teacher": noise(key_list[3], (TOKENS, D), 1.0, 6.0, ((0, 32),)),
        "cotangent": noise(key_list[4], (TOKENS, D), 1.0, 6.0, ((0, 32),)),
        "ln1_gain": jnp.clip(1.0 + 0.18 * jax.random.normal(key_list[5], (D,), jnp.float32), 0.099609375, 1.8984375).astype(jnp.bfloat16),
        "ln1_bias": noise(key_list[6], (D,), 0.3, 1.75, ((0, 8),)),
        "w_q": noise(key_list[7], (D, D), D ** -0.5, 0.25, ((0, 8), (1, 4))),
        "w_k": noise(key_list[8], (D, D), D ** -0.5, 0.25, ((0, 8), (1, 4))),
        "w_v": noise(key_list[9], (D, D), D ** -0.5, 0.25, ((0, 8), (1, 4))),
        "b_q": noise(key_list[10], (H, HD), 0.5, 3.0, ((0, 4), (1, 8))),
        "b_v": noise(key_list[11], (H, HD), 0.5, 3.0, ((0, 4), (1, 8))),
        "w_o": noise(key_list[12], (D, D), (D // 16) ** -0.5, 1.0, ((0, 4), (1, 8))),
        "b_o": noise(key_list[13], (D,), 0.5, 3.0, ((0, 8),)),
        "ln2_gain": jnp.clip(1.0 + 0.18 * jax.random.normal(key_list[14], (D,), jnp.float32), 0.099609375, 1.8984375).astype(jnp.bfloat16),
        "ln2_bias": noise(key_list[15], (D,), 0.3, 1.75, ((0, 8),)),
        "w_up": noise(key_list[16], (D, FF), D ** -0.5, 0.25, ((0, 8), (1, 4))),
        "b_up": noise(key_list[17], (FF // 64, 64), 0.5, 3.0, ((0, 4), (1, 8))),
        "w_down": noise(key_list[18], (FF, D), (FF // 4) ** -0.5, 0.25, ((0, 4), (1, 8))),
        "b_down": noise(key_list[19], (D,), 0.5, 3.0, ((0, 8),)),
    }


HIGHEST_PRECISION = lax.Precision.HIGHEST

@jax.custom_vjp
def low(v):
    return lax.optimization_barrier(v.astype(jnp.bfloat16)).astype(jnp.float32)

@jax.custom_vjp
def low_back(v):
    return v

def low_keep(v):
    return (low(v), None)

def low_pass(kept, grad):
    return (grad,)

def back_keep(v):
    return (v, None)

def back_low(kept, grad):
    return (low(grad),)
low.defvjp(low_keep, low_pass)
low_back.defvjp(back_keep, back_low)

def layer_norm(values, gains, offsets):
    center = values - lax.optimization_barrier(jnp.mean(values, axis=-1, keepdims=True))
    spread = lax.optimization_barrier(jnp.mean(center * center, axis=-1, keepdims=True))
    return center * lax.rsqrt(spread + 1e-05) * gains + offsets

def quick_gelu(values):
    return values * jax.nn.sigmoid(1.702 * values)

def attend_sequence(inputs):
    queries, keys_seq, values_seq, segment_seq = inputs
    scores = low_back(jnp.einsum('qhd,khd->hqk', queries, keys_seq, precision=HIGHEST_PRECISION) * HD ** (-0.5))
    position = jnp.arange(LEN, dtype=jnp.int32)
    allowed = (segment_seq[:, None] == segment_seq[None, :]) & (position[None, :] <= position[:, None])
    scores = jnp.where(allowed[None], scores, -1e+30)
    row_max = lax.optimization_barrier(jnp.max(scores, axis=-1, keepdims=True))
    exponent = jnp.exp(scores - row_max)
    weights = exponent / lax.optimization_barrier(jnp.sum(exponent, axis=-1, keepdims=True))
    return jnp.einsum('hqk,khd->qhd', low(weights), values_seq, precision=HIGHEST_PRECISION)

def block_forward(input_rows, params, segment_group, cot_rows, teacher_rows, mask_rows, valid_total):
    gain_one, bias_one, w_query, w_key, w_value, b_query, b_value, w_out, b_out, gain_two, bias_two, w_upper, b_upper, w_lower, b_lower = params
    row_count = input_rows.shape[0]
    seq_count = row_count // LEN
    normed_one = low(layer_norm(input_rows, gain_one, bias_one))

    def project(weight, offset):
        return low(low_back(jnp.dot(normed_one, weight, precision=HIGHEST_PRECISION) + offset))
    queries = project(w_query, b_query.reshape(-1))
    keys_all = project(w_key, 0.0)
    values_all = project(w_value, b_value.reshape(-1))
    four_shape = (seq_count, LEN, H, HD)
    attended = lax.map(jax.checkpoint(attend_sequence), (queries.reshape(four_shape), keys_all.reshape(four_shape), values_all.reshape(four_shape), segment_group))
    attended = low(low_back(attended.reshape(row_count, D)))
    attention = low_back(jnp.dot(attended, w_out, precision=HIGHEST_PRECISION))
    hidden_one = input_rows + attention + b_out
    normed_two = low(layer_norm(hidden_one, gain_two, bias_two))
    pre_act = low_back(jnp.dot(normed_two, w_upper, precision=HIGHEST_PRECISION) + b_upper.reshape(-1))
    activated = low(quick_gelu(pre_act))
    branch = low_back(jnp.dot(activated, w_lower, precision=HIGHEST_PRECISION))
    out_full = hidden_one + branch + b_lower
    difference = out_full - teacher_rows
    square_sum = jnp.sum(mask_rows * lax.optimization_barrier(jnp.mean(difference * difference, axis=-1)))
    objective = jnp.sum(cot_rows * out_full) + D * TOKENS * 0.5 * square_sum / valid_total
    return (objective, (out_full, square_sum))

def reference(layer_input, segment_ids, valid_mask, teacher, cotangent, ln1_gain, ln1_bias, w_q, w_k, w_v, b_q, b_v, w_o, b_o, ln2_gain, ln2_bias, w_up, b_up, w_down, b_down):
    params = tuple((item.astype(jnp.float32) for item in (ln1_gain, ln1_bias, w_q, w_k, w_v, b_q, b_v, w_o, b_o, ln2_gain, ln2_bias, w_up, b_up, w_down, b_down)))
    mask_float = valid_mask.astype(jnp.float32)
    valid_total = jnp.sum(mask_float)
    group_size = math.gcd(SEQUENCES, max(1, 4096 // LEN))
    step_count = SEQUENCES // group_size
    group_rows = group_size * LEN
    input_groups = layer_input.astype(jnp.float32).reshape(step_count, group_rows, D)
    teacher_groups = teacher.astype(jnp.float32).reshape(step_count, group_rows, D)
    cot_groups = cotangent.astype(jnp.float32).reshape(step_count, group_rows, D)
    mask_groups = mask_float.reshape(step_count, group_rows)
    segment_groups = segment_ids.reshape(step_count, group_size, LEN)

    def one_group(carried, inputs):
        input_group, segment_group, teacher_group, cot_group, mask_group = inputs

        def objective(input_in, params_in):
            return block_forward(input_in, params_in, segment_group, cot_group, teacher_group, mask_group, valid_total)
        value_out, pull_back, extra = jax.vjp(objective, input_group, params, has_aux=True)
        grad_input, grad_params = pull_back(jnp.ones_like(value_out))
        summed = (jax.tree.map(jnp.add, carried[0], grad_params), carried[1] + extra[1])
        return (summed, (extra[0].astype(jnp.bfloat16), grad_input))
    start_sums = (tuple((jnp.zeros_like(item) for item in params)), jnp.zeros((), jnp.float32))
    (grad_params, square_total), (out_groups, grad_groups) = lax.scan(one_group, start_sums, (input_groups, segment_groups, teacher_groups, cot_groups, mask_groups))
    loss = 0.5 * square_total / valid_total
    return (out_groups.reshape(TOKENS, D), loss, grad_groups.reshape(TOKENS, D)) + tuple(grad_params)
```

```python
import functools

import jax
import jax.numpy as jnp
from jax import lax
from jax.experimental import pallas as pl
from jax.experimental.pallas import tpu as pltpu
from jax.sharding import PartitionSpec as P

D = 512
H = 8
HD = 64
LEN = 1024
HALO = 512
PAIR = 2 * HD
NEG = -1e30
SCALE = HD ** (-0.5)
F32 = jnp.float32
BF16 = jnp.bfloat16
MIB = 1 << 20

CONTRACT_LAST = (((1,), (1,)), ((), ()))


def dot(a, b):
    return jnp.dot(a, b, preferred_element_type=F32)


def dot_t(a, b):
    return lax.dot_general(a, b, CONTRACT_LAST, preferred_element_type=F32)


def normalize(x):
    center = x - jnp.mean(x, axis=-1, keepdims=True)
    rstd = lax.rsqrt(jnp.mean(center * center, axis=-1, keepdims=True) + 1e-05)
    return center * rstd, rstd


def norm_pull(g, gain, xhat, rstd):
    gx = g * gain
    return rstd * (
        gx
        - jnp.mean(gx, axis=-1, keepdims=True)
        - xhat * jnp.mean(gx * xhat, axis=-1, keepdims=True)
    )


def fold(x):
    return jnp.sum(x.reshape(x.shape[0] // 8, 8, x.shape[1]), axis=0)


def rows_of(start, size, unit=128):
    return pl.ds(pl.multiple_of(start, unit), size)


def forward_kernel(
    qb, x_ref, vec_ref, w_ref, idr_ref, idc_ref, n_ref, q_ref, k_ref, v_ref, o_ref, lse_ref, bias_ref, stat_ref
):
    ext, own = x_ref.shape[0], o_ref.shape[0]
    window = HALO + qb

    def project(i, carry):
        rows = rows_of(i * 128, 128)
        xhat, _ = normalize(x_ref[rows, :].astype(F32))
        n1 = (xhat * vec_ref[0:1, :] + vec_ref[1:2, :]).astype(BF16)
        n_ref[rows, :] = n1
        k_ref[rows, :] = dot(n1, w_ref[:, D : 2 * D]).astype(BF16)
        v_ref[rows, :] = (dot(n1, w_ref[:, 2 * D : 3 * D]) + vec_ref[3:4, :]).astype(BF16)
        return carry

    lax.fori_loop(0, ext // 128, project, 0)

    def project_q(i, carry):
        rows = rows_of(i * 128, 128)
        q = dot(n_ref[rows_of(HALO + i * 128, 128), :], w_ref[:, 0:D]) + vec_ref[2:3, :]
        q_ref[rows, :] = q.astype(BF16) * jnp.asarray(SCALE, BF16)
        return carry

    lax.fori_loop(0, own // 128, project_q, 0)

    def query_block(i, carry):
        first = i * qb
        key = lax.broadcasted_iota(jnp.int32, (qb, window), 1)
        query = lax.broadcasted_iota(jnp.int32, (qb, window), 0)
        same = idc_ref[rows_of(HALO + first, qb), :] == idr_ref[:, rows_of(first, window)]
        bias_ref[...] = jnp.where(same & (key <= query + HALO), 0.0, NEG)

        def pair(g, inner):
            lanes = rows_of(g * PAIR, PAIR)
            lane = lax.broadcasted_iota(jnp.int32, (qb, PAIR), 1)
            keys = k_ref[rows_of(first, window), lanes]
            values = v_ref[rows_of(first, window), lanes]
            both = q_ref[rows_of(first, qb), lanes]
            got = None
            for h in range(2):
                mine = (lane < HD) if h == 0 else (lane >= HD)
                s = dot_t(jnp.where(mine, both, jnp.zeros_like(both)), keys) + bias_ref[...]
                top = jnp.max(s, axis=-1, keepdims=True)
                p = jnp.exp(s - top)
                total = jnp.sum(p, axis=-1, keepdims=True)
                o = dot(p.astype(BF16), values) / total
                got = o if h == 0 else jnp.where(mine, o, got)
                stat_ref[...] = jnp.where(lane == 2 * g + h, top + jnp.log(total), stat_ref[...])
            o_ref[rows_of(first, qb), lanes] = got.astype(BF16)
            return inner

        lax.fori_loop(0, D // PAIR, pair, 0)
        lse_ref[:, rows_of(first, qb)] = jnp.transpose(stat_ref[...])[0:H, :]
        return carry

    stat_ref[...] = jnp.zeros_like(stat_ref)
    lax.fori_loop(0, own // qb, query_block, 0)


def attention_forward(x_ext, vecs, w_qkv, id_row, id_col, own):
    ext = x_ext.shape[0]
    qb = 256 if own % 256 == 0 else 128
    shapes = (
        jax.ShapeDtypeStruct((ext, D), BF16),
        jax.ShapeDtypeStruct((own, D), BF16),
        jax.ShapeDtypeStruct((ext, D), BF16),
        jax.ShapeDtypeStruct((ext, D), BF16),
        jax.ShapeDtypeStruct((own, D), BF16),
        jax.ShapeDtypeStruct((H, own), F32),
    )
    return pl.pallas_call(
        functools.partial(forward_kernel, qb),
        out_shape=shapes,
        scratch_shapes=[pltpu.VMEM((qb, HALO + qb), F32), pltpu.VMEM((qb, 128), F32)],
        compiler_params=pltpu.CompilerParams(vmem_limit_bytes=48 * MIB),
        name="attention_forward",
    )(x_ext, vecs, w_qkv, id_row, id_col)


def middle_kernel(
    rb,
    scale_ref,
    x_ref,
    o_ref,
    teacher_ref,
    cot_ref,
    mask_ref,
    vec_ref,
    bup_ref,
    wo_ref,
    wup_ref,
    wdn_ref,
    out_ref,
    gh_ref,
    go_ref,
    delta_ref,
    gwo_ref,
    gwup_ref,
    gwdn_ref,
    small_ref,
    gbup_ref,
    slope_ref,
    hid_ref,
    gpre_ref,
    n2t_ref,
    gmlpt_ref,
    gattnt_ref,
):
    own = x_ref.shape[0]
    ff = wup_ref.shape[1]
    chunk = 512
    small_ref[...] = jnp.zeros_like(small_ref)
    head_of = lax.broadcasted_iota(jnp.int32, (D, 128), 0) // HD
    pick = (head_of == lax.broadcasted_iota(jnp.int32, (D, 128), 1)).astype(BF16)

    def block(i, carry):
        rows = rows_of(i * rb, rb)
        out_bias, gain, offset, down_bias = (vec_ref[j : j + 1, :] for j in range(4))
        h1 = x_ref[rows, :].astype(F32) + dot_t(o_ref[rows, :], wo_ref[...]) + out_bias
        xhat, rstd = normalize(h1)
        n2 = xhat * gain + offset
        n2_low = n2.astype(BF16)
        n2t_ref[:, rows] = jnp.transpose(n2).astype(BF16)
        for c in range(0, ff, chunk):
            pre = dot(n2_low, wup_ref[:, c : c + chunk]) + bup_ref[:, c : c + chunk]
            s = jax.nn.sigmoid(1.702 * pre)
            value = pre * s
            hid_ref[rows, c : c + chunk] = value.astype(BF16)
            slope_ref[:, c : c + chunk] = s + 1.702 * value * (1.0 - s)
        out = h1 + dot_t(hid_ref[rows, :], wdn_ref[...]) + down_bias
        out_ref[rows, :] = out.astype(BF16)
        valid = mask_ref[rows, :]
        diff = (out - teacher_ref[rows, :].astype(F32)) * valid
        g_out = cot_ref[rows, :].astype(F32) + scale_ref[0, 0] * diff
        small_ref[0:8, :] += fold(g_out)
        small_ref[8:16, :] += fold(diff * diff)
        g_mlp = g_out.astype(BF16)
        gmlpt_ref[:, rows] = jnp.transpose(g_out).astype(BF16)
        for c in range(0, ff, chunk):
            g_hid = dot(g_mlp, wdn_ref[:, c : c + chunk])
            gpre_ref[rows, c : c + chunk] = (g_hid * slope_ref[:, c : c + chunk]).astype(BF16)
        g_n2 = dot_t(gpre_ref[rows, :], wup_ref[...])
        small_ref[16:24, :] += fold(g_n2 * xhat)
        small_ref[24:32, :] += fold(g_n2)
        g_h1 = g_out + norm_pull(g_n2, gain, xhat, rstd)
        gh_ref[rows, :] = g_h1
        small_ref[32:40, :] += fold(g_h1)
        gattnt_ref[:, rows] = jnp.transpose(g_h1).astype(BF16)
        g_o = dot(g_h1.astype(BF16), wo_ref[...]).astype(BF16)
        go_ref[rows, :] = g_o
        product = g_o.astype(F32) * o_ref[rows, :].astype(F32)
        high = product.astype(BF16)
        low = (product - high.astype(F32)).astype(BF16)
        delta_ref[:, rows] = jnp.transpose(dot(high, pick) + dot(low, pick))[0:H, :]
        return carry

    lax.fori_loop(0, own // rb, block, 0)
    ones = jnp.ones((8, own), BF16)

    def grads(i, carry):
        cols = rows_of(i * chunk, chunk)
        gwdn_ref[:, cols] = dot(gmlpt_ref[...], hid_ref[:, cols]).astype(BF16)
        gwup_ref[:, cols] = dot(n2t_ref[...], gpre_ref[:, cols]).astype(BF16)
        gbup_ref[:, cols] = dot(ones, gpre_ref[:, cols])
        return carry

    lax.fori_loop(0, ff // chunk, grads, 0)
    gwo_ref[...] = dot(gattnt_ref[...], o_ref[...]).astype(BF16)


def middle(scale, x, o, teacher, cot, mask, vecs, b_up, w_o, w_up, w_dn):
    own, ff = x.shape[0], w_up.shape[1]
    rb = 256 if own % 256 == 0 else 128
    shapes = (
        jax.ShapeDtypeStruct((own, D), BF16),
        jax.ShapeDtypeStruct((own, D), F32),
        jax.ShapeDtypeStruct((own, D), BF16),
        jax.ShapeDtypeStruct((H, own), F32),
        jax.ShapeDtypeStruct((D, D), BF16),
        jax.ShapeDtypeStruct((D, ff), BF16),
        jax.ShapeDtypeStruct((D, ff), BF16),
        jax.ShapeDtypeStruct((40, D), F32),
        jax.ShapeDtypeStruct((8, ff), F32),
    )
    whole = pl.BlockSpec(memory_space=pltpu.VMEM)
    return pl.pallas_call(
        functools.partial(middle_kernel, rb),
        out_shape=shapes,
        in_specs=[pl.BlockSpec(memory_space=pltpu.SMEM)] + [whole] * 10,
        out_specs=[whole] * len(shapes),
        scratch_shapes=[
            pltpu.VMEM((rb, ff), F32),
            pltpu.VMEM((own, ff), BF16),
            pltpu.VMEM((own, ff), BF16),
            pltpu.VMEM((D, own), BF16),
            pltpu.VMEM((D, own), BF16),
            pltpu.VMEM((D, own), BF16),
        ],
        compiler_params=pltpu.CompilerParams(vmem_limit_bytes=56 * MIB),
        name="middle",
    )(scale, x, o, teacher, cot, mask, vecs, b_up, w_o, w_up, w_dn)


def backward_kernel(
    qb,
    q_ref,
    k_ref,
    v_ref,
    go_ref,
    lse_ref,
    delta_ref,
    idr_ref,
    idc_ref,
    n_ref,
    x_ref,
    w_ref,
    gn_halo_ref,
    gn_ref,
    gw_ref,
    small_ref,
    bias_ref,
    kt_ref,
    nt_ref,
    dqt_ref,
    dk_ref,
    dv_ref,
    g_ref,
):
    ext, own = k_ref.shape[0], q_ref.shape[0]
    window = HALO + qb
    dk_ref[...] = jnp.zeros_like(dk_ref)
    dv_ref[...] = jnp.zeros_like(dv_ref)
    small_ref[...] = jnp.zeros_like(small_ref)

    def turn(i, carry):
        rows = rows_of(i * 128, 128)
        kt_ref[:, rows] = jnp.transpose(k_ref[rows, :].astype(F32)).astype(BF16)
        nt_ref[:, rows] = jnp.transpose(n_ref[rows, :].astype(F32)).astype(BF16)
        return carry

    lax.fori_loop(0, ext // 128, turn, 0)

    def query_block(i, carry):
        first = i * qb
        key = lax.broadcasted_iota(jnp.int32, (window, qb), 0)
        query = lax.broadcasted_iota(jnp.int32, (window, qb), 1)
        same = idc_ref[rows_of(first, window), :] == idr_ref[:, rows_of(HALO + first, qb)]
        bias_ref[...] = jnp.where(same & (key <= query + HALO), 0.0, NEG)

        def pair(g, inner):
            lanes = rows_of(g * PAIR, PAIR)
            lane = lax.broadcasted_iota(jnp.int32, (qb, PAIR), 1)
            keys = k_ref[rows_of(first, window), lanes]
            values = v_ref[rows_of(first, window), lanes]
            both_q = q_ref[rows_of(first, qb), lanes]
            both_g = go_ref[rows_of(first, qb), lanes]
            all_lse = lse_ref[:, rows_of(first, qb)]
            all_delta = delta_ref[:, rows_of(first, qb)]
            line = lax.broadcasted_iota(jnp.int32, (H, qb), 0)
            dk, dv = None, None
            for h in range(2):
                head = 2 * g + h
                mine = (lane < HD) if h == 0 else (lane >= HD)
                q = jnp.where(mine, both_q, jnp.zeros_like(both_q))
                g_o = jnp.where(mine, both_g, jnp.zeros_like(both_g))
                lse = jnp.sum(jnp.where(line == head, all_lse, 0.0), axis=0, keepdims=True)
                delta = jnp.sum(jnp.where(line == head, all_delta, 0.0), axis=0, keepdims=True)
                p = jnp.exp(dot_t(keys, q) + bias_ref[...] - lse)
                ds = (p * (dot_t(values, g_o) - delta)).astype(BF16)
                dv_h = dot(p.astype(BF16), g_o)
                dk_h = dot(ds, q)
                dk, dv = (dk_h, dv_h) if h == 0 else (dk + dk_h, dv + dv_h)
                dqt_ref[rows_of(head * HD, HD, HD), rows_of(first, qb)] = dot(
                    kt_ref[rows_of(head * HD, HD, HD), rows_of(first, window)], ds
                )
            dk_ref[rows_of(first, window), lanes] += dk
            dv_ref[rows_of(first, window), lanes] += dv
            return inner

        lax.fori_loop(0, D // PAIR, pair, 0)
        return carry

    lax.fori_loop(0, own // qb, query_block, 0)

    def gather(i, carry):
        rows = rows_of(i * 128, 128)
        g_ref[rows, D : 2 * D] = dk_ref[rows, :].astype(BF16)
        g_ref[rows, 2 * D : 3 * D] = dv_ref[rows, :].astype(BF16)
        return carry

    lax.fori_loop(0, ext // 128, gather, 0)

    def gather_q(i, carry):
        cols = rows_of(i * 128, 128)
        g_ref[rows_of(HALO + i * 128, 128), 0:D] = (jnp.transpose(dqt_ref[:, cols]) * SCALE).astype(BF16)
        return carry

    lax.fori_loop(0, own // 128, gather_q, 0)

    def norms(rows, g_n1):
        xhat, _ = normalize(x_ref[rows, :].astype(F32))
        small_ref[0:8, :] += fold(g_n1 * xhat)
        small_ref[8:16, :] += fold(g_n1)

    def pull_halo(i, carry):
        rows = rows_of(i * 128, 128)
        g_n1 = dot_t(g_ref[rows, D : 3 * D], w_ref[:, D : 3 * D])
        gn_halo_ref[rows, :] = g_n1.astype(BF16)
        norms(rows, g_n1)
        return carry

    lax.fori_loop(0, HALO // 128, pull_halo, 0)

    def pull_own(i, carry):
        rows = rows_of(HALO + i * 128, 128)
        g_n1 = dot_t(g_ref[rows, :], w_ref[...])
        gn_ref[rows_of(i * 128, 128), :] = g_n1
        norms(rows, g_n1)
        return carry

    lax.fori_loop(0, own // 128, pull_own, 0)
    gw_ref[:, 0:D] = dot(nt_ref[:, HALO:], g_ref[HALO:, 0:D]).astype(BF16)
    gw_ref[:, D : 2 * D] = dot(nt_ref[...], g_ref[:, D : 2 * D]).astype(BF16)
    gw_ref[:, 2 * D : 3 * D] = dot(nt_ref[...], g_ref[:, 2 * D : 3 * D]).astype(BF16)
    small_ref[16:24, :] = dot(jnp.ones((8, own), BF16), g_ref[HALO:, 0:D])
    small_ref[24:32, :] = dot(jnp.ones((8, ext), BF16), g_ref[:, 2 * D : 3 * D])


def attention_backward(q, k, v, g_o, lse, delta, id_row, id_col, n1, x_ext, w_qkv):
    ext, own = k.shape[0], q.shape[0]
    qb = 256 if own % 256 == 0 else 128
    shapes = (
        jax.ShapeDtypeStruct((HALO, D), BF16),
        jax.ShapeDtypeStruct((own, D), F32),
        jax.ShapeDtypeStruct((D, 3 * D), BF16),
        jax.ShapeDtypeStruct((32, D), F32),
    )
    return pl.pallas_call(
        functools.partial(backward_kernel, qb),
        out_shape=shapes,
        scratch_shapes=[
            pltpu.VMEM((HALO + qb, qb), F32),
            pltpu.VMEM((D, ext), BF16),
            pltpu.VMEM((D, ext), BF16),
            pltpu.VMEM((D, own), F32),
            pltpu.VMEM((ext, D), F32),
            pltpu.VMEM((ext, D), F32),
            pltpu.VMEM((ext, 3 * D), BF16),
        ],
        compiler_params=pltpu.CompilerParams(vmem_limit_bytes=56 * MIB),
        name="attention_backward",
    )(q, k, v, g_o, lse, delta, id_row, id_col, n1, x_ext, w_qkv)


def finish_kernel(x_ref, gn_ref, gh_ref, vec_ref, out_ref):
    def block(i, carry):
        rows = rows_of(i * 128, 128)
        xhat, rstd = normalize(x_ref[rows, :].astype(F32))
        out_ref[rows, :] = gh_ref[rows, :] + norm_pull(gn_ref[rows, :], vec_ref[0:1, :], xhat, rstd)
        return carry

    lax.fori_loop(0, x_ref.shape[0] // 128, block, 0)


def finish(x, g_n1, g_h1, vecs):
    return pl.pallas_call(
        finish_kernel,
        out_shape=jax.ShapeDtypeStruct(x.shape, F32),
        compiler_params=pltpu.CompilerParams(vmem_limit_bytes=32 * MIB),
        name="finish",
    )(x, g_n1, g_h1, vecs)


def hops(rows):
    plan, left, step = [], HALO, 1
    while left > 0:
        take = min(rows, left)
        plan.append((step, take))
        left, step = left - take, step + 1
    return plan


def local(
    layer_input,
    segment_ids,
    valid_mask,
    teacher,
    cotangent,
    ln1_gain,
    ln1_bias,
    w_q,
    w_k,
    w_v,
    b_q,
    b_v,
    w_o,
    b_o,
    ln2_gain,
    ln2_bias,
    w_up,
    b_up,
    w_down,
    b_down,
):
    fsdp_size = lax.axis_size("fsdp")
    tensor_size = lax.axis_size("tp")
    place = lax.axis_index("tp")
    own = layer_input.shape[0]
    tokens_all = own * fsdp_size * tensor_size
    rows_d = w_q.shape[0]
    cols_h, cols_f = w_q.shape[1], w_up.shape[1]

    parts = []
    for step, take in hops(own):
        route = [(i, i + step) for i in range(tensor_size - step)]
        parts.insert(0, lax.ppermute(layer_input[own - take :], "tp", route))
    x_ext = jnp.concatenate(parts + [layer_input], axis=0)
    ids = segment_ids + LEN * jnp.arange(segment_ids.shape[0], dtype=jnp.int32)[:, None]
    ids = jnp.concatenate([jnp.full((HALO,), -1, jnp.int32), ids.reshape(-1)])
    ids = lax.dynamic_slice_in_dim(ids, place * own, HALO + own)
    id_row, id_col = ids[None, :], ids[:, None]

    pack = jnp.concatenate([w_q, w_k, w_v, w_o.T, w_up, w_down.T], axis=1)
    count = jnp.sum(valid_mask)
    count_high = count // 256
    vectors = jnp.concatenate([ln1_gain, ln1_bias, b_o, ln2_gain, ln2_bias, b_down])
    heads = jnp.concatenate([b_q.reshape(-1), b_v.reshape(-1), b_up.reshape(-1)])
    digits = jnp.stack([count_high, count - 256 * count_high]).astype(BF16)
    small = jnp.concatenate([vectors, heads, digits])
    width = pack.shape[1]
    lines = -(-small.shape[0] // width)
    small = jnp.pad(small, (0, lines * width - small.shape[0])).reshape(lines, width)
    shard = jnp.concatenate([pack, small], axis=0)
    every = lax.all_gather(lax.all_gather(shard, "tp", axis=0), "fsdp", axis=0)
    big = every[:, :, :rows_d, :]

    def columns(start, size):
        part = big[:, :, :, start : start + size]
        return part.transpose(0, 2, 1, 3).reshape(fsdp_size * rows_d, tensor_size * size)

    w_qkv = jnp.concatenate([columns(j * cols_h, cols_h) for j in range(3)], axis=1)
    w_ot = columns(3 * cols_h, cols_h)
    w_up_all = columns(4 * cols_h, cols_f)
    w_dn_all = columns(4 * cols_h + cols_f, cols_f)
    few = every[:, :, rows_d:, :].reshape(fsdp_size, tensor_size, -1).astype(F32)
    six = few[:, 0, : 6 * rows_d].reshape(fsdp_size, 6, rows_d).transpose(1, 0, 2).reshape(6, D)
    at = 6 * rows_d

    def by_head(start, shape):
        size = shape[0] * shape[1]
        part = few[:, :, start : start + size].reshape((fsdp_size, tensor_size) + shape)
        return part.transpose(1, 2, 0, 3).reshape(1, -1)

    bq_all = by_head(at, b_q.shape)
    at += b_q.size
    bv_all = by_head(at, b_v.shape)
    at += b_v.size
    bup_all = by_head(at, b_up.shape)
    at += b_up.size
    valid_total = 256.0 * jnp.sum(few[:, :, at]) + jnp.sum(few[:, :, at + 1])

    vec_one = jnp.concatenate([six[0:2], bq_all, bv_all], axis=0)
    vec_two = jnp.stack([six[2], six[3], six[4], six[5]])
    n1, q, k, v, o, lse = attention_forward(x_ext, vec_one, w_qkv, id_row, id_col, own)
    scale = (tokens_all / valid_total).reshape(1, 1)
    mask = valid_mask.astype(F32)[:, None]
    layer_out, g_h1, g_o, delta, g_wo, g_wup, g_wdn, small_two, g_bup = middle(
        scale, layer_input, o, teacher, cotangent, mask, vec_two, bup_all, w_ot, w_up_all, w_dn_all
    )
    gn_halo, gn_own, g_qkv, small_one = attention_backward(
        q, k, v, g_o, lse, delta, id_row, id_col, n1, x_ext, w_qkv
    )

    total = gn_own
    left = HALO
    for step, take in hops(own):
        route = [(i + step, i) for i in range(tensor_size - step)]
        part = lax.ppermute(gn_halo[left - take : left], "tp", route).astype(F32)
        total = total + jnp.pad(part, ((own - take, 0), (0, 0)))
        left -= take
    grad_input = finish(layer_input, total, g_h1, vec_one)

    def split(grad, size):
        return grad.reshape(fsdp_size, rows_d, tensor_size, size).transpose(0, 2, 1, 3)

    g_pack = jnp.concatenate(
        [split(g_qkv[:, j * D : (j + 1) * D], cols_h) for j in range(3)]
        + [split(g_wo, cols_h), split(g_wup, cols_f), split(g_wdn, cols_f)],
        axis=3,
    )
    ones = [small_one[8 * j : 8 * j + 8].sum(0) for j in range(2)] + [small_one[16], small_one[24]]
    twos = [small_two[8 * j : 8 * j + 8].sum(0) for j in range(5)]
    loss_part = 0.5 / D * jnp.sum(twos[1]) / valid_total
    six_grads = jnp.stack([ones[0], ones[1], twos[4], twos[2], twos[3], twos[0]])
    six_grads = six_grads.reshape(6, fsdp_size, 1, rows_d).transpose(1, 2, 0, 3)
    six_grads = jnp.broadcast_to(
        six_grads.reshape(fsdp_size, 1, -1), (fsdp_size, tensor_size, 6 * rows_d)
    )

    def heads_of(grad, shape):
        part = grad.reshape((tensor_size, shape[0], fsdp_size, shape[1]))
        return part.transpose(2, 0, 1, 3).reshape(fsdp_size, tensor_size, -1)

    loss_high = loss_part.astype(BF16).astype(F32)
    losses = jnp.broadcast_to(
        jnp.stack([loss_high, loss_part - loss_high]), (fsdp_size, tensor_size, 2)
    )
    g_small = jnp.concatenate(
        [
            six_grads,
            heads_of(ones[2], b_q.shape),
            heads_of(ones[3], b_v.shape),
            heads_of(g_bup[0], b_up.shape),
            losses,
        ],
        axis=2,
    ).astype(BF16)
    g_small = jnp.pad(g_small, ((0, 0), (0, 0), (0, lines * width - g_small.shape[2])))
    g_all = jnp.concatenate([g_pack, g_small.reshape(fsdp_size, tensor_size, lines, width)], axis=2)
    mine = lax.psum_scatter(g_all, "fsdp", scatter_dimension=0, tiled=False)
    mine = lax.psum_scatter(mine, "tp", scatter_dimension=0, tiled=False).astype(F32)
    g_mat, g_vec = mine[:rows_d], mine[rows_d:].reshape(-1)
    c3, c4 = 3 * cols_h, 4 * cols_h
    six_out = g_vec[: 6 * rows_d].reshape(6, rows_d)
    at = 6 * rows_d
    grad_bq = g_vec[at : at + b_q.size].reshape(b_q.shape)
    at += b_q.size
    grad_bv = g_vec[at : at + b_v.size].reshape(b_v.shape)
    at += b_v.size
    grad_bup = g_vec[at : at + b_up.size].reshape(b_up.shape)
    at += b_up.size
    loss = g_vec[at] + g_vec[at + 1]
    return (
        layer_out,
        loss,
        grad_input,
        six_out[0],
        six_out[1],
        g_mat[:, 0:cols_h],
        g_mat[:, cols_h : 2 * cols_h],
        g_mat[:, 2 * cols_h : c3],
        grad_bq,
        grad_bv,
        g_mat[:, c3:c4].T,
        six_out[2],
        six_out[3],
        six_out[4],
        g_mat[:, c4 : c4 + cols_f],
        grad_bup,
        g_mat[:, c4 + cols_f :].T,
        six_out[5],
    )


def solution(mesh):
    tokens = P(("fsdp", "tp"), None)
    rows, crossed, heads = P("fsdp"), P("fsdp", "tp"), P("tp", "fsdp")
    placed = (
        tokens,
        P("fsdp", None),
        P(("fsdp", "tp")),
        tokens,
        tokens,
        rows,
        rows,
        crossed,
        crossed,
        crossed,
        heads,
        heads,
        heads,
        rows,
        rows,
        rows,
        crossed,
        heads,
        heads,
        rows,
    )
    given = (
        tokens,
        P(),
        tokens,
        rows,
        rows,
        crossed,
        crossed,
        crossed,
        heads,
        heads,
        heads,
        rows,
        rows,
        rows,
        crossed,
        heads,
        heads,
        rows,
    )
    return jax.shard_map(local, mesh=mesh, in_specs=placed, out_specs=given, check_vma=False)
```

```python
import functools

import jax
import jax.numpy as jnp
from jax import lax
from jax.experimental import pallas as pl
from jax.experimental.pallas import tpu as pltpu
from jax.sharding import PartitionSpec as P

D = 512
H = 8
HD = 64
LEN = 1024
HALO = 512
PAIR = 2 * HD
NEG = -1e30
SCALE = HD ** (-0.5)
F32 = jnp.float32
BF16 = jnp.bfloat16
MIB = 1 << 20

CONTRACT_LAST = (((1,), (1,)), ((), ()))


def dot(a, b):
    return jnp.dot(a, b, preferred_element_type=F32)


def dot_t(a, b):
    return lax.dot_general(a, b, CONTRACT_LAST, preferred_element_type=F32)


def normalize(x):
    center = x - jnp.mean(x, axis=-1, keepdims=True)
    rstd = lax.rsqrt(jnp.mean(center * center, axis=-1, keepdims=True) + 1e-05)
    return center * rstd, rstd


def norm_pull(g, gain, xhat, rstd):
    gx = g * gain
    return rstd * (
        gx
        - jnp.mean(gx, axis=-1, keepdims=True)
        - xhat * jnp.mean(gx * xhat, axis=-1, keepdims=True)
    )


def fold(x):
    return jnp.sum(x.reshape(x.shape[0] // 8, 8, x.shape[1]), axis=0)


def rows_of(start, size, unit=128):
    return pl.ds(pl.multiple_of(start, unit), size)


def forward_kernel(
    qb, x_ref, vec_ref, w_ref, idr_ref, idc_ref, n_ref, q_ref, k_ref, v_ref, o_ref, lse_ref, bias_ref, stat_ref
):
    ext, own = x_ref.shape[0], o_ref.shape[0]
    window = HALO + qb

    def project(i, carry):
        rows = rows_of(i * 128, 128)
        xhat, _ = normalize(x_ref[rows, :].astype(F32))
        n1 = (xhat * vec_ref[0:1, :] + vec_ref[1:2, :]).astype(BF16)
        n_ref[rows, :] = n1
        k_ref[rows, :] = dot(n1, w_ref[:, D : 2 * D]).astype(BF16)
        v_ref[rows, :] = (dot(n1, w_ref[:, 2 * D : 3 * D]) + vec_ref[3:4, :]).astype(BF16)
        return carry

    lax.fori_loop(0, ext // 128, project, 0)

    def project_q(i, carry):
        rows = rows_of(i * 128, 128)
        q = dot(n_ref[rows_of(HALO + i * 128, 128), :], w_ref[:, 0:D]) + vec_ref[2:3, :]
        q_ref[rows, :] = q.astype(BF16) * jnp.asarray(SCALE, BF16)
        return carry

    lax.fori_loop(0, own // 128, project_q, 0)

    def query_block(i, carry):
        first = i * qb
        key = lax.broadcasted_iota(jnp.int32, (qb, window), 1)
        query = lax.broadcasted_iota(jnp.int32, (qb, window), 0)
        same = idc_ref[rows_of(HALO + first, qb), :] == idr_ref[:, rows_of(first, window)]
        bias_ref[...] = jnp.where(same & (key <= query + HALO), 0.0, NEG)

        def pair(g, inner):
            lanes = rows_of(g * PAIR, PAIR)
            lane = lax.broadcasted_iota(jnp.int32, (qb, PAIR), 1)
            keys = k_ref[rows_of(first, window), lanes]
            values = v_ref[rows_of(first, window), lanes]
            both = q_ref[rows_of(first, qb), lanes]
            got = None
            for h in range(2):
                mine = (lane < HD) if h == 0 else (lane >= HD)
                s = dot_t(jnp.where(mine, both, jnp.zeros_like(both)), keys) + bias_ref[...]
                top = jnp.max(s, axis=-1, keepdims=True)
                p = jnp.exp(s - top)
                total = jnp.sum(p, axis=-1, keepdims=True)
                o = dot(p.astype(BF16), values) / total
                got = o if h == 0 else jnp.where(mine, o, got)
                stat_ref[...] = jnp.where(lane == 2 * g + h, top + jnp.log(total), stat_ref[...])
            o_ref[rows_of(first, qb), lanes] = got.astype(BF16)
            return inner

        lax.fori_loop(0, D // PAIR, pair, 0)
        lse_ref[:, rows_of(first, qb)] = jnp.transpose(stat_ref[...])[0:H, :]
        return carry

    stat_ref[...] = jnp.zeros_like(stat_ref)
    lax.fori_loop(0, own // qb, query_block, 0)


def attention_forward(x_ext, vecs, w_qkv, id_row, id_col, own):
    ext = x_ext.shape[0]
    qb = 256 if own % 256 == 0 else 128
    shapes = (
        jax.ShapeDtypeStruct((ext, D), BF16),
        jax.ShapeDtypeStruct((own, D), BF16),
        jax.ShapeDtypeStruct((ext, D), BF16),
        jax.ShapeDtypeStruct((ext, D), BF16),
        jax.ShapeDtypeStruct((own, D), BF16),
        jax.ShapeDtypeStruct((H, own), F32),
    )
    return pl.pallas_call(
        functools.partial(forward_kernel, qb),
        out_shape=shapes,
        scratch_shapes=[pltpu.VMEM((qb, HALO + qb), F32), pltpu.VMEM((qb, 128), F32)],
        compiler_params=pltpu.CompilerParams(vmem_limit_bytes=48 * MIB),
        name="attention_forward",
    )(x_ext, vecs, w_qkv, id_row, id_col)


def middle_kernel(
    rb,
    scale_ref,
    x_ref,
    o_ref,
    teacher_ref,
    cot_ref,
    mask_ref,
    vec_ref,
    bup_ref,
    wo_ref,
    wup_ref,
    wdn_ref,
    out_ref,
    gh_ref,
    go_ref,
    delta_ref,
    gwo_ref,
    gwup_ref,
    gwdn_ref,
    small_ref,
    gbup_ref,
    slope_ref,
    hid_ref,
    gpre_ref,
    n2t_ref,
    gmlpt_ref,
    gattnt_ref,
):
    own = x_ref.shape[0]
    ff = wup_ref.shape[1]
    chunk = 512
    small_ref[...] = jnp.zeros_like(small_ref)
    head_of = lax.broadcasted_iota(jnp.int32, (D, 128), 0) // HD
    pick = (head_of == lax.broadcasted_iota(jnp.int32, (D, 128), 1)).astype(BF16)

    def block(i, carry):
        rows = rows_of(i * rb, rb)
        out_bias, gain, offset, down_bias = (vec_ref[j : j + 1, :] for j in range(4))
        h1 = x_ref[rows, :].astype(F32) + dot_t(o_ref[rows, :], wo_ref[...]) + out_bias
        xhat, rstd = normalize(h1)
        n2 = xhat * gain + offset
        n2_low = n2.astype(BF16)
        n2t_ref[:, rows] = jnp.transpose(n2).astype(BF16)
        for c in range(0, ff, chunk):
            pre = dot(n2_low, wup_ref[:, c : c + chunk]) + bup_ref[:, c : c + chunk]
            s = jax.nn.sigmoid(1.702 * pre)
            value = pre * s
            hid_ref[rows, c : c + chunk] = value.astype(BF16)
            slope_ref[:, c : c + chunk] = s + 1.702 * value * (1.0 - s)
        out = h1 + dot_t(hid_ref[rows, :], wdn_ref[...]) + down_bias
        out_ref[rows, :] = out.astype(BF16)
        valid = mask_ref[rows, :]
        diff = (out - teacher_ref[rows, :].astype(F32)) * valid
        g_out = cot_ref[rows, :].astype(F32) + scale_ref[0, 0] * diff
        small_ref[0:8, :] += fold(g_out)
        small_ref[8:16, :] += fold(diff * diff)
        g_mlp = g_out.astype(BF16)
        gmlpt_ref[:, rows] = jnp.transpose(g_out).astype(BF16)
        for c in range(0, ff, chunk):
            g_hid = dot(g_mlp, wdn_ref[:, c : c + chunk])
            gpre_ref[rows, c : c + chunk] = (g_hid * slope_ref[:, c : c + chunk]).astype(BF16)
        g_n2 = dot_t(gpre_ref[rows, :], wup_ref[...])
        small_ref[16:24, :] += fold(g_n2 * xhat)
        small_ref[24:32, :] += fold(g_n2)
        g_h1 = g_out + norm_pull(g_n2, gain, xhat, rstd)
        gh_ref[rows, :] = g_h1
        small_ref[32:40, :] += fold(g_h1)
        gattnt_ref[:, rows] = jnp.transpose(g_h1).astype(BF16)
        g_o = dot(g_h1.astype(BF16), wo_ref[...]).astype(BF16)
        go_ref[rows, :] = g_o
        product = g_o.astype(F32) * o_ref[rows, :].astype(F32)
        high = product.astype(BF16)
        low = (product - high.astype(F32)).astype(BF16)
        delta_ref[:, rows] = jnp.transpose(dot(high, pick) + dot(low, pick))[0:H, :]
        return carry

    lax.fori_loop(0, own // rb, block, 0)
    ones = jnp.ones((8, own), BF16)

    def grads(i, carry):
        cols = rows_of(i * chunk, chunk)
        gwdn_ref[:, cols] = dot(gmlpt_ref[...], hid_ref[:, cols]).astype(BF16)
        gwup_ref[:, cols] = dot(n2t_ref[...], gpre_ref[:, cols]).astype(BF16)
        gbup_ref[:, cols] = dot(ones, gpre_ref[:, cols])
        return carry

    lax.fori_loop(0, ff // chunk, grads, 0)
    gwo_ref[...] = dot(gattnt_ref[...], o_ref[...]).astype(BF16)


def middle(scale, x, o, teacher, cot, mask, vecs, b_up, w_o, w_up, w_dn):
    own, ff = x.shape[0], w_up.shape[1]
    rb = 256 if own % 256 == 0 else 128
    shapes = (
        jax.ShapeDtypeStruct((own, D), BF16),
        jax.ShapeDtypeStruct((own, D), F32),
        jax.ShapeDtypeStruct((own, D), BF16),
        jax.ShapeDtypeStruct((H, own), F32),
        jax.ShapeDtypeStruct((D, D), BF16),
        jax.ShapeDtypeStruct((D, ff), BF16),
        jax.ShapeDtypeStruct((D, ff), BF16),
        jax.ShapeDtypeStruct((40, D), F32),
        jax.ShapeDtypeStruct((8, ff), F32),
    )
    whole = pl.BlockSpec(memory_space=pltpu.VMEM)
    return pl.pallas_call(
        functools.partial(middle_kernel, rb),
        out_shape=shapes,
        in_specs=[pl.BlockSpec(memory_space=pltpu.SMEM)] + [whole] * 10,
        out_specs=[whole] * len(shapes),
        scratch_shapes=[
            pltpu.VMEM((rb, ff), F32),
            pltpu.VMEM((own, ff), BF16),
            pltpu.VMEM((own, ff), BF16),
            pltpu.VMEM((D, own), BF16),
            pltpu.VMEM((D, own), BF16),
            pltpu.VMEM((D, own), BF16),
        ],
        compiler_params=pltpu.CompilerParams(vmem_limit_bytes=56 * MIB),
        name="middle",
    )(scale, x, o, teacher, cot, mask, vecs, b_up, w_o, w_up, w_dn)


def backward_kernel(
    qb,
    q_ref,
    k_ref,
    v_ref,
    go_ref,
    lse_ref,
    delta_ref,
    idr_ref,
    idc_ref,
    n_ref,
    x_ref,
    w_ref,
    gn_halo_ref,
    gn_ref,
    gw_ref,
    small_ref,
    bias_ref,
    kt_ref,
    nt_ref,
    dqt_ref,
    dk_ref,
    dv_ref,
    g_ref,
):
    ext, own = k_ref.shape[0], q_ref.shape[0]
    window = HALO + qb
    dk_ref[...] = jnp.zeros_like(dk_ref)
    dv_ref[...] = jnp.zeros_like(dv_ref)
    small_ref[...] = jnp.zeros_like(small_ref)

    def turn(i, carry):
        rows = rows_of(i * 128, 128)
        kt_ref[:, rows] = jnp.transpose(k_ref[rows, :].astype(F32)).astype(BF16)
        nt_ref[:, rows] = jnp.transpose(n_ref[rows, :].astype(F32)).astype(BF16)
        return carry

    lax.fori_loop(0, ext // 128, turn, 0)

    def query_block(i, carry):
        first = i * qb
        key = lax.broadcasted_iota(jnp.int32, (window, qb), 0)
        query = lax.broadcasted_iota(jnp.int32, (window, qb), 1)
        same = idc_ref[rows_of(first, window), :] == idr_ref[:, rows_of(HALO + first, qb)]
        bias_ref[...] = jnp.where(same & (key <= query + HALO), 0.0, NEG)

        def pair(g, inner):
            lanes = rows_of(g * PAIR, PAIR)
            lane = lax.broadcasted_iota(jnp.int32, (qb, PAIR), 1)
            keys = k_ref[rows_of(first, window), lanes]
            values = v_ref[rows_of(first, window), lanes]
            both_q = q_ref[rows_of(first, qb), lanes]
            both_g = go_ref[rows_of(first, qb), lanes]
            all_lse = lse_ref[:, rows_of(first, qb)]
            all_delta = delta_ref[:, rows_of(first, qb)]
            line = lax.broadcasted_iota(jnp.int32, (H, qb), 0)
            dk, dv = None, None
            for h in range(2):
                head = 2 * g + h
                mine = (lane < HD) if h == 0 else (lane >= HD)
                q = jnp.where(mine, both_q, jnp.zeros_like(both_q))
                g_o = jnp.where(mine, both_g, jnp.zeros_like(both_g))
                lse = jnp.sum(jnp.where(line == head, all_lse, 0.0), axis=0, keepdims=True)
                delta = jnp.sum(jnp.where(line == head, all_delta, 0.0), axis=0, keepdims=True)
                p = jnp.exp(dot_t(keys, q) + bias_ref[...] - lse)
                ds = (p * (dot_t(values, g_o) - delta)).astype(BF16)
                dv_h = dot(p.astype(BF16), g_o)
                dk_h = dot(ds, q)
                dk, dv = (dk_h, dv_h) if h == 0 else (dk + dk_h, dv + dv_h)
                dqt_ref[rows_of(head * HD, HD, HD), rows_of(first, qb)] = dot(
                    kt_ref[rows_of(head * HD, HD, HD), rows_of(first, window)], ds
                )
            dk_ref[rows_of(first, window), lanes] += dk
            dv_ref[rows_of(first, window), lanes] += dv
            return inner

        lax.fori_loop(0, D // PAIR, pair, 0)
        return carry

    lax.fori_loop(0, own // qb, query_block, 0)

    def gather(i, carry):
        rows = rows_of(i * 128, 128)
        g_ref[rows, D : 2 * D] = dk_ref[rows, :].astype(BF16)
        g_ref[rows, 2 * D : 3 * D] = dv_ref[rows, :].astype(BF16)
        return carry

    lax.fori_loop(0, ext // 128, gather, 0)

    def gather_q(i, carry):
        cols = rows_of(i * 128, 128)
        g_ref[rows_of(HALO + i * 128, 128), 0:D] = (jnp.transpose(dqt_ref[:, cols]) * SCALE).astype(BF16)
        return carry

    lax.fori_loop(0, own // 128, gather_q, 0)

    def norms(rows, g_n1):
        xhat, _ = normalize(x_ref[rows, :].astype(F32))
        small_ref[0:8, :] += fold(g_n1 * xhat)
        small_ref[8:16, :] += fold(g_n1)

    def pull_halo(i, carry):
        rows = rows_of(i * 128, 128)
        g_n1 = dot_t(g_ref[rows, D : 3 * D], w_ref[:, D : 3 * D])
        gn_halo_ref[rows, :] = g_n1.astype(BF16)
        norms(rows, g_n1)
        return carry

    lax.fori_loop(0, HALO // 128, pull_halo, 0)

    def pull_own(i, carry):
        rows = rows_of(HALO + i * 128, 128)
        g_n1 = dot_t(g_ref[rows, :], w_ref[...])
        gn_ref[rows_of(i * 128, 128), :] = g_n1
        norms(rows, g_n1)
        return carry

    lax.fori_loop(0, own // 128, pull_own, 0)
    gw_ref[:, 0:D] = dot(nt_ref[:, HALO:], g_ref[HALO:, 0:D]).astype(BF16)
    gw_ref[:, D : 2 * D] = dot(nt_ref[...], g_ref[:, D : 2 * D]).astype(BF16)
    gw_ref[:, 2 * D : 3 * D] = dot(nt_ref[...], g_ref[:, 2 * D : 3 * D]).astype(BF16)
    small_ref[16:24, :] = dot(jnp.ones((8, own), BF16), g_ref[HALO:, 0:D])
    small_ref[24:32, :] = dot(jnp.ones((8, ext), BF16), g_ref[:, 2 * D : 3 * D])


def attention_backward(q, k, v, g_o, lse, delta, id_row, id_col, n1, x_ext, w_qkv):
    ext, own = k.shape[0], q.shape[0]
    qb = 256 if own % 256 == 0 else 128
    shapes = (
        jax.ShapeDtypeStruct((HALO, D), BF16),
        jax.ShapeDtypeStruct((own, D), F32),
        jax.ShapeDtypeStruct((D, 3 * D), BF16),
        jax.ShapeDtypeStruct((32, D), F32),
    )
    return pl.pallas_call(
        functools.partial(backward_kernel, qb),
        out_shape=shapes,
        scratch_shapes=[
            pltpu.VMEM((HALO + qb, qb), F32),
            pltpu.VMEM((D, ext), BF16),
            pltpu.VMEM((D, ext), BF16),
            pltpu.VMEM((D, own), F32),
            pltpu.VMEM((ext, D), F32),
            pltpu.VMEM((ext, D), F32),
            pltpu.VMEM((ext, 3 * D), BF16),
        ],
        compiler_params=pltpu.CompilerParams(vmem_limit_bytes=56 * MIB),
        name="attention_backward",
    )(q, k, v, g_o, lse, delta, id_row, id_col, n1, x_ext, w_qkv)


def finish_kernel(x_ref, gn_ref, gh_ref, vec_ref, out_ref):
    def block(i, carry):
        rows = rows_of(i * 128, 128)
        xhat, rstd = normalize(x_ref[rows, :].astype(F32))
        out_ref[rows, :] = gh_ref[rows, :] + norm_pull(gn_ref[rows, :], vec_ref[0:1, :], xhat, rstd)
        return carry

    lax.fori_loop(0, x_ref.shape[0] // 128, block, 0)


def finish(x, g_n1, g_h1, vecs):
    return pl.pallas_call(
        finish_kernel,
        out_shape=jax.ShapeDtypeStruct(x.shape, F32),
        compiler_params=pltpu.CompilerParams(vmem_limit_bytes=32 * MIB),
        name="finish",
    )(x, g_n1, g_h1, vecs)


def hops(rows):
    plan, left, step = [], HALO, 1
    while left > 0:
        take = min(rows, left)
        plan.append((step, take))
        left, step = left - take, step + 1
    return plan


def local(
    layer_input,
    segment_ids,
    valid_mask,
    teacher,
    cotangent,
    ln1_gain,
    ln1_bias,
    w_q,
    w_k,
    w_v,
    b_q,
    b_v,
    w_o,
    b_o,
    ln2_gain,
    ln2_bias,
    w_up,
    b_up,
    w_down,
    b_down,
):
    fsdp_size = lax.axis_size("fsdp")
    tensor_size = lax.axis_size("tp")
    place = lax.axis_index("tp")
    own = layer_input.shape[0]
    tokens_all = own * fsdp_size * tensor_size
    rows_d = w_q.shape[0]
    cols_h, cols_f = w_q.shape[1], w_up.shape[1]

    parts = []
    for step, take in hops(own):
        route = [(i, i + step) for i in range(tensor_size - step)]
        parts.insert(0, lax.ppermute(layer_input[own - take :], "tp", route))
    x_ext = jnp.concatenate(parts + [layer_input], axis=0)
    ids = segment_ids + LEN * jnp.arange(segment_ids.shape[0], dtype=jnp.int32)[:, None]
    ids = jnp.concatenate([jnp.full((HALO,), -1, jnp.int32), ids.reshape(-1)])
    ids = lax.dynamic_slice_in_dim(ids, place * own, HALO + own)
    id_row, id_col = ids[None, :], ids[:, None]

    pack = jnp.concatenate([w_q, w_k, w_v, w_o.T, w_up, w_down.T], axis=1)
    count = jnp.sum(valid_mask)
    count_high = count // 256
    vectors = jnp.concatenate([ln1_gain, ln1_bias, b_o, ln2_gain, ln2_bias, b_down])
    heads = jnp.concatenate([b_q.reshape(-1), b_v.reshape(-1), b_up.reshape(-1)])
    digits = jnp.stack([count_high, count - 256 * count_high]).astype(BF16)
    small = jnp.concatenate([vectors, heads, digits])
    width = pack.shape[1]
    lines = -(-small.shape[0] // width)
    small = jnp.pad(small, (0, lines * width - small.shape[0])).reshape(lines, width)
    shard = jnp.concatenate([pack, small], axis=0)
    every = lax.all_gather(lax.all_gather(shard, "tp", axis=0), "fsdp", axis=0)
    big = every[:, :, :rows_d, :]

    def columns(start, size):
        part = big[:, :, :, start : start + size]
        return part.transpose(0, 2, 1, 3).reshape(fsdp_size * rows_d, tensor_size * size)

    w_qkv = jnp.concatenate([columns(j * cols_h, cols_h) for j in range(3)], axis=1)
    w_ot = columns(3 * cols_h, cols_h)
    w_up_all = columns(4 * cols_h, cols_f)
    w_dn_all = columns(4 * cols_h + cols_f, cols_f)
    few = every[:, :, rows_d:, :].reshape(fsdp_size, tensor_size, -1).astype(F32)
    six = few[:, 0, : 6 * rows_d].reshape(fsdp_size, 6, rows_d).transpose(1, 0, 2).reshape(6, D)
    at = 6 * rows_d

    def by_head(start, shape):
        size = shape[0] * shape[1]
        part = few[:, :, start : start + size].reshape((fsdp_size, tensor_size) + shape)
        return part.transpose(1, 2, 0, 3).reshape(1, -1)

    bq_all = by_head(at, b_q.shape)
    at += b_q.size
    bv_all = by_head(at, b_v.shape)
    at += b_v.size
    bup_all = by_head(at, b_up.shape)
    at += b_up.size
    valid_total = 256.0 * jnp.sum(few[:, :, at]) + jnp.sum(few[:, :, at + 1])

    vec_one = jnp.concatenate([six[0:2], bq_all, bv_all], axis=0)
    vec_two = jnp.stack([six[2], six[3], six[4], six[5]])
    n1, q, k, v, o, lse = attention_forward(x_ext, vec_one, w_qkv, id_row, id_col, own)
    scale = (tokens_all / valid_total).reshape(1, 1)
    mask = valid_mask.astype(F32)[:, None]
    layer_out, g_h1, g_o, delta, g_wo, g_wup, g_wdn, small_two, g_bup = middle(
        scale, layer_input, o, teacher, cotangent, mask, vec_two, bup_all, w_ot, w_up_all, w_dn_all
    )
    gn_halo, gn_own, g_qkv, small_one = attention_backward(
        q, k, v, g_o, lse, delta, id_row, id_col, n1, x_ext, w_qkv
    )

    total = gn_own
    left = HALO
    for step, take in hops(own):
        route = [(i + step, i) for i in range(tensor_size - step)]
        part = lax.ppermute(gn_halo[left - take : left], "tp", route).astype(F32)
        total = total + jnp.pad(part, ((own - take, 0), (0, 0)))
        left -= take
    grad_input = finish(layer_input, total, g_h1, vec_one)

    def split(grad, size):
        return grad.reshape(fsdp_size, rows_d, tensor_size, size).transpose(0, 2, 1, 3)

    g_pack = jnp.concatenate(
        [split(g_qkv[:, j * D : (j + 1) * D], cols_h) for j in range(3)]
        + [split(g_wo, cols_h), split(g_wup, cols_f), split(g_wdn, cols_f)],
        axis=3,
    )
    ones = [small_one[8 * j : 8 * j + 8].sum(0) for j in range(2)] + [small_one[16], small_one[24]]
    twos = [small_two[8 * j : 8 * j + 8].sum(0) for j in range(5)]
    loss_part = 0.5 / D * jnp.sum(twos[1]) / valid_total
    six_grads = jnp.stack([ones[0], ones[1], twos[4], twos[2], twos[3], twos[0]])
    six_grads = six_grads.reshape(6, fsdp_size, 1, rows_d).transpose(1, 2, 0, 3)
    six_grads = jnp.broadcast_to(
        six_grads.reshape(fsdp_size, 1, -1), (fsdp_size, tensor_size, 6 * rows_d)
    )

    def heads_of(grad, shape):
        part = grad.reshape((tensor_size, shape[0], fsdp_size, shape[1]))
        return part.transpose(2, 0, 1, 3).reshape(fsdp_size, tensor_size, -1)

    loss_high = loss_part.astype(BF16).astype(F32)
    losses = jnp.broadcast_to(
        jnp.stack([loss_high, loss_part - loss_high]), (fsdp_size, tensor_size, 2)
    )
    g_small = jnp.concatenate(
        [
            six_grads,
            heads_of(ones[2], b_q.shape),
            heads_of(ones[3], b_v.shape),
            heads_of(g_bup[0], b_up.shape),
            losses,
        ],
        axis=2,
    ).astype(BF16)
    g_small = jnp.pad(g_small, ((0, 0), (0, 0), (0, lines * width - g_small.shape[2])))
    g_all = jnp.concatenate([g_pack, g_small.reshape(fsdp_size, tensor_size, lines, width)], axis=2)
    mine = lax.psum_scatter(g_all, "fsdp", scatter_dimension=0, tiled=False)
    mine = lax.psum_scatter(mine, "tp", scatter_dimension=0, tiled=False).astype(F32)
    g_mat, g_vec = mine[:rows_d], mine[rows_d:].reshape(-1)
    c3, c4 = 3 * cols_h, 4 * cols_h
    six_out = g_vec[: 6 * rows_d].reshape(6, rows_d)
    at = 6 * rows_d
    grad_bq = g_vec[at : at + b_q.size].reshape(b_q.shape)
    at += b_q.size
    grad_bv = g_vec[at : at + b_v.size].reshape(b_v.shape)
    at += b_v.size
    grad_bup = g_vec[at : at + b_up.size].reshape(b_up.shape)
    at += b_up.size
    loss = g_vec[at] + g_vec[at + 1]
    return (
        layer_out,
        loss,
        grad_input,
        six_out[0],
        six_out[1],
        g_mat[:, 0:cols_h],
        g_mat[:, cols_h : 2 * cols_h],
        g_mat[:, 2 * cols_h : c3],
        grad_bq,
        grad_bv,
        g_mat[:, c3:c4].T,
        six_out[2],
        six_out[3],
        six_out[4],
        g_mat[:, c4 : c4 + cols_f],
        grad_bup,
        g_mat[:, c4 + cols_f :].T,
        six_out[5],
    )


ROWS = D // 8
EXTRA = 8
COLS = D // 4
FFC = 512
WA = 3 * COLS
WF = COLS + 2 * FFC
MASKS_A = (0, 2, 4, 6, 1, 3, 5, 7)
SMALL = pl.CostEstimate(flops=1, bytes_accessed=1, transcendentals=0)
ANY = pl.BlockSpec(memory_space=pl.ANY)
VMEM = pl.BlockSpec(memory_space=pltpu.VMEM)


def params(mib):
    return pltpu.CompilerParams(vmem_limit_bytes=mib * MIB)


def lane_of(shape):
    return lax.broadcasted_iota(jnp.int32, shape, len(shape) - 1)


def pack_kernel(
    wq_ref, wk_ref, wv_ref, wo_ref, wup_ref, wdn_ref, g1, b1, bo, g2, b2, bd, bq, bv, bup, mask_ref, a_ref, f_ref
):
    me = lax.axis_index("fsdp")
    a_ref[0:ROWS, 0:COLS] = wq_ref[...]
    a_ref[0:ROWS, COLS : 2 * COLS] = wk_ref[...]
    a_ref[0:ROWS, 2 * COLS : 3 * COLS] = wv_ref[...]
    f_ref[:, 0:COLS] = wo_ref[...]
    f_ref[:, COLS : COLS + FFC] = wup_ref[...]
    f_ref[:, COLS + FFC :] = wdn_ref[...]
    count = jnp.sum(mask_ref[...].astype(F32)).reshape(1, 1)
    high = jnp.floor(count / 256.0)
    lane = lane_of((1, 128))
    digits = jnp.where(lane == 0, high, jnp.where(lane == 1, count - 256.0 * high, 0.0))
    vectors = [r[...].astype(F32).reshape(1, ROWS) for r in (g1, b1, bo, g2, b2, bd)]
    rows = [jnp.concatenate([v, v], axis=1) for v in vectors] + [digits, jnp.zeros((1, 128), F32)]
    a_ref[ROWS:, 0:128] = jnp.concatenate(rows, axis=0).astype(BF16)

    def spread(ref):
        block = ref[...].astype(F32)
        count, piece = block.shape
        lanes = count * HD
        lane = lane_of((1, lanes))
        row = jnp.zeros((1, lanes), F32)
        for i in range(count):
            for j in range(piece):
                at = i * HD + me * piece + j
                row = jnp.where(lane == at, block[i : i + 1, j : j + 1], row)
        return row

    ups = spread(bup)
    rows = [spread(bq), spread(bv)] + [ups[:, 128 * j : 128 * j + 128] for j in range(4)]
    rows.append(jnp.zeros((2, 128), F32))
    a_ref[ROWS:, 128:256] = jnp.concatenate(rows, axis=0).astype(BF16)
    a_ref[ROWS:, 256:384] = jnp.zeros((EXTRA, 128), BF16)


def pack_weights(args):
    return pl.pallas_call(
        pack_kernel,
        out_shape=(
            jax.ShapeDtypeStruct((ROWS + EXTRA, WA), BF16),
            jax.ShapeDtypeStruct((ROWS, WF), BF16),
        ),
        compiler_params=params(60),
        name="pack_weights",
    )(*args)


def project_kernel(
    tokens_all, x_ref, halo_ref, p0, p1, p2, p3, p4, p5, p6, p7,
    q_ref, k_ref, v_ref, kt_ref, nt_ref, w_ref, vec_ref, bup_ref, scale_ref, ext_ref, head_ref, sem
):
    me, place = lax.axis_index("fsdp"), lax.axis_index("tp")
    pieces = (p0, p1, p2, p3, p4, p5, p6, p7)

    def each(act):
        for j, (ref, mask) in enumerate(zip(pieces, MASKS_A)):
            owner = lax.bitwise_xor(me, mask)
            for s in range(4):
                tp = lax.bitwise_and(place - s + 4, 3)
                act(j, ref, owner, s, tp)

    def start_ext(j, ref, owner, s, tp):
        pltpu.make_async_copy(ref.at[s, pl.ds(ROWS, EXTRA), :], ext_ref.at[4 * j + s], sem.at[0]).start()

    def start_w(j, ref, owner, s, tp):
        pltpu.make_async_copy(
            ref.at[s, pl.ds(0, ROWS), :],
            w_ref.at[rows_of(owner * ROWS, ROWS, ROWS), rows_of(tp * WA, WA)],
            sem.at[1],
        ).start()

    each(start_ext)
    each(start_w)
    pltpu.make_async_copy(ext_ref, ext_ref, sem.at[0]).wait()
    lane = lane_of((EXTRA, D))
    vectors = jnp.zeros((EXTRA, D), F32)
    total = jnp.zeros((EXTRA, 128), F32)
    for j, mask in enumerate(MASKS_A):
        block = ext_ref[4 * j, :, 0:128].astype(F32)
        wide = jnp.concatenate([block] * 4, axis=1)
        vectors = jnp.where(lane // ROWS == lax.bitwise_xor(me, mask), wide, vectors)
        for s in range(4):
            total += ext_ref[4 * j + s, :, 0:128].astype(F32)
    vec_ref[...] = vectors
    valid = 256.0 * total[6:7, 0:1] + total[6:7, 1:2]
    scale_ref[...] = jnp.concatenate(
        [jnp.broadcast_to(tokens_all / valid, (4, 128)), jnp.broadcast_to(0.5 / D / valid, (4, 128))], axis=0
    )
    for s in range(4):
        tp = lax.bitwise_and(place - s + 4, 3)
        block = jnp.zeros((EXTRA, 128), F32)
        for j in range(8):
            block += ext_ref[4 * j + s, :, 128:256].astype(F32)
        head_ref[:, rows_of(tp * COLS, COLS)] = block
        for i in range(4):
            bup_ref[:, rows_of(tp * FFC + 128 * i, 128)] = jnp.broadcast_to(block[2 + i : 3 + i], (8, 128))
    pltpu.make_async_copy(w_ref, w_ref, sem.at[1]).wait()
    gain, offset = vectors[0:1], vectors[1:2]

    def rows_done(x, at):
        xhat, _ = normalize(x.astype(F32))
        n1 = xhat * gain + offset
        turned = jnp.transpose(n1).astype(BF16)
        for i in range(8):
            slot = lax.bitwise_xor(me, i)
            nt_ref[rows_of(slot * ROWS, ROWS, ROWS), rows_of(at, 128)] = turned[ROWS * i : ROWS * (i + 1)]
        made = dot(n1.astype(BF16), w_ref[...])
        for t in range(4):
            lanes = slice(t * COLS, (t + 1) * COLS)
            k = made[:, t * WA + COLS : t * WA + 2 * COLS]
            k_ref[rows_of(at, 128), lanes] = k.astype(BF16)
            kt_ref[lanes, rows_of(at, 128)] = jnp.transpose(k).astype(BF16)
            v = made[:, t * WA + 2 * COLS : (t + 1) * WA] + head_ref[1:2, lanes]
            v_ref[rows_of(at, 128), lanes] = v.astype(BF16)
        return made

    def halo_rows(i, carry):
        rows_done(halo_ref[rows_of(i * 128, 128), :], i * 128)
        return carry

    lax.fori_loop(0, HALO // 128, halo_rows, 0)

    def own_rows(i, carry):
        rows = rows_of(i * 128, 128)
        made = rows_done(x_ref[rows, :], HALO + i * 128)
        for t in range(4):
            lanes = slice(t * COLS, (t + 1) * COLS)
            q = (made[:, t * WA : t * WA + COLS] + head_ref[0:1, lanes]).astype(BF16)
            q_ref[rows, lanes] = q * jnp.asarray(SCALE, BF16)
        return carry

    lax.fori_loop(0, x_ref.shape[0] // 128, own_rows, 0)


def project(x, halo, pieces, tokens_all):
    own = x.shape[0]
    ext = HALO + own
    shapes = (
        jax.ShapeDtypeStruct((own, D), BF16),
        jax.ShapeDtypeStruct((ext, D), BF16),
        jax.ShapeDtypeStruct((ext, D), BF16),
        jax.ShapeDtypeStruct((D, ext), BF16),
        jax.ShapeDtypeStruct((D, ext), BF16),
        jax.ShapeDtypeStruct((D, 4 * WA), BF16),
        jax.ShapeDtypeStruct((EXTRA, D), F32),
        jax.ShapeDtypeStruct((8, 4 * FFC), F32),
        jax.ShapeDtypeStruct((8, 128), F32),
    )
    return pl.pallas_call(
        functools.partial(project_kernel, float(tokens_all)),
        out_shape=shapes,
        in_specs=[VMEM, VMEM] + [ANY] * 8,
        out_specs=[VMEM] * len(shapes),
        scratch_shapes=[
            pltpu.VMEM((32, EXTRA, WA), BF16),
            pltpu.VMEM((EXTRA, D), F32),
            pltpu.SemaphoreType.DMA((2,)),
        ],
        compiler_params=params(20),
        cost_estimate=SMALL,
        name="project",
    )(x, halo, *pieces)


def attend_kernel(q_ref, k_ref, v_ref, idr_ref, idc_ref, o_ref, lse_ref, bias_ref, stat_ref):
    own = o_ref.shape[0]
    qb, window = bias_ref.shape[1:]

    @pl.when(pl.program_id(0) == 0)
    def _():
        stat_ref[...] = jnp.zeros_like(stat_ref)

        def mask(i, carry):
            first = i * qb
            key = lax.broadcasted_iota(jnp.int32, (qb, window), 1)
            query = lax.broadcasted_iota(jnp.int32, (qb, window), 0)
            same = idc_ref[rows_of(HALO + first, qb), :] == idr_ref[:, rows_of(first, window)]
            bias_ref[i] = jnp.where(same & (key <= query + HALO), 0.0, NEG)
            return carry

        lax.fori_loop(0, own // qb, mask, 0)

    def query_block(i, carry):
        first = i * qb
        lane = lane_of((qb, PAIR))
        keys, values = k_ref[rows_of(first, window), :], v_ref[rows_of(first, window), :]
        both = q_ref[rows_of(first, qb), :]
        got = None
        for h in range(2):
            mine = (lane < HD) if h == 0 else (lane >= HD)
            s = dot_t(jnp.where(mine, both, jnp.zeros_like(both)), keys) + bias_ref[i]
            top = jnp.max(s, axis=-1, keepdims=True)
            p = jnp.exp(s - top)
            total = jnp.sum(p, axis=-1, keepdims=True)
            o = dot(p.astype(BF16), values) / total
            got = o if h == 0 else jnp.where(mine, o, got)
            stat_ref[:, h : h + 1] = top + jnp.log(total)
        o_ref[rows_of(first, qb), :] = got.astype(BF16)
        lse_ref[0, :, rows_of(first, qb)] = jnp.transpose(stat_ref[...])[0:8, :]
        return carry

    lax.fori_loop(0, own // qb, query_block, 0)


def attend(q, k, v, id_row, id_col, first_pair, pairs):
    own, ext = q.shape[0], k.shape[0]
    qb = 256
    at = lambda i: (0, first_pair + i)
    flat = lambda i: (0, 0)
    return pl.pallas_call(
        attend_kernel,
        grid=(pairs,),
        out_shape=(
            jax.ShapeDtypeStruct((own, pairs * PAIR), BF16),
            jax.ShapeDtypeStruct((pairs, 8, own), F32),
        ),
        in_specs=[
            pl.BlockSpec((own, PAIR), at),
            pl.BlockSpec((ext, PAIR), at),
            pl.BlockSpec((ext, PAIR), at),
            pl.BlockSpec((1, ext), flat),
            pl.BlockSpec((ext, 1), flat),
        ],
        out_specs=[pl.BlockSpec((own, PAIR), lambda i: (0, i)), pl.BlockSpec((1, 8, own), lambda i: (i, 0, 0))],
        scratch_shapes=[pltpu.VMEM((own // qb, qb, HALO + qb), F32), pltpu.VMEM((qb, 128), F32)],
        compiler_params=params(14),
        cost_estimate=SMALL,
        name="attend",
    )(q, k, v, id_row, id_col)


PIECES_F = ((0, (0, 1, 2, 3)), (2, (0, 1, 2, 3)), (4, (0, 1, 2, 3)), (6, (0, 1)), (6, (2, 3)))


def central_kernel(
    rb, x_ref, oa_ref, ob_ref, teacher_ref, cot_ref, mask_ref, vec_ref, bup_ref, scale_ref,
    p0, p1, p2, p3, p4, p5, p6, p7, p8, p9,
    out_ref, gh_ref, go_ref, delta_ref, theirs_ref, mine_ref, small_ref, gbup_ref,
    wo_ref, wup_ref, wdn_ref, o_ref, slope_ref, hid_ref, gpre_ref, n2t_ref, gmlpt_ref, gattnt_ref, sem
):
    me, place = lax.axis_index("fsdp"), lax.axis_index("tp")
    own, ff = x_ref.shape[0], 4 * FFC
    pieces = (p0, p1, p2, p3, p4, p5, p6, p7, p8, p9)
    parts = ((wo_ref, 0, COLS), (wup_ref, COLS, FFC), (wdn_ref, COLS + FFC, FFC))
    for n, (dst, start, size) in enumerate(parts):
        for j, ref in enumerate(pieces):
            mask, steps = PIECES_F[j % 5]
            owner = lax.bitwise_xor(me, mask + j // 5)
            for i, s in enumerate(steps):
                tp = lax.bitwise_and(place - s + 4, 3)
                pltpu.make_async_copy(
                    ref.at[i, :, pl.ds(start, size)],
                    dst.at[rows_of(owner * ROWS, ROWS, ROWS), rows_of(tp * size, size)],
                    sem.at[n],
                ).start()
    small_ref[...] = jnp.zeros_like(small_ref)
    o_ref[:, 0 : D // 2] = oa_ref[...]
    o_ref[:, D // 2 :] = ob_ref[...]
    head_of = lax.broadcasted_iota(jnp.int32, (D, 128), 0) // HD
    pick = (head_of == lax.broadcasted_iota(jnp.int32, (D, 128), 1)).astype(BF16)
    out_bias, gain, offset, down_bias = (vec_ref[j : j + 1, :] for j in range(2, 6))

    def turn(dst, rows, value):
        turned = jnp.transpose(value).astype(BF16)
        for i in range(8):
            slot = lax.bitwise_xor(me, i)
            dst[rows_of(slot * ROWS, ROWS, ROWS), rows] = turned[ROWS * i : ROWS * (i + 1)]

    for n, (dst, _, _) in enumerate(parts):
        pltpu.make_async_copy(dst, dst, sem.at[n]).wait()

    def block(i, carry):
        rows = rows_of(i * rb, rb)
        h1 = x_ref[rows, :].astype(F32) + dot_t(o_ref[rows, :], wo_ref[...]) + out_bias
        xhat, rstd = normalize(h1)
        n2 = xhat * gain + offset
        n2_low = n2.astype(BF16)
        turn(n2t_ref, rows, n2)
        for c in range(0, ff, FFC):
            pre = dot(n2_low, wup_ref[:, c : c + FFC]) + bup_ref[0:1, c : c + FFC]
            s = jax.nn.sigmoid(1.702 * pre)
            value = pre * s
            hid_ref[rows, c : c + FFC] = value.astype(BF16)
            slope_ref[:, c : c + FFC] = s + 1.702 * value * (1.0 - s)
        out = h1 + dot_t(hid_ref[rows, :], wdn_ref[...]) + down_bias
        out_ref[rows, :] = out.astype(BF16)
        diff = (out - teacher_ref[rows, :].astype(F32)) * mask_ref[rows, :]
        g_out = cot_ref[rows, :].astype(F32) + scale_ref[0:1, 0:1] * diff
        small_ref[0:8, :] += fold(g_out)
        small_ref[8:16, :] += fold(diff * diff)
        g_mlp = g_out.astype(BF16)
        turn(gmlpt_ref, rows, g_out)
        for c in range(0, ff, FFC):
            g_hid = dot(g_mlp, wdn_ref[:, c : c + FFC])
            gpre_ref[rows, c : c + FFC] = (g_hid * slope_ref[:, c : c + FFC]).astype(BF16)
        g_n2 = dot_t(gpre_ref[rows, :], wup_ref[...])
        small_ref[16:24, :] += fold(g_n2 * xhat)
        small_ref[24:32, :] += fold(g_n2)
        g_h1 = g_out + norm_pull(g_n2, gain, xhat, rstd)
        gh_ref[rows, :] = g_h1
        small_ref[32:40, :] += fold(g_h1)
        turn(gattnt_ref, rows, g_h1)
        g_o = dot(g_h1.astype(BF16), wo_ref[...]).astype(BF16)
        go_ref[rows, :] = g_o
        product = g_o.astype(F32) * o_ref[rows, :].astype(F32)
        high = product.astype(BF16)
        low = (product - high.astype(F32)).astype(BF16)
        turned = jnp.transpose(dot(high, pick) + dot(low, pick))
        for g in range(4):
            delta_ref[g, 0:2, rows] = turned[2 * g : 2 * g + 2, :]
        return carry

    lax.fori_loop(0, own // rb, block, 0)
    ones = jnp.ones((8, own), BF16)

    def keep(grad, s, start, size):
        low = grad.astype(BF16)
        for r in range(8):
            dst = theirs_ref if r % 2 else mine_ref
            dst[r // 2, s, :, start : start + size] = low[ROWS * r : ROWS * (r + 1)]

    def grads(s, carry):
        tp = lax.bitwise_and(place + s, 3)
        cols = rows_of(tp * FFC, FFC)
        keep(dot(gattnt_ref[...], o_ref[:, rows_of(tp * COLS, COLS)]), s, 0, COLS)
        keep(dot(n2t_ref[...], gpre_ref[:, cols]), s, COLS, FFC)
        keep(dot(gmlpt_ref[...], hid_ref[:, cols]), s, COLS + FFC, FFC)
        gbup_ref[:, cols] = dot(ones, gpre_ref[:, cols])
        return carry

    lax.fori_loop(0, 4, grads, 0)


def central(x, o_a, o_b, teacher, cot, mask, vec, bup, scale, pieces):
    own = x.shape[0]
    rb = 256
    shapes = (
        jax.ShapeDtypeStruct((own, D), BF16),
        jax.ShapeDtypeStruct((own, D), F32),
        jax.ShapeDtypeStruct((own, D), BF16),
        jax.ShapeDtypeStruct((4, 8, own), F32),
        jax.ShapeDtypeStruct((4, 4, ROWS, WF), BF16),
        jax.ShapeDtypeStruct((4, 4, ROWS, WF), BF16),
        jax.ShapeDtypeStruct((40, D), F32),
        jax.ShapeDtypeStruct((8, 4 * FFC), F32),
    )
    return pl.pallas_call(
        functools.partial(central_kernel, rb),
        out_shape=shapes,
        in_specs=[VMEM] * 9 + [ANY] * 10,
        out_specs=[VMEM] * len(shapes),
        scratch_shapes=[
            pltpu.VMEM((D, D), BF16),
            pltpu.VMEM((D, 4 * FFC), BF16),
            pltpu.VMEM((D, 4 * FFC), BF16),
            pltpu.VMEM((own, D), BF16),
            pltpu.VMEM((rb, 4 * FFC), F32),
            pltpu.VMEM((own, 4 * FFC), BF16),
            pltpu.VMEM((own, 4 * FFC), BF16),
            pltpu.VMEM((D, own), BF16),
            pltpu.VMEM((D, own), BF16),
            pltpu.VMEM((D, own), BF16),
            pltpu.SemaphoreType.DMA((3,)),
        ],
        compiler_params=params(36),
        cost_estimate=SMALL,
        name="central",
    )(x, o_a, o_b, teacher, cot, mask, vec, bup, scale, *pieces)


def pair_core(q_ref, k_ref, v_ref, go_ref, lse_ref, delta_ref, idr_ref, idc_ref, kt_ref, nt_ref,
              g_ref, theirs_ref, mine_ref, bias_ref, dqt_ref, dk_ref, dv_ref):
    ext, own = k_ref.shape[0], q_ref.shape[0]
    window, qb = bias_ref.shape
    dk_ref[...] = jnp.zeros_like(dk_ref)
    dv_ref[...] = jnp.zeros_like(dv_ref)

    def query_block(i, carry):
        first = i * qb
        key = lax.broadcasted_iota(jnp.int32, (window, qb), 0)
        query = lax.broadcasted_iota(jnp.int32, (window, qb), 1)
        same = idc_ref[rows_of(first, window), :] == idr_ref[:, rows_of(HALO + first, qb)]
        bias_ref[...] = jnp.where(same & (key <= query + HALO), 0.0, NEG)
        lane = lane_of((qb, PAIR))
        keys, values = k_ref[rows_of(first, window), :], v_ref[rows_of(first, window), :]
        both_q, both_g = q_ref[rows_of(first, qb), :], go_ref[rows_of(first, qb), :]
        all_lse, all_delta = lse_ref[0, :, rows_of(first, qb)], delta_ref[0, :, rows_of(first, qb)]
        for h in range(2):
            mine = (lane < HD) if h == 0 else (lane >= HD)
            q = jnp.where(mine, both_q, jnp.zeros_like(both_q))
            g_o = jnp.where(mine, both_g, jnp.zeros_like(both_g))
            p = jnp.exp(dot_t(keys, q) + bias_ref[...] - all_lse[h : h + 1])
            ds = (p * (dot_t(values, g_o) - all_delta[h : h + 1])).astype(BF16)
            dv_ref[rows_of(first, window), :] += dot(p.astype(BF16), g_o)
            dk_ref[rows_of(first, window), :] += dot(ds, q)
            dqt_ref[h * HD : (h + 1) * HD, rows_of(first, qb)] = dot(
                kt_ref[h * HD : (h + 1) * HD, rows_of(first, window)], ds
            )
        return carry

    lax.fori_loop(0, own // qb, query_block, 0)
    g_ref[0:HALO, 0:COLS] = jnp.zeros((HALO, COLS), BF16)

    def gather(i, carry):
        rows = rows_of(i * 128, 128)
        g_ref[rows, COLS : 2 * COLS] = dk_ref[rows, :].astype(BF16)
        g_ref[rows, 2 * COLS :] = dv_ref[rows, :].astype(BF16)
        return carry

    lax.fori_loop(0, ext // 128, gather, 0)

    def gather_q(i, carry):
        cols = rows_of(i * 128, 128)
        g_ref[rows_of(HALO + i * 128, 128), 0:COLS] = (jnp.transpose(dqt_ref[:, cols]) * SCALE).astype(BF16)
        return carry

    lax.fori_loop(0, own // 128, gather_q, 0)
    low = dot(nt_ref[...], g_ref[...]).astype(BF16)
    for r in range(8):
        dst = theirs_ref if r % 2 else mine_ref
        dst[r // 2, 0, 0:ROWS, :] = low[ROWS * r : ROWS * (r + 1)]


def pair_kernel(sc_ref, q_ref, k_ref, v_ref, go_ref, lse_ref, delta_ref, idr_ref, idc_ref, kt_ref, nt_ref, *rest):
    g_ref, theirs_ref, mine_ref, *scratch = rest[-7:]
    pair_core(q_ref, k_ref, v_ref, go_ref, lse_ref, delta_ref, idr_ref, idc_ref, kt_ref, nt_ref,
              g_ref, theirs_ref, mine_ref, *scratch)


def pair_backward(step, where, q, k, v, g_o, lse, delta, id_row, id_col, kt, nt, before):
    own, ext = q.shape[0], k.shape[0]
    qb = 256

    def at(i, sc):
        return (0, lax.bitwise_and(sc[0] + step, 3))

    def deep(i, sc):
        return (lax.bitwise_and(sc[0] + step, 3), 0, 0)

    def down(i, sc):
        return (lax.bitwise_and(sc[0] + step, 3), 0)

    flat = lambda i, sc: (0, 0)
    send = jax.ShapeDtypeStruct((4, 4, ROWS + EXTRA, WA), BF16)
    block = pl.BlockSpec((4, 1, ROWS + EXTRA, WA), lambda i, sc: (0, step, 0, 0))
    return pl.pallas_call(
        pair_kernel,
        grid_spec=pltpu.PrefetchScalarGridSpec(
            num_scalar_prefetch=1,
            grid=(1,),
            in_specs=[
                pl.BlockSpec((own, PAIR), at),
                pl.BlockSpec((ext, PAIR), at),
                pl.BlockSpec((ext, PAIR), at),
                pl.BlockSpec((own, PAIR), at),
                pl.BlockSpec((1, 8, own), deep),
                pl.BlockSpec((1, 8, own), deep),
                pl.BlockSpec((1, ext), flat),
                pl.BlockSpec((ext, 1), flat),
                pl.BlockSpec((PAIR, ext), down),
                pl.BlockSpec((D, ext), flat),
            ]
            + [ANY] * len(before),
            out_specs=[pl.BlockSpec((ext, WA), flat), block, block],
            scratch_shapes=[
                pltpu.VMEM((HALO + qb, qb), F32),
                pltpu.VMEM((PAIR, own), F32),
                pltpu.VMEM((ext, PAIR), F32),
                pltpu.VMEM((ext, PAIR), F32),
            ],
        ),
        out_shape=(jax.ShapeDtypeStruct((ext, WA), BF16), send, send),
        input_output_aliases={11: 1, 12: 2} if before else {},
        compiler_params=params(14),
        cost_estimate=SMALL,
        name="pair_backward",
    )(where, q, k, v, g_o, lse, delta, id_row, id_col, kt, nt, *before)


def pull_kernel(x_ref, halo_ref, g0, g1, g2, g3, w_ref, small_in, gbup_ref, scale_ref, theirs_in, mine_in,
                gn_halo_ref, gn_ref, theirs_ref, mine_ref, small_ref, bias_ref):
    me, place = lax.axis_index("fsdp"), lax.axis_index("tp")
    own, ext = x_ref.shape[0], g0.shape[0]
    grads = (g0, g1, g2, g3)
    small_ref[...] = jnp.zeros_like(small_ref)

    def pull(at, skip):
        total = None
        for s, ref in enumerate(grads):
            tp = lax.bitwise_and(place + s, 3)
            part = dot_t(
                ref[rows_of(at, 128), skip:], w_ref[:, rows_of(tp * WA + skip, WA - skip)]
            )
            total = part if total is None else total + part
        return total

    def norms(x, g_n1):
        xhat, _ = normalize(x.astype(F32))
        small_ref[0:8, :] += fold(g_n1 * xhat)
        small_ref[8:16, :] += fold(g_n1)

    def pull_halo(i, carry):
        rows = rows_of(i * 128, 128)
        g_n1 = pull(i * 128, COLS)
        gn_halo_ref[rows, :] = g_n1.astype(BF16)
        norms(halo_ref[rows, :], g_n1)
        return carry

    lax.fori_loop(0, HALO // 128, pull_halo, 0)

    def pull_own(i, carry):
        rows = rows_of(i * 128, 128)
        g_n1 = pull(HALO + i * 128, 0)
        gn_ref[rows, :] = g_n1
        norms(x_ref[rows, :], g_n1)
        return carry

    lax.fori_loop(0, own // 128, pull_own, 0)

    ones = jnp.ones((8, ext), BF16)
    for s, ref in enumerate(grads):
        bias_ref[s] = dot(ones, ref[...])[0:1]
    sums = lambda ref, j: jnp.sum(ref[8 * j : 8 * j + 8, :], axis=0, keepdims=True)
    loss = jnp.sum(sums(small_in, 1), axis=1, keepdims=True) * scale_ref[4:5, 0:1]
    vectors = jnp.concatenate(
        [sums(small_ref, 0), sums(small_ref, 1), sums(small_in, 4), sums(small_in, 2), sums(small_in, 3),
         sums(small_in, 0), jnp.zeros((2, D), F32)],
        axis=0,
    )
    high = loss.astype(BF16).astype(F32)
    row, lane = lax.broadcasted_iota(jnp.int32, (EXTRA, 128), 0), lane_of((EXTRA, 128))
    for r in range(8):
        owner = lax.bitwise_xor(me, r)
        block = pltpu.roll(vectors, lax.rem(D - owner * ROWS, D), 1)[:, 0:128]
        block = jnp.where((row == 6) & (lane == 0), high, block)
        block = jnp.where((row == 6) & (lane == 1), loss - high, block)
        dst = theirs_ref if r % 2 else mine_ref
        for s in range(4):
            tp = lax.bitwise_and(place + s, 3)
            ups = gbup_ref[0:1, rows_of(tp * FFC, FFC)]
            mids = jnp.concatenate(
                [bias_ref[s][:, 0:COLS], bias_ref[s][:, 2 * COLS :]]
                + [ups[:, 128 * j : 128 * j + 128] for j in range(4)]
                + [jnp.zeros((2, 128), F32)],
                axis=0,
            )
            dst[r // 2, s, :, 0:128] = block.astype(BF16)
            dst[r // 2, s, :, 128:256] = mids.astype(BF16)
            dst[r // 2, s, :, 256:384] = jnp.zeros((EXTRA, 128), BF16)


def pull_back(x, halo, grads, w, small_two, gbup, scale, theirs, mine):
    own, ext = x.shape[0], grads[0].shape[0]
    full = lambda a: pl.BlockSpec(a.shape, lambda i: (0,) * a.ndim)
    send = jax.ShapeDtypeStruct(theirs.shape, BF16)
    tail = pl.BlockSpec((4, 4, EXTRA, WA), lambda i: (0, 0, ROWS // EXTRA, 0))
    given = (x, halo, *grads, w, small_two, gbup, scale)
    return pl.pallas_call(
        pull_kernel,
        grid=(1,),
        in_specs=[full(a) for a in given] + [ANY, ANY],
        out_specs=[
            pl.BlockSpec((HALO, D), lambda i: (0, 0)),
            pl.BlockSpec((own, D), lambda i: (0, 0)),
            tail,
            tail,
        ],
        out_shape=(
            jax.ShapeDtypeStruct((HALO, D), BF16),
            jax.ShapeDtypeStruct((own, D), F32),
            send,
            send,
        ),
        scratch_shapes=[pltpu.VMEM((16, D), F32), pltpu.VMEM((4, 1, WA), F32)],
        input_output_aliases={10: 2, 11: 3},
        compiler_params=params(20),
        cost_estimate=SMALL,
        name="pull_back",
    )(*given, theirs, mine)


def close_kernel(x_ref, gn_ref, back_ref, gh_ref, vec_ref, out_ref):
    own = x_ref.shape[0]

    def block(at, extra):
        rows = rows_of(at, 128)
        xhat, rstd = normalize(x_ref[rows, :].astype(F32))
        g_n1 = gn_ref[rows, :] + extra
        out_ref[rows, :] = gh_ref[rows, :] + norm_pull(g_n1, vec_ref[0:1, :], xhat, rstd)

    def first(i, carry):
        block(i * 128, 0.0)
        return carry

    def second(i, carry):
        block(own - HALO + i * 128, back_ref[rows_of(i * 128, 128), :].astype(F32))
        return carry

    lax.fori_loop(0, (own - HALO) // 128, first, 0)
    lax.fori_loop(0, HALO // 128, second, 0)


def close(x, g_n1, back, g_h1, vec):
    return pl.pallas_call(
        close_kernel,
        out_shape=jax.ShapeDtypeStruct(x.shape, F32),
        compiler_params=params(12),
        cost_estimate=SMALL,
        name="close",
    )(x, g_n1, back, g_h1, vec)


def unpack_f_kernel(k_ref, r1, r2, r3, wo_ref, wup_ref, wdn_ref):
    total = (k_ref[0].astype(F32) + r1[...].astype(F32)) + (r2[...].astype(F32) + r3[...].astype(F32))
    wo_ref[...] = total[:, 0:COLS]
    wup_ref[...] = total[:, COLS : COLS + FFC]
    wdn_ref[...] = total[:, COLS + FFC :]


def unpack_f(k, r1, r2, r3):
    return pl.pallas_call(
        unpack_f_kernel,
        out_shape=(
            jax.ShapeDtypeStruct((ROWS, COLS), F32),
            jax.ShapeDtypeStruct((ROWS, FFC), F32),
            jax.ShapeDtypeStruct((ROWS, FFC), F32),
        ),
        compiler_params=params(8),
        name="unpack_f",
    )(k, r1, r2, r3)


def unpack_a_kernel(k_ref, r1, r2, r3, wq_ref, wk_ref, wv_ref, bq_ref, bv_ref, bup_ref, vec_ref):
    me = lax.axis_index("fsdp")
    total = (k_ref[0].astype(F32) + r1[...].astype(F32)) + (r2[...].astype(F32) + r3[...].astype(F32))
    wq_ref[...] = total[0:ROWS, 0:COLS]
    wk_ref[...] = total[0:ROWS, COLS : 2 * COLS]
    wv_ref[...] = total[0:ROWS, 2 * COLS :]
    vec_ref[...] = total[ROWS:, 0:128]
    mids = pltpu.roll(total[ROWS:, 128:256], lax.rem(128 - me * 8, 128), 1)
    for i in range(2):
        bq_ref[i : i + 1, :] = mids[0:1, i * HD : i * HD + 8]
        bv_ref[i : i + 1, :] = mids[1:2, i * HD : i * HD + 8]
    for i in range(8):
        at = (i % 2) * HD
        bup_ref[i : i + 1, :] = mids[2 + i // 2 : 3 + i // 2, at : at + 8]


def unpack_a(k, r1, r2, r3):
    small = jax.ShapeDtypeStruct((ROWS, COLS), F32)
    return pl.pallas_call(
        unpack_a_kernel,
        out_shape=(
            small,
            small,
            small,
            jax.ShapeDtypeStruct((2, 8), F32),
            jax.ShapeDtypeStruct((2, 8), F32),
            jax.ShapeDtypeStruct((8, 8), F32),
            jax.ShapeDtypeStruct((EXTRA, 128), F32),
        ),
        compiler_params=params(8),
        name="unpack_a",
    )(k, r1, r2, r3)


def to_mask(x, mask):
    return lax.ppermute(x, "fsdp", [(i, i ^ mask) for i in range(8)])


def to_step(x, step):
    return lax.ppermute(x, "tp", [(i, (i + step) % 4) for i in range(4)])


def add(a, b):
    return (a.astype(F32) + b.astype(F32)).astype(BF16)


def after(values, others):
    return lax.optimization_barrier((values, others))[0]


def local_fast(
    layer_input, segment_ids, valid_mask, teacher, cotangent, ln1_gain, ln1_bias, w_q, w_k, w_v, b_q, b_v,
    w_o, b_o, ln2_gain, ln2_bias, w_up, b_up, w_down, b_down
):
    place = lax.axis_index("tp")
    own = layer_input.shape[0]
    tokens_all = own * lax.axis_size("fsdp") * lax.axis_size("tp")

    shard_a, shard_f = pack_weights(
        (w_q, w_k, w_v, w_o.T, w_up, w_down.T, ln1_gain, ln1_bias, b_o, ln2_gain, ln2_bias, b_down, b_q, b_v, b_up,
         valid_mask)
    )
    halo = lax.ppermute(layer_input[own - HALO :], "tp", [(i, i + 1) for i in range(3)])
    line_a = jnp.stack([shard_a] + [to_step(shard_a, s) for s in (1, 2, 3)])
    near_a = [line_a] + [to_mask(line_a, m) for m in (2, 4, 6)]
    pieces_a = near_a + [to_mask(a, 1) for a in near_a]
    shard_f = after(shard_f, pieces_a[4])
    steps_f = [shard_f] + [to_step(shard_f, s) for s in (1, 2, 3)]

    ids = segment_ids + LEN * jnp.arange(segment_ids.shape[0], dtype=jnp.int32)[:, None]
    ids = jnp.concatenate([jnp.full((HALO,), -1, jnp.int32), ids.reshape(-1)])
    ids = lax.dynamic_slice_in_dim(ids, place * own, HALO + own)
    id_row, id_col = ids[None, :], ids[:, None]
    mask = valid_mask.astype(F32)[:, None]
    where = place.reshape(1).astype(jnp.int32)

    q, k, v, kt, nt, w_all, vec, bup, scale = project(layer_input, halo, pieces_a, tokens_all)
    line_f = jnp.stack(after(steps_f, q))
    q_a = after(q, line_f)
    f_x, f_y = to_mask(line_f, 2), to_mask(line_f, 4)
    o_a, lse_a = attend(q_a, k, v, id_row, id_col, 0, 2)
    q_b = after(q, o_a)
    o_b, lse_b = attend(q_b, k, v, id_row, id_col, 2, 2)
    f_x, f_y = after((f_x, f_y), o_b)
    near_f = [line_f, f_x, f_y, to_mask(f_y[0:2], 2), to_mask(f_x[2:4], 4)]
    pieces_f = near_f + [to_mask(a, 1) for a in near_f]
    layer_out, g_h1, g_o, delta, theirs_f, mine_f, small_two, gbup = central(
        layer_input, o_a, o_b, teacher, cotangent, mask, vec, bup, scale, pieces_f
    )
    lse = jnp.concatenate([lse_a, lse_b])

    def backward(step, before):
        return pair_backward(step, where, q, k, v, g_o, lse, delta, id_row, id_col, kt, nt, before)

    g0, *sums = backward(0, ())
    half = add(after(mine_f, g0), to_mask(theirs_f, 1))
    from_x, from_y = to_mask(half[3, 0:2], 2), to_mask(half[3, 2:4], 4)
    sums = after(sums, half)
    g1, *sums = backward(1, sums)
    from_x, from_y = after((from_x, from_y), g1)
    for_x = jnp.concatenate([half[1, 0:2], add(half[1, 2:4], from_y)])
    for_y = jnp.concatenate([add(half[2, 0:2], from_x), half[2, 2:4]])
    got_x, got_y = to_mask(for_x, 2), to_mask(for_y, 4)
    sums = after(sums, (for_x, for_y))
    g2, *sums = backward(2, sums)
    g3, *sums = backward(3, sums)
    got_x, got_y = after((got_x, got_y), g3)
    line = (half[0].astype(F32) + got_x.astype(F32) + got_y.astype(F32)).astype(BF16)
    line_up = [line[s] for s in (1, 2, 3)]
    sums = after(sums, line_up)
    grad_wo, grad_wup, grad_wdn = unpack_f(line, *[to_step(line_up[s - 1], s) for s in (1, 2, 3)])

    gn_halo, gn_own, theirs_a, mine_a = pull_back(
        layer_input, halo, (g0, g1, g2, g3), w_all, small_two, gbup, scale, *sums
    )
    back = lax.ppermute(gn_halo, "tp", [(i + 1, i) for i in range(3)])
    half = add(mine_a, to_mask(theirs_a, 1))
    from_x, from_y, from_xy = (to_mask(half[m], 2 * m) for m in (1, 2, 3))
    line = (half[0].astype(F32) + from_x.astype(F32) + from_y.astype(F32) + from_xy.astype(F32)).astype(BF16)
    grad_wq, grad_wk, grad_wv, grad_bq, grad_bv, grad_bup, few = unpack_a(
        line, *[to_step(line[s], s) for s in (1, 2, 3)]
    )
    grad_input = close(layer_input, gn_own, back, g_h1, vec)
    six = [few[j, 0:ROWS] for j in range(6)]
    loss = few[6, 0] + few[6, 1]
    return (
        layer_out, loss, grad_input, six[0], six[1], grad_wq, grad_wk, grad_wv, grad_bq, grad_bv, grad_wo.T, six[2],
        six[3], six[4], grad_wup, grad_bup, grad_wdn.T, six[5]
    )


def solution(mesh):
    tokens = P(("fsdp", "tp"), None)
    rows, crossed, heads = P("fsdp"), P("fsdp", "tp"), P("tp", "fsdp")
    placed = (
        tokens,
        P("fsdp", None),
        P(("fsdp", "tp")),
        tokens,
        tokens,
        rows,
        rows,
        crossed,
        crossed,
        crossed,
        heads,
        heads,
        heads,
        rows,
        rows,
        rows,
        crossed,
        heads,
        heads,
        rows,
    )
    given = (
        tokens,
        P(),
        tokens,
        rows,
        rows,
        crossed,
        crossed,
        crossed,
        heads,
        heads,
        heads,
        rows,
        rows,
        rows,
        crossed,
        heads,
        heads,
        rows,
    )
    sizes = (mesh.shape["fsdp"], mesh.shape["tp"])
    body = local_fast if sizes == (8, 4) else local
    return jax.shard_map(body, mesh=mesh, in_specs=placed, out_specs=given, check_vma=False)
```

```python
import functools

import jax
import jax.numpy as jnp
from jax import lax
from jax.experimental import pallas as pl
from jax.experimental.pallas import tpu as pltpu
from jax.sharding import PartitionSpec as P

D = 512
H = 8
HD = 64
LEN = 1024
HALO = 512
PAIR = 2 * HD
NEG = -1e30
SCALE = HD ** (-0.5)
F32 = jnp.float32
BF16 = jnp.bfloat16
MIB = 1 << 20

CONTRACT_LAST = (((1,), (1,)), ((), ()))


def dot(a, b):
    return jnp.dot(a, b, preferred_element_type=F32)


def dot_t(a, b):
    return lax.dot_general(a, b, CONTRACT_LAST, preferred_element_type=F32)


def normalize(x):
    center = x - jnp.mean(x, axis=-1, keepdims=True)
    rstd = lax.rsqrt(jnp.mean(center * center, axis=-1, keepdims=True) + 1e-05)
    return center * rstd, rstd


def norm_pull(g, gain, xhat, rstd):
    gx = g * gain
    return rstd * (
        gx
        - jnp.mean(gx, axis=-1, keepdims=True)
        - xhat * jnp.mean(gx * xhat, axis=-1, keepdims=True)
    )


def fold(x):
    return jnp.sum(x.reshape(x.shape[0] // 8, 8, x.shape[1]), axis=0)


def rows_of(start, size, unit=128):
    return pl.ds(pl.multiple_of(start, unit), size)


def forward_kernel(
    qb, x_ref, vec_ref, w_ref, idr_ref, idc_ref, n_ref, q_ref, k_ref, v_ref, o_ref, lse_ref, bias_ref, stat_ref
):
    ext, own = x_ref.shape[0], o_ref.shape[0]
    window = HALO + qb

    def project(i, carry):
        rows = rows_of(i * 128, 128)
        xhat, _ = normalize(x_ref[rows, :].astype(F32))
        n1 = (xhat * vec_ref[0:1, :] + vec_ref[1:2, :]).astype(BF16)
        n_ref[rows, :] = n1
        k_ref[rows, :] = dot(n1, w_ref[:, D : 2 * D]).astype(BF16)
        v_ref[rows, :] = (dot(n1, w_ref[:, 2 * D : 3 * D]) + vec_ref[3:4, :]).astype(BF16)
        return carry

    lax.fori_loop(0, ext // 128, project, 0)

    def project_q(i, carry):
        rows = rows_of(i * 128, 128)
        q = dot(n_ref[rows_of(HALO + i * 128, 128), :], w_ref[:, 0:D]) + vec_ref[2:3, :]
        q_ref[rows, :] = q.astype(BF16) * jnp.asarray(SCALE, BF16)
        return carry

    lax.fori_loop(0, own // 128, project_q, 0)

    def query_block(i, carry):
        first = i * qb
        key = lax.broadcasted_iota(jnp.int32, (qb, window), 1)
        query = lax.broadcasted_iota(jnp.int32, (qb, window), 0)
        same = idc_ref[rows_of(HALO + first, qb), :] == idr_ref[:, rows_of(first, window)]
        bias_ref[...] = jnp.where(same & (key <= query + HALO), 0.0, NEG)

        def pair(g, inner):
            lanes = rows_of(g * PAIR, PAIR)
            lane = lax.broadcasted_iota(jnp.int32, (qb, PAIR), 1)
            keys = k_ref[rows_of(first, window), lanes]
            values = v_ref[rows_of(first, window), lanes]
            both = q_ref[rows_of(first, qb), lanes]
            got = None
            for h in range(2):
                mine = (lane < HD) if h == 0 else (lane >= HD)
                s = dot_t(jnp.where(mine, both, jnp.zeros_like(both)), keys) + bias_ref[...]
                top = jnp.max(s, axis=-1, keepdims=True)
                p = jnp.exp(s - top)
                total = jnp.sum(p, axis=-1, keepdims=True)
                o = dot(p.astype(BF16), values) / total
                got = o if h == 0 else jnp.where(mine, o, got)
                stat_ref[...] = jnp.where(lane == 2 * g + h, top + jnp.log(total), stat_ref[...])
            o_ref[rows_of(first, qb), lanes] = got.astype(BF16)
            return inner

        lax.fori_loop(0, D // PAIR, pair, 0)
        lse_ref[:, rows_of(first, qb)] = jnp.transpose(stat_ref[...])[0:H, :]
        return carry

    stat_ref[...] = jnp.zeros_like(stat_ref)
    lax.fori_loop(0, own // qb, query_block, 0)


def attention_forward(x_ext, vecs, w_qkv, id_row, id_col, own):
    ext = x_ext.shape[0]
    qb = 256 if own % 256 == 0 else 128
    shapes = (
        jax.ShapeDtypeStruct((ext, D), BF16),
        jax.ShapeDtypeStruct((own, D), BF16),
        jax.ShapeDtypeStruct((ext, D), BF16),
        jax.ShapeDtypeStruct((ext, D), BF16),
        jax.ShapeDtypeStruct((own, D), BF16),
        jax.ShapeDtypeStruct((H, own), F32),
    )
    return pl.pallas_call(
        functools.partial(forward_kernel, qb),
        out_shape=shapes,
        scratch_shapes=[pltpu.VMEM((qb, HALO + qb), F32), pltpu.VMEM((qb, 128), F32)],
        compiler_params=pltpu.CompilerParams(vmem_limit_bytes=48 * MIB),
        name="attention_forward",
    )(x_ext, vecs, w_qkv, id_row, id_col)


def middle_kernel(
    rb,
    scale_ref,
    x_ref,
    o_ref,
    teacher_ref,
    cot_ref,
    mask_ref,
    vec_ref,
    bup_ref,
    wo_ref,
    wup_ref,
    wdn_ref,
    out_ref,
    gh_ref,
    go_ref,
    delta_ref,
    gwo_ref,
    gwup_ref,
    gwdn_ref,
    small_ref,
    gbup_ref,
    slope_ref,
    hid_ref,
    gpre_ref,
    n2t_ref,
    gmlpt_ref,
    gattnt_ref,
):
    own = x_ref.shape[0]
    ff = wup_ref.shape[1]
    chunk = 512
    small_ref[...] = jnp.zeros_like(small_ref)
    head_of = lax.broadcasted_iota(jnp.int32, (D, 128), 0) // HD
    pick = (head_of == lax.broadcasted_iota(jnp.int32, (D, 128), 1)).astype(BF16)

    def block(i, carry):
        rows = rows_of(i * rb, rb)
        out_bias, gain, offset, down_bias = (vec_ref[j : j + 1, :] for j in range(4))
        h1 = x_ref[rows, :].astype(F32) + dot_t(o_ref[rows, :], wo_ref[...]) + out_bias
        xhat, rstd = normalize(h1)
        n2 = xhat * gain + offset
        n2_low = n2.astype(BF16)
        n2t_ref[:, rows] = jnp.transpose(n2).astype(BF16)
        for c in range(0, ff, chunk):
            pre = dot(n2_low, wup_ref[:, c : c + chunk]) + bup_ref[:, c : c + chunk]
            s = jax.nn.sigmoid(1.702 * pre)
            value = pre * s
            hid_ref[rows, c : c + chunk] = value.astype(BF16)
            slope_ref[:, c : c + chunk] = s + 1.702 * value * (1.0 - s)
        out = h1 + dot_t(hid_ref[rows, :], wdn_ref[...]) + down_bias
        out_ref[rows, :] = out.astype(BF16)
        valid = mask_ref[rows, :]
        diff = (out - teacher_ref[rows, :].astype(F32)) * valid
        g_out = cot_ref[rows, :].astype(F32) + scale_ref[0, 0] * diff
        small_ref[0:8, :] += fold(g_out)
        small_ref[8:16, :] += fold(diff * diff)
        g_mlp = g_out.astype(BF16)
        gmlpt_ref[:, rows] = jnp.transpose(g_out).astype(BF16)
        for c in range(0, ff, chunk):
            g_hid = dot(g_mlp, wdn_ref[:, c : c + chunk])
            gpre_ref[rows, c : c + chunk] = (g_hid * slope_ref[:, c : c + chunk]).astype(BF16)
        g_n2 = dot_t(gpre_ref[rows, :], wup_ref[...])
        small_ref[16:24, :] += fold(g_n2 * xhat)
        small_ref[24:32, :] += fold(g_n2)
        g_h1 = g_out + norm_pull(g_n2, gain, xhat, rstd)
        gh_ref[rows, :] = g_h1
        small_ref[32:40, :] += fold(g_h1)
        gattnt_ref[:, rows] = jnp.transpose(g_h1).astype(BF16)
        g_o = dot(g_h1.astype(BF16), wo_ref[...]).astype(BF16)
        go_ref[rows, :] = g_o
        product = g_o.astype(F32) * o_ref[rows, :].astype(F32)
        high = product.astype(BF16)
        low = (product - high.astype(F32)).astype(BF16)
        delta_ref[:, rows] = jnp.transpose(dot(high, pick) + dot(low, pick))[0:H, :]
        return carry

    lax.fori_loop(0, own // rb, block, 0)
    ones = jnp.ones((8, own), BF16)

    def grads(i, carry):
        cols = rows_of(i * chunk, chunk)
        gwdn_ref[:, cols] = dot(gmlpt_ref[...], hid_ref[:, cols]).astype(BF16)
        gwup_ref[:, cols] = dot(n2t_ref[...], gpre_ref[:, cols]).astype(BF16)
        gbup_ref[:, cols] = dot(ones, gpre_ref[:, cols])
        return carry

    lax.fori_loop(0, ff // chunk, grads, 0)
    gwo_ref[...] = dot(gattnt_ref[...], o_ref[...]).astype(BF16)


def middle(scale, x, o, teacher, cot, mask, vecs, b_up, w_o, w_up, w_dn):
    own, ff = x.shape[0], w_up.shape[1]
    rb = 256 if own % 256 == 0 else 128
    shapes = (
        jax.ShapeDtypeStruct((own, D), BF16),
        jax.ShapeDtypeStruct((own, D), F32),
        jax.ShapeDtypeStruct((own, D), BF16),
        jax.ShapeDtypeStruct((H, own), F32),
        jax.ShapeDtypeStruct((D, D), BF16),
        jax.ShapeDtypeStruct((D, ff), BF16),
        jax.ShapeDtypeStruct((D, ff), BF16),
        jax.ShapeDtypeStruct((40, D), F32),
        jax.ShapeDtypeStruct((8, ff), F32),
    )
    whole = pl.BlockSpec(memory_space=pltpu.VMEM)
    return pl.pallas_call(
        functools.partial(middle_kernel, rb),
        out_shape=shapes,
        in_specs=[pl.BlockSpec(memory_space=pltpu.SMEM)] + [whole] * 10,
        out_specs=[whole] * len(shapes),
        scratch_shapes=[
            pltpu.VMEM((rb, ff), F32),
            pltpu.VMEM((own, ff), BF16),
            pltpu.VMEM((own, ff), BF16),
            pltpu.VMEM((D, own), BF16),
            pltpu.VMEM((D, own), BF16),
            pltpu.VMEM((D, own), BF16),
        ],
        compiler_params=pltpu.CompilerParams(vmem_limit_bytes=56 * MIB),
        name="middle",
    )(scale, x, o, teacher, cot, mask, vecs, b_up, w_o, w_up, w_dn)


def backward_kernel(
    qb,
    q_ref,
    k_ref,
    v_ref,
    go_ref,
    lse_ref,
    delta_ref,
    idr_ref,
    idc_ref,
    n_ref,
    x_ref,
    w_ref,
    gn_halo_ref,
    gn_ref,
    gw_ref,
    small_ref,
    bias_ref,
    kt_ref,
    nt_ref,
    dqt_ref,
    dk_ref,
    dv_ref,
    g_ref,
):
    ext, own = k_ref.shape[0], q_ref.shape[0]
    window = HALO + qb
    dk_ref[...] = jnp.zeros_like(dk_ref)
    dv_ref[...] = jnp.zeros_like(dv_ref)
    small_ref[...] = jnp.zeros_like(small_ref)

    def turn(i, carry):
        rows = rows_of(i * 128, 128)
        kt_ref[:, rows] = jnp.transpose(k_ref[rows, :].astype(F32)).astype(BF16)
        nt_ref[:, rows] = jnp.transpose(n_ref[rows, :].astype(F32)).astype(BF16)
        return carry

    lax.fori_loop(0, ext // 128, turn, 0)

    def query_block(i, carry):
        first = i * qb
        key = lax.broadcasted_iota(jnp.int32, (window, qb), 0)
        query = lax.broadcasted_iota(jnp.int32, (window, qb), 1)
        same = idc_ref[rows_of(first, window), :] == idr_ref[:, rows_of(HALO + first, qb)]
        bias_ref[...] = jnp.where(same & (key <= query + HALO), 0.0, NEG)

        def pair(g, inner):
            lanes = rows_of(g * PAIR, PAIR)
            lane = lax.broadcasted_iota(jnp.int32, (qb, PAIR), 1)
            keys = k_ref[rows_of(first, window), lanes]
            values = v_ref[rows_of(first, window), lanes]
            both_q = q_ref[rows_of(first, qb), lanes]
            both_g = go_ref[rows_of(first, qb), lanes]
            all_lse = lse_ref[:, rows_of(first, qb)]
            all_delta = delta_ref[:, rows_of(first, qb)]
            line = lax.broadcasted_iota(jnp.int32, (H, qb), 0)
            dk, dv = None, None
            for h in range(2):
                head = 2 * g + h
                mine = (lane < HD) if h == 0 else (lane >= HD)
                q = jnp.where(mine, both_q, jnp.zeros_like(both_q))
                g_o = jnp.where(mine, both_g, jnp.zeros_like(both_g))
                lse = jnp.sum(jnp.where(line == head, all_lse, 0.0), axis=0, keepdims=True)
                delta = jnp.sum(jnp.where(line == head, all_delta, 0.0), axis=0, keepdims=True)
                p = jnp.exp(dot_t(keys, q) + bias_ref[...] - lse)
                ds = (p * (dot_t(values, g_o) - delta)).astype(BF16)
                dv_h = dot(p.astype(BF16), g_o)
                dk_h = dot(ds, q)
                dk, dv = (dk_h, dv_h) if h == 0 else (dk + dk_h, dv + dv_h)
                dqt_ref[rows_of(head * HD, HD, HD), rows_of(first, qb)] = dot(
                    kt_ref[rows_of(head * HD, HD, HD), rows_of(first, window)], ds
                )
            dk_ref[rows_of(first, window), lanes] += dk
            dv_ref[rows_of(first, window), lanes] += dv
            return inner

        lax.fori_loop(0, D // PAIR, pair, 0)
        return carry

    lax.fori_loop(0, own // qb, query_block, 0)

    def gather(i, carry):
        rows = rows_of(i * 128, 128)
        g_ref[rows, D : 2 * D] = dk_ref[rows, :].astype(BF16)
        g_ref[rows, 2 * D : 3 * D] = dv_ref[rows, :].astype(BF16)
        return carry

    lax.fori_loop(0, ext // 128, gather, 0)

    def gather_q(i, carry):
        cols = rows_of(i * 128, 128)
        g_ref[rows_of(HALO + i * 128, 128), 0:D] = (jnp.transpose(dqt_ref[:, cols]) * SCALE).astype(BF16)
        return carry

    lax.fori_loop(0, own // 128, gather_q, 0)

    def norms(rows, g_n1):
        xhat, _ = normalize(x_ref[rows, :].astype(F32))
        small_ref[0:8, :] += fold(g_n1 * xhat)
        small_ref[8:16, :] += fold(g_n1)

    def pull_halo(i, carry):
        rows = rows_of(i * 128, 128)
        g_n1 = dot_t(g_ref[rows, D : 3 * D], w_ref[:, D : 3 * D])
        gn_halo_ref[rows, :] = g_n1.astype(BF16)
        norms(rows, g_n1)
        return carry

    lax.fori_loop(0, HALO // 128, pull_halo, 0)

    def pull_own(i, carry):
        rows = rows_of(HALO + i * 128, 128)
        g_n1 = dot_t(g_ref[rows, :], w_ref[...])
        gn_ref[rows_of(i * 128, 128), :] = g_n1
        norms(rows, g_n1)
        return carry

    lax.fori_loop(0, own // 128, pull_own, 0)
    gw_ref[:, 0:D] = dot(nt_ref[:, HALO:], g_ref[HALO:, 0:D]).astype(BF16)
    gw_ref[:, D : 2 * D] = dot(nt_ref[...], g_ref[:, D : 2 * D]).astype(BF16)
    gw_ref[:, 2 * D : 3 * D] = dot(nt_ref[...], g_ref[:, 2 * D : 3 * D]).astype(BF16)
    small_ref[16:24, :] = dot(jnp.ones((8, own), BF16), g_ref[HALO:, 0:D])
    small_ref[24:32, :] = dot(jnp.ones((8, ext), BF16), g_ref[:, 2 * D : 3 * D])


def attention_backward(q, k, v, g_o, lse, delta, id_row, id_col, n1, x_ext, w_qkv):
    ext, own = k.shape[0], q.shape[0]
    qb = 256 if own % 256 == 0 else 128
    shapes = (
        jax.ShapeDtypeStruct((HALO, D), BF16),
        jax.ShapeDtypeStruct((own, D), F32),
        jax.ShapeDtypeStruct((D, 3 * D), BF16),
        jax.ShapeDtypeStruct((32, D), F32),
    )
    return pl.pallas_call(
        functools.partial(backward_kernel, qb),
        out_shape=shapes,
        scratch_shapes=[
            pltpu.VMEM((HALO + qb, qb), F32),
            pltpu.VMEM((D, ext), BF16),
            pltpu.VMEM((D, ext), BF16),
            pltpu.VMEM((D, own), F32),
            pltpu.VMEM((ext, D), F32),
            pltpu.VMEM((ext, D), F32),
            pltpu.VMEM((ext, 3 * D), BF16),
        ],
        compiler_params=pltpu.CompilerParams(vmem_limit_bytes=56 * MIB),
        name="attention_backward",
    )(q, k, v, g_o, lse, delta, id_row, id_col, n1, x_ext, w_qkv)


def finish_kernel(x_ref, gn_ref, gh_ref, vec_ref, out_ref):
    def block(i, carry):
        rows = rows_of(i * 128, 128)
        xhat, rstd = normalize(x_ref[rows, :].astype(F32))
        out_ref[rows, :] = gh_ref[rows, :] + norm_pull(gn_ref[rows, :], vec_ref[0:1, :], xhat, rstd)
        return carry

    lax.fori_loop(0, x_ref.shape[0] // 128, block, 0)


def finish(x, g_n1, g_h1, vecs):
    return pl.pallas_call(
        finish_kernel,
        out_shape=jax.ShapeDtypeStruct(x.shape, F32),
        compiler_params=pltpu.CompilerParams(vmem_limit_bytes=32 * MIB),
        name="finish",
    )(x, g_n1, g_h1, vecs)


def hops(rows):
    plan, left, step = [], HALO, 1
    while left > 0:
        take = min(rows, left)
        plan.append((step, take))
        left, step = left - take, step + 1
    return plan


def local(
    layer_input,
    segment_ids,
    valid_mask,
    teacher,
    cotangent,
    ln1_gain,
    ln1_bias,
    w_q,
    w_k,
    w_v,
    b_q,
    b_v,
    w_o,
    b_o,
    ln2_gain,
    ln2_bias,
    w_up,
    b_up,
    w_down,
    b_down,
):
    fsdp_size = lax.axis_size("fsdp")
    tensor_size = lax.axis_size("tp")
    place = lax.axis_index("tp")
    own = layer_input.shape[0]
    tokens_all = own * fsdp_size * tensor_size
    rows_d = w_q.shape[0]
    cols_h, cols_f = w_q.shape[1], w_up.shape[1]

    parts = []
    for step, take in hops(own):
        route = [(i, i + step) for i in range(tensor_size - step)]
        parts.insert(0, lax.ppermute(layer_input[own - take :], "tp", route))
    x_ext = jnp.concatenate(parts + [layer_input], axis=0)
    ids = segment_ids + LEN * jnp.arange(segment_ids.shape[0], dtype=jnp.int32)[:, None]
    ids = jnp.concatenate([jnp.full((HALO,), -1, jnp.int32), ids.reshape(-1)])
    ids = lax.dynamic_slice_in_dim(ids, place * own, HALO + own)
    id_row, id_col = ids[None, :], ids[:, None]

    pack = jnp.concatenate([w_q, w_k, w_v, w_o.T, w_up, w_down.T], axis=1)
    count = jnp.sum(valid_mask)
    count_high = count // 256
    vectors = jnp.concatenate([ln1_gain, ln1_bias, b_o, ln2_gain, ln2_bias, b_down])
    heads = jnp.concatenate([b_q.reshape(-1), b_v.reshape(-1), b_up.reshape(-1)])
    digits = jnp.stack([count_high, count - 256 * count_high]).astype(BF16)
    small = jnp.concatenate([vectors, heads, digits])
    width = pack.shape[1]
    lines = -(-small.shape[0] // width)
    small = jnp.pad(small, (0, lines * width - small.shape[0])).reshape(lines, width)
    shard = jnp.concatenate([pack, small], axis=0)
    every = lax.all_gather(lax.all_gather(shard, "tp", axis=0), "fsdp", axis=0)
    big = every[:, :, :rows_d, :]

    def columns(start, size):
        part = big[:, :, :, start : start + size]
        return part.transpose(0, 2, 1, 3).reshape(fsdp_size * rows_d, tensor_size * size)

    w_qkv = jnp.concatenate([columns(j * cols_h, cols_h) for j in range(3)], axis=1)
    w_ot = columns(3 * cols_h, cols_h)
    w_up_all = columns(4 * cols_h, cols_f)
    w_dn_all = columns(4 * cols_h + cols_f, cols_f)
    few = every[:, :, rows_d:, :].reshape(fsdp_size, tensor_size, -1).astype(F32)
    six = few[:, 0, : 6 * rows_d].reshape(fsdp_size, 6, rows_d).transpose(1, 0, 2).reshape(6, D)
    at = 6 * rows_d

    def by_head(start, shape):
        size = shape[0] * shape[1]
        part = few[:, :, start : start + size].reshape((fsdp_size, tensor_size) + shape)
        return part.transpose(1, 2, 0, 3).reshape(1, -1)

    bq_all = by_head(at, b_q.shape)
    at += b_q.size
    bv_all = by_head(at, b_v.shape)
    at += b_v.size
    bup_all = by_head(at, b_up.shape)
    at += b_up.size
    valid_total = 256.0 * jnp.sum(few[:, :, at]) + jnp.sum(few[:, :, at + 1])

    vec_one = jnp.concatenate([six[0:2], bq_all, bv_all], axis=0)
    vec_two = jnp.stack([six[2], six[3], six[4], six[5]])
    n1, q, k, v, o, lse = attention_forward(x_ext, vec_one, w_qkv, id_row, id_col, own)
    scale = (tokens_all / valid_total).reshape(1, 1)
    mask = valid_mask.astype(F32)[:, None]
    layer_out, g_h1, g_o, delta, g_wo, g_wup, g_wdn, small_two, g_bup = middle(
        scale, layer_input, o, teacher, cotangent, mask, vec_two, bup_all, w_ot, w_up_all, w_dn_all
    )
    gn_halo, gn_own, g_qkv, small_one = attention_backward(
        q, k, v, g_o, lse, delta, id_row, id_col, n1, x_ext, w_qkv
    )

    total = gn_own
    left = HALO
    for step, take in hops(own):
        route = [(i + step, i) for i in range(tensor_size - step)]
        part = lax.ppermute(gn_halo[left - take : left], "tp", route).astype(F32)
        total = total + jnp.pad(part, ((own - take, 0), (0, 0)))
        left -= take
    grad_input = finish(layer_input, total, g_h1, vec_one)

    def split(grad, size):
        return grad.reshape(fsdp_size, rows_d, tensor_size, size).transpose(0, 2, 1, 3)

    g_pack = jnp.concatenate(
        [split(g_qkv[:, j * D : (j + 1) * D], cols_h) for j in range(3)]
        + [split(g_wo, cols_h), split(g_wup, cols_f), split(g_wdn, cols_f)],
        axis=3,
    )
    ones = [small_one[8 * j : 8 * j + 8].sum(0) for j in range(2)] + [small_one[16], small_one[24]]
    twos = [small_two[8 * j : 8 * j + 8].sum(0) for j in range(5)]
    loss_part = 0.5 / D * jnp.sum(twos[1]) / valid_total
    six_grads = jnp.stack([ones[0], ones[1], twos[4], twos[2], twos[3], twos[0]])
    six_grads = six_grads.reshape(6, fsdp_size, 1, rows_d).transpose(1, 2, 0, 3)
    six_grads = jnp.broadcast_to(
        six_grads.reshape(fsdp_size, 1, -1), (fsdp_size, tensor_size, 6 * rows_d)
    )

    def heads_of(grad, shape):
        part = grad.reshape((tensor_size, shape[0], fsdp_size, shape[1]))
        return part.transpose(2, 0, 1, 3).reshape(fsdp_size, tensor_size, -1)

    loss_high = loss_part.astype(BF16).astype(F32)
    losses = jnp.broadcast_to(
        jnp.stack([loss_high, loss_part - loss_high]), (fsdp_size, tensor_size, 2)
    )
    g_small = jnp.concatenate(
        [
            six_grads,
            heads_of(ones[2], b_q.shape),
            heads_of(ones[3], b_v.shape),
            heads_of(g_bup[0], b_up.shape),
            losses,
        ],
        axis=2,
    ).astype(BF16)
    g_small = jnp.pad(g_small, ((0, 0), (0, 0), (0, lines * width - g_small.shape[2])))
    g_all = jnp.concatenate([g_pack, g_small.reshape(fsdp_size, tensor_size, lines, width)], axis=2)
    mine = lax.psum_scatter(g_all, "fsdp", scatter_dimension=0, tiled=False)
    mine = lax.psum_scatter(mine, "tp", scatter_dimension=0, tiled=False).astype(F32)
    g_mat, g_vec = mine[:rows_d], mine[rows_d:].reshape(-1)
    c3, c4 = 3 * cols_h, 4 * cols_h
    six_out = g_vec[: 6 * rows_d].reshape(6, rows_d)
    at = 6 * rows_d
    grad_bq = g_vec[at : at + b_q.size].reshape(b_q.shape)
    at += b_q.size
    grad_bv = g_vec[at : at + b_v.size].reshape(b_v.shape)
    at += b_v.size
    grad_bup = g_vec[at : at + b_up.size].reshape(b_up.shape)
    at += b_up.size
    loss = g_vec[at] + g_vec[at + 1]
    return (
        layer_out,
        loss,
        grad_input,
        six_out[0],
        six_out[1],
        g_mat[:, 0:cols_h],
        g_mat[:, cols_h : 2 * cols_h],
        g_mat[:, 2 * cols_h : c3],
        grad_bq,
        grad_bv,
        g_mat[:, c3:c4].T,
        six_out[2],
        six_out[3],
        six_out[4],
        g_mat[:, c4 : c4 + cols_f],
        grad_bup,
        g_mat[:, c4 + cols_f :].T,
        six_out[5],
    )


ROWS = D // 8
EXTRA = 8
COLS = D // 4
FFC = 512
WA = 3 * COLS
WF = COLS + 2 * FFC
ALL = (0, 1, 2, 3)
PIECES_A = ((0, ALL), (2, ALL), (4, ALL), (6, ALL), (1, ALL[0:2]), (1, ALL[2:4]), (3, ALL), (5, ALL), (7, ALL))
SMALL = pl.CostEstimate(flops=1, bytes_accessed=1, transcendentals=0)


def about(us):
    return pl.CostEstimate(flops=us * 1000000, bytes_accessed=us * 3300000, transcendentals=0)


ANY = pl.BlockSpec(memory_space=pl.ANY)
VMEM = pl.BlockSpec(memory_space=pltpu.VMEM)
FAR = pl.BlockSpec(memory_space=pl.ANY)


def params(mib):
    return pltpu.CompilerParams(vmem_limit_bytes=mib * MIB)


def lane_of(shape):
    return lax.broadcasted_iota(jnp.int32, shape, len(shape) - 1)


def pack_kernel(
    wq_ref, wk_ref, wv_ref, wo_ref, wup_ref, wdn_ref, g1, b1, bo, g2, b2, bd, bq, bv, bup, mask_ref, a_ref, f_ref
):
    me = lax.axis_index("fsdp")
    a_ref[0:ROWS, 0:COLS] = wq_ref[...]
    a_ref[0:ROWS, COLS : 2 * COLS] = wk_ref[...]
    a_ref[0:ROWS, 2 * COLS : 3 * COLS] = wv_ref[...]
    f_ref[:, 0:COLS] = wo_ref[...]
    f_ref[:, COLS : COLS + FFC] = wup_ref[...]
    f_ref[:, COLS + FFC :] = wdn_ref[...]
    count = jnp.sum(mask_ref[...].astype(F32)).reshape(1, 1)
    high = jnp.floor(count / 256.0)
    lane = lane_of((1, 128))
    digits = jnp.where(lane == 0, high, jnp.where(lane == 1, count - 256.0 * high, 0.0))
    vectors = [r[...].astype(F32).reshape(1, ROWS) for r in (g1, b1, bo, g2, b2, bd)]
    rows = [jnp.concatenate([v, v], axis=1) for v in vectors] + [digits, jnp.zeros((1, 128), F32)]
    a_ref[ROWS:, 0:128] = jnp.concatenate(rows, axis=0).astype(BF16)

    def spread(ref):
        block = ref[...].astype(F32)
        count, piece = block.shape
        lanes = count * HD
        lane = lane_of((1, lanes))
        row = jnp.zeros((1, lanes), F32)
        for i in range(count):
            for j in range(piece):
                at = i * HD + me * piece + j
                row = jnp.where(lane == at, block[i : i + 1, j : j + 1], row)
        return row

    ups = spread(bup)
    rows = [spread(bq), spread(bv)] + [ups[:, 128 * j : 128 * j + 128] for j in range(4)]
    rows.append(jnp.zeros((2, 128), F32))
    a_ref[ROWS:, 128:256] = jnp.concatenate(rows, axis=0).astype(BF16)
    a_ref[ROWS:, 256:384] = jnp.zeros((EXTRA, 128), BF16)


def pack_weights(args):
    return pl.pallas_call(
        pack_kernel,
        out_shape=(
            jax.ShapeDtypeStruct((ROWS + EXTRA, WA), BF16),
            jax.ShapeDtypeStruct((ROWS, WF), BF16),
        ),
        compiler_params=params(60),
        name="pack_weights",
    )(*args)


def project_kernel(
    tokens_all, x_ref, p0, p1, p2, p3, p4, p5, p6, p7, p8,
    q_ref, k_ref, v_ref, kt_ref, nt_ref, w_ref, vec_ref, bup_ref, scale_ref, head_ref, ext_ref, sem
):
    me, place = lax.axis_index("fsdp"), lax.axis_index("tp")
    pieces = (p0, p1, p2, p3, p4, p5, p6, p7, p8)

    def each(act):
        for ref, (mask, steps) in zip(pieces, PIECES_A):
            owner = lax.bitwise_xor(me, mask)
            for i, s in enumerate(steps):
                tp = lax.bitwise_and(place - s + 4, 3)
                act(ref.at[i], 4 * mask + s, owner, tp)

    def start_ext(ref, slot, owner, tp):
        pltpu.make_async_copy(ref.at[pl.ds(ROWS, EXTRA), :], ext_ref.at[slot], sem.at[0]).start()

    def start_w(ref, slot, owner, tp):
        pltpu.make_async_copy(
            ref.at[pl.ds(0, ROWS), :],
            w_ref.at[rows_of(owner * ROWS, ROWS, ROWS), rows_of(tp * WA, WA)],
            sem.at[1],
        ).start()

    each(start_ext)
    each(start_w)
    pltpu.make_async_copy(ext_ref, ext_ref, sem.at[0]).wait()
    lane = lane_of((EXTRA, D))
    vectors = jnp.zeros((EXTRA, D), F32)
    total = jnp.zeros((EXTRA, 128), F32)
    for j in range(8):
        block = ext_ref[4 * j, :, 0:128].astype(F32)
        wide = jnp.concatenate([block] * 4, axis=1)
        vectors = jnp.where(lane // ROWS == lax.bitwise_xor(me, j), wide, vectors)
        for s in range(4):
            total += ext_ref[4 * j + s, :, 0:128].astype(F32)
    vec_ref[...] = vectors
    valid = 256.0 * total[6:7, 0:1] + total[6:7, 1:2]
    scale_ref[...] = jnp.concatenate(
        [jnp.broadcast_to(tokens_all / valid, (4, 128)), jnp.broadcast_to(0.5 / D / valid, (4, 128))], axis=0
    )
    for s in range(4):
        tp = lax.bitwise_and(place - s + 4, 3)
        block = jnp.zeros((EXTRA, 128), F32)
        for j in range(8):
            block += ext_ref[4 * j + s, :, 128:256].astype(F32)
        head_ref[:, rows_of(tp * COLS, COLS)] = block
        for i in range(4):
            bup_ref[:, rows_of(tp * FFC + 128 * i, 128)] = jnp.broadcast_to(block[2 + i : 3 + i], (8, 128))
    pltpu.make_async_copy(w_ref, w_ref, sem.at[1]).wait()

    def own_rows(i, carry):
        rows = rows_of(i * 128, 128)
        n1 = first_norm(x_ref[rows, :], vectors, me, nt_ref, rows)
        made = dot(n1, w_ref[...])
        for t in range(4):
            lanes = slice(t * COLS, (t + 1) * COLS)
            q = (made[:, t * WA : t * WA + COLS] + head_ref[0:1, lanes]).astype(BF16)
            q_ref[rows, lanes] = q * jnp.asarray(SCALE, BF16)
            keep_keys(made[:, t * WA + COLS : (t + 1) * WA], head_ref, k_ref, v_ref, kt_ref, rows, lanes)
        return carry

    lax.fori_loop(0, x_ref.shape[0] // 128, own_rows, 0)


def first_norm(x, vectors, me, nt_ref, rows):
    xhat, _ = normalize(x.astype(F32))
    n1 = xhat * vectors[0:1] + vectors[1:2]
    turned = jnp.transpose(n1).astype(BF16)
    for i in range(8):
        slot = lax.bitwise_xor(me, i)
        nt_ref[rows_of(slot * ROWS, ROWS, ROWS), rows] = turned[ROWS * i : ROWS * (i + 1)]
    return n1.astype(BF16)


def keep_keys(made, head_ref, k_ref, v_ref, kt_ref, rows, lanes):
    k = made[:, 0:COLS]
    k_ref[rows, lanes] = k.astype(BF16)
    kt_ref[lanes, rows] = jnp.transpose(k).astype(BF16)
    v_ref[rows, lanes] = (made[:, COLS:] + head_ref[1:2, lanes]).astype(BF16)


def project(x, pieces, tokens_all):
    own = x.shape[0]
    shapes = (
        jax.ShapeDtypeStruct((own, D), BF16),
        jax.ShapeDtypeStruct((own, D), BF16),
        jax.ShapeDtypeStruct((own, D), BF16),
        jax.ShapeDtypeStruct((D, own), BF16),
        jax.ShapeDtypeStruct((D, own), BF16),
        jax.ShapeDtypeStruct((D, 4 * WA), BF16),
        jax.ShapeDtypeStruct((EXTRA, D), F32),
        jax.ShapeDtypeStruct((8, 4 * FFC), F32),
        jax.ShapeDtypeStruct((8, 128), F32),
        jax.ShapeDtypeStruct((EXTRA, D), F32),
    )
    return pl.pallas_call(
        functools.partial(project_kernel, float(tokens_all)),
        out_shape=shapes,
        in_specs=[VMEM] + [FAR] * 9,
        out_specs=[VMEM] * len(shapes),
        scratch_shapes=[pltpu.VMEM((32, EXTRA, WA), BF16), pltpu.SemaphoreType.DMA((2,))],
        compiler_params=params(16),
        cost_estimate=SMALL,
        name="project",
    )(x, *pieces)


def project_halo_kernel(x_ref, w_ref, vec_ref, head_ref, k_ref, v_ref, kt_ref, nt_ref):
    me = lax.axis_index("fsdp")

    def halo_rows(i, carry):
        rows = rows_of(i * 128, 128)
        n1 = first_norm(x_ref[rows, :], vec_ref[...], me, nt_ref, rows)
        for t in range(4):
            made = dot(n1, w_ref[:, t * WA + COLS : (t + 1) * WA])
            keep_keys(made, head_ref, k_ref, v_ref, kt_ref, rows, slice(t * COLS, (t + 1) * COLS))
        return carry

    lax.fori_loop(0, HALO // 128, halo_rows, 0)


def project_halo(x, w, vec, head):
    shape = jax.ShapeDtypeStruct((HALO, D), BF16)
    turned = jax.ShapeDtypeStruct((D, HALO), BF16)
    return pl.pallas_call(
        project_halo_kernel,
        out_shape=(shape, shape, turned, turned),
        compiler_params=params(12),
        cost_estimate=SMALL,
        name="project_halo",
    )(x, w, vec, head)


QB = 256
WINDOW = HALO + QB


def mask_rows(idr_ref, idc_ref, first):
    key = lax.broadcasted_iota(jnp.int32, (QB, WINDOW), 1)
    query = lax.broadcasted_iota(jnp.int32, (QB, WINDOW), 0)
    same = idc_ref[rows_of(HALO + first, QB), :] == idr_ref[:, rows_of(first, WINDOW)]
    return jnp.where(same & (key <= query + HALO), 0.0, NEG)


def mask_cols(idr_ref, idc_ref, first):
    key = lax.broadcasted_iota(jnp.int32, (WINDOW, QB), 0)
    query = lax.broadcasted_iota(jnp.int32, (WINDOW, QB), 1)
    same = idc_ref[rows_of(first, WINDOW), :] == idr_ref[:, rows_of(HALO + first, QB)]
    return jnp.where(same & (key <= query + HALO), 0.0, NEG)


def attend_block(both, keys, values, bias, stat_ref):
    lane = lane_of((QB, PAIR))
    got = None
    for h in range(2):
        mine = (lane < HD) if h == 0 else (lane >= HD)
        s = dot_t(jnp.where(mine, both, jnp.zeros_like(both)), keys) + bias[...]
        top = jnp.max(s, axis=-1, keepdims=True)
        p = jnp.exp(s - top)
        total = jnp.sum(p, axis=-1, keepdims=True)
        o = dot(p.astype(BF16), values) / total
        got = o if h == 0 else jnp.where(mine, o, got)
        stat_ref[:, h : h + 1] = top + jnp.log(total)
    return got.astype(BF16), jnp.transpose(stat_ref[...])[0:8, :]


def attend_far_kernel(q_ref, k_ref, v_ref, idr_ref, idc_ref, o_ref, lse_ref, bias_ref, stat_ref):
    @pl.when(pl.program_id(0) == 0)
    def _():
        stat_ref[...] = jnp.zeros_like(stat_ref)
        bias_ref[...] = mask_rows(idr_ref, idc_ref, HALO)

    o_ref[...], lse_ref[0] = attend_block(q_ref[...], k_ref[...], v_ref[...], bias_ref, stat_ref)


def attend_far(q, k, v, id_row, id_col):
    own = q.shape[0]
    return pl.pallas_call(
        attend_far_kernel,
        grid=(4,),
        out_shape=(jax.ShapeDtypeStruct((own, D), BF16), jax.ShapeDtypeStruct((4, 8, own), F32)),
        in_specs=[
            pl.BlockSpec((QB, PAIR), lambda g: (HALO // QB, g)),
            pl.BlockSpec((own, PAIR), lambda g: (0, g)),
            pl.BlockSpec((own, PAIR), lambda g: (0, g)),
            pl.BlockSpec(id_row.shape, lambda g: (0, 0)),
            pl.BlockSpec(id_col.shape, lambda g: (0, 0)),
        ],
        out_specs=[
            pl.BlockSpec((QB, PAIR), lambda g: (HALO // QB, g)),
            pl.BlockSpec((1, 8, QB), lambda g: (g, 0, HALO // QB)),
        ],
        scratch_shapes=[pltpu.VMEM((QB, WINDOW), F32), pltpu.VMEM((QB, 128), F32)],
        compiler_params=params(10),
        cost_estimate=SMALL,
        name="attend_far",
    )(q, k, v, id_row, id_col)


def attend_near_kernel(
    q_ref, kh_ref, ko_ref, vh_ref, vo_ref, idr_ref, idc_ref, o_in, lse_in, o_ref, lse_ref, bias_ref, k_ref, v_ref, stat_ref
):
    @pl.when(pl.program_id(0) == 0)
    def _():
        stat_ref[...] = jnp.zeros_like(stat_ref)
        for i in range(HALO // QB):
            bias_ref[i] = mask_rows(idr_ref, idc_ref, i * QB)

    for dst, halo, own in ((k_ref, kh_ref, ko_ref), (v_ref, vh_ref, vo_ref)):
        dst[0:HALO, :] = halo[...]
        dst[HALO:, :] = own[...]

    def block(i, carry):
        first = i * QB
        window, rows = rows_of(first, WINDOW), rows_of(first, QB)
        o, lse = attend_block(q_ref[rows, :], k_ref[window, :], v_ref[window, :], bias_ref.at[i], stat_ref)
        o_ref[rows, :] = o
        lse_ref[0, :, rows] = lse
        return carry

    lax.fori_loop(0, HALO // QB, block, 0)


def attend_near(base, q, k_halo, k, v_halo, v, id_row, id_col, o, lse):
    at = lambda i: (0, base + i)
    block = pl.BlockSpec((HALO, PAIR), at)
    return pl.pallas_call(
        attend_near_kernel,
        grid=(2,),
        out_shape=(jax.ShapeDtypeStruct(o.shape, BF16), jax.ShapeDtypeStruct(lse.shape, F32)),
        in_specs=[block] * 5
        + [
            pl.BlockSpec(id_row.shape, lambda i: (0, 0)),
            pl.BlockSpec(id_col.shape, lambda i: (0, 0)),
            ANY,
            ANY,
        ],
        out_specs=[block, pl.BlockSpec((1, 8, HALO), lambda i: (base + i, 0, 0))],
        scratch_shapes=[
            pltpu.VMEM((HALO // QB, QB, WINDOW), F32),
            pltpu.VMEM((2 * HALO, PAIR), BF16),
            pltpu.VMEM((2 * HALO, PAIR), BF16),
            pltpu.VMEM((QB, 128), F32),
        ],
        input_output_aliases={7: 0, 8: 1},
        compiler_params=params(12),
        cost_estimate=SMALL,
        name="attend_near",
    )(q, k_halo, k, v_halo, v, id_row, id_col, o, lse)


PIECES_F = ((0, (0,)), (0, (1,)), (0, (2,)), (0, (3,)), (2, (0, 1, 2, 3)), (4, (0, 1, 2, 3)), (6, (0, 1)), (6, (2, 3)))


def central_kernel(
    rb, x_ref, o_ref, teacher_ref, cot_ref, mask_ref, vec_ref, bup_ref, scale_ref,
    *rest
):
    pieces = rest[:16]
    (
    out_ref, gh_ref, go_ref, delta_ref, theirs_ref, mine_ref, small_ref, gbup_ref,
    wo_ref, wup_ref, wdn_ref, slope_ref, hid_ref, gpre_ref, n2t_ref, gmlpt_ref, gattnt_ref, sem
    ) = rest[16:]
    me, place = lax.axis_index("fsdp"), lax.axis_index("tp")
    own, ff = x_ref.shape[0], 4 * FFC
    parts = ((wo_ref, 0, COLS), (wup_ref, COLS, FFC), (wdn_ref, COLS + FFC, FFC))
    for n, (dst, start, size) in enumerate(parts):
        for j, ref in enumerate(pieces):
            mask, steps = PIECES_F[j % 8]
            owner = lax.bitwise_xor(me, mask + j // 8)
            for i, s in enumerate(steps):
                tp = lax.bitwise_and(place - s + 4, 3)
                pltpu.make_async_copy(
                    ref.at[i, :, pl.ds(start, size)],
                    dst.at[rows_of(owner * ROWS, ROWS, ROWS), rows_of(tp * size, size)],
                    sem.at[n],
                ).start()
    small_ref[...] = jnp.zeros_like(small_ref)
    head_of = lax.broadcasted_iota(jnp.int32, (D, 128), 0) // HD
    pick = (head_of == lax.broadcasted_iota(jnp.int32, (D, 128), 1)).astype(BF16)
    out_bias, gain, offset, down_bias = (vec_ref[j : j + 1, :] for j in range(2, 6))

    def turn(dst, rows, value):
        turned = jnp.transpose(value).astype(BF16)
        for i in range(8):
            slot = lax.bitwise_xor(me, i)
            dst[rows_of(slot * ROWS, ROWS, ROWS), rows] = turned[ROWS * i : ROWS * (i + 1)]

    for n, (dst, _, _) in enumerate(parts):
        pltpu.make_async_copy(dst, dst, sem.at[n]).wait()

    def block(i, carry):
        rows = rows_of(i * rb, rb)
        h1 = x_ref[rows, :].astype(F32) + dot_t(o_ref[rows, :], wo_ref[...]) + out_bias
        xhat, rstd = normalize(h1)
        n2 = xhat * gain + offset
        n2_low = n2.astype(BF16)
        turn(n2t_ref, rows, n2)
        for c in range(0, ff, FFC):
            pre = dot(n2_low, wup_ref[:, c : c + FFC]) + bup_ref[0:1, c : c + FFC]
            s = jax.nn.sigmoid(1.702 * pre)
            value = pre * s
            hid_ref[rows, c : c + FFC] = value.astype(BF16)
            slope_ref[:, c : c + FFC] = s + 1.702 * value * (1.0 - s)
        out = h1 + dot_t(hid_ref[rows, :], wdn_ref[...]) + down_bias
        out_ref[rows, :] = out.astype(BF16)
        diff = (out - teacher_ref[rows, :].astype(F32)) * mask_ref[rows, :]
        g_out = cot_ref[rows, :].astype(F32) + scale_ref[0:1, 0:1] * diff
        small_ref[0:8, :] += fold(g_out)
        small_ref[8:16, :] += fold(diff * diff)
        g_mlp = g_out.astype(BF16)
        turn(gmlpt_ref, rows, g_out)
        for c in range(0, ff, FFC):
            g_hid = dot(g_mlp, wdn_ref[:, c : c + FFC])
            gpre_ref[rows, c : c + FFC] = (g_hid * slope_ref[:, c : c + FFC]).astype(BF16)
        g_n2 = dot_t(gpre_ref[rows, :], wup_ref[...])
        small_ref[16:24, :] += fold(g_n2 * xhat)
        small_ref[24:32, :] += fold(g_n2)
        g_h1 = g_out + norm_pull(g_n2, gain, xhat, rstd)
        gh_ref[rows, :] = g_h1
        small_ref[32:40, :] += fold(g_h1)
        turn(gattnt_ref, rows, g_h1)
        g_o = dot(g_h1.astype(BF16), wo_ref[...]).astype(BF16)
        go_ref[rows, :] = g_o
        product = g_o.astype(F32) * o_ref[rows, :].astype(F32)
        high = product.astype(BF16)
        low = (product - high.astype(F32)).astype(BF16)
        turned = jnp.transpose(dot(high, pick) + dot(low, pick))
        for g in range(4):
            delta_ref[g, 0:2, rows] = turned[2 * g : 2 * g + 2, :]
        return carry

    lax.fori_loop(0, own // rb, block, 0)
    ones = jnp.ones((8, own), BF16)

    def keep(grad, s, start, size):
        low = grad.astype(BF16)
        for r in range(8):
            dst = theirs_ref if r % 2 else mine_ref
            dst[r // 2, s, :, start : start + size] = low[ROWS * r : ROWS * (r + 1)]

    def grads(s, carry):
        tp = lax.bitwise_and(place + s, 3)
        cols = rows_of(tp * FFC, FFC)
        keep(dot(gattnt_ref[...], o_ref[:, rows_of(tp * COLS, COLS)]), s, 0, COLS)
        keep(dot(n2t_ref[...], gpre_ref[:, cols]), s, COLS, FFC)
        keep(dot(gmlpt_ref[...], hid_ref[:, cols]), s, COLS + FFC, FFC)
        gbup_ref[:, cols] = dot(ones, gpre_ref[:, cols])
        return carry

    lax.fori_loop(0, 4, grads, 0)


def central(x, o, teacher, cot, mask, vec, bup, scale, pieces):
    own = x.shape[0]
    rb = 256
    shapes = (
        jax.ShapeDtypeStruct((own, D), BF16),
        jax.ShapeDtypeStruct((own, D), F32),
        jax.ShapeDtypeStruct((own, D), BF16),
        jax.ShapeDtypeStruct((4, 8, own), F32),
        jax.ShapeDtypeStruct((4, 4, ROWS, WF), BF16),
        jax.ShapeDtypeStruct((4, 4, ROWS, WF), BF16),
        jax.ShapeDtypeStruct((40, D), F32),
        jax.ShapeDtypeStruct((8, 4 * FFC), F32),
    )
    return pl.pallas_call(
        functools.partial(central_kernel, rb),
        out_shape=shapes,
        in_specs=[VMEM] * 8 + [FAR] * 16,
        out_specs=[VMEM] * len(shapes),
        scratch_shapes=[
            pltpu.VMEM((D, D), BF16),
            pltpu.VMEM((D, 4 * FFC), BF16),
            pltpu.VMEM((D, 4 * FFC), BF16),
            pltpu.VMEM((rb, 4 * FFC), F32),
            pltpu.VMEM((own, 4 * FFC), BF16),
            pltpu.VMEM((own, 4 * FFC), BF16),
            pltpu.VMEM((D, own), BF16),
            pltpu.VMEM((D, own), BF16),
            pltpu.VMEM((D, own), BF16),
            pltpu.SemaphoreType.DMA((3,)),
        ],
        compiler_params=params(36),
        cost_estimate=SMALL,
        name="central",
    )(x, o, teacher, cot, mask, vec, bup, scale, *pieces)


def pull_block(both_q, both_g, keys, values, keys_t, bias, lse, delta, dk_ref, dv_ref, window):
    lane = lane_of((QB, PAIR))
    turned = []
    for h in range(2):
        mine = (lane < HD) if h == 0 else (lane >= HD)
        q = jnp.where(mine, both_q, jnp.zeros_like(both_q))
        g_o = jnp.where(mine, both_g, jnp.zeros_like(both_g))
        p = jnp.exp(dot_t(keys, q) + bias[...] - lse[h : h + 1])
        ds = (p * (dot_t(values, g_o) - delta[h : h + 1])).astype(BF16)
        dv_ref[window, :] += dot(p.astype(BF16), g_o)
        dk_ref[window, :] += dot(ds, q)
        turned.append(dot(keys_t[h * HD : (h + 1) * HD, :], ds))
    return (jnp.transpose(jnp.concatenate(turned, axis=0)) * SCALE).astype(BF16)


def pull_near_kernel(
    q_ref, go_ref, kh_ref, ko_ref, vh_ref, vo_ref, lse_ref, delta_ref, idr_ref, idc_ref, kth_ref, kto_ref, *rest
):
    gh_ref, gq_ref, part_ref, bias_ref, k_ref, v_ref, kt_ref, dk_ref, dv_ref = rest[-9:]

    @pl.when(pl.program_id(0) == 0)
    def _():
        for i in range(HALO // QB):
            bias_ref[i] = mask_cols(idr_ref, idc_ref, i * QB)

    for dst, halo, own in ((k_ref, kh_ref, ko_ref), (v_ref, vh_ref, vo_ref)):
        dst[0:HALO, :] = halo[...]
        dst[HALO:, :] = own[...]
    kt_ref[:, 0:HALO] = kth_ref[...]
    kt_ref[:, HALO:] = kto_ref[...]
    dk_ref[...] = jnp.zeros_like(dk_ref)
    dv_ref[...] = jnp.zeros_like(dv_ref)

    def block(i, carry):
        first = i * QB
        window, rows = rows_of(first, WINDOW), rows_of(first, QB)
        gq_ref[rows, :] = pull_block(
            q_ref[rows, :], go_ref[rows, :], k_ref[window, :], v_ref[window, :], kt_ref[:, window],
            bias_ref.at[i], lse_ref[0, :, rows], delta_ref[0, :, rows], dk_ref, dv_ref, window
        )
        return carry

    lax.fori_loop(0, HALO // QB, block, 0)
    for n, ref in enumerate((dk_ref, dv_ref)):
        lanes = slice(n * PAIR, (n + 1) * PAIR)
        gh_ref[:, lanes] = ref[0:HALO, :].astype(BF16)
        part_ref[:, lanes] = ref[HALO:, :]


def pull_near(base, q, g_o, k_halo, k, v_halo, v, lse, delta, id_row, id_col, kt_halo, kt, before):
    at = lambda i: (0, base + i)
    block = pl.BlockSpec((HALO, PAIR), at)
    deep = pl.BlockSpec((1, 8, HALO), lambda i: (base + i, 0, 0))
    down = pl.BlockSpec((PAIR, HALO), lambda i: (base + i, 0))
    wide = pl.BlockSpec((HALO, 2 * PAIR), at)
    return pl.pallas_call(
        pull_near_kernel,
        grid=(2,),
        out_shape=(
            jax.ShapeDtypeStruct((HALO, 2 * D), BF16),
            jax.ShapeDtypeStruct((HALO, D), BF16),
            jax.ShapeDtypeStruct((HALO, 2 * D), F32),
        ),
        in_specs=[block] * 6
        + [
            deep,
            deep,
            pl.BlockSpec(id_row.shape, lambda i: (0, 0)),
            pl.BlockSpec(id_col.shape, lambda i: (0, 0)),
            down,
            down,
        ]
        + [ANY] * len(before),
        out_specs=[wide, block, wide],
        scratch_shapes=[
            pltpu.VMEM((HALO // QB, WINDOW, QB), F32),
            pltpu.VMEM((2 * HALO, PAIR), BF16),
            pltpu.VMEM((2 * HALO, PAIR), BF16),
            pltpu.VMEM((PAIR, 2 * HALO), BF16),
            pltpu.VMEM((2 * HALO, PAIR), F32),
            pltpu.VMEM((2 * HALO, PAIR), F32),
        ],
        input_output_aliases={12: 0, 13: 1, 14: 2} if before else {},
        compiler_params=params(14),
        cost_estimate=SMALL,
        name="pull_near",
    )(q, g_o, k_halo, k, v_halo, v, lse, delta, id_row, id_col, kt_halo, kt, *before)


def pull_far_kernel(
    q_ref, go_ref, k_ref, v_ref, lse_ref, delta_ref, idr_ref, idc_ref, kt_ref, gq_ref, part_ref, g_ref, bias_ref, dk_ref, dv_ref
):
    @pl.when(pl.program_id(0) == 0)
    def _():
        bias_ref[...] = mask_cols(idr_ref, idc_ref, HALO)

    for n, ref in enumerate((dk_ref, dv_ref)):
        ref[0:HALO, :] = part_ref[:, n * PAIR : (n + 1) * PAIR]
        ref[HALO:, :] = jnp.zeros((QB, PAIR), F32)
    g_ref[0:HALO, 0:COLS] = gq_ref[...]
    g_ref[HALO:, 0:COLS] = pull_block(
        q_ref[...], go_ref[...], k_ref[...], v_ref[...], kt_ref[...],
        bias_ref, lse_ref[0], delta_ref[0], dk_ref, dv_ref, slice(None)
    )
    g_ref[:, COLS : 2 * COLS] = dk_ref[...].astype(BF16)
    g_ref[:, 2 * COLS :] = dv_ref[...].astype(BF16)


def pull_far(q, g_o, k, v, lse, delta, id_row, id_col, kt, gq_near, part):
    own = q.shape[0]
    last = pl.BlockSpec((QB, PAIR), lambda g: (HALO // QB, g))
    full = pl.BlockSpec((own, PAIR), lambda g: (0, g))
    deep = pl.BlockSpec((1, 8, QB), lambda g: (g, 0, HALO // QB))
    return pl.pallas_call(
        pull_far_kernel,
        grid=(4,),
        out_shape=jax.ShapeDtypeStruct((own, 4 * WA), BF16),
        in_specs=[
            last,
            last,
            full,
            full,
            deep,
            deep,
            pl.BlockSpec(id_row.shape, lambda g: (0, 0)),
            pl.BlockSpec(id_col.shape, lambda g: (0, 0)),
            pl.BlockSpec((PAIR, own), lambda g: (g, 0)),
            pl.BlockSpec((HALO, PAIR), lambda g: (0, g)),
            pl.BlockSpec((HALO, 2 * PAIR), lambda g: (0, g)),
        ],
        out_specs=pl.BlockSpec((own, WA), lambda g: (0, g)),
        scratch_shapes=[
            pltpu.VMEM((WINDOW, QB), F32),
            pltpu.VMEM((own, PAIR), F32),
            pltpu.VMEM((own, PAIR), F32),
        ],
        compiler_params=params(12),
        cost_estimate=SMALL,
        name="pull_far",
    )(q, g_o, k, v, lse, delta, id_row, id_col, kt, gq_near, part)


def norm_sums(small_ref, x, g_n1):
    xhat, _ = normalize(x.astype(F32))
    small_ref[0:8, :] += fold(g_n1 * xhat)
    small_ref[8:16, :] += fold(g_n1)


def halo_back_kernel(g_ref, w_ref, x_ref, out_ref, small_ref):
    small_ref[...] = jnp.zeros_like(small_ref)

    def block(i, carry):
        rows = rows_of(i * 128, 128)
        total = None
        for t in range(4):
            part = dot_t(g_ref[rows, t * 2 * COLS : (t + 1) * 2 * COLS], w_ref[:, t * WA + COLS : (t + 1) * WA])
            total = part if total is None else total + part
        out_ref[rows, :] = total.astype(BF16)
        norm_sums(small_ref, x_ref[rows, :], total)
        return carry

    lax.fori_loop(0, HALO // 128, block, 0)


def halo_back(g_halo, w, halo):
    return pl.pallas_call(
        halo_back_kernel,
        out_shape=(jax.ShapeDtypeStruct((HALO, D), BF16), jax.ShapeDtypeStruct((16, D), F32)),
        compiler_params=params(10),
        cost_estimate=SMALL,
        name="halo_back",
    )(g_halo, w, halo)


def own_back_kernel(
    x_ref, gh_ref, g_ref, nth_ref, nto_ref, w_ref, small_halo, small_two, gbup_ref, scale_ref,
    gn_ref, theirs_ref, mine_ref, small_ref, sum_ref
):
    me, place = lax.axis_index("fsdp"), lax.axis_index("tp")
    own = x_ref.shape[0]
    small_ref[...] = small_halo[...]

    def block(i, carry):
        rows = rows_of(i * 128, 128)
        g_n1 = dot_t(g_ref[rows, :], w_ref[...])
        gn_ref[rows, :] = g_n1
        norm_sums(small_ref, x_ref[rows, :], g_n1)
        return carry

    lax.fori_loop(0, own // 128, block, 0)
    sums = lambda ref, j: jnp.sum(ref[8 * j : 8 * j + 8, :], axis=0, keepdims=True)
    loss = jnp.sum(sums(small_two, 1), axis=1, keepdims=True) * scale_ref[4:5, 0:1]
    vectors = jnp.concatenate(
        [sums(small_ref, 0), sums(small_ref, 1), sums(small_two, 4), sums(small_two, 2), sums(small_two, 3),
         sums(small_two, 0), jnp.zeros((2, D), F32)],
        axis=0,
    )
    high = loss.astype(BF16).astype(F32)
    row, lane = lax.broadcasted_iota(jnp.int32, (EXTRA, 128), 0), lane_of((EXTRA, 128))
    ones_own, ones_halo = jnp.ones((8, own), BF16), jnp.ones((8, HALO), BF16)

    def grads(s, carry):
        tp = lax.bitwise_and(place + s, 3)
        g_own = g_ref[:, rows_of(tp * WA, WA)]
        g_halo = gh_ref[:, rows_of(tp * 2 * COLS, 2 * COLS)]
        total = dot(nto_ref[...], g_own)
        more = dot(nth_ref[...], g_halo)
        low = jnp.concatenate([total[:, 0:COLS], total[:, COLS:] + more], axis=1).astype(BF16)
        by_own, by_halo = dot(ones_own, g_own)[0:1], dot(ones_halo, g_halo)[0:1]
        ups = gbup_ref[0:1, rows_of(tp * FFC, FFC)]
        mids = jnp.concatenate(
            [by_own[:, 0:COLS], by_own[:, 2 * COLS :] + by_halo[:, COLS:]]
            + [ups[:, 128 * j : 128 * j + 128] for j in range(4)]
            + [jnp.zeros((2, 128), F32)],
            axis=0,
        ).astype(BF16)
        for r in range(8):
            dst = theirs_ref if r % 2 else mine_ref
            dst[r // 2, s, 0:ROWS, :] = low[ROWS * r : ROWS * (r + 1)]
            dst[r // 2, s, ROWS:, 128:256] = mids
        return carry

    lax.fori_loop(0, 4, grads, 0)
    for r in range(8):
        owner = lax.bitwise_xor(me, r)
        block = pltpu.roll(vectors, lax.rem(D - owner * ROWS, D), 1)[:, 0:128]
        block = jnp.where((row == 6) & (lane == 0), high, block)
        block = jnp.where((row == 6) & (lane == 1), loss - high, block).astype(BF16)
        dst = theirs_ref if r % 2 else mine_ref
        for s in range(4):
            dst[r // 2, s, ROWS:, 0:128] = block
            dst[r // 2, s, ROWS:, 256:384] = jnp.zeros((EXTRA, 128), BF16)


def own_back(x, g_halo, g_own, nt_halo, nt, w, small_halo, small_two, gbup, scale):
    own = x.shape[0]
    send = jax.ShapeDtypeStruct((4, 4, ROWS + EXTRA, WA), BF16)
    return pl.pallas_call(
        own_back_kernel,
        out_shape=(jax.ShapeDtypeStruct((own, D), F32), send, send),
        scratch_shapes=[pltpu.VMEM((16, D), F32), pltpu.VMEM((8, 128), F32)],
        compiler_params=params(16),
        cost_estimate=SMALL,
        name="own_back",
    )(x, g_halo, g_own, nt_halo, nt, w, small_halo, small_two, gbup, scale)


def close_kernel(x_ref, gn_ref, back_ref, gh_ref, vec_ref, out_ref):
    own = x_ref.shape[0]

    def block(at, extra):
        rows = rows_of(at, 128)
        xhat, rstd = normalize(x_ref[rows, :].astype(F32))
        g_n1 = gn_ref[rows, :] + extra
        out_ref[rows, :] = gh_ref[rows, :] + norm_pull(g_n1, vec_ref[0:1, :], xhat, rstd)

    def first(i, carry):
        block(i * 128, 0.0)
        return carry

    def second(i, carry):
        block(own - HALO + i * 128, back_ref[rows_of(i * 128, 128), :].astype(F32))
        return carry

    lax.fori_loop(0, (own - HALO) // 128, first, 0)
    lax.fori_loop(0, HALO // 128, second, 0)


def close(x, g_n1, back, g_h1, vec):
    return pl.pallas_call(
        close_kernel,
        out_shape=jax.ShapeDtypeStruct(x.shape, F32),
        compiler_params=params(12),
        cost_estimate=SMALL,
        name="close",
    )(x, g_n1, back, g_h1, vec)


def unpack_f_kernel(k_ref, r1, r2, r3, wo_ref, wup_ref, wdn_ref):
    total = (k_ref[0].astype(F32) + r1[...].astype(F32)) + (r2[...].astype(F32) + r3[...].astype(F32))
    wo_ref[...] = total[:, 0:COLS]
    wup_ref[...] = total[:, COLS : COLS + FFC]
    wdn_ref[...] = total[:, COLS + FFC :]


def unpack_f(k, r1, r2, r3):
    return pl.pallas_call(
        unpack_f_kernel,
        out_shape=(
            jax.ShapeDtypeStruct((ROWS, COLS), F32),
            jax.ShapeDtypeStruct((ROWS, FFC), F32),
            jax.ShapeDtypeStruct((ROWS, FFC), F32),
        ),
        compiler_params=params(8),
        name="unpack_f",
    )(k, r1, r2, r3)


def unpack_a_kernel(k_ref, r1, r2, r3, wq_ref, wk_ref, wv_ref, bq_ref, bv_ref, bup_ref, vec_ref):
    me = lax.axis_index("fsdp")
    total = (k_ref[0].astype(F32) + r1[...].astype(F32)) + (r2[...].astype(F32) + r3[...].astype(F32))
    wq_ref[...] = total[0:ROWS, 0:COLS]
    wk_ref[...] = total[0:ROWS, COLS : 2 * COLS]
    wv_ref[...] = total[0:ROWS, 2 * COLS :]
    vec_ref[...] = total[ROWS:, 0:128]
    mids = pltpu.roll(total[ROWS:, 128:256], lax.rem(128 - me * 8, 128), 1)
    for i in range(2):
        bq_ref[i : i + 1, :] = mids[0:1, i * HD : i * HD + 8]
        bv_ref[i : i + 1, :] = mids[1:2, i * HD : i * HD + 8]
    for i in range(8):
        at = (i % 2) * HD
        bup_ref[i : i + 1, :] = mids[2 + i // 2 : 3 + i // 2, at : at + 8]


def unpack_a(k, r1, r2, r3):
    small = jax.ShapeDtypeStruct((ROWS, COLS), F32)
    return pl.pallas_call(
        unpack_a_kernel,
        out_shape=(
            small,
            small,
            small,
            jax.ShapeDtypeStruct((2, 8), F32),
            jax.ShapeDtypeStruct((2, 8), F32),
            jax.ShapeDtypeStruct((8, 8), F32),
            jax.ShapeDtypeStruct((EXTRA, 128), F32),
        ),
        compiler_params=params(8),
        name="unpack_a",
    )(k, r1, r2, r3)


def to_mask(x, mask):
    return lax.ppermute(x, "fsdp", [(i, i ^ mask) for i in range(8)])


def to_step(x, step):
    return lax.ppermute(x, "tp", [(i, (i + step) % 4) for i in range(4)])


def add(a, b):
    return (a.astype(F32) + b.astype(F32)).astype(BF16)


def after(values, others):
    return lax.optimization_barrier((values, others))[0]


def local_fast(
    layer_input, segment_ids, valid_mask, teacher, cotangent, ln1_gain, ln1_bias, w_q, w_k, w_v, b_q, b_v,
    w_o, b_o, ln2_gain, ln2_bias, w_up, b_up, w_down, b_down
):
    place = lax.axis_index("tp")
    own = layer_input.shape[0]
    tokens_all = own * lax.axis_size("fsdp") * lax.axis_size("tp")

    shard_a, shard_f = pack_weights(
        (w_q, w_k, w_v, w_o.T, w_up, w_down.T, ln1_gain, ln1_bias, b_o, ln2_gain, ln2_bias, b_down, b_q, b_v, b_up,
         valid_mask)
    )
    steps_a = [shard_a] + [to_step(shard_a, s) for s in (1, 2, 3)]
    line_a = jnp.stack(steps_a)
    steps_f = [shard_f] + [to_step(shard_f, s) for s in (1, 2, 3)]
    over_f = [to_mask(x, 1) for x in steps_f]
    near_a = [to_mask(line_a, m) for m in (2, 4, 6)]
    halves_a = after([jnp.stack(steps_a[0:2]), jnp.stack(steps_a[2:4])], steps_f)
    over_a = [to_mask(a, 1) for a in halves_a]
    line_f = jnp.stack(after(steps_f, (over_a, near_a)))
    pieces_a = [line_a] + near_a + over_a + [to_mask(a, 1) for a in near_a]
    halo = lax.ppermute(layer_input[own - HALO :], "tp", [(i, i + 1) for i in range(3)])
    f_x, f_y = to_mask(line_f, 2), to_mask(line_f, 4)

    ids = segment_ids + LEN * jnp.arange(segment_ids.shape[0], dtype=jnp.int32)[:, None]
    ids = jnp.concatenate([jnp.full((HALO,), -1, jnp.int32), ids.reshape(-1)])
    ids = lax.dynamic_slice_in_dim(ids, place * own, HALO + own)
    id_row, id_col = ids[None, :], ids[:, None]
    mask = valid_mask.astype(F32)[:, None]

    q, k, v, kt, nt, w_all, vec, bup, scale, head = project(after(layer_input, over_f), pieces_a, tokens_all)
    o, lse = attend_far(q, k, v, id_row, id_col)
    f_x, f_y = after((f_x, f_y), o)
    halo = after(halo, o)
    f_xy = [to_mask(f_y[0:2], 2), to_mask(f_x[2:4], 4)]
    k_halo, v_halo, kt_halo, nt_halo = project_halo(halo, w_all, vec, head)
    o, lse = attend_near(0, q, k_halo, k, v_halo, v, id_row, id_col, o, lse)
    o, lse = attend_near(2, q, k_halo, k, v_halo, v, id_row, id_col, o, lse)
    near_f = [f_x, f_y] + after(f_xy, o)
    pieces_f = [x[None] for x in steps_f] + near_f + [x[None] for x in over_f] + [to_mask(a, 1) for a in near_f]
    layer_out, g_h1, g_o, delta, theirs_f, mine_f, small_two, gbup = central(
        layer_input, o, teacher, cotangent, mask, vec, bup, scale, pieces_f
    )

    def near(base, g_o, before):
        return pull_near(base, q, g_o, k_halo, k, v_halo, v, lse, delta, id_row, id_col, kt_halo, kt, before)

    begun = near(0, g_o, ())
    half = add(after(mine_f, begun), to_mask(theirs_f, 1))
    from_x, from_y = to_mask(half[3, 0:2], 2), to_mask(half[3, 2:4], 4)
    g_halo, gq_near, part = near(2, after(g_o, half), begun)
    gn_halo, small_halo = halo_back(g_halo, w_all, halo)
    back = lax.ppermute(gn_halo, "tp", [(i + 1, i) for i in range(3)])
    from_x, from_y = after((from_x, from_y), gn_halo)
    for_x = jnp.concatenate([half[1, 0:2], add(half[1, 2:4], from_y)])
    for_y = jnp.concatenate([add(half[2, 0:2], from_x), half[2, 2:4]])
    got_x, got_y = to_mask(for_x, 2), to_mask(for_y, 4)
    g_own = pull_far(after(q, (for_x, for_y)), g_o, k, v, lse, delta, id_row, id_col, kt, gq_near, part)
    gn_own, theirs_a, mine_a = own_back(
        layer_input, g_halo, g_own, nt_halo, nt, w_all, small_halo, small_two, gbup, scale
    )
    got_x, got_y = after((got_x, got_y), gn_own)
    line = (half[0].astype(F32) + got_x.astype(F32) + got_y.astype(F32)).astype(BF16)
    grad_wo, grad_wup, grad_wdn = unpack_f(line, *[to_step(line[s], s) for s in (1, 2, 3)])

    half = add(mine_a, to_mask(after(theirs_a, back), 1))
    from_x, from_y, from_xy = (to_mask(half[m], 2 * m) for m in (1, 2, 3))
    line = (half[0].astype(F32) + from_x.astype(F32) + from_y.astype(F32) + from_xy.astype(F32)).astype(BF16)
    grad_wq, grad_wk, grad_wv, grad_bq, grad_bv, grad_bup, few = unpack_a(
        line, *[to_step(line[s], s) for s in (1, 2, 3)]
    )
    grad_input = close(layer_input, gn_own, back, g_h1, vec)
    six = [few[j, 0:ROWS] for j in range(6)]
    loss = few[6, 0] + few[6, 1]
    return (
        layer_out, loss, grad_input, six[0], six[1], grad_wq, grad_wk, grad_wv, grad_bq, grad_bv, grad_wo.T, six[2],
        six[3], six[4], grad_wup, grad_bup, grad_wdn.T, six[5]
    )


def solution(mesh):
    tokens = P(("fsdp", "tp"), None)
    rows, crossed, heads = P("fsdp"), P("fsdp", "tp"), P("tp", "fsdp")
    placed = (
        tokens,
        P("fsdp", None),
        P(("fsdp", "tp")),
        tokens,
        tokens,
        rows,
        rows,
        crossed,
        crossed,
        crossed,
        heads,
        heads,
        heads,
        rows,
        rows,
        rows,
        crossed,
        heads,
        heads,
        rows,
    )
    given = (
        tokens,
        P(),
        tokens,
        rows,
        rows,
        crossed,
        crossed,
        crossed,
        heads,
        heads,
        heads,
        rows,
        rows,
        rows,
        crossed,
        heads,
        heads,
        rows,
    )
    sizes = (mesh.shape["fsdp"], mesh.shape["tp"])
    body = local_fast if sizes == (8, 4) else local
    return jax.shard_map(body, mesh=mesh, in_specs=placed, out_specs=given, check_vma=False)
```

```python
import functools

import jax
import jax.numpy as jnp
from jax import lax
from jax.experimental import pallas as pl
from jax.experimental.pallas import tpu as pltpu
from jax.sharding import PartitionSpec as P

D = 512
H = 8
HD = 64
LEN = 1024
HALO = 512
PAIR = 2 * HD
NEG = -1e30
SCALE = HD ** (-0.5)
F32 = jnp.float32
BF16 = jnp.bfloat16
MIB = 1 << 20

CONTRACT_LAST = (((1,), (1,)), ((), ()))


def dot(a, b):
    return jnp.dot(a, b, preferred_element_type=F32)


def dot_t(a, b):
    return lax.dot_general(a, b, CONTRACT_LAST, preferred_element_type=F32)


def normalize(x):
    center = x - jnp.mean(x, axis=-1, keepdims=True)
    rstd = lax.rsqrt(jnp.mean(center * center, axis=-1, keepdims=True) + 1e-05)
    return center * rstd, rstd


def norm_pull(g, gain, xhat, rstd):
    gx = g * gain
    return rstd * (
        gx
        - jnp.mean(gx, axis=-1, keepdims=True)
        - xhat * jnp.mean(gx * xhat, axis=-1, keepdims=True)
    )


def fold(x):
    return jnp.sum(x.reshape(x.shape[0] // 8, 8, x.shape[1]), axis=0)


def rows_of(start, size, unit=128):
    return pl.ds(pl.multiple_of(start, unit), size)


def forward_kernel(
    qb, x_ref, vec_ref, w_ref, idr_ref, idc_ref, n_ref, q_ref, k_ref, v_ref, o_ref, lse_ref, bias_ref, stat_ref
):
    ext, own = x_ref.shape[0], o_ref.shape[0]
    window = HALO + qb

    def project(i, carry):
        rows = rows_of(i * 128, 128)
        xhat, _ = normalize(x_ref[rows, :].astype(F32))
        n1 = (xhat * vec_ref[0:1, :] + vec_ref[1:2, :]).astype(BF16)
        n_ref[rows, :] = n1
        k_ref[rows, :] = dot(n1, w_ref[:, D : 2 * D]).astype(BF16)
        v_ref[rows, :] = (dot(n1, w_ref[:, 2 * D : 3 * D]) + vec_ref[3:4, :]).astype(BF16)
        return carry

    lax.fori_loop(0, ext // 128, project, 0)

    def project_q(i, carry):
        rows = rows_of(i * 128, 128)
        q = dot(n_ref[rows_of(HALO + i * 128, 128), :], w_ref[:, 0:D]) + vec_ref[2:3, :]
        q_ref[rows, :] = q.astype(BF16) * jnp.asarray(SCALE, BF16)
        return carry

    lax.fori_loop(0, own // 128, project_q, 0)

    def query_block(i, carry):
        first = i * qb
        key = lax.broadcasted_iota(jnp.int32, (qb, window), 1)
        query = lax.broadcasted_iota(jnp.int32, (qb, window), 0)
        same = idc_ref[rows_of(HALO + first, qb), :] == idr_ref[:, rows_of(first, window)]
        bias_ref[...] = jnp.where(same & (key <= query + HALO), 0.0, NEG)

        def pair(g, inner):
            lanes = rows_of(g * PAIR, PAIR)
            lane = lax.broadcasted_iota(jnp.int32, (qb, PAIR), 1)
            keys = k_ref[rows_of(first, window), lanes]
            values = v_ref[rows_of(first, window), lanes]
            both = q_ref[rows_of(first, qb), lanes]
            got = None
            for h in range(2):
                mine = (lane < HD) if h == 0 else (lane >= HD)
                s = dot_t(jnp.where(mine, both, jnp.zeros_like(both)), keys) + bias_ref[...]
                top = jnp.max(s, axis=-1, keepdims=True)
                p = jnp.exp(s - top)
                total = jnp.sum(p, axis=-1, keepdims=True)
                o = dot(p.astype(BF16), values) / total
                got = o if h == 0 else jnp.where(mine, o, got)
                stat_ref[...] = jnp.where(lane == 2 * g + h, top + jnp.log(total), stat_ref[...])
            o_ref[rows_of(first, qb), lanes] = got.astype(BF16)
            return inner

        lax.fori_loop(0, D // PAIR, pair, 0)
        lse_ref[:, rows_of(first, qb)] = jnp.transpose(stat_ref[...])[0:H, :]
        return carry

    stat_ref[...] = jnp.zeros_like(stat_ref)
    lax.fori_loop(0, own // qb, query_block, 0)


def attention_forward(x_ext, vecs, w_qkv, id_row, id_col, own):
    ext = x_ext.shape[0]
    qb = 256 if own % 256 == 0 else 128
    shapes = (
        jax.ShapeDtypeStruct((ext, D), BF16),
        jax.ShapeDtypeStruct((own, D), BF16),
        jax.ShapeDtypeStruct((ext, D), BF16),
        jax.ShapeDtypeStruct((ext, D), BF16),
        jax.ShapeDtypeStruct((own, D), BF16),
        jax.ShapeDtypeStruct((H, own), F32),
    )
    return pl.pallas_call(
        functools.partial(forward_kernel, qb),
        out_shape=shapes,
        scratch_shapes=[pltpu.VMEM((qb, HALO + qb), F32), pltpu.VMEM((qb, 128), F32)],
        compiler_params=pltpu.CompilerParams(vmem_limit_bytes=48 * MIB),
        name="attention_forward",
    )(x_ext, vecs, w_qkv, id_row, id_col)


def middle_kernel(
    rb,
    scale_ref,
    x_ref,
    o_ref,
    teacher_ref,
    cot_ref,
    mask_ref,
    vec_ref,
    bup_ref,
    wo_ref,
    wup_ref,
    wdn_ref,
    out_ref,
    gh_ref,
    go_ref,
    delta_ref,
    gwo_ref,
    gwup_ref,
    gwdn_ref,
    small_ref,
    gbup_ref,
    slope_ref,
    hid_ref,
    gpre_ref,
    n2t_ref,
    gmlpt_ref,
    gattnt_ref,
):
    own = x_ref.shape[0]
    ff = wup_ref.shape[1]
    chunk = 512
    small_ref[...] = jnp.zeros_like(small_ref)
    head_of = lax.broadcasted_iota(jnp.int32, (D, 128), 0) // HD
    pick = (head_of == lax.broadcasted_iota(jnp.int32, (D, 128), 1)).astype(BF16)

    def block(i, carry):
        rows = rows_of(i * rb, rb)
        out_bias, gain, offset, down_bias = (vec_ref[j : j + 1, :] for j in range(4))
        h1 = x_ref[rows, :].astype(F32) + dot_t(o_ref[rows, :], wo_ref[...]) + out_bias
        xhat, rstd = normalize(h1)
        n2 = xhat * gain + offset
        n2_low = n2.astype(BF16)
        n2t_ref[:, rows] = jnp.transpose(n2).astype(BF16)
        for c in range(0, ff, chunk):
            pre = dot(n2_low, wup_ref[:, c : c + chunk]) + bup_ref[:, c : c + chunk]
            s = jax.nn.sigmoid(1.702 * pre)
            value = pre * s
            hid_ref[rows, c : c + chunk] = value.astype(BF16)
            slope_ref[:, c : c + chunk] = s + 1.702 * value * (1.0 - s)
        out = h1 + dot_t(hid_ref[rows, :], wdn_ref[...]) + down_bias
        out_ref[rows, :] = out.astype(BF16)
        valid = mask_ref[rows, :]
        diff = (out - teacher_ref[rows, :].astype(F32)) * valid
        g_out = cot_ref[rows, :].astype(F32) + scale_ref[0, 0] * diff
        small_ref[0:8, :] += fold(g_out)
        small_ref[8:16, :] += fold(diff * diff)
        g_mlp = g_out.astype(BF16)
        gmlpt_ref[:, rows] = jnp.transpose(g_out).astype(BF16)
        for c in range(0, ff, chunk):
            g_hid = dot(g_mlp, wdn_ref[:, c : c + chunk])
            gpre_ref[rows, c : c + chunk] = (g_hid * slope_ref[:, c : c + chunk]).astype(BF16)
        g_n2 = dot_t(gpre_ref[rows, :], wup_ref[...])
        small_ref[16:24, :] += fold(g_n2 * xhat)
        small_ref[24:32, :] += fold(g_n2)
        g_h1 = g_out + norm_pull(g_n2, gain, xhat, rstd)
        gh_ref[rows, :] = g_h1
        small_ref[32:40, :] += fold(g_h1)
        gattnt_ref[:, rows] = jnp.transpose(g_h1).astype(BF16)
        g_o = dot(g_h1.astype(BF16), wo_ref[...]).astype(BF16)
        go_ref[rows, :] = g_o
        product = g_o.astype(F32) * o_ref[rows, :].astype(F32)
        high = product.astype(BF16)
        low = (product - high.astype(F32)).astype(BF16)
        delta_ref[:, rows] = jnp.transpose(dot(high, pick) + dot(low, pick))[0:H, :]
        return carry

    lax.fori_loop(0, own // rb, block, 0)
    ones = jnp.ones((8, own), BF16)

    def grads(i, carry):
        cols = rows_of(i * chunk, chunk)
        gwdn_ref[:, cols] = dot(gmlpt_ref[...], hid_ref[:, cols]).astype(BF16)
        gwup_ref[:, cols] = dot(n2t_ref[...], gpre_ref[:, cols]).astype(BF16)
        gbup_ref[:, cols] = dot(ones, gpre_ref[:, cols])
        return carry

    lax.fori_loop(0, ff // chunk, grads, 0)
    gwo_ref[...] = dot(gattnt_ref[...], o_ref[...]).astype(BF16)


def middle(scale, x, o, teacher, cot, mask, vecs, b_up, w_o, w_up, w_dn):
    own, ff = x.shape[0], w_up.shape[1]
    rb = 256 if own % 256 == 0 else 128
    shapes = (
        jax.ShapeDtypeStruct((own, D), BF16),
        jax.ShapeDtypeStruct((own, D), F32),
        jax.ShapeDtypeStruct((own, D), BF16),
        jax.ShapeDtypeStruct((H, own), F32),
        jax.ShapeDtypeStruct((D, D), BF16),
        jax.ShapeDtypeStruct((D, ff), BF16),
        jax.ShapeDtypeStruct((D, ff), BF16),
        jax.ShapeDtypeStruct((40, D), F32),
        jax.ShapeDtypeStruct((8, ff), F32),
    )
    whole = pl.BlockSpec(memory_space=pltpu.VMEM)
    return pl.pallas_call(
        functools.partial(middle_kernel, rb),
        out_shape=shapes,
        in_specs=[pl.BlockSpec(memory_space=pltpu.SMEM)] + [whole] * 10,
        out_specs=[whole] * len(shapes),
        scratch_shapes=[
            pltpu.VMEM((rb, ff), F32),
            pltpu.VMEM((own, ff), BF16),
            pltpu.VMEM((own, ff), BF16),
            pltpu.VMEM((D, own), BF16),
            pltpu.VMEM((D, own), BF16),
            pltpu.VMEM((D, own), BF16),
        ],
        compiler_params=pltpu.CompilerParams(vmem_limit_bytes=56 * MIB),
        name="middle",
    )(scale, x, o, teacher, cot, mask, vecs, b_up, w_o, w_up, w_dn)


def backward_kernel(
    qb,
    q_ref,
    k_ref,
    v_ref,
    go_ref,
    lse_ref,
    delta_ref,
    idr_ref,
    idc_ref,
    n_ref,
    x_ref,
    w_ref,
    gn_halo_ref,
    gn_ref,
    gw_ref,
    small_ref,
    bias_ref,
    kt_ref,
    nt_ref,
    dqt_ref,
    dk_ref,
    dv_ref,
    g_ref,
):
    ext, own = k_ref.shape[0], q_ref.shape[0]
    window = HALO + qb
    dk_ref[...] = jnp.zeros_like(dk_ref)
    dv_ref[...] = jnp.zeros_like(dv_ref)
    small_ref[...] = jnp.zeros_like(small_ref)

    def turn(i, carry):
        rows = rows_of(i * 128, 128)
        kt_ref[:, rows] = jnp.transpose(k_ref[rows, :].astype(F32)).astype(BF16)
        nt_ref[:, rows] = jnp.transpose(n_ref[rows, :].astype(F32)).astype(BF16)
        return carry

    lax.fori_loop(0, ext // 128, turn, 0)

    def query_block(i, carry):
        first = i * qb
        key = lax.broadcasted_iota(jnp.int32, (window, qb), 0)
        query = lax.broadcasted_iota(jnp.int32, (window, qb), 1)
        same = idc_ref[rows_of(first, window), :] == idr_ref[:, rows_of(HALO + first, qb)]
        bias_ref[...] = jnp.where(same & (key <= query + HALO), 0.0, NEG)

        def pair(g, inner):
            lanes = rows_of(g * PAIR, PAIR)
            lane = lax.broadcasted_iota(jnp.int32, (qb, PAIR), 1)
            keys = k_ref[rows_of(first, window), lanes]
            values = v_ref[rows_of(first, window), lanes]
            both_q = q_ref[rows_of(first, qb), lanes]
            both_g = go_ref[rows_of(first, qb), lanes]
            all_lse = lse_ref[:, rows_of(first, qb)]
            all_delta = delta_ref[:, rows_of(first, qb)]
            line = lax.broadcasted_iota(jnp.int32, (H, qb), 0)
            dk, dv = None, None
            for h in range(2):
                head = 2 * g + h
                mine = (lane < HD) if h == 0 else (lane >= HD)
                q = jnp.where(mine, both_q, jnp.zeros_like(both_q))
                g_o = jnp.where(mine, both_g, jnp.zeros_like(both_g))
                lse = jnp.sum(jnp.where(line == head, all_lse, 0.0), axis=0, keepdims=True)
                delta = jnp.sum(jnp.where(line == head, all_delta, 0.0), axis=0, keepdims=True)
                p = jnp.exp(dot_t(keys, q) + bias_ref[...] - lse)
                ds = (p * (dot_t(values, g_o) - delta)).astype(BF16)
                dv_h = dot(p.astype(BF16), g_o)
                dk_h = dot(ds, q)
                dk, dv = (dk_h, dv_h) if h == 0 else (dk + dk_h, dv + dv_h)
                dqt_ref[rows_of(head * HD, HD, HD), rows_of(first, qb)] = dot(
                    kt_ref[rows_of(head * HD, HD, HD), rows_of(first, window)], ds
                )
            dk_ref[rows_of(first, window), lanes] += dk
            dv_ref[rows_of(first, window), lanes] += dv
            return inner

        lax.fori_loop(0, D // PAIR, pair, 0)
        return carry

    lax.fori_loop(0, own // qb, query_block, 0)

    def gather(i, carry):
        rows = rows_of(i * 128, 128)
        g_ref[rows, D : 2 * D] = dk_ref[rows, :].astype(BF16)
        g_ref[rows, 2 * D : 3 * D] = dv_ref[rows, :].astype(BF16)
        return carry

    lax.fori_loop(0, ext // 128, gather, 0)

    def gather_q(i, carry):
        cols = rows_of(i * 128, 128)
        g_ref[rows_of(HALO + i * 128, 128), 0:D] = (jnp.transpose(dqt_ref[:, cols]) * SCALE).astype(BF16)
        return carry

    lax.fori_loop(0, own // 128, gather_q, 0)

    def norms(rows, g_n1):
        xhat, _ = normalize(x_ref[rows, :].astype(F32))
        small_ref[0:8, :] += fold(g_n1 * xhat)
        small_ref[8:16, :] += fold(g_n1)

    def pull_halo(i, carry):
        rows = rows_of(i * 128, 128)
        g_n1 = dot_t(g_ref[rows, D : 3 * D], w_ref[:, D : 3 * D])
        gn_halo_ref[rows, :] = g_n1.astype(BF16)
        norms(rows, g_n1)
        return carry

    lax.fori_loop(0, HALO // 128, pull_halo, 0)

    def pull_own(i, carry):
        rows = rows_of(HALO + i * 128, 128)
        g_n1 = dot_t(g_ref[rows, :], w_ref[...])
        gn_ref[rows_of(i * 128, 128), :] = g_n1
        norms(rows, g_n1)
        return carry

    lax.fori_loop(0, own // 128, pull_own, 0)
    gw_ref[:, 0:D] = dot(nt_ref[:, HALO:], g_ref[HALO:, 0:D]).astype(BF16)
    gw_ref[:, D : 2 * D] = dot(nt_ref[...], g_ref[:, D : 2 * D]).astype(BF16)
    gw_ref[:, 2 * D : 3 * D] = dot(nt_ref[...], g_ref[:, 2 * D : 3 * D]).astype(BF16)
    small_ref[16:24, :] = dot(jnp.ones((8, own), BF16), g_ref[HALO:, 0:D])
    small_ref[24:32, :] = dot(jnp.ones((8, ext), BF16), g_ref[:, 2 * D : 3 * D])


def attention_backward(q, k, v, g_o, lse, delta, id_row, id_col, n1, x_ext, w_qkv):
    ext, own = k.shape[0], q.shape[0]
    qb = 256 if own % 256 == 0 else 128
    shapes = (
        jax.ShapeDtypeStruct((HALO, D), BF16),
        jax.ShapeDtypeStruct((own, D), F32),
        jax.ShapeDtypeStruct((D, 3 * D), BF16),
        jax.ShapeDtypeStruct((32, D), F32),
    )
    return pl.pallas_call(
        functools.partial(backward_kernel, qb),
        out_shape=shapes,
        scratch_shapes=[
            pltpu.VMEM((HALO + qb, qb), F32),
            pltpu.VMEM((D, ext), BF16),
            pltpu.VMEM((D, ext), BF16),
            pltpu.VMEM((D, own), F32),
            pltpu.VMEM((ext, D), F32),
            pltpu.VMEM((ext, D), F32),
            pltpu.VMEM((ext, 3 * D), BF16),
        ],
        compiler_params=pltpu.CompilerParams(vmem_limit_bytes=56 * MIB),
        name="attention_backward",
    )(q, k, v, g_o, lse, delta, id_row, id_col, n1, x_ext, w_qkv)


def finish_kernel(x_ref, gn_ref, gh_ref, vec_ref, out_ref):
    def block(i, carry):
        rows = rows_of(i * 128, 128)
        xhat, rstd = normalize(x_ref[rows, :].astype(F32))
        out_ref[rows, :] = gh_ref[rows, :] + norm_pull(gn_ref[rows, :], vec_ref[0:1, :], xhat, rstd)
        return carry

    lax.fori_loop(0, x_ref.shape[0] // 128, block, 0)


def finish(x, g_n1, g_h1, vecs):
    return pl.pallas_call(
        finish_kernel,
        out_shape=jax.ShapeDtypeStruct(x.shape, F32),
        compiler_params=pltpu.CompilerParams(vmem_limit_bytes=32 * MIB),
        name="finish",
    )(x, g_n1, g_h1, vecs)


def hops(rows):
    plan, left, step = [], HALO, 1
    while left > 0:
        take = min(rows, left)
        plan.append((step, take))
        left, step = left - take, step + 1
    return plan


def local(
    layer_input,
    segment_ids,
    valid_mask,
    teacher,
    cotangent,
    ln1_gain,
    ln1_bias,
    w_q,
    w_k,
    w_v,
    b_q,
    b_v,
    w_o,
    b_o,
    ln2_gain,
    ln2_bias,
    w_up,
    b_up,
    w_down,
    b_down,
):
    fsdp_size = lax.axis_size("fsdp")
    tensor_size = lax.axis_size("tp")
    place = lax.axis_index("tp")
    own = layer_input.shape[0]
    tokens_all = own * fsdp_size * tensor_size
    rows_d = w_q.shape[0]
    cols_h, cols_f = w_q.shape[1], w_up.shape[1]

    parts = []
    for step, take in hops(own):
        route = [(i, i + step) for i in range(tensor_size - step)]
        parts.insert(0, lax.ppermute(layer_input[own - take :], "tp", route))
    x_ext = jnp.concatenate(parts + [layer_input], axis=0)
    ids = segment_ids + LEN * jnp.arange(segment_ids.shape[0], dtype=jnp.int32)[:, None]
    ids = jnp.concatenate([jnp.full((HALO,), -1, jnp.int32), ids.reshape(-1)])
    ids = lax.dynamic_slice_in_dim(ids, place * own, HALO + own)
    id_row, id_col = ids[None, :], ids[:, None]

    pack = jnp.concatenate([w_q, w_k, w_v, w_o.T, w_up, w_down.T], axis=1)
    count = jnp.sum(valid_mask)
    count_high = count // 256
    vectors = jnp.concatenate([ln1_gain, ln1_bias, b_o, ln2_gain, ln2_bias, b_down])
    heads = jnp.concatenate([b_q.reshape(-1), b_v.reshape(-1), b_up.reshape(-1)])
    digits = jnp.stack([count_high, count - 256 * count_high]).astype(BF16)
    small = jnp.concatenate([vectors, heads, digits])
    width = pack.shape[1]
    lines = -(-small.shape[0] // width)
    small = jnp.pad(small, (0, lines * width - small.shape[0])).reshape(lines, width)
    shard = jnp.concatenate([pack, small], axis=0)
    every = lax.all_gather(lax.all_gather(shard, "tp", axis=0), "fsdp", axis=0)
    big = every[:, :, :rows_d, :]

    def columns(start, size):
        part = big[:, :, :, start : start + size]
        return part.transpose(0, 2, 1, 3).reshape(fsdp_size * rows_d, tensor_size * size)

    w_qkv = jnp.concatenate([columns(j * cols_h, cols_h) for j in range(3)], axis=1)
    w_ot = columns(3 * cols_h, cols_h)
    w_up_all = columns(4 * cols_h, cols_f)
    w_dn_all = columns(4 * cols_h + cols_f, cols_f)
    few = every[:, :, rows_d:, :].reshape(fsdp_size, tensor_size, -1).astype(F32)
    six = few[:, 0, : 6 * rows_d].reshape(fsdp_size, 6, rows_d).transpose(1, 0, 2).reshape(6, D)
    at = 6 * rows_d

    def by_head(start, shape):
        size = shape[0] * shape[1]
        part = few[:, :, start : start + size].reshape((fsdp_size, tensor_size) + shape)
        return part.transpose(1, 2, 0, 3).reshape(1, -1)

    bq_all = by_head(at, b_q.shape)
    at += b_q.size
    bv_all = by_head(at, b_v.shape)
    at += b_v.size
    bup_all = by_head(at, b_up.shape)
    at += b_up.size
    valid_total = 256.0 * jnp.sum(few[:, :, at]) + jnp.sum(few[:, :, at + 1])

    vec_one = jnp.concatenate([six[0:2], bq_all, bv_all], axis=0)
    vec_two = jnp.stack([six[2], six[3], six[4], six[5]])
    n1, q, k, v, o, lse = attention_forward(x_ext, vec_one, w_qkv, id_row, id_col, own)
    scale = (tokens_all / valid_total).reshape(1, 1)
    mask = valid_mask.astype(F32)[:, None]
    layer_out, g_h1, g_o, delta, g_wo, g_wup, g_wdn, small_two, g_bup = middle(
        scale, layer_input, o, teacher, cotangent, mask, vec_two, bup_all, w_ot, w_up_all, w_dn_all
    )
    gn_halo, gn_own, g_qkv, small_one = attention_backward(
        q, k, v, g_o, lse, delta, id_row, id_col, n1, x_ext, w_qkv
    )

    total = gn_own
    left = HALO
    for step, take in hops(own):
        route = [(i + step, i) for i in range(tensor_size - step)]
        part = lax.ppermute(gn_halo[left - take : left], "tp", route).astype(F32)
        total = total + jnp.pad(part, ((own - take, 0), (0, 0)))
        left -= take
    grad_input = finish(layer_input, total, g_h1, vec_one)

    def split(grad, size):
        return grad.reshape(fsdp_size, rows_d, tensor_size, size).transpose(0, 2, 1, 3)

    g_pack = jnp.concatenate(
        [split(g_qkv[:, j * D : (j + 1) * D], cols_h) for j in range(3)]
        + [split(g_wo, cols_h), split(g_wup, cols_f), split(g_wdn, cols_f)],
        axis=3,
    )
    ones = [small_one[8 * j : 8 * j + 8].sum(0) for j in range(2)] + [small_one[16], small_one[24]]
    twos = [small_two[8 * j : 8 * j + 8].sum(0) for j in range(5)]
    loss_part = 0.5 / D * jnp.sum(twos[1]) / valid_total
    six_grads = jnp.stack([ones[0], ones[1], twos[4], twos[2], twos[3], twos[0]])
    six_grads = six_grads.reshape(6, fsdp_size, 1, rows_d).transpose(1, 2, 0, 3)
    six_grads = jnp.broadcast_to(
        six_grads.reshape(fsdp_size, 1, -1), (fsdp_size, tensor_size, 6 * rows_d)
    )

    def heads_of(grad, shape):
        part = grad.reshape((tensor_size, shape[0], fsdp_size, shape[1]))
        return part.transpose(2, 0, 1, 3).reshape(fsdp_size, tensor_size, -1)

    loss_high = loss_part.astype(BF16).astype(F32)
    losses = jnp.broadcast_to(
        jnp.stack([loss_high, loss_part - loss_high]), (fsdp_size, tensor_size, 2)
    )
    g_small = jnp.concatenate(
        [
            six_grads,
            heads_of(ones[2], b_q.shape),
            heads_of(ones[3], b_v.shape),
            heads_of(g_bup[0], b_up.shape),
            losses,
        ],
        axis=2,
    ).astype(BF16)
    g_small = jnp.pad(g_small, ((0, 0), (0, 0), (0, lines * width - g_small.shape[2])))
    g_all = jnp.concatenate([g_pack, g_small.reshape(fsdp_size, tensor_size, lines, width)], axis=2)
    mine = lax.psum_scatter(g_all, "fsdp", scatter_dimension=0, tiled=False)
    mine = lax.psum_scatter(mine, "tp", scatter_dimension=0, tiled=False).astype(F32)
    g_mat, g_vec = mine[:rows_d], mine[rows_d:].reshape(-1)
    c3, c4 = 3 * cols_h, 4 * cols_h
    six_out = g_vec[: 6 * rows_d].reshape(6, rows_d)
    at = 6 * rows_d
    grad_bq = g_vec[at : at + b_q.size].reshape(b_q.shape)
    at += b_q.size
    grad_bv = g_vec[at : at + b_v.size].reshape(b_v.shape)
    at += b_v.size
    grad_bup = g_vec[at : at + b_up.size].reshape(b_up.shape)
    at += b_up.size
    loss = g_vec[at] + g_vec[at + 1]
    return (
        layer_out,
        loss,
        grad_input,
        six_out[0],
        six_out[1],
        g_mat[:, 0:cols_h],
        g_mat[:, cols_h : 2 * cols_h],
        g_mat[:, 2 * cols_h : c3],
        grad_bq,
        grad_bv,
        g_mat[:, c3:c4].T,
        six_out[2],
        six_out[3],
        six_out[4],
        g_mat[:, c4 : c4 + cols_f],
        grad_bup,
        g_mat[:, c4 + cols_f :].T,
        six_out[5],
    )


ROWS = D // 8
EXTRA = 8
COLS = D // 4
FFC = 512
WA = 3 * COLS
WF = COLS + 2 * FFC
ALL = (0, 1, 2, 3)
PIECES_A = ((0, ALL), (2, ALL), (4, ALL), (6, ALL), (1, ALL[0:2]), (1, ALL[2:4]), (3, ALL), (5, ALL), (7, ALL))
SMALL = pl.CostEstimate(flops=1, bytes_accessed=1, transcendentals=0)


def about(us):
    return pl.CostEstimate(flops=us * 1000000, bytes_accessed=us * 3300000, transcendentals=0)


ANY = pl.BlockSpec(memory_space=pl.ANY)
VMEM = pl.BlockSpec(memory_space=pltpu.VMEM)
FAR = pl.BlockSpec(memory_space=pl.ANY)


def params(mib):
    return pltpu.CompilerParams(vmem_limit_bytes=mib * MIB)


def lane_of(shape):
    return lax.broadcasted_iota(jnp.int32, shape, len(shape) - 1)


def pack_kernel(
    wq_ref, wk_ref, wv_ref, wo_ref, wup_ref, wdn_ref, g1, b1, bo, g2, b2, bd, bq, bv, bup, mask_ref, a_ref, f_ref
):
    me = lax.axis_index("fsdp")
    a_ref[0:ROWS, 0:COLS] = wq_ref[...]
    a_ref[0:ROWS, COLS : 2 * COLS] = wk_ref[...]
    a_ref[0:ROWS, 2 * COLS : 3 * COLS] = wv_ref[...]
    f_ref[:, 0:COLS] = wo_ref[...]
    f_ref[:, COLS : COLS + FFC] = wup_ref[...]
    f_ref[:, COLS + FFC :] = wdn_ref[...]
    count = jnp.sum(mask_ref[...].astype(F32)).reshape(1, 1)
    high = jnp.floor(count / 256.0)
    lane = lane_of((1, 128))
    digits = jnp.where(lane == 0, high, jnp.where(lane == 1, count - 256.0 * high, 0.0))
    vectors = [r[...].astype(F32).reshape(1, ROWS) for r in (g1, b1, bo, g2, b2, bd)]
    rows = [jnp.concatenate([v, v], axis=1) for v in vectors] + [digits, jnp.zeros((1, 128), F32)]
    a_ref[ROWS:, 0:128] = jnp.concatenate(rows, axis=0).astype(BF16)

    def spread(ref):
        block = ref[...].astype(F32)
        count, piece = block.shape
        lanes = count * HD
        lane = lane_of((1, lanes))
        row = jnp.zeros((1, lanes), F32)
        for i in range(count):
            for j in range(piece):
                at = i * HD + me * piece + j
                row = jnp.where(lane == at, block[i : i + 1, j : j + 1], row)
        return row

    ups = spread(bup)
    rows = [spread(bq), spread(bv)] + [ups[:, 128 * j : 128 * j + 128] for j in range(4)]
    rows.append(jnp.zeros((2, 128), F32))
    a_ref[ROWS:, 128:256] = jnp.concatenate(rows, axis=0).astype(BF16)
    a_ref[ROWS:, 256:384] = jnp.zeros((EXTRA, 128), BF16)


def pack_weights(args):
    return pl.pallas_call(
        pack_kernel,
        out_shape=(
            jax.ShapeDtypeStruct((ROWS + EXTRA, WA), BF16),
            jax.ShapeDtypeStruct((ROWS, WF), BF16),
        ),
        compiler_params=params(60),
        name="pack_weights",
    )(*args)


def project_kernel(
    tokens_all, x_ref, idc_ref, p0, p1, p2, p3, p4, p5, p6, p7, p8,
    q_ref, k_ref, v_ref, kt_ref, nt_ref, w_ref, vec_ref, bup_ref, scale_ref, head_ref, ext_ref, sem
):
    me, place = lax.axis_index("fsdp"), lax.axis_index("tp")
    pieces = (p0, p1, p2, p3, p4, p5, p6, p7, p8)

    def each(act):
        for ref, (mask, steps) in zip(pieces, PIECES_A):
            owner = lax.bitwise_xor(me, mask)
            for i, s in enumerate(steps):
                tp = lax.bitwise_and(place - s + 4, 3)
                act(ref.at[i], 4 * mask + s, owner, tp)

    def start_ext(ref, slot, owner, tp):
        pltpu.make_async_copy(ref.at[pl.ds(ROWS, EXTRA), :], ext_ref.at[slot], sem.at[0]).start()

    def start_w(ref, slot, owner, tp):
        pltpu.make_async_copy(
            ref.at[pl.ds(0, ROWS), :],
            w_ref.at[rows_of(owner * ROWS, ROWS, ROWS), rows_of(tp * WA, WA)],
            sem.at[1],
        ).start()

    each(start_ext)
    each(start_w)
    pltpu.make_async_copy(ext_ref, ext_ref, sem.at[0]).wait()
    lane = lane_of((EXTRA, D))
    vectors = jnp.zeros((EXTRA, D), F32)
    total = jnp.zeros((EXTRA, 128), F32)
    for j in range(8):
        block = ext_ref[4 * j, :, 0:128].astype(F32)
        wide = jnp.concatenate([block] * 4, axis=1)
        vectors = jnp.where(lane // ROWS == lax.bitwise_xor(me, j), wide, vectors)
        for s in range(4):
            total += ext_ref[4 * j + s, :, 0:128].astype(F32)
    vec_ref[...] = vectors
    valid = 256.0 * total[6:7, 0:1] + total[6:7, 1:2]
    scale_ref[...] = jnp.concatenate(
        [jnp.broadcast_to(tokens_all / valid, (4, 128)), jnp.broadcast_to(0.5 / D / valid, (4, 128))], axis=0
    )
    for s in range(4):
        tp = lax.bitwise_and(place - s + 4, 3)
        block = jnp.zeros((EXTRA, 128), F32)
        for j in range(8):
            block += ext_ref[4 * j + s, :, 128:256].astype(F32)
        head_ref[:, rows_of(tp * COLS, COLS)] = block
        for i in range(4):
            bup_ref[:, rows_of(tp * FFC + 128 * i, 128)] = jnp.broadcast_to(block[2 + i : 3 + i], (8, 128))
    pltpu.make_async_copy(w_ref, w_ref, sem.at[1]).wait()

    def own_rows(i, carry):
        rows = rows_of(i * 128, 128)
        n1 = first_norm(x_ref[rows, :], vectors, me, nt_ref, rows)
        made = dot(n1, w_ref[...])
        spare_q, spare_k, spare_v = spare_lanes(idc_ref[rows_of(HALO + i * 128, 128), :])
        for t in range(4):
            lanes = slice(t * COLS, (t + 1) * COLS)
            q = (made[:, t * WA : t * WA + COLS] + head_ref[0:1, lanes]).astype(BF16)
            keep_heads(q_ref, rows, t, q * jnp.asarray(SCALE, BF16), spare_q)
            keep_keys(made[:, t * WA + COLS : (t + 1) * WA], head_ref, k_ref, v_ref, kt_ref, rows, t, spare_k, spare_v)
        return carry

    lax.fori_loop(0, x_ref.shape[0] // 128, own_rows, 0)


DOCS = 48
TERMS = 3


def spare_lanes(ids):
    shape = (ids.shape[0], PAIR)
    at = lax.bitwise_and(lane_of(shape), HD - 1)
    same = at == ids
    ones = jnp.where((at >= DOCS) & (at < DOCS + TERMS), 1.0, 0.0)
    spare_q = jnp.where(same & (at < DOCS), 1.0, 0.0).astype(BF16)
    spare_k = jnp.where(at < DOCS, jnp.where(same, 0.0, NEG), ones).astype(BF16)
    return spare_q, spare_k, ones.astype(BF16)


def three_terms(x):
    high = x.astype(BF16)
    rest = x - high.astype(F32)
    middle = rest.astype(BF16)
    return high, middle, (rest - middle.astype(F32)).astype(BF16)


def keep_heads(ref, rows, pair, value, spare):
    lane = lane_of(value.shape)
    for h in range(2):
        at = (2 * pair + h) * PAIR
        mine = (lane < HD) if h == 0 else (lane >= HD)
        ref[rows, at : at + PAIR] = jnp.where(mine, value, spare)


def first_norm(x, vectors, me, nt_ref, rows):
    xhat, _ = normalize(x.astype(F32))
    n1 = xhat * vectors[0:1] + vectors[1:2]
    turned = jnp.transpose(n1).astype(BF16)
    for i in range(8):
        slot = lax.bitwise_xor(me, i)
        nt_ref[rows_of(slot * ROWS, ROWS, ROWS), rows] = turned[ROWS * i : ROWS * (i + 1)]
    return n1.astype(BF16)


def keep_keys(made, head_ref, k_ref, v_ref, kt_ref, rows, t, spare_k, spare_v):
    lanes = slice(t * COLS, (t + 1) * COLS)
    k = made[:, 0:COLS]
    keep_heads(k_ref, rows, t, k.astype(BF16), spare_k)
    kt_ref[lanes, rows] = jnp.transpose(k).astype(BF16)
    keep_heads(v_ref, rows, t, (made[:, COLS:] + head_ref[1:2, lanes]).astype(BF16), spare_v)


def project(x, id_col, pieces, tokens_all):
    own = x.shape[0]
    shapes = (
        jax.ShapeDtypeStruct((own, 2 * D), BF16),
        jax.ShapeDtypeStruct((own, 2 * D), BF16),
        jax.ShapeDtypeStruct((own, 2 * D), BF16),
        jax.ShapeDtypeStruct((D, own), BF16),
        jax.ShapeDtypeStruct((D, own), BF16),
        jax.ShapeDtypeStruct((D, 4 * WA), BF16),
        jax.ShapeDtypeStruct((EXTRA, D), F32),
        jax.ShapeDtypeStruct((8, 4 * FFC), F32),
        jax.ShapeDtypeStruct((8, 128), F32),
        jax.ShapeDtypeStruct((EXTRA, D), F32),
    )
    return pl.pallas_call(
        functools.partial(project_kernel, float(tokens_all)),
        out_shape=shapes,
        in_specs=[VMEM, VMEM] + [FAR] * 9,
        out_specs=[VMEM] * len(shapes),
        scratch_shapes=[pltpu.VMEM((32, EXTRA, WA), BF16), pltpu.SemaphoreType.DMA((2,))],
        compiler_params=params(6),
        cost_estimate=SMALL,
        name="project",
    )(x, id_col, *pieces)


def project_halo_kernel(x_ref, idc_ref, w_ref, vec_ref, head_ref, k_ref, v_ref, kt_ref, nt_ref):
    me = lax.axis_index("fsdp")

    def halo_rows(i, carry):
        rows = rows_of(i * 128, 128)
        n1 = first_norm(x_ref[rows, :], vec_ref[...], me, nt_ref, rows)
        _, spare_k, spare_v = spare_lanes(idc_ref[rows, :])
        for t in range(4):
            made = dot(n1, w_ref[:, t * WA + COLS : (t + 1) * WA])
            keep_keys(made, head_ref, k_ref, v_ref, kt_ref, rows, t, spare_k, spare_v)
        return carry

    lax.fori_loop(0, HALO // 128, halo_rows, 0)


def project_halo(x, id_col, w, vec, head):
    shape = jax.ShapeDtypeStruct((HALO, 2 * D), BF16)
    turned = jax.ShapeDtypeStruct((D, HALO), BF16)
    return pl.pallas_call(
        project_halo_kernel,
        out_shape=(shape, shape, turned, turned),
        compiler_params=params(6),
        cost_estimate=SMALL,
        name="project_halo",
    )(x, id_col, w, vec, head)


QB = 256


def causal(by_rows):
    key = lax.broadcasted_iota(jnp.int32, (QB, QB), 1 if by_rows else 0)
    query = lax.broadcasted_iota(jnp.int32, (QB, QB), 0 if by_rows else 1)
    return jnp.where(key <= query, 0.0, NEG)


def staged(units, stages, lag=1, beside=()):
    steps = len(units) + lag * (len(stages) - 1)
    for n in range(steps):
        for depth, stage in enumerate(stages):
            if 0 <= n - lag * depth < len(units):
                stage(units[n - lag * depth])
        if n < len(beside):
            beside[n]()
    for extra in beside[steps:]:
        extra()


def attend_heads(heads, bias_ref):
    lane = lane_of((QB, PAIR))
    at = lax.bitwise_and(lane, HD - 1)

    def score(one):
        q = one["q"][one["rows"], one["lanes"]]
        one["s"] = []
        for keys, _, where, last in one["parts"]:
            s = dot_t(q, keys[where, one["lanes"]])
            one["s"].append(s + bias_ref[...] if last else s)

    def soften(one):
        one["top"] = functools.reduce(jnp.maximum, [jnp.max(s, axis=-1, keepdims=True) for s in one["s"]])
        one["p"] = [jnp.exp(s - one["top"]).astype(BF16) for s in one.pop("s")]

    def attend(one):
        total = None
        for p, (_, values, where, _) in zip(one.pop("p"), one["parts"]):
            part = dot(p, values[where, one["lanes"]])
            total = part if total is None else total + part
        first = (HD if one["h"] == 0 else 0) + DOCS
        weight = total[:, first : first + 1]
        mine = (lane < HD) if one["h"] == 0 else (lane >= HD)
        q = one["q"][one["rows"], one["lanes"]]
        for i, term in enumerate(three_terms(-(one["top"] + jnp.log(weight)))):
            q = jnp.where((at == DOCS + i) & ~mine, jnp.broadcast_to(term, q.shape), q)
        one["take"](one["h"], (total / weight).astype(BF16), q)

    staged(heads, (score, soften, attend), 2)


def keep_attended(o_ref, qa_ref, rows, pair):
    lane = lane_of((QB, PAIR))

    def take(h, o, q):
        lanes = slice(pair * PAIR, (pair + 1) * PAIR)
        qa_ref[rows, (2 * pair + h) * PAIR : (2 * pair + h + 1) * PAIR] = q
        o_ref[rows, lanes] = o if h == 0 else jnp.where(lane < HD, o_ref[rows, lanes], o)

    return take


def head_lanes(pair, h):
    return slice((2 * pair + h) * PAIR, (2 * pair + h + 1) * PAIR)


def attend_far_kernel(q_ref, k_ref, v_ref, o_ref, qa_ref, bias_ref):
    bias_ref[...] = causal(True)
    parts = ((k_ref, v_ref, slice(0, HALO), False), (k_ref, v_ref, slice(HALO, HALO + QB), True))
    heads = []
    for pair in range(4):
        take = keep_attended(o_ref, qa_ref, slice(0, QB), pair)
        for h in range(2):
            heads.append(
                dict(q=q_ref, rows=slice(HALO, HALO + QB), lanes=head_lanes(pair, h), h=h, parts=parts, take=take)
            )
    attend_heads(heads, bias_ref)


def attend_far(q, k, v):
    return pl.pallas_call(
        attend_far_kernel,
        out_shape=(jax.ShapeDtypeStruct((QB, D), BF16), jax.ShapeDtypeStruct((QB, 2 * D), BF16)),
        in_specs=[VMEM] * 3,
        out_specs=[VMEM] * 2,
        scratch_shapes=[pltpu.VMEM((QB, QB), F32)],
        compiler_params=params(8),
        cost_estimate=SMALL,
        name="attend_far",
    )(q, k, v)


def near_parts(halo, own):
    return (
        ((*halo, slice(0, HALO), False), (*own, slice(0, QB), True)),
        ((*halo, slice(QB, HALO), False), (*own, slice(0, QB), False), (*own, slice(QB, HALO), True)),
    )


def attend_near_kernel(base, q_ref, kh_ref, ko_ref, vh_ref, vo_ref, o_ref, qa_ref, bias_ref):
    bias_ref[...] = causal(True)
    heads = []
    for pair in range(2):
        for i, parts in enumerate(near_parts((kh_ref, vh_ref), (ko_ref, vo_ref))):
            rows = slice(i * QB, (i + 1) * QB)
            take = keep_attended(o_ref, qa_ref, rows, pair)
            for h in range(2):
                heads.append(dict(q=q_ref, rows=rows, lanes=head_lanes(base + pair, h), h=h, parts=parts, take=take))
    attend_heads(heads, bias_ref)


def attend_near(base, q, k_halo, k, v_halo, v):
    return pl.pallas_call(
        functools.partial(attend_near_kernel, base),
        out_shape=(jax.ShapeDtypeStruct((HALO, D // 2), BF16), jax.ShapeDtypeStruct((HALO, D), BF16)),
        in_specs=[VMEM] * 5,
        out_specs=[VMEM] * 2,
        scratch_shapes=[pltpu.VMEM((QB, QB), F32)],
        compiler_params=params(8),
        cost_estimate=SMALL,
        name="attend_near",
    )(q, k_halo, k, v_halo, v)


PIECES_F = ((0, (0,)), (0, (1,)), (0, (2,)), (0, (3,)), (2, (0, 1, 2, 3)), (4, (0, 1, 2, 3)), (6, (0, 1)), (6, (2, 3)))


def central_kernel(
    rb, x_ref, oa_ref, ob_ref, oc_ref, teacher_ref, cot_ref, mask_ref, vec_ref, bup_ref, scale_ref,
    *rest
):
    pieces = rest[:16]
    (
    out_ref, gh_ref, ga_ref, theirs_ref, mine_ref, small_ref, gbup_ref,
    wo_ref, wup_ref, wdn_ref, slope_ref, hid_ref, gpre_ref, n2t_ref, gmlpt_ref, gattnt_ref, place_ref, o_ref,
    h1_ref, xhat_ref, n2_ref, gmlp_ref, sem
    ) = rest[16:]
    me, place = lax.axis_index("fsdp"), lax.axis_index("tp")
    own, ff = x_ref.shape[0], 4 * FFC
    parts = ((wo_ref, 0, COLS), (wup_ref, COLS, FFC), (wdn_ref, COLS + FFC, FFC))
    for n, (dst, start, size) in enumerate(parts):
        for j, ref in enumerate(pieces):
            mask, steps = PIECES_F[j % 8]
            owner = lax.bitwise_xor(me, mask + j // 8)
            for i, s in enumerate(steps):
                tp = lax.bitwise_and(place - s + 4, 3)
                pltpu.make_async_copy(
                    ref.at[i, :, pl.ds(start, size)],
                    dst.at[rows_of(owner * ROWS, ROWS, ROWS), rows_of(tp * size, size)],
                    sem.at[n],
                ).start()
    small_ref[...] = jnp.zeros_like(small_ref)
    head_of = lax.broadcasted_iota(jnp.int32, (D, 128), 0) // HD
    pick = (head_of == lax.broadcasted_iota(jnp.int32, (D, 128), 1)).astype(BF16)
    out_bias, gain, offset, down_bias = (vec_ref[j : j + 1, :] for j in range(2, 6))
    source = lax.broadcasted_iota(jnp.int32, (TERMS * 128, H * PAIR), 0)
    target = lax.broadcasted_iota(jnp.int32, (TERMS * 128, H * PAIR), 1)
    head, term = target // PAIR, lax.bitwise_and(target, HD - 1) - DOCS
    outside = (lax.bitwise_and(target, PAIR - 1) >= HD) == (lax.bitwise_and(head, 1) == 0)
    placed = outside & (lax.bitwise_and(source, 127) == head) & (source // 128 == term)
    place_ref[...] = jnp.where(placed, 1.0, 0.0).astype(BF16)
    o_ref[0:HALO, 0 : D // 2] = oa_ref[...]
    o_ref[0:HALO, D // 2 :] = ob_ref[...]
    o_ref[HALO:, :] = oc_ref[...]

    def turn(dst, rows, value):
        turned = jnp.transpose(value).astype(BF16)
        for i in range(8):
            slot = lax.bitwise_xor(me, i)
            dst[rows_of(slot * ROWS, ROWS, ROWS), rows] = turned[ROWS * i : ROWS * (i + 1)]

    def arrived(n):
        pltpu.make_async_copy(parts[n][0], parts[n][0], sem.at[n]).wait()

    blocks = [dict(rows=slice(i * rb, (i + 1) * rb)) for i in range(own // rb)]

    def attention_out(one):
        one["attn"] = dot_t(o_ref[one["rows"], :], wo_ref[...])

    def second_norm(one):
        rows = one["rows"]
        h1 = x_ref[rows, :].astype(F32) + one.pop("attn") + out_bias
        xhat, rstd = normalize(h1)
        n2 = xhat * gain + offset
        h1_ref[rows, :] = h1
        xhat_ref[rows, :] = xhat
        one["rstd"] = rstd
        n2_ref[rows, :] = n2.astype(BF16)
        turn(n2t_ref, rows, n2)

    arrived(0)
    staged(blocks, (attention_out, second_norm))
    arrived(1)

    columns = [
        dict(rows=one["rows"], cols=slice(c * FFC, (c + 1) * FFC)) for c in range(4) for one in blocks
    ]

    def up(one):
        one["pre"] = dot(n2_ref[one["rows"], :], wup_ref[:, one["cols"]]) + bup_ref[0:1, one["cols"]]

    def gelu(one):
        pre = one.pop("pre")
        s = jax.nn.sigmoid(1.702 * pre)
        value = pre * s
        hid_ref[one["rows"], one["cols"]] = value.astype(BF16)
        slope_ref[one["rows"], one["cols"]] = s * (1.702 * (pre - value) + 1.0)

    staged(columns, (up, gelu))
    arrived(2)

    def down(one):
        one["mlp"] = dot_t(hid_ref[one["rows"], :], wdn_ref[...])

    def output(one):
        rows = one["rows"]
        out = h1_ref[rows, :] + one.pop("mlp") + down_bias
        out_ref[rows, :] = out.astype(BF16)
        diff = (out - teacher_ref[rows, :].astype(F32)) * mask_ref[rows, :]
        g_out = cot_ref[rows, :].astype(F32) + scale_ref[0:1, 0:1] * diff
        gh_ref[rows, :] = g_out
        small_ref[0:8, :] += fold(g_out)
        small_ref[8:16, :] += fold(diff * diff)
        gmlp_ref[rows, :] = g_out.astype(BF16)
        turn(gmlpt_ref, rows, g_out)

    staged(blocks, (down, output))

    def hidden(one):
        one["g"] = dot(gmlp_ref[one["rows"], :], wdn_ref[:, one["cols"]])

    def slope(one):
        g_pre = one.pop("g") * slope_ref[one["rows"], one["cols"]]
        gpre_ref[one["rows"], one["cols"]] = g_pre.astype(BF16)

    staged(columns, (hidden, slope))

    def into_norm(one):
        one["g"] = dot_t(gpre_ref[one["rows"], :], wup_ref[...])

    def pull_norm(one):
        rows, g_n2, xhat = one["rows"], one.pop("g"), xhat_ref[one["rows"], :]
        small_ref[16:24, :] += fold(g_n2 * xhat)
        small_ref[24:32, :] += fold(g_n2)
        g_h1 = gh_ref[rows, :] + norm_pull(g_n2, gain, xhat, one.pop("rstd"))
        gh_ref[rows, :] = g_h1
        small_ref[32:40, :] += fold(g_h1)
        turn(gattnt_ref, rows, g_h1)
        one["go"] = dot(g_h1.astype(BF16), wo_ref[...]).astype(BF16)

    def pull_out(one):
        rows, g_o = one["rows"], one.pop("go")
        product = g_o.astype(F32) * o_ref[rows, :].astype(F32)
        high = product.astype(BF16)
        low = (product - high.astype(F32)).astype(BF16)
        terms = jnp.concatenate(three_terms(-(dot(high, pick) + dot(low, pick))), axis=1)
        spare = dot(terms, place_ref[...]).astype(BF16)
        lane = lane_of((rb, PAIR))
        for n in range(H):
            mine = (lane < HD) if n % 2 == 0 else (lane >= HD)
            pair = g_o[:, (n // 2) * PAIR : (n // 2 + 1) * PAIR]
            ga_ref[rows, n * PAIR : (n + 1) * PAIR] = jnp.where(mine, pair, spare[:, n * PAIR : (n + 1) * PAIR])

    def keep(grad, s, start, size):
        low = grad.astype(BF16)
        for r in range(8):
            dst = theirs_ref if r % 2 else mine_ref
            dst[r // 2, s, :, start : start + size] = low[ROWS * r : ROWS * (r + 1)]

    def their(s, size):
        return rows_of(lax.bitwise_and(place + s, 3) * size, size)

    def by_down(s):
        keep(dot(gmlpt_ref[...], hid_ref[:, their(s, FFC)]), s, COLS + FFC, FFC)

    staged(
        blocks, (into_norm, pull_norm, pull_out), beside=[functools.partial(by_down, s) for s in range(4)]
    )
    ones = jnp.ones((8, own), BF16)
    gbup_ref[...] = dot(ones, gpre_ref[...])
    for s in range(4):
        keep(dot(n2t_ref[...], gpre_ref[:, their(s, FFC)]), s, COLS, FFC)
        keep(dot(gattnt_ref[...], o_ref[:, their(s, COLS)]), s, 0, COLS)


def central(x, o_near, o_more, o_far, teacher, cot, mask, vec, bup, scale, pieces):
    own = x.shape[0]
    rb = 256
    shapes = (
        jax.ShapeDtypeStruct((own, D), BF16),
        jax.ShapeDtypeStruct((own, D), F32),
        jax.ShapeDtypeStruct((own, 2 * D), BF16),
        jax.ShapeDtypeStruct((4, 4, ROWS, WF), BF16),
        jax.ShapeDtypeStruct((4, 4, ROWS, WF), BF16),
        jax.ShapeDtypeStruct((40, D), F32),
        jax.ShapeDtypeStruct((8, 4 * FFC), F32),
    )
    return pl.pallas_call(
        functools.partial(central_kernel, rb),
        out_shape=shapes,
        in_specs=[VMEM] * 10 + [FAR] * 16,
        out_specs=[VMEM] * len(shapes),
        scratch_shapes=[
            pltpu.VMEM((D, D), BF16),
            pltpu.VMEM((D, 4 * FFC), BF16),
            pltpu.VMEM((D, 4 * FFC), BF16),
            pltpu.VMEM((own, 4 * FFC), F32),
            pltpu.VMEM((own, 4 * FFC), BF16),
            pltpu.VMEM((own, 4 * FFC), BF16),
            pltpu.VMEM((D, own), BF16),
            pltpu.VMEM((D, own), BF16),
            pltpu.VMEM((D, own), BF16),
            pltpu.VMEM((TERMS * 128, H * PAIR), BF16),
            pltpu.VMEM((own, D), BF16),
            pltpu.VMEM((own, D), F32),
            pltpu.VMEM((own, D), F32),
            pltpu.VMEM((own, D), BF16),
            pltpu.VMEM((own, D), BF16),
            pltpu.SemaphoreType.DMA((3,)),
        ],
        compiler_params=params(30),
        cost_estimate=SMALL,
        name="central",
    )(x, o_near, o_more, o_far, teacher, cot, mask, vec, bup, scale, *pieces)


def pull_units(units, bias_ref):
    lane = lane_of((QB, PAIR))

    def mask(x, h):
        return jnp.where((lane < HD) if h == 0 else (lane >= HD), x, jnp.zeros_like(x))

    def score(one):
        keys, values, _, where, _ = one["part"]
        one["s"] = dot_t(keys[where, one["lanes"]], one["q"][one["rows"], one["qlanes"]])
        one["d"] = dot_t(values[where, one["lanes"]], one["g"][one["grows"], one["lanes"]])

    def soften(one):
        s = one.pop("s")
        p = jnp.exp(s + bias_ref[...] if one["part"][4] else s)
        one["p"], one["ds"] = p.astype(BF16), (p * one.pop("d")).astype(BF16)

    def finish(one):
        _, _, keys_t, where, last = one["part"]
        h, sums = one["h"], one["sums"]
        part = dot(keys_t[one["tlanes"], where], one["ds"])
        sums[h] = part if h not in sums else sums[h] + part
        if h == 0:
            sums["before"] = one
            return
        two = (sums.pop("before"), one)
        q = jnp.concatenate([mask(u["q"][u["rows"], u["qlanes"]], u["h"]) for u in two], axis=0)
        g = jnp.concatenate([mask(u["g"][u["grows"], u["lanes"]], u["h"]) for u in two], axis=0)
        dk = dot(jnp.concatenate([u.pop("ds") for u in two], axis=1), q)
        dv = dot(jnp.concatenate([u.pop("p") for u in two], axis=1), g)
        one["take"](dk, dv)
        if last:
            both = jnp.concatenate([sums[0], sums[1]], axis=0)
            one["take_q"]((jnp.transpose(both) * SCALE).astype(BF16))

    staged(units, (score, soften, finish), 2)


def block_units(q_ref, rows, q_pair, g_ref, grows, pair, parts, takes, take_q):
    sums, units = {}, []
    for part, take in zip(parts, takes):
        for h in range(2):
            units.append(
                dict(
                    q=q_ref, rows=rows, qlanes=head_lanes(q_pair, h), g=g_ref, grows=grows, lanes=head_lanes(pair, h), h=h,
                    part=part, tlanes=slice((2 * pair + h) * HD, (2 * pair + h + 1) * HD), take=take, take_q=take_q, sums=sums,
                )
            )
    return units


def pull_near_kernel(base, q_ref, g_ref, kh_ref, ko_ref, vh_ref, vo_ref, kth_ref, kto_ref, gh_ref, gq_ref, part_ref, bias_ref, late_ref):
    bias_ref[...] = causal(False)
    halo, own = (kh_ref, vh_ref, kth_ref), (ko_ref, vo_ref, kto_ref)
    units = []
    for pair in range(2):
        lanes_k = slice(2 * pair * PAIR, (2 * pair + 1) * PAIR)
        lanes_v = slice((2 * pair + 1) * PAIR, (2 * pair + 2) * PAIR)

        def halo_first(dk, dv, both=((lanes_k, 0), (lanes_v, 1))):
            for lanes, n in both:
                d = (dk, dv)[n]
                gh_ref[0:QB, lanes] = d[0:QB].astype(BF16)
                late_ref[:, lanes] = d[QB:]

        def halo_second(dk, dv, both=((lanes_k, 0), (lanes_v, 1))):
            for lanes, n in both:
                gh_ref[QB:, lanes] = (late_ref[:, lanes] + (dk, dv)[n]).astype(BF16)

        def own_first(dk, dv, both=((lanes_k, 0), (lanes_v, 1))):
            for lanes, n in both:
                part_ref[0:QB, lanes] = (dk, dv)[n]

        def own_more(dk, dv, both=((lanes_k, 0), (lanes_v, 1))):
            for lanes, n in both:
                part_ref[0:QB, lanes] += (dk, dv)[n]

        def own_last(dk, dv, both=((lanes_k, 0), (lanes_v, 1))):
            for lanes, n in both:
                part_ref[QB:, lanes] = (dk, dv)[n]

        takes = ((halo_first, own_first), (halo_second, own_more, own_last))
        for i, parts in enumerate(near_parts(halo, own)):
            rows = slice(i * QB, (i + 1) * QB)

            def take_q(dq, rows=rows, pair=pair):
                gq_ref[rows, pair * PAIR : (pair + 1) * PAIR] = dq

            units += block_units(q_ref, rows, pair, g_ref, rows, base + pair, parts, takes[i], take_q)
    pull_units(units, bias_ref)


def pull_near(base, qa, ga, k_halo, k, v_halo, v, kt_halo, kt):
    return pl.pallas_call(
        functools.partial(pull_near_kernel, base),
        out_shape=(
            jax.ShapeDtypeStruct((HALO, D), BF16),
            jax.ShapeDtypeStruct((HALO, D // 2), BF16),
            jax.ShapeDtypeStruct((HALO, D), F32),
        ),
        in_specs=[VMEM] * 8,
        out_specs=[VMEM] * 3,
        scratch_shapes=[pltpu.VMEM((QB, QB), F32), pltpu.VMEM((QB, D), F32)],
        compiler_params=params(10),
        cost_estimate=SMALL,
        name="pull_near",
    )(qa, ga, k_halo, k, v_halo, v, kt_halo, kt)


def pull_far_kernel(q_ref, go_ref, k_ref, v_ref, kt_ref, qa_ref, qb_ref, pa_ref, pb_ref, g_ref, bias_ref):
    bias_ref[...] = causal(False)
    refs = (k_ref, v_ref, kt_ref)
    parts = ((*refs, slice(0, HALO), False), (*refs, slice(HALO, HALO + QB), True))
    units = []
    for pair in range(4):
        at, within = pair * WA, 2 * (pair % 2) * PAIR
        near_q, near_part = ((qa_ref, pa_ref), (qb_ref, pb_ref))[pair // 2]
        g_ref[0:HALO, at : at + COLS] = near_q[:, within // 2 : within // 2 + PAIR]

        def older(dk, dv, at=at, within=within, near_part=near_part):
            for n, d in enumerate((dk, dv)):
                total = near_part[:, within + n * PAIR : within + (n + 1) * PAIR] + d
                g_ref[0:HALO, at + (n + 1) * COLS : at + (n + 2) * COLS] = total.astype(BF16)

        def newest(dk, dv, at=at):
            for n, d in enumerate((dk, dv)):
                g_ref[HALO:, at + (n + 1) * COLS : at + (n + 2) * COLS] = d.astype(BF16)

        def take_q(dq, at=at):
            g_ref[HALO:, at : at + COLS] = dq

        own = slice(HALO, HALO + QB)
        units += block_units(q_ref, slice(0, QB), pair, go_ref, own, pair, parts, (older, newest), take_q)
    pull_units(units, bias_ref)


def pull_far(qa, ga, k, v, kt, gq_near, gq_more, part_near, part_more):
    own = k.shape[0]
    return pl.pallas_call(
        pull_far_kernel,
        out_shape=jax.ShapeDtypeStruct((own, 4 * WA), BF16),
        in_specs=[VMEM] * 9,
        out_specs=VMEM,
        scratch_shapes=[pltpu.VMEM((QB, QB), F32)],
        compiler_params=params(10),
        cost_estimate=SMALL,
        name="pull_far",
    )(qa, ga, k, v, kt, gq_near, gq_more, part_near, part_more)


def norm_sums(small_ref, x, g_n1):
    xhat, _ = normalize(x.astype(F32))
    small_ref[0:8, :] += fold(g_n1 * xhat)
    small_ref[8:16, :] += fold(g_n1)


def halo_back_kernel(ga_ref, gb_ref, w_ref, x_ref, out_ref, small_ref):
    small_ref[...] = jnp.zeros_like(small_ref)

    def block(i, carry):
        rows = rows_of(i * 128, 128)
        total = None
        for t in range(4):
            g = (ga_ref, gb_ref)[t // 2][rows, (t % 2) * 2 * COLS : (t % 2 + 1) * 2 * COLS]
            part = dot_t(g, w_ref[:, t * WA + COLS : (t + 1) * WA])
            total = part if total is None else total + part
        out_ref[rows, :] = total.astype(BF16)
        norm_sums(small_ref, x_ref[rows, :], total)
        return carry

    lax.fori_loop(0, HALO // 128, block, 0)


def halo_back(g_near, g_more, w, halo):
    return pl.pallas_call(
        halo_back_kernel,
        out_shape=(jax.ShapeDtypeStruct((HALO, D), BF16), jax.ShapeDtypeStruct((16, D), F32)),
        compiler_params=params(6),
        cost_estimate=SMALL,
        name="halo_back",
    )(g_near, g_more, w, halo)


def own_back_kernel(
    x_ref, ga_ref, gb_ref, g_ref, nth_ref, nto_ref, w_ref, small_halo, small_two, gbup_ref, scale_ref,
    gn_ref, theirs_ref, mine_ref, small_ref, gh_ref
):
    me, place = lax.axis_index("fsdp"), lax.axis_index("tp")
    own = x_ref.shape[0]
    small_ref[...] = small_halo[...]
    gh_ref[:, 0:D] = ga_ref[...]
    gh_ref[:, D:] = gb_ref[...]

    def block(i, carry):
        rows = rows_of(i * 128, 128)
        g_n1 = dot_t(g_ref[rows, :], w_ref[...])
        gn_ref[rows, :] = g_n1
        norm_sums(small_ref, x_ref[rows, :], g_n1)
        return carry

    lax.fori_loop(0, own // 128, block, 0)
    sums = lambda ref, j: jnp.sum(ref[8 * j : 8 * j + 8, :], axis=0, keepdims=True)
    loss = jnp.sum(sums(small_two, 1), axis=1, keepdims=True) * scale_ref[4:5, 0:1]
    vectors = jnp.concatenate(
        [sums(small_ref, 0), sums(small_ref, 1), sums(small_two, 4), sums(small_two, 2), sums(small_two, 3),
         sums(small_two, 0), jnp.zeros((2, D), F32)],
        axis=0,
    )
    high = loss.astype(BF16).astype(F32)
    row, lane = lax.broadcasted_iota(jnp.int32, (EXTRA, 128), 0), lane_of((EXTRA, 128))
    ones_own, ones_halo = jnp.ones((8, own), BF16), jnp.ones((8, HALO), BF16)

    def grads(s, carry):
        tp = lax.bitwise_and(place + s, 3)
        g_own = g_ref[:, rows_of(tp * WA, WA)]
        g_halo = gh_ref[:, rows_of(tp * 2 * COLS, 2 * COLS)]
        total = dot(nto_ref[...], g_own)
        more = dot(nth_ref[...], g_halo)
        low = jnp.concatenate([total[:, 0:COLS], total[:, COLS:] + more], axis=1).astype(BF16)
        by_own, by_halo = dot(ones_own, g_own)[0:1], dot(ones_halo, g_halo)[0:1]
        ups = gbup_ref[0:1, rows_of(tp * FFC, FFC)]
        mids = jnp.concatenate(
            [by_own[:, 0:COLS], by_own[:, 2 * COLS :] + by_halo[:, COLS:]]
            + [ups[:, 128 * j : 128 * j + 128] for j in range(4)]
            + [jnp.zeros((2, 128), F32)],
            axis=0,
        ).astype(BF16)
        for r in range(8):
            dst = theirs_ref if r % 2 else mine_ref
            dst[r // 2, s, 0:ROWS, :] = low[ROWS * r : ROWS * (r + 1)]
            dst[r // 2, s, ROWS:, 128:256] = mids
        return carry

    lax.fori_loop(0, 4, grads, 0)
    for r in range(8):
        owner = lax.bitwise_xor(me, r)
        block = pltpu.roll(vectors, lax.rem(D - owner * ROWS, D), 1)[:, 0:128]
        block = jnp.where((row == 6) & (lane == 0), high, block)
        block = jnp.where((row == 6) & (lane == 1), loss - high, block).astype(BF16)
        dst = theirs_ref if r % 2 else mine_ref
        for s in range(4):
            dst[r // 2, s, ROWS:, 0:128] = block
            dst[r // 2, s, ROWS:, 256:384] = jnp.zeros((EXTRA, 128), BF16)


def own_back(x, g_near, g_more, g_own, nt_halo, nt, w, small_halo, small_two, gbup, scale):
    own = x.shape[0]
    send = jax.ShapeDtypeStruct((4, 4, ROWS + EXTRA, WA), BF16)
    return pl.pallas_call(
        own_back_kernel,
        out_shape=(jax.ShapeDtypeStruct((own, D), F32), send, send),
        scratch_shapes=[pltpu.VMEM((16, D), F32), pltpu.VMEM((HALO, 2 * D), BF16)],
        compiler_params=params(10),
        cost_estimate=SMALL,
        name="own_back",
    )(x, g_near, g_more, g_own, nt_halo, nt, w, small_halo, small_two, gbup, scale)


def close_kernel(x_ref, gn_ref, back_ref, gh_ref, vec_ref, out_ref):
    own = x_ref.shape[0]

    def block(at, extra):
        rows = rows_of(at, 128)
        xhat, rstd = normalize(x_ref[rows, :].astype(F32))
        g_n1 = gn_ref[rows, :] + extra
        out_ref[rows, :] = gh_ref[rows, :] + norm_pull(g_n1, vec_ref[0:1, :], xhat, rstd)

    def first(i, carry):
        block(i * 128, 0.0)
        return carry

    def second(i, carry):
        block(own - HALO + i * 128, back_ref[rows_of(i * 128, 128), :].astype(F32))
        return carry

    lax.fori_loop(0, (own - HALO) // 128, first, 0)
    lax.fori_loop(0, HALO // 128, second, 0)


def close(x, g_n1, back, g_h1, vec):
    return pl.pallas_call(
        close_kernel,
        out_shape=jax.ShapeDtypeStruct(x.shape, F32),
        compiler_params=params(8),
        cost_estimate=SMALL,
        name="close",
    )(x, g_n1, back, g_h1, vec)


def unpack_f_kernel(k_ref, r1, r2, r3, wo_ref, wup_ref, wdn_ref):
    total = (k_ref[0].astype(F32) + r1[...].astype(F32)) + (r2[...].astype(F32) + r3[...].astype(F32))
    wo_ref[...] = total[:, 0:COLS]
    wup_ref[...] = total[:, COLS : COLS + FFC]
    wdn_ref[...] = total[:, COLS + FFC :]


def unpack_f(k, r1, r2, r3):
    return pl.pallas_call(
        unpack_f_kernel,
        out_shape=(
            jax.ShapeDtypeStruct((ROWS, COLS), F32),
            jax.ShapeDtypeStruct((ROWS, FFC), F32),
            jax.ShapeDtypeStruct((ROWS, FFC), F32),
        ),
        compiler_params=params(6),
        name="unpack_f",
    )(k, r1, r2, r3)


def unpack_a_kernel(k_ref, r1, r2, r3, wq_ref, wk_ref, wv_ref, bq_ref, bv_ref, bup_ref, vec_ref):
    me = lax.axis_index("fsdp")
    total = (k_ref[0].astype(F32) + r1[...].astype(F32)) + (r2[...].astype(F32) + r3[...].astype(F32))
    wq_ref[...] = total[0:ROWS, 0:COLS]
    wk_ref[...] = total[0:ROWS, COLS : 2 * COLS]
    wv_ref[...] = total[0:ROWS, 2 * COLS :]
    vec_ref[...] = total[ROWS:, 0:128]
    mids = pltpu.roll(total[ROWS:, 128:256], lax.rem(128 - me * 8, 128), 1)
    for i in range(2):
        bq_ref[i : i + 1, :] = mids[0:1, i * HD : i * HD + 8]
        bv_ref[i : i + 1, :] = mids[1:2, i * HD : i * HD + 8]
    for i in range(8):
        at = (i % 2) * HD
        bup_ref[i : i + 1, :] = mids[2 + i // 2 : 3 + i // 2, at : at + 8]


def unpack_a(k, r1, r2, r3):
    small = jax.ShapeDtypeStruct((ROWS, COLS), F32)
    return pl.pallas_call(
        unpack_a_kernel,
        out_shape=(
            small,
            small,
            small,
            jax.ShapeDtypeStruct((2, 8), F32),
            jax.ShapeDtypeStruct((2, 8), F32),
            jax.ShapeDtypeStruct((8, 8), F32),
            jax.ShapeDtypeStruct((EXTRA, 128), F32),
        ),
        compiler_params=params(6),
        name="unpack_a",
    )(k, r1, r2, r3)


def to_mask(x, mask):
    return lax.ppermute(x, "fsdp", [(i, i ^ mask) for i in range(8)])


def to_step(x, step):
    return lax.ppermute(x, "tp", [(i, (i + step) % 4) for i in range(4)])


def add(a, b):
    return (a.astype(F32) + b.astype(F32)).astype(BF16)


def after(values, others):
    return lax.optimization_barrier((values, others))[0]


def local_fast(
    layer_input, segment_ids, valid_mask, teacher, cotangent, ln1_gain, ln1_bias, w_q, w_k, w_v, b_q, b_v,
    w_o, b_o, ln2_gain, ln2_bias, w_up, b_up, w_down, b_down
):
    place = lax.axis_index("tp")
    own = layer_input.shape[0]
    tokens_all = own * lax.axis_size("fsdp") * lax.axis_size("tp")

    shard_a, shard_f = pack_weights(
        (w_q, w_k, w_v, w_o.T, w_up, w_down.T, ln1_gain, ln1_bias, b_o, ln2_gain, ln2_bias, b_down, b_q, b_v, b_up,
         valid_mask)
    )
    steps_a = [shard_a] + [to_step(shard_a, s) for s in (1, 2, 3)]
    line_a = jnp.stack(steps_a)
    steps_f = [shard_f] + [to_step(shard_f, s) for s in (1, 2, 3)]
    over_f = [to_mask(x, 1) for x in steps_f]
    near_a = [to_mask(line_a, m) for m in (2, 4, 6)]
    halves_a = after([jnp.stack(steps_a[0:2]), jnp.stack(steps_a[2:4])], steps_f)
    over_a = [to_mask(a, 1) for a in halves_a]
    line_f = jnp.stack(after(steps_f, (over_a, near_a)))
    pieces_a = [line_a] + near_a + over_a + [to_mask(a, 1) for a in near_a]
    halo = lax.ppermute(layer_input[own - HALO :], "tp", [(i, i + 1) for i in range(3)])
    f_x, f_y = to_mask(line_f, 2), to_mask(line_f, 4)

    ids = segment_ids + 16 * jnp.arange(segment_ids.shape[0], dtype=jnp.int32)[:, None]
    ids = jnp.concatenate([jnp.full((HALO,), -1, jnp.int32), ids.reshape(-1)])
    id_col = lax.dynamic_slice_in_dim(ids, place * own, HALO + own)[:, None]
    mask = valid_mask.astype(F32)[:, None]

    q, k, v, kt, nt, w_all, vec, bup, scale, head = project(after(layer_input, over_f), id_col, pieces_a, tokens_all)
    o_far, qa_far = attend_far(q, k, v)
    f_x, f_y = after((f_x, f_y), o_far)
    halo = after(halo, o_far)
    f_xy = [to_mask(f_y[0:2], 2), to_mask(f_x[2:4], 4)]
    k_halo, v_halo, kt_halo, nt_halo = project_halo(halo, id_col, w_all, vec, head)
    o_near, qa_near = attend_near(0, q, k_halo, k, v_halo, v)
    q = after(q, o_near)
    o_more, qa_more = attend_near(2, q, k_halo, k, v_halo, v)
    near_f = [f_x, f_y] + after(f_xy, o_more)
    pieces_f = [x[None] for x in steps_f] + near_f + [x[None] for x in over_f] + [to_mask(a, 1) for a in near_f]
    layer_out, g_h1, ga, theirs_f, mine_f, small_two, gbup = central(
        layer_input, o_near, o_more, o_far, teacher, cotangent, mask, vec, bup, scale, pieces_f
    )

    def near(base, qa, ga):
        return pull_near(base, qa, ga, k_halo, k, v_halo, v, kt_halo, kt)

    g_near, gq_near, part_near = near(0, qa_near, ga)
    half = add(after(mine_f, g_near), to_mask(theirs_f, 1))
    from_x, from_y = to_mask(half[3, 0:2], 2), to_mask(half[3, 2:4], 4)
    g_more, gq_more, part_more = near(2, after(qa_more, half), ga)
    gn_halo, small_halo = halo_back(g_near, g_more, w_all, halo)
    back = lax.ppermute(gn_halo, "tp", [(i + 1, i) for i in range(3)])
    from_x, from_y = after((from_x, from_y), gn_halo)
    for_x = jnp.concatenate([half[1, 0:2], add(half[1, 2:4], from_y)])
    for_y = jnp.concatenate([add(half[2, 0:2], from_x), half[2, 2:4]])
    got_x, got_y = to_mask(for_x, 2), to_mask(for_y, 4)
    g_own = pull_far(after(qa_far, (for_x, for_y)), ga, k, v, kt, gq_near, gq_more, part_near, part_more)
    gn_own, theirs_a, mine_a = own_back(
        layer_input, g_near, g_more, g_own, nt_halo, nt, w_all, small_halo, small_two, gbup, scale
    )
    got_x, got_y = after((got_x, got_y), gn_own)
    line = (half[0].astype(F32) + got_x.astype(F32) + got_y.astype(F32)).astype(BF16)
    grad_wo, grad_wup, grad_wdn = unpack_f(line, *[to_step(line[s], s) for s in (1, 2, 3)])

    half = add(mine_a, to_mask(after(theirs_a, back), 1))
    from_x, from_y, from_xy = (to_mask(half[m], 2 * m) for m in (1, 2, 3))
    line = (half[0].astype(F32) + from_x.astype(F32) + from_y.astype(F32) + from_xy.astype(F32)).astype(BF16)
    grad_wq, grad_wk, grad_wv, grad_bq, grad_bv, grad_bup, few = unpack_a(
        line, *[to_step(line[s], s) for s in (1, 2, 3)]
    )
    grad_input = close(layer_input, gn_own, back, g_h1, vec)
    six = [few[j, 0:ROWS] for j in range(6)]
    loss = few[6, 0] + few[6, 1]
    return (
        layer_out, loss, grad_input, six[0], six[1], grad_wq, grad_wk, grad_wv, grad_bq, grad_bv, grad_wo.T, six[2],
        six[3], six[4], grad_wup, grad_bup, grad_wdn.T, six[5]
    )


def solution(mesh):
    tokens = P(("fsdp", "tp"), None)
    rows, crossed, heads = P("fsdp"), P("fsdp", "tp"), P("tp", "fsdp")
    placed = (
        tokens,
        P("fsdp", None),
        P(("fsdp", "tp")),
        tokens,
        tokens,
        rows,
        rows,
        crossed,
        crossed,
        crossed,
        heads,
        heads,
        heads,
        rows,
        rows,
        rows,
        crossed,
        heads,
        heads,
        rows,
    )
    given = (
        tokens,
        P(),
        tokens,
        rows,
        rows,
        crossed,
        crossed,
        crossed,
        heads,
        heads,
        heads,
        rows,
        rows,
        rows,
        crossed,
        heads,
        heads,
        rows,
    )
    sizes = (mesh.shape["fsdp"], mesh.shape["tp"])
    body = local_fast if sizes == (8, 4) else local
    return jax.shard_map(body, mesh=mesh, in_specs=placed, out_specs=given, check_vma=False)
```

```python
import functools

import jax
import jax.numpy as jnp
from jax import lax
from jax.experimental import pallas as pl
from jax.experimental.pallas import tpu as pltpu
from jax.sharding import PartitionSpec as P

D = 512
H = 8
HD = 64
LEN = 1024
HALO = 512
PAIR = 2 * HD
NEG = -1e30
SCALE = HD ** (-0.5)
F32 = jnp.float32
BF16 = jnp.bfloat16
MIB = 1 << 20

CONTRACT_LAST = (((1,), (1,)), ((), ()))


def dot(a, b):
    return jnp.dot(a, b, preferred_element_type=F32)


def dot_t(a, b):
    return lax.dot_general(a, b, CONTRACT_LAST, preferred_element_type=F32)


def normalize(x):
    center = x - jnp.mean(x, axis=-1, keepdims=True)
    rstd = lax.rsqrt(jnp.mean(center * center, axis=-1, keepdims=True) + 1e-05)
    return center * rstd, rstd


def norm_pull(g, gain, xhat, rstd):
    gx = g * gain
    return rstd * (
        gx
        - jnp.mean(gx, axis=-1, keepdims=True)
        - xhat * jnp.mean(gx * xhat, axis=-1, keepdims=True)
    )


def fold(x):
    return jnp.sum(x.reshape(x.shape[0] // 8, 8, x.shape[1]), axis=0)


def rows_of(start, size, unit=128):
    return pl.ds(pl.multiple_of(start, unit), size)


def forward_kernel(
    qb, x_ref, vec_ref, w_ref, idr_ref, idc_ref, n_ref, q_ref, k_ref, v_ref, o_ref, lse_ref, bias_ref, stat_ref
):
    ext, own = x_ref.shape[0], o_ref.shape[0]
    window = HALO + qb

    def project(i, carry):
        rows = rows_of(i * 128, 128)
        xhat, _ = normalize(x_ref[rows, :].astype(F32))
        n1 = (xhat * vec_ref[0:1, :] + vec_ref[1:2, :]).astype(BF16)
        n_ref[rows, :] = n1
        k_ref[rows, :] = dot(n1, w_ref[:, D : 2 * D]).astype(BF16)
        v_ref[rows, :] = (dot(n1, w_ref[:, 2 * D : 3 * D]) + vec_ref[3:4, :]).astype(BF16)
        return carry

    lax.fori_loop(0, ext // 128, project, 0)

    def project_q(i, carry):
        rows = rows_of(i * 128, 128)
        q = dot(n_ref[rows_of(HALO + i * 128, 128), :], w_ref[:, 0:D]) + vec_ref[2:3, :]
        q_ref[rows, :] = q.astype(BF16) * jnp.asarray(SCALE, BF16)
        return carry

    lax.fori_loop(0, own // 128, project_q, 0)

    def query_block(i, carry):
        first = i * qb
        key = lax.broadcasted_iota(jnp.int32, (qb, window), 1)
        query = lax.broadcasted_iota(jnp.int32, (qb, window), 0)
        same = idc_ref[rows_of(HALO + first, qb), :] == idr_ref[:, rows_of(first, window)]
        bias_ref[...] = jnp.where(same & (key <= query + HALO), 0.0, NEG)

        def pair(g, inner):
            lanes = rows_of(g * PAIR, PAIR)
            lane = lax.broadcasted_iota(jnp.int32, (qb, PAIR), 1)
            keys = k_ref[rows_of(first, window), lanes]
            values = v_ref[rows_of(first, window), lanes]
            both = q_ref[rows_of(first, qb), lanes]
            got = None
            for h in range(2):
                mine = (lane < HD) if h == 0 else (lane >= HD)
                s = dot_t(jnp.where(mine, both, jnp.zeros_like(both)), keys) + bias_ref[...]
                top = jnp.max(s, axis=-1, keepdims=True)
                p = jnp.exp(s - top)
                total = jnp.sum(p, axis=-1, keepdims=True)
                o = dot(p.astype(BF16), values) / total
                got = o if h == 0 else jnp.where(mine, o, got)
                stat_ref[...] = jnp.where(lane == 2 * g + h, top + jnp.log(total), stat_ref[...])
            o_ref[rows_of(first, qb), lanes] = got.astype(BF16)
            return inner

        lax.fori_loop(0, D // PAIR, pair, 0)
        lse_ref[:, rows_of(first, qb)] = jnp.transpose(stat_ref[...])[0:H, :]
        return carry

    stat_ref[...] = jnp.zeros_like(stat_ref)
    lax.fori_loop(0, own // qb, query_block, 0)


def attention_forward(x_ext, vecs, w_qkv, id_row, id_col, own):
    ext = x_ext.shape[0]
    qb = 256 if own % 256 == 0 else 128
    shapes = (
        jax.ShapeDtypeStruct((ext, D), BF16),
        jax.ShapeDtypeStruct((own, D), BF16),
        jax.ShapeDtypeStruct((ext, D), BF16),
        jax.ShapeDtypeStruct((ext, D), BF16),
        jax.ShapeDtypeStruct((own, D), BF16),
        jax.ShapeDtypeStruct((H, own), F32),
    )
    return pl.pallas_call(
        functools.partial(forward_kernel, qb),
        out_shape=shapes,
        scratch_shapes=[pltpu.VMEM((qb, HALO + qb), F32), pltpu.VMEM((qb, 128), F32)],
        compiler_params=pltpu.CompilerParams(vmem_limit_bytes=48 * MIB),
        name="attention_forward",
    )(x_ext, vecs, w_qkv, id_row, id_col)


def middle_kernel(
    rb,
    scale_ref,
    x_ref,
    o_ref,
    teacher_ref,
    cot_ref,
    mask_ref,
    vec_ref,
    bup_ref,
    wo_ref,
    wup_ref,
    wdn_ref,
    out_ref,
    gh_ref,
    go_ref,
    delta_ref,
    gwo_ref,
    gwup_ref,
    gwdn_ref,
    small_ref,
    gbup_ref,
    slope_ref,
    hid_ref,
    gpre_ref,
    n2t_ref,
    gmlpt_ref,
    gattnt_ref,
):
    own = x_ref.shape[0]
    ff = wup_ref.shape[1]
    chunk = 512
    small_ref[...] = jnp.zeros_like(small_ref)
    head_of = lax.broadcasted_iota(jnp.int32, (D, 128), 0) // HD
    pick = (head_of == lax.broadcasted_iota(jnp.int32, (D, 128), 1)).astype(BF16)

    def block(i, carry):
        rows = rows_of(i * rb, rb)
        out_bias, gain, offset, down_bias = (vec_ref[j : j + 1, :] for j in range(4))
        h1 = x_ref[rows, :].astype(F32) + dot_t(o_ref[rows, :], wo_ref[...]) + out_bias
        xhat, rstd = normalize(h1)
        n2 = xhat * gain + offset
        n2_low = n2.astype(BF16)
        n2t_ref[:, rows] = jnp.transpose(n2).astype(BF16)
        for c in range(0, ff, chunk):
            pre = dot(n2_low, wup_ref[:, c : c + chunk]) + bup_ref[:, c : c + chunk]
            s = jax.nn.sigmoid(1.702 * pre)
            value = pre * s
            hid_ref[rows, c : c + chunk] = value.astype(BF16)
            slope_ref[:, c : c + chunk] = s + 1.702 * value * (1.0 - s)
        out = h1 + dot_t(hid_ref[rows, :], wdn_ref[...]) + down_bias
        out_ref[rows, :] = out.astype(BF16)
        valid = mask_ref[rows, :]
        diff = (out - teacher_ref[rows, :].astype(F32)) * valid
        g_out = cot_ref[rows, :].astype(F32) + scale_ref[0, 0] * diff
        small_ref[0:8, :] += fold(g_out)
        small_ref[8:16, :] += fold(diff * diff)
        g_mlp = g_out.astype(BF16)
        gmlpt_ref[:, rows] = jnp.transpose(g_out).astype(BF16)
        for c in range(0, ff, chunk):
            g_hid = dot(g_mlp, wdn_ref[:, c : c + chunk])
            gpre_ref[rows, c : c + chunk] = (g_hid * slope_ref[:, c : c + chunk]).astype(BF16)
        g_n2 = dot_t(gpre_ref[rows, :], wup_ref[...])
        small_ref[16:24, :] += fold(g_n2 * xhat)
        small_ref[24:32, :] += fold(g_n2)
        g_h1 = g_out + norm_pull(g_n2, gain, xhat, rstd)
        gh_ref[rows, :] = g_h1
        small_ref[32:40, :] += fold(g_h1)
        gattnt_ref[:, rows] = jnp.transpose(g_h1).astype(BF16)
        g_o = dot(g_h1.astype(BF16), wo_ref[...]).astype(BF16)
        go_ref[rows, :] = g_o
        product = g_o.astype(F32) * o_ref[rows, :].astype(F32)
        high = product.astype(BF16)
        low = (product - high.astype(F32)).astype(BF16)
        delta_ref[:, rows] = jnp.transpose(dot(high, pick) + dot(low, pick))[0:H, :]
        return carry

    lax.fori_loop(0, own // rb, block, 0)
    ones = jnp.ones((8, own), BF16)

    def grads(i, carry):
        cols = rows_of(i * chunk, chunk)
        gwdn_ref[:, cols] = dot(gmlpt_ref[...], hid_ref[:, cols]).astype(BF16)
        gwup_ref[:, cols] = dot(n2t_ref[...], gpre_ref[:, cols]).astype(BF16)
        gbup_ref[:, cols] = dot(ones, gpre_ref[:, cols])
        return carry

    lax.fori_loop(0, ff // chunk, grads, 0)
    gwo_ref[...] = dot(gattnt_ref[...], o_ref[...]).astype(BF16)


def middle(scale, x, o, teacher, cot, mask, vecs, b_up, w_o, w_up, w_dn):
    own, ff = x.shape[0], w_up.shape[1]
    rb = 256 if own % 256 == 0 else 128
    shapes = (
        jax.ShapeDtypeStruct((own, D), BF16),
        jax.ShapeDtypeStruct((own, D), F32),
        jax.ShapeDtypeStruct((own, D), BF16),
        jax.ShapeDtypeStruct((H, own), F32),
        jax.ShapeDtypeStruct((D, D), BF16),
        jax.ShapeDtypeStruct((D, ff), BF16),
        jax.ShapeDtypeStruct((D, ff), BF16),
        jax.ShapeDtypeStruct((40, D), F32),
        jax.ShapeDtypeStruct((8, ff), F32),
    )
    whole = pl.BlockSpec(memory_space=pltpu.VMEM)
    return pl.pallas_call(
        functools.partial(middle_kernel, rb),
        out_shape=shapes,
        in_specs=[pl.BlockSpec(memory_space=pltpu.SMEM)] + [whole] * 10,
        out_specs=[whole] * len(shapes),
        scratch_shapes=[
            pltpu.VMEM((rb, ff), F32),
            pltpu.VMEM((own, ff), BF16),
            pltpu.VMEM((own, ff), BF16),
            pltpu.VMEM((D, own), BF16),
            pltpu.VMEM((D, own), BF16),
            pltpu.VMEM((D, own), BF16),
        ],
        compiler_params=pltpu.CompilerParams(vmem_limit_bytes=56 * MIB),
        name="middle",
    )(scale, x, o, teacher, cot, mask, vecs, b_up, w_o, w_up, w_dn)


def backward_kernel(
    qb,
    q_ref,
    k_ref,
    v_ref,
    go_ref,
    lse_ref,
    delta_ref,
    idr_ref,
    idc_ref,
    n_ref,
    x_ref,
    w_ref,
    gn_halo_ref,
    gn_ref,
    gw_ref,
    small_ref,
    bias_ref,
    kt_ref,
    nt_ref,
    dqt_ref,
    dk_ref,
    dv_ref,
    g_ref,
):
    ext, own = k_ref.shape[0], q_ref.shape[0]
    window = HALO + qb
    dk_ref[...] = jnp.zeros_like(dk_ref)
    dv_ref[...] = jnp.zeros_like(dv_ref)
    small_ref[...] = jnp.zeros_like(small_ref)

    def turn(i, carry):
        rows = rows_of(i * 128, 128)
        kt_ref[:, rows] = jnp.transpose(k_ref[rows, :].astype(F32)).astype(BF16)
        nt_ref[:, rows] = jnp.transpose(n_ref[rows, :].astype(F32)).astype(BF16)
        return carry

    lax.fori_loop(0, ext // 128, turn, 0)

    def query_block(i, carry):
        first = i * qb
        key = lax.broadcasted_iota(jnp.int32, (window, qb), 0)
        query = lax.broadcasted_iota(jnp.int32, (window, qb), 1)
        same = idc_ref[rows_of(first, window), :] == idr_ref[:, rows_of(HALO + first, qb)]
        bias_ref[...] = jnp.where(same & (key <= query + HALO), 0.0, NEG)

        def pair(g, inner):
            lanes = rows_of(g * PAIR, PAIR)
            lane = lax.broadcasted_iota(jnp.int32, (qb, PAIR), 1)
            keys = k_ref[rows_of(first, window), lanes]
            values = v_ref[rows_of(first, window), lanes]
            both_q = q_ref[rows_of(first, qb), lanes]
            both_g = go_ref[rows_of(first, qb), lanes]
            all_lse = lse_ref[:, rows_of(first, qb)]
            all_delta = delta_ref[:, rows_of(first, qb)]
            line = lax.broadcasted_iota(jnp.int32, (H, qb), 0)
            dk, dv = None, None
            for h in range(2):
                head = 2 * g + h
                mine = (lane < HD) if h == 0 else (lane >= HD)
                q = jnp.where(mine, both_q, jnp.zeros_like(both_q))
                g_o = jnp.where(mine, both_g, jnp.zeros_like(both_g))
                lse = jnp.sum(jnp.where(line == head, all_lse, 0.0), axis=0, keepdims=True)
                delta = jnp.sum(jnp.where(line == head, all_delta, 0.0), axis=0, keepdims=True)
                p = jnp.exp(dot_t(keys, q) + bias_ref[...] - lse)
                ds = (p * (dot_t(values, g_o) - delta)).astype(BF16)
                dv_h = dot(p.astype(BF16), g_o)
                dk_h = dot(ds, q)
                dk, dv = (dk_h, dv_h) if h == 0 else (dk + dk_h, dv + dv_h)
                dqt_ref[rows_of(head * HD, HD, HD), rows_of(first, qb)] = dot(
                    kt_ref[rows_of(head * HD, HD, HD), rows_of(first, window)], ds
                )
            dk_ref[rows_of(first, window), lanes] += dk
            dv_ref[rows_of(first, window), lanes] += dv
            return inner

        lax.fori_loop(0, D // PAIR, pair, 0)
        return carry

    lax.fori_loop(0, own // qb, query_block, 0)

    def gather(i, carry):
        rows = rows_of(i * 128, 128)
        g_ref[rows, D : 2 * D] = dk_ref[rows, :].astype(BF16)
        g_ref[rows, 2 * D : 3 * D] = dv_ref[rows, :].astype(BF16)
        return carry

    lax.fori_loop(0, ext // 128, gather, 0)

    def gather_q(i, carry):
        cols = rows_of(i * 128, 128)
        g_ref[rows_of(HALO + i * 128, 128), 0:D] = (jnp.transpose(dqt_ref[:, cols]) * SCALE).astype(BF16)
        return carry

    lax.fori_loop(0, own // 128, gather_q, 0)

    def norms(rows, g_n1):
        xhat, _ = normalize(x_ref[rows, :].astype(F32))
        small_ref[0:8, :] += fold(g_n1 * xhat)
        small_ref[8:16, :] += fold(g_n1)

    def pull_halo(i, carry):
        rows = rows_of(i * 128, 128)
        g_n1 = dot_t(g_ref[rows, D : 3 * D], w_ref[:, D : 3 * D])
        gn_halo_ref[rows, :] = g_n1.astype(BF16)
        norms(rows, g_n1)
        return carry

    lax.fori_loop(0, HALO // 128, pull_halo, 0)

    def pull_own(i, carry):
        rows = rows_of(HALO + i * 128, 128)
        g_n1 = dot_t(g_ref[rows, :], w_ref[...])
        gn_ref[rows_of(i * 128, 128), :] = g_n1
        norms(rows, g_n1)
        return carry

    lax.fori_loop(0, own // 128, pull_own, 0)
    gw_ref[:, 0:D] = dot(nt_ref[:, HALO:], g_ref[HALO:, 0:D]).astype(BF16)
    gw_ref[:, D : 2 * D] = dot(nt_ref[...], g_ref[:, D : 2 * D]).astype(BF16)
    gw_ref[:, 2 * D : 3 * D] = dot(nt_ref[...], g_ref[:, 2 * D : 3 * D]).astype(BF16)
    small_ref[16:24, :] = dot(jnp.ones((8, own), BF16), g_ref[HALO:, 0:D])
    small_ref[24:32, :] = dot(jnp.ones((8, ext), BF16), g_ref[:, 2 * D : 3 * D])


def attention_backward(q, k, v, g_o, lse, delta, id_row, id_col, n1, x_ext, w_qkv):
    ext, own = k.shape[0], q.shape[0]
    qb = 256 if own % 256 == 0 else 128
    shapes = (
        jax.ShapeDtypeStruct((HALO, D), BF16),
        jax.ShapeDtypeStruct((own, D), F32),
        jax.ShapeDtypeStruct((D, 3 * D), BF16),
        jax.ShapeDtypeStruct((32, D), F32),
    )
    return pl.pallas_call(
        functools.partial(backward_kernel, qb),
        out_shape=shapes,
        scratch_shapes=[
            pltpu.VMEM((HALO + qb, qb), F32),
            pltpu.VMEM((D, ext), BF16),
            pltpu.VMEM((D, ext), BF16),
            pltpu.VMEM((D, own), F32),
            pltpu.VMEM((ext, D), F32),
            pltpu.VMEM((ext, D), F32),
            pltpu.VMEM((ext, 3 * D), BF16),
        ],
        compiler_params=pltpu.CompilerParams(vmem_limit_bytes=56 * MIB),
        name="attention_backward",
    )(q, k, v, g_o, lse, delta, id_row, id_col, n1, x_ext, w_qkv)


def finish_kernel(x_ref, gn_ref, gh_ref, vec_ref, out_ref):
    def block(i, carry):
        rows = rows_of(i * 128, 128)
        xhat, rstd = normalize(x_ref[rows, :].astype(F32))
        out_ref[rows, :] = gh_ref[rows, :] + norm_pull(gn_ref[rows, :], vec_ref[0:1, :], xhat, rstd)
        return carry

    lax.fori_loop(0, x_ref.shape[0] // 128, block, 0)


def finish(x, g_n1, g_h1, vecs):
    return pl.pallas_call(
        finish_kernel,
        out_shape=jax.ShapeDtypeStruct(x.shape, F32),
        compiler_params=pltpu.CompilerParams(vmem_limit_bytes=32 * MIB),
        name="finish",
    )(x, g_n1, g_h1, vecs)


def hops(rows):
    plan, left, step = [], HALO, 1
    while left > 0:
        take = min(rows, left)
        plan.append((step, take))
        left, step = left - take, step + 1
    return plan


def local(
    layer_input,
    segment_ids,
    valid_mask,
    teacher,
    cotangent,
    ln1_gain,
    ln1_bias,
    w_q,
    w_k,
    w_v,
    b_q,
    b_v,
    w_o,
    b_o,
    ln2_gain,
    ln2_bias,
    w_up,
    b_up,
    w_down,
    b_down,
):
    fsdp_size = lax.axis_size("fsdp")
    tensor_size = lax.axis_size("tp")
    place = lax.axis_index("tp")
    own = layer_input.shape[0]
    tokens_all = own * fsdp_size * tensor_size
    rows_d = w_q.shape[0]
    cols_h, cols_f = w_q.shape[1], w_up.shape[1]

    parts = []
    for step, take in hops(own):
        route = [(i, i + step) for i in range(tensor_size - step)]
        parts.insert(0, lax.ppermute(layer_input[own - take :], "tp", route))
    x_ext = jnp.concatenate(parts + [layer_input], axis=0)
    ids = segment_ids + LEN * jnp.arange(segment_ids.shape[0], dtype=jnp.int32)[:, None]
    ids = jnp.concatenate([jnp.full((HALO,), -1, jnp.int32), ids.reshape(-1)])
    ids = lax.dynamic_slice_in_dim(ids, place * own, HALO + own)
    id_row, id_col = ids[None, :], ids[:, None]

    pack = jnp.concatenate([w_q, w_k, w_v, w_o.T, w_up, w_down.T], axis=1)
    count = jnp.sum(valid_mask)
    count_high = count // 256
    vectors = jnp.concatenate([ln1_gain, ln1_bias, b_o, ln2_gain, ln2_bias, b_down])
    heads = jnp.concatenate([b_q.reshape(-1), b_v.reshape(-1), b_up.reshape(-1)])
    digits = jnp.stack([count_high, count - 256 * count_high]).astype(BF16)
    small = jnp.concatenate([vectors, heads, digits])
    width = pack.shape[1]
    lines = -(-small.shape[0] // width)
    small = jnp.pad(small, (0, lines * width - small.shape[0])).reshape(lines, width)
    shard = jnp.concatenate([pack, small], axis=0)
    every = lax.all_gather(lax.all_gather(shard, "tp", axis=0), "fsdp", axis=0)
    big = every[:, :, :rows_d, :]

    def columns(start, size):
        part = big[:, :, :, start : start + size]
        return part.transpose(0, 2, 1, 3).reshape(fsdp_size * rows_d, tensor_size * size)

    w_qkv = jnp.concatenate([columns(j * cols_h, cols_h) for j in range(3)], axis=1)
    w_ot = columns(3 * cols_h, cols_h)
    w_up_all = columns(4 * cols_h, cols_f)
    w_dn_all = columns(4 * cols_h + cols_f, cols_f)
    few = every[:, :, rows_d:, :].reshape(fsdp_size, tensor_size, -1).astype(F32)
    six = few[:, 0, : 6 * rows_d].reshape(fsdp_size, 6, rows_d).transpose(1, 0, 2).reshape(6, D)
    at = 6 * rows_d

    def by_head(start, shape):
        size = shape[0] * shape[1]
        part = few[:, :, start : start + size].reshape((fsdp_size, tensor_size) + shape)
        return part.transpose(1, 2, 0, 3).reshape(1, -1)

    bq_all = by_head(at, b_q.shape)
    at += b_q.size
    bv_all = by_head(at, b_v.shape)
    at += b_v.size
    bup_all = by_head(at, b_up.shape)
    at += b_up.size
    valid_total = 256.0 * jnp.sum(few[:, :, at]) + jnp.sum(few[:, :, at + 1])

    vec_one = jnp.concatenate([six[0:2], bq_all, bv_all], axis=0)
    vec_two = jnp.stack([six[2], six[3], six[4], six[5]])
    n1, q, k, v, o, lse = attention_forward(x_ext, vec_one, w_qkv, id_row, id_col, own)
    scale = (tokens_all / valid_total).reshape(1, 1)
    mask = valid_mask.astype(F32)[:, None]
    layer_out, g_h1, g_o, delta, g_wo, g_wup, g_wdn, small_two, g_bup = middle(
        scale, layer_input, o, teacher, cotangent, mask, vec_two, bup_all, w_ot, w_up_all, w_dn_all
    )
    gn_halo, gn_own, g_qkv, small_one = attention_backward(
        q, k, v, g_o, lse, delta, id_row, id_col, n1, x_ext, w_qkv
    )

    total = gn_own
    left = HALO
    for step, take in hops(own):
        route = [(i + step, i) for i in range(tensor_size - step)]
        part = lax.ppermute(gn_halo[left - take : left], "tp", route).astype(F32)
        total = total + jnp.pad(part, ((own - take, 0), (0, 0)))
        left -= take
    grad_input = finish(layer_input, total, g_h1, vec_one)

    def split(grad, size):
        return grad.reshape(fsdp_size, rows_d, tensor_size, size).transpose(0, 2, 1, 3)

    g_pack = jnp.concatenate(
        [split(g_qkv[:, j * D : (j + 1) * D], cols_h) for j in range(3)]
        + [split(g_wo, cols_h), split(g_wup, cols_f), split(g_wdn, cols_f)],
        axis=3,
    )
    ones = [small_one[8 * j : 8 * j + 8].sum(0) for j in range(2)] + [small_one[16], small_one[24]]
    twos = [small_two[8 * j : 8 * j + 8].sum(0) for j in range(5)]
    loss_part = 0.5 / D * jnp.sum(twos[1]) / valid_total
    six_grads = jnp.stack([ones[0], ones[1], twos[4], twos[2], twos[3], twos[0]])
    six_grads = six_grads.reshape(6, fsdp_size, 1, rows_d).transpose(1, 2, 0, 3)
    six_grads = jnp.broadcast_to(
        six_grads.reshape(fsdp_size, 1, -1), (fsdp_size, tensor_size, 6 * rows_d)
    )

    def heads_of(grad, shape):
        part = grad.reshape((tensor_size, shape[0], fsdp_size, shape[1]))
        return part.transpose(2, 0, 1, 3).reshape(fsdp_size, tensor_size, -1)

    loss_high = loss_part.astype(BF16).astype(F32)
    losses = jnp.broadcast_to(
        jnp.stack([loss_high, loss_part - loss_high]), (fsdp_size, tensor_size, 2)
    )
    g_small = jnp.concatenate(
        [
            six_grads,
            heads_of(ones[2], b_q.shape),
            heads_of(ones[3], b_v.shape),
            heads_of(g_bup[0], b_up.shape),
            losses,
        ],
        axis=2,
    ).astype(BF16)
    g_small = jnp.pad(g_small, ((0, 0), (0, 0), (0, lines * width - g_small.shape[2])))
    g_all = jnp.concatenate([g_pack, g_small.reshape(fsdp_size, tensor_size, lines, width)], axis=2)
    mine = lax.psum_scatter(g_all, "fsdp", scatter_dimension=0, tiled=False)
    mine = lax.psum_scatter(mine, "tp", scatter_dimension=0, tiled=False).astype(F32)
    g_mat, g_vec = mine[:rows_d], mine[rows_d:].reshape(-1)
    c3, c4 = 3 * cols_h, 4 * cols_h
    six_out = g_vec[: 6 * rows_d].reshape(6, rows_d)
    at = 6 * rows_d
    grad_bq = g_vec[at : at + b_q.size].reshape(b_q.shape)
    at += b_q.size
    grad_bv = g_vec[at : at + b_v.size].reshape(b_v.shape)
    at += b_v.size
    grad_bup = g_vec[at : at + b_up.size].reshape(b_up.shape)
    at += b_up.size
    loss = g_vec[at] + g_vec[at + 1]
    return (
        layer_out,
        loss,
        grad_input,
        six_out[0],
        six_out[1],
        g_mat[:, 0:cols_h],
        g_mat[:, cols_h : 2 * cols_h],
        g_mat[:, 2 * cols_h : c3],
        grad_bq,
        grad_bv,
        g_mat[:, c3:c4].T,
        six_out[2],
        six_out[3],
        six_out[4],
        g_mat[:, c4 : c4 + cols_f],
        grad_bup,
        g_mat[:, c4 + cols_f :].T,
        six_out[5],
    )


ROWS = D // 8
EXTRA = 8
COLS = D // 4
FFC = 512
WA = 3 * COLS
WF = COLS + 2 * FFC
TALL = D + 16
ALL = (0, 1, 2, 3)
PIECES_A = ((0, ALL), (2, ALL), (4, ALL), (6, ALL), (1, ALL[0:2]), (1, ALL[2:4]), (3, ALL), (5, ALL), (7, ALL))
SMALL = pl.CostEstimate(flops=1, bytes_accessed=1, transcendentals=0)


def about(us):
    return pl.CostEstimate(flops=us * 1000000, bytes_accessed=us * 3300000, transcendentals=0)


ANY = pl.BlockSpec(memory_space=pl.ANY)
VMEM = pl.BlockSpec(memory_space=pltpu.VMEM)
FAR = pl.BlockSpec(memory_space=pl.ANY)


def params(mib):
    return pltpu.CompilerParams(vmem_limit_bytes=mib * MIB)


def lane_of(shape):
    return lax.broadcasted_iota(jnp.int32, shape, len(shape) - 1)


def pack_kernel(
    wq_ref, wk_ref, wv_ref, wo_ref, wup_ref, wdn_ref, g1, b1, bo, g2, b2, bd, bq, bv, bup, mask_ref, a_ref, f_ref
):
    me = lax.axis_index("fsdp")
    a_ref[0:ROWS, 0:COLS] = wq_ref[...]
    a_ref[0:ROWS, COLS : 2 * COLS] = wk_ref[...]
    a_ref[0:ROWS, 2 * COLS : 3 * COLS] = wv_ref[...]
    f_ref[:, 0:COLS] = wo_ref[...]
    f_ref[:, COLS : COLS + FFC] = wup_ref[...]
    f_ref[:, COLS + FFC :] = wdn_ref[...]
    count = jnp.sum(mask_ref[...].astype(F32)).reshape(1, 1)
    high = jnp.floor(count / 256.0)
    lane = lane_of((1, 128))
    digits = jnp.where(lane == 0, high, jnp.where(lane == 1, count - 256.0 * high, 0.0))
    vectors = [r[...].astype(F32).reshape(1, ROWS) for r in (g1, b1, bo, g2, b2, bd)]
    rows = [jnp.concatenate([v, v], axis=1) for v in vectors] + [digits, jnp.zeros((1, 128), F32)]
    a_ref[ROWS:, 0:128] = jnp.concatenate(rows, axis=0).astype(BF16)

    def spread(ref):
        block = ref[...].astype(F32)
        count, piece = block.shape
        lanes = count * HD
        lane = lane_of((1, lanes))
        row = jnp.zeros((1, lanes), F32)
        for i in range(count):
            for j in range(piece):
                at = i * HD + me * piece + j
                row = jnp.where(lane == at, block[i : i + 1, j : j + 1], row)
        return row

    ups = spread(bup)
    rows = [spread(bq), spread(bv)] + [ups[:, 128 * j : 128 * j + 128] for j in range(4)]
    rows.append(jnp.zeros((2, 128), F32))
    a_ref[ROWS:, 128:256] = jnp.concatenate(rows, axis=0).astype(BF16)
    a_ref[ROWS:, 256:384] = jnp.zeros((EXTRA, 128), BF16)


def pack_weights(args):
    return pl.pallas_call(
        pack_kernel,
        out_shape=(
            jax.ShapeDtypeStruct((ROWS + EXTRA, WA), BF16),
            jax.ShapeDtypeStruct((ROWS, WF), BF16),
        ),
        compiler_params=params(60),
        name="pack_weights",
    )(*args)


def project_kernel(
    tokens_all, x_ref, idc_ref, p0, p1, p2, p3, p4, p5, p6, p7, p8,
    q_ref, k_ref, v_ref, kt_ref, nt_ref, w_ref, vec_ref, bup_ref, scale_ref, head_ref, ext_ref, sem
):
    me, place = lax.axis_index("fsdp"), lax.axis_index("tp")
    pieces = (p0, p1, p2, p3, p4, p5, p6, p7, p8)

    def each(act):
        for ref, (mask, steps) in zip(pieces, PIECES_A):
            owner = lax.bitwise_xor(me, mask)
            for i, s in enumerate(steps):
                tp = lax.bitwise_and(place - s + 4, 3)
                act(ref.at[i], 4 * mask + s, owner, tp)

    def start_ext(ref, slot, owner, tp):
        pltpu.make_async_copy(ref.at[pl.ds(ROWS, EXTRA), :], ext_ref.at[slot], sem.at[0]).start()

    def start_w(ref, slot, owner, tp):
        pltpu.make_async_copy(
            ref.at[pl.ds(0, ROWS), :],
            w_ref.at[rows_of(owner * ROWS, ROWS, ROWS), rows_of(tp * WA, WA)],
            sem.at[1],
        ).start()

    each(start_ext)
    each(start_w)
    pltpu.make_async_copy(ext_ref, ext_ref, sem.at[0]).wait()
    lane = lane_of((EXTRA, D))
    vectors = jnp.zeros((EXTRA, D), F32)
    total = jnp.zeros((EXTRA, 128), F32)
    for j in range(8):
        block = ext_ref[4 * j, :, 0:128].astype(F32)
        wide = jnp.concatenate([block] * 4, axis=1)
        vectors = jnp.where(lane // ROWS == lax.bitwise_xor(me, j), wide, vectors)
        for s in range(4):
            total += ext_ref[4 * j + s, :, 0:128].astype(F32)
    vec_ref[...] = vectors
    valid = 256.0 * total[6:7, 0:1] + total[6:7, 1:2]
    scale_ref[...] = jnp.concatenate(
        [jnp.broadcast_to(tokens_all / valid, (4, 128)), jnp.broadcast_to(0.5 / D / valid, (4, 128))], axis=0
    )
    for s in range(4):
        tp = lax.bitwise_and(place - s + 4, 3)
        block = jnp.zeros((EXTRA, 128), F32)
        for j in range(8):
            block += ext_ref[4 * j + s, :, 128:256].astype(F32)
        head_ref[:, rows_of(tp * COLS, COLS)] = block
        for i in range(4):
            bup_ref[:, rows_of(tp * FFC + 128 * i, 128)] = jnp.broadcast_to(block[2 + i : 3 + i], (8, 128))
    pltpu.make_async_copy(w_ref, w_ref, sem.at[1]).wait()

    def own_rows(i, carry):
        rows = rows_of(i * 128, 128)
        n1 = first_norm(x_ref[rows, :], vectors, me, nt_ref, rows)
        made = dot(n1, w_ref[...])
        spare_q, spare_k, spare_v = spare_lanes(idc_ref[rows_of(HALO + i * 128, 128), :])
        for t in range(4):
            lanes = slice(t * COLS, (t + 1) * COLS)
            q = (made[:, t * WA : t * WA + COLS] + head_ref[0:1, lanes]).astype(BF16)
            keep_heads(q_ref, rows, t, q * jnp.asarray(SCALE, BF16), spare_q)
            keep_keys(made[:, t * WA + COLS : (t + 1) * WA], head_ref, k_ref, v_ref, kt_ref, rows, t, spare_k, spare_v)
        return carry

    lax.fori_loop(0, x_ref.shape[0] // 128, own_rows, 0)


DOCS = 48
TERMS = 3


def spare_lanes(ids):
    shape = (ids.shape[0], PAIR)
    at = lax.bitwise_and(lane_of(shape), HD - 1)
    same = at == ids
    ones = jnp.where((at >= DOCS) & (at < DOCS + TERMS), 1.0, 0.0)
    spare_q = jnp.where(same & (at < DOCS), 1.0, 0.0).astype(BF16)
    spare_k = jnp.where(at < DOCS, jnp.where(same, 0.0, NEG), ones).astype(BF16)
    return spare_q, spare_k, ones.astype(BF16)


def three_terms(x):
    high = x.astype(BF16)
    rest = x - high.astype(F32)
    middle = rest.astype(BF16)
    return high, middle, (rest - middle.astype(F32)).astype(BF16)


def keep_heads(ref, rows, pair, value, spare):
    lane = lane_of(value.shape)
    for h in range(2):
        at = (2 * pair + h) * PAIR
        mine = (lane < HD) if h == 0 else (lane >= HD)
        ref[rows, at : at + PAIR] = jnp.where(mine, value, spare)


def first_norm(x, vectors, me, nt_ref, rows):
    xhat, _ = normalize(x.astype(F32))
    n1 = xhat * vectors[0:1] + vectors[1:2]
    turned = jnp.transpose(n1).astype(BF16)
    for i in range(8):
        slot = lax.bitwise_xor(me, i)
        nt_ref[rows_of(slot * ROWS, ROWS, ROWS), rows] = turned[ROWS * i : ROWS * (i + 1)]
    nt_ref[D:, rows] = jnp.ones((TALL - D, x.shape[0]), BF16)
    return n1.astype(BF16)


def keep_keys(made, head_ref, k_ref, v_ref, kt_ref, rows, t, spare_k, spare_v):
    lanes = slice(t * COLS, (t + 1) * COLS)
    k = made[:, 0:COLS]
    keep_heads(k_ref, rows, t, k.astype(BF16), spare_k)
    kt_ref[lanes, rows] = jnp.transpose(k).astype(BF16)
    keep_heads(v_ref, rows, t, (made[:, COLS:] + head_ref[1:2, lanes]).astype(BF16), spare_v)


def project(x, id_col, pieces, tokens_all):
    own = x.shape[0]
    shapes = (
        jax.ShapeDtypeStruct((own, 2 * D), BF16),
        jax.ShapeDtypeStruct((own, 2 * D), BF16),
        jax.ShapeDtypeStruct((own, 2 * D), BF16),
        jax.ShapeDtypeStruct((D, own), BF16),
        jax.ShapeDtypeStruct((TALL, own), BF16),
        jax.ShapeDtypeStruct((D, 4 * WA), BF16),
        jax.ShapeDtypeStruct((EXTRA, D), F32),
        jax.ShapeDtypeStruct((8, 4 * FFC), F32),
        jax.ShapeDtypeStruct((8, 128), F32),
        jax.ShapeDtypeStruct((EXTRA, D), F32),
    )
    return pl.pallas_call(
        functools.partial(project_kernel, float(tokens_all)),
        out_shape=shapes,
        in_specs=[VMEM, VMEM] + [FAR] * 9,
        out_specs=[VMEM] * len(shapes),
        scratch_shapes=[pltpu.VMEM((32, EXTRA, WA), BF16), pltpu.SemaphoreType.DMA((2,))],
        compiler_params=params(6),
        cost_estimate=SMALL,
        name="project",
    )(x, id_col, *pieces)


def project_halo_kernel(x_ref, idc_ref, w_ref, vec_ref, head_ref, k_ref, v_ref, kt_ref, nt_ref):
    me = lax.axis_index("fsdp")

    def halo_rows(i, carry):
        rows = rows_of(i * 128, 128)
        n1 = first_norm(x_ref[rows, :], vec_ref[...], me, nt_ref, rows)
        _, spare_k, spare_v = spare_lanes(idc_ref[rows, :])
        for t in range(4):
            made = dot(n1, w_ref[:, t * WA + COLS : (t + 1) * WA])
            keep_keys(made, head_ref, k_ref, v_ref, kt_ref, rows, t, spare_k, spare_v)
        return carry

    lax.fori_loop(0, HALO // 128, halo_rows, 0)


def project_halo(x, id_col, w, vec, head):
    shape = jax.ShapeDtypeStruct((HALO, 2 * D), BF16)
    turned, tall = (jax.ShapeDtypeStruct((size, HALO), BF16) for size in (D, TALL))
    return pl.pallas_call(
        project_halo_kernel,
        out_shape=(shape, shape, turned, tall),
        compiler_params=params(6),
        cost_estimate=SMALL,
        name="project_halo",
    )(x, id_col, w, vec, head)


QB = 256


def causal(by_rows):
    key = lax.broadcasted_iota(jnp.int32, (QB, QB), 1 if by_rows else 0)
    query = lax.broadcasted_iota(jnp.int32, (QB, QB), 0 if by_rows else 1)
    return jnp.where(key <= query, 0.0, NEG)


def staged(units, stages, lag=1, beside=()):
    steps = len(units) + lag * (len(stages) - 1)
    for n in range(steps):
        for depth, stage in enumerate(stages):
            if 0 <= n - lag * depth < len(units):
                stage(units[n - lag * depth])
        if n < len(beside):
            beside[n]()
    for extra in beside[steps:]:
        extra()


def attend_heads(heads, bias_ref):
    lane = lane_of((QB, PAIR))
    at = lax.bitwise_and(lane, HD - 1)

    def score(one):
        q = one["q"][one["rows"], one["lanes"]]
        one["s"] = []
        for keys, _, where, last in one["parts"]:
            s = dot_t(q, keys[where, one["lanes"]])
            one["s"].append(s + bias_ref[...] if last else s)

    def soften(one):
        one["top"] = functools.reduce(jnp.maximum, [jnp.max(s, axis=-1, keepdims=True) for s in one["s"]])
        one["p"] = [jnp.exp(s - one["top"]).astype(BF16) for s in one.pop("s")]

    def attend(one):
        total = None
        for p, (_, values, where, _) in zip(one.pop("p"), one["parts"]):
            part = dot(p, values[where, one["lanes"]])
            total = part if total is None else total + part
        first = (HD if one["h"] == 0 else 0) + DOCS
        weight = total[:, first : first + 1]
        mine = (lane < HD) if one["h"] == 0 else (lane >= HD)
        q = one["q"][one["rows"], one["lanes"]]
        for i, term in enumerate(three_terms(-(one["top"] + jnp.log(weight)))):
            q = jnp.where((at == DOCS + i) & ~mine, jnp.broadcast_to(term, q.shape), q)
        one["take"](one["h"], (total / weight).astype(BF16), q)

    staged(heads, (score, soften, attend), 2)


def keep_attended(o_ref, qa_ref, rows, pair):
    lane = lane_of((QB, PAIR))

    def take(h, o, q):
        lanes = rows_of(pair * PAIR, PAIR)
        qa_ref[rows, head_lanes(pair, h)] = q
        o_ref[rows, lanes] = o if h == 0 else jnp.where(lane < HD, o_ref[rows, lanes], o)

    return take


def head_lanes(pair, h):
    return rows_of((2 * pair + h) * PAIR, PAIR)


def each_two(count, act):
    def step(i, carry):
        act((2 * i, 2 * i + 1))
        return carry

    lax.fori_loop(0, count, step, 0)


def attend_far_kernel(q_ref, k_ref, v_ref, o_ref, qa_ref, bias_ref):
    bias_ref[...] = causal(True)
    parts = ((k_ref, v_ref, slice(0, HALO), False), (k_ref, v_ref, slice(HALO, HALO + QB), True))

    def two(pairs):
        heads = []
        for pair in pairs:
            take = keep_attended(o_ref, qa_ref, slice(0, QB), pair)
            for h in range(2):
                heads.append(
                    dict(q=q_ref, rows=slice(HALO, HALO + QB), lanes=head_lanes(pair, h), h=h, parts=parts, take=take)
                )
        attend_heads(heads, bias_ref)

    each_two(2, two)


def attend_far(q, k, v):
    return pl.pallas_call(
        attend_far_kernel,
        out_shape=(jax.ShapeDtypeStruct((QB, D), BF16), jax.ShapeDtypeStruct((QB, 2 * D), BF16)),
        in_specs=[VMEM] * 3,
        out_specs=[VMEM] * 2,
        scratch_shapes=[pltpu.VMEM((QB, QB), F32)],
        compiler_params=params(8),
        cost_estimate=SMALL,
        name="attend_far",
    )(q, k, v)


def near_parts(halo, own):
    return (
        ((*halo, slice(0, HALO), False), (*own, slice(0, QB), True)),
        ((*halo, slice(QB, HALO), False), (*own, slice(0, QB), False), (*own, slice(QB, HALO), True)),
    )


def attend_near_kernel(q_ref, kh_ref, ko_ref, vh_ref, vo_ref, o_ref, qa_ref, bias_ref):
    bias_ref[...] = causal(True)

    def two(pairs):
        heads = []
        for pair in pairs:
            for i, parts in enumerate(near_parts((kh_ref, vh_ref), (ko_ref, vo_ref))):
                rows = slice(i * QB, (i + 1) * QB)
                take = keep_attended(o_ref, qa_ref, rows, pair)
                for h in range(2):
                    heads.append(dict(q=q_ref, rows=rows, lanes=head_lanes(pair, h), h=h, parts=parts, take=take))
        attend_heads(heads, bias_ref)

    each_two(2, two)


def attend_near(q, k_halo, k, v_halo, v):
    return pl.pallas_call(
        attend_near_kernel,
        out_shape=(jax.ShapeDtypeStruct((HALO, D), BF16), jax.ShapeDtypeStruct((HALO, 2 * D), BF16)),
        in_specs=[VMEM] * 5,
        out_specs=[VMEM] * 2,
        scratch_shapes=[pltpu.VMEM((QB, QB), F32)],
        compiler_params=params(8),
        cost_estimate=SMALL,
        name="attend_near",
    )(q, k_halo, k, v_halo, v)


PIECES_F = ((0, (0,)), (0, (1,)), (0, (2,)), (0, (3,)), (2, (0, 1, 2, 3)), (4, (0, 1, 2, 3)), (6, (0, 1)), (6, (2, 3)))


def central_kernel(
    rb, x_ref, oa_ref, oc_ref, teacher_ref, cot_ref, mask_ref, vec_ref, bup_ref, scale_ref,
    *rest
):
    pieces = rest[:16]
    (
    out_ref, gh_ref, ga_ref, theirs_ref, mine_ref, small_ref, gbup_ref,
    wo_ref, wup_ref, wdn_ref, slope_ref, hid_ref, gpre_ref, n2t_ref, gmlpt_ref, gattnt_ref, place_ref, o_ref,
    h1_ref, xhat_ref, n2_ref, gmlp_ref, sem
    ) = rest[16:]
    me, place = lax.axis_index("fsdp"), lax.axis_index("tp")
    own, ff = x_ref.shape[0], 4 * FFC
    parts = ((wo_ref, 0, COLS), (wup_ref, COLS, FFC), (wdn_ref, COLS + FFC, FFC))
    for n, (dst, start, size) in enumerate(parts):
        for j, ref in enumerate(pieces):
            mask, steps = PIECES_F[j % 8]
            owner = lax.bitwise_xor(me, mask + j // 8)
            for i, s in enumerate(steps):
                tp = lax.bitwise_and(place - s + 4, 3)
                pltpu.make_async_copy(
                    ref.at[i, :, pl.ds(start, size)],
                    dst.at[rows_of(owner * ROWS, ROWS, ROWS), rows_of(tp * size, size)],
                    sem.at[n],
                ).start()
    small_ref[...] = jnp.zeros_like(small_ref)
    head_of = lax.broadcasted_iota(jnp.int32, (D, 128), 0) // HD
    pick = (head_of == lax.broadcasted_iota(jnp.int32, (D, 128), 1)).astype(BF16)
    out_bias, gain, offset, down_bias = (vec_ref[j : j + 1, :] for j in range(2, 6))
    n2t_ref[D:, :] = jnp.ones((TALL - D, own), BF16)
    source = lax.broadcasted_iota(jnp.int32, (TERMS * 128, H * PAIR), 0)
    target = lax.broadcasted_iota(jnp.int32, (TERMS * 128, H * PAIR), 1)
    head, term = target // PAIR, lax.bitwise_and(target, HD - 1) - DOCS
    outside = (lax.bitwise_and(target, PAIR - 1) >= HD) == (lax.bitwise_and(head, 1) == 0)
    placed = outside & (lax.bitwise_and(source, 127) == head) & (source // 128 == term)
    place_ref[...] = jnp.where(placed, 1.0, 0.0).astype(BF16)
    o_ref[0:HALO, :] = oa_ref[...]
    o_ref[HALO:, :] = oc_ref[...]

    def turn(dst, rows, value):
        turned = jnp.transpose(value).astype(BF16)
        for i in range(8):
            slot = lax.bitwise_xor(me, i)
            dst[rows_of(slot * ROWS, ROWS, ROWS), rows] = turned[ROWS * i : ROWS * (i + 1)]

    def arrived(n):
        pltpu.make_async_copy(parts[n][0], parts[n][0], sem.at[n]).wait()

    blocks = [dict(rows=slice(i * rb, (i + 1) * rb)) for i in range(own // rb)]

    def attention_out(one):
        one["attn"] = dot_t(o_ref[one["rows"], :], wo_ref[...])

    def second_norm(one):
        rows = one["rows"]
        h1 = x_ref[rows, :].astype(F32) + one.pop("attn") + out_bias
        xhat, rstd = normalize(h1)
        n2 = xhat * gain + offset
        h1_ref[rows, :] = h1
        xhat_ref[rows, :] = xhat
        one["rstd"] = rstd
        n2_ref[rows, :] = n2.astype(BF16)
        turn(n2t_ref, rows, n2)

    arrived(0)
    staged(blocks, (attention_out, second_norm))
    arrived(1)

    def by_columns(stages):
        def step(c, carry):
            cols = rows_of(c * FFC, FFC)
            staged([dict(rows=one["rows"], cols=cols) for one in blocks], stages)
            return carry

        lax.fori_loop(0, 4, step, 0)

    def up(one):
        one["pre"] = dot(n2_ref[one["rows"], :], wup_ref[:, one["cols"]]) + bup_ref[0:1, one["cols"]]

    def gelu(one):
        pre = one.pop("pre")
        s = jax.nn.sigmoid(1.702 * pre)
        value = pre * s
        hid_ref[one["rows"], one["cols"]] = value.astype(BF16)
        slope_ref[one["rows"], one["cols"]] = s * (1.702 * (pre - value) + 1.0)

    by_columns((up, gelu))
    arrived(2)

    def down(one):
        one["mlp"] = dot_t(hid_ref[one["rows"], :], wdn_ref[...])

    def output(one):
        rows = one["rows"]
        out = h1_ref[rows, :] + one.pop("mlp") + down_bias
        out_ref[rows, :] = out.astype(BF16)
        diff = (out - teacher_ref[rows, :].astype(F32)) * mask_ref[rows, :]
        g_out = cot_ref[rows, :].astype(F32) + scale_ref[0:1, 0:1] * diff
        gh_ref[rows, :] = g_out
        small_ref[0:8, :] += fold(g_out)
        small_ref[8:16, :] += fold(diff * diff)
        gmlp_ref[rows, :] = g_out.astype(BF16)
        turn(gmlpt_ref, rows, g_out)

    staged(blocks, (down, output))

    def hidden(one):
        one["g"] = dot(gmlp_ref[one["rows"], :], wdn_ref[:, one["cols"]])

    def slope(one):
        g_pre = one.pop("g") * slope_ref[one["rows"], one["cols"]]
        gpre_ref[one["rows"], one["cols"]] = g_pre.astype(BF16)

    by_columns((hidden, slope))

    def into_norm(one):
        one["g"] = dot_t(gpre_ref[one["rows"], :], wup_ref[...])

    def pull_norm(one):
        rows, g_n2, xhat = one["rows"], one.pop("g"), xhat_ref[one["rows"], :]
        small_ref[16:24, :] += fold(g_n2 * xhat)
        small_ref[24:32, :] += fold(g_n2)
        g_h1 = gh_ref[rows, :] + norm_pull(g_n2, gain, xhat, one.pop("rstd"))
        gh_ref[rows, :] = g_h1
        small_ref[32:40, :] += fold(g_h1)
        turn(gattnt_ref, rows, g_h1)
        one["go"] = dot(g_h1.astype(BF16), wo_ref[...]).astype(BF16)

    def pull_out(one):
        rows, g_o = one["rows"], one.pop("go")
        product = g_o.astype(F32) * o_ref[rows, :].astype(F32)
        high = product.astype(BF16)
        low = (product - high.astype(F32)).astype(BF16)
        terms = jnp.concatenate(three_terms(-(dot(high, pick) + dot(low, pick))), axis=1)
        spare = dot(terms, place_ref[...]).astype(BF16)
        lane = lane_of((rb, PAIR))
        for n in range(H):
            mine = (lane < HD) if n % 2 == 0 else (lane >= HD)
            pair = g_o[:, (n // 2) * PAIR : (n // 2 + 1) * PAIR]
            ga_ref[rows, n * PAIR : (n + 1) * PAIR] = jnp.where(mine, pair, spare[:, n * PAIR : (n + 1) * PAIR])

    def keep(grad, s, start, size):
        low = grad.astype(BF16)
        for r in range(8):
            dst = theirs_ref if r % 2 else mine_ref
            dst[r // 2, s, :, start : start + size] = low[ROWS * r : ROWS * (r + 1)]

    def their(s, size):
        return rows_of(lax.bitwise_and(place + s, 3) * size, size)

    def by_down(s):
        keep(dot(gmlpt_ref[...], hid_ref[:, their(s, FFC)]), s, COLS + FFC, FFC)

    staged(
        blocks, (into_norm, pull_norm, pull_out), beside=[functools.partial(by_down, s) for s in range(4)]
    )
    for s in range(4):
        total = dot(n2t_ref[...], gpre_ref[:, their(s, FFC)])
        gbup_ref[:, their(s, FFC)] = total[D : D + 8]
        keep(total, s, COLS, FFC)
        keep(dot(gattnt_ref[...], o_ref[:, their(s, COLS)]), s, 0, COLS)


def central(x, o_near, o_far, teacher, cot, mask, vec, bup, scale, pieces):
    own = x.shape[0]
    rb = 256
    shapes = (
        jax.ShapeDtypeStruct((own, D), BF16),
        jax.ShapeDtypeStruct((own, D), F32),
        jax.ShapeDtypeStruct((own, 2 * D), BF16),
        jax.ShapeDtypeStruct((4, 4, ROWS, WF), BF16),
        jax.ShapeDtypeStruct((4, 4, ROWS, WF), BF16),
        jax.ShapeDtypeStruct((40, D), F32),
        jax.ShapeDtypeStruct((8, 4 * FFC), F32),
    )
    return pl.pallas_call(
        functools.partial(central_kernel, rb),
        out_shape=shapes,
        in_specs=[VMEM] * 9 + [FAR] * 16,
        out_specs=[VMEM] * len(shapes),
        scratch_shapes=[
            pltpu.VMEM((D, D), BF16),
            pltpu.VMEM((D, 4 * FFC), BF16),
            pltpu.VMEM((D, 4 * FFC), BF16),
            pltpu.VMEM((own, 4 * FFC), F32),
            pltpu.VMEM((own, 4 * FFC), BF16),
            pltpu.VMEM((own, 4 * FFC), BF16),
            pltpu.VMEM((TALL, own), BF16),
            pltpu.VMEM((D, own), BF16),
            pltpu.VMEM((D, own), BF16),
            pltpu.VMEM((TERMS * 128, H * PAIR), BF16),
            pltpu.VMEM((own, D), BF16),
            pltpu.VMEM((own, D), F32),
            pltpu.VMEM((own, D), F32),
            pltpu.VMEM((own, D), BF16),
            pltpu.VMEM((own, D), BF16),
            pltpu.SemaphoreType.DMA((3,)),
        ],
        compiler_params=params(30),
        cost_estimate=SMALL,
        name="central",
    )(x, o_near, o_far, teacher, cot, mask, vec, bup, scale, *pieces)


def pull_units(units, bias_ref):
    lane = lane_of((QB, PAIR))

    def mask(x, h):
        return jnp.where((lane < HD) if h == 0 else (lane >= HD), x, jnp.zeros_like(x))

    def score(one):
        keys, values, _, where, _ = one["part"]
        one["s"] = dot_t(keys[where, one["lanes"]], one["q"][one["rows"], one["qlanes"]])
        one["d"] = dot_t(values[where, one["lanes"]], one["g"][one["grows"], one["lanes"]])

    def soften(one):
        s = one.pop("s")
        p = jnp.exp(s + bias_ref[...] if one["part"][4] else s)
        one["p"], one["ds"] = p.astype(BF16), (p * one.pop("d")).astype(BF16)

    def finish(one):
        _, _, keys_t, where, last = one["part"]
        h, sums = one["h"], one["sums"]
        part = dot(keys_t[one["tlanes"], where], one["ds"])
        sums[h] = part if h not in sums else sums[h] + part
        if h == 0:
            sums["before"] = one
            return
        two = (sums.pop("before"), one)
        q = jnp.concatenate([mask(u["q"][u["rows"], u["qlanes"]], u["h"]) for u in two], axis=0)
        g = jnp.concatenate([mask(u["g"][u["grows"], u["lanes"]], u["h"]) for u in two], axis=0)
        dk = dot(jnp.concatenate([u.pop("ds") for u in two], axis=1), q)
        dv = dot(jnp.concatenate([u.pop("p") for u in two], axis=1), g)
        one["take"](dk, dv)
        if last:
            both = jnp.concatenate([sums[0], sums[1]], axis=0)
            one["take_q"]((jnp.transpose(both) * SCALE).astype(BF16))

    staged(units, (score, soften, finish), 2)


def block_units(q_ref, rows, q_pair, g_ref, grows, pair, parts, takes, take_q):
    sums, units = {}, []
    for part, take in zip(parts, takes):
        for h in range(2):
            units.append(
                dict(
                    q=q_ref, rows=rows, qlanes=head_lanes(q_pair, h), g=g_ref, grows=grows, lanes=head_lanes(pair, h), h=h,
                    part=part, tlanes=rows_of((2 * pair + h) * HD, HD, HD), take=take, take_q=take_q, sums=sums,
                )
            )
    return units


def pull_near_kernel(base, q_ref, g_ref, kh_ref, ko_ref, vh_ref, vo_ref, kth_ref, kto_ref, gh_ref, gq_ref, part_ref, bias_ref, late_ref):
    bias_ref[...] = causal(False)
    halo, own = (kh_ref, vh_ref, kth_ref), (ko_ref, vo_ref, kto_ref)

    def one(pair, carry):
        lanes = (rows_of(2 * pair * PAIR, PAIR), rows_of((2 * pair + 1) * PAIR, PAIR))

        def halo_first(*grads):
            for at, d in zip(lanes, grads):
                gh_ref[0:QB, at] = d[0:QB].astype(BF16)
                late_ref[:, at] = d[QB:]

        def halo_second(*grads):
            for at, d in zip(lanes, grads):
                gh_ref[QB:, at] = (late_ref[:, at] + d).astype(BF16)

        def own_first(*grads):
            for at, d in zip(lanes, grads):
                part_ref[0:QB, at] = d

        def own_more(*grads):
            for at, d in zip(lanes, grads):
                part_ref[0:QB, at] += d

        def own_last(*grads):
            for at, d in zip(lanes, grads):
                part_ref[QB:, at] = d

        units, takes = [], ((halo_first, own_first), (halo_second, own_more, own_last))
        for i, parts in enumerate(near_parts(halo, own)):
            rows = slice(i * QB, (i + 1) * QB)

            def take_q(dq, rows=rows):
                gq_ref[rows, rows_of(pair * PAIR, PAIR)] = dq

            units += block_units(q_ref, rows, base + pair, g_ref, rows, base + pair, parts, takes[i], take_q)
        pull_units(units, bias_ref)
        return carry

    lax.fori_loop(0, 2, one, 0)


def pull_near(base, qa, ga, k_halo, k, v_halo, v, kt_halo, kt):
    return pl.pallas_call(
        functools.partial(pull_near_kernel, base),
        out_shape=(
            jax.ShapeDtypeStruct((HALO, D), BF16),
            jax.ShapeDtypeStruct((HALO, D // 2), BF16),
            jax.ShapeDtypeStruct((HALO, D), F32),
        ),
        in_specs=[VMEM] * 8,
        out_specs=[VMEM] * 3,
        scratch_shapes=[pltpu.VMEM((QB, QB), F32), pltpu.VMEM((QB, D), F32)],
        compiler_params=params(10),
        cost_estimate=SMALL,
        name="pull_near",
    )(qa, ga, k_halo, k, v_halo, v, kt_halo, kt)


def pull_far_kernel(q_ref, go_ref, k_ref, v_ref, kt_ref, qa_ref, qb_ref, pa_ref, pb_ref, g_ref, bias_ref):
    bias_ref[...] = causal(False)
    refs = (k_ref, v_ref, kt_ref)
    parts = ((*refs, slice(0, HALO), False), (*refs, slice(HALO, HALO + QB), True))

    def two(inside, carry):
        units = []
        for half, near_q, near_part in ((0, qa_ref, pa_ref), (1, qb_ref, pb_ref)):
            pair = 2 * half + inside
            lanes = tuple(rows_of(pair * WA + n * COLS, COLS) for n in range(3))
            within = tuple(rows_of((2 * inside + n) * PAIR, PAIR) for n in range(2))
            g_ref[0:HALO, lanes[0]] = near_q[:, rows_of(inside * PAIR, PAIR)]

            def older(*grads, lanes=lanes, within=within, near_part=near_part):
                for n, d in enumerate(grads):
                    g_ref[0:HALO, lanes[n + 1]] = (near_part[:, within[n]] + d).astype(BF16)

            def newest(*grads, lanes=lanes):
                for n, d in enumerate(grads):
                    g_ref[HALO:, lanes[n + 1]] = d.astype(BF16)

            def take_q(dq, lanes=lanes):
                g_ref[HALO:, lanes[0]] = dq

            own = slice(HALO, HALO + QB)
            units += block_units(q_ref, slice(0, QB), pair, go_ref, own, pair, parts, (older, newest), take_q)
        pull_units(units, bias_ref)
        return carry

    lax.fori_loop(0, 2, two, 0)


def pull_far(qa, ga, k, v, kt, gq_near, gq_more, part_near, part_more):
    own = k.shape[0]
    return pl.pallas_call(
        pull_far_kernel,
        out_shape=jax.ShapeDtypeStruct((own, 4 * WA), BF16),
        in_specs=[VMEM] * 9,
        out_specs=VMEM,
        scratch_shapes=[pltpu.VMEM((QB, QB), F32)],
        compiler_params=params(10),
        cost_estimate=SMALL,
        name="pull_far",
    )(qa, ga, k, v, kt, gq_near, gq_more, part_near, part_more)


def norm_sums(small_ref, x, g_n1):
    xhat, _ = normalize(x.astype(F32))
    small_ref[0:8, :] += fold(g_n1 * xhat)
    small_ref[8:16, :] += fold(g_n1)


def halo_back_kernel(ga_ref, gb_ref, w_ref, x_ref, out_ref, small_ref):
    small_ref[...] = jnp.zeros_like(small_ref)

    def pull(one):
        total = None
        for t in range(4):
            g = (ga_ref, gb_ref)[t // 2][one["rows"], (t % 2) * 2 * COLS : (t % 2 + 1) * 2 * COLS]
            part = dot_t(g, w_ref[:, t * WA + COLS : (t + 1) * WA])
            total = part if total is None else total + part
        one["g"] = total

    def norms(one):
        g_n1 = one.pop("g")
        out_ref[one["rows"], :] = g_n1.astype(BF16)
        norm_sums(small_ref, x_ref[one["rows"], :], g_n1)

    staged([dict(rows=slice(i * QB, (i + 1) * QB)) for i in range(HALO // QB)], (pull, norms))


def halo_back(g_near, g_more, w, halo):
    return pl.pallas_call(
        halo_back_kernel,
        out_shape=(jax.ShapeDtypeStruct((HALO, D), BF16), jax.ShapeDtypeStruct((16, D), F32)),
        compiler_params=params(6),
        cost_estimate=SMALL,
        name="halo_back",
    )(g_near, g_more, w, halo)


def own_back_kernel(
    x_ref, ga_ref, gb_ref, g_ref, nth_ref, nto_ref, w_ref, small_halo, small_two, gbup_ref, scale_ref,
    gn_ref, theirs_ref, mine_ref, small_ref, gh_ref
):
    me, place = lax.axis_index("fsdp"), lax.axis_index("tp")
    own = x_ref.shape[0]
    small_ref[...] = small_halo[...]
    gh_ref[:, 0:D] = ga_ref[...]
    gh_ref[:, D:] = gb_ref[...]

    def pull(one):
        one["g"] = dot_t(g_ref[one["rows"], :], w_ref[...])

    def norms(one):
        g_n1 = one.pop("g")
        gn_ref[one["rows"], :] = g_n1
        norm_sums(small_ref, x_ref[one["rows"], :], g_n1)

    staged([dict(rows=slice(i * QB, (i + 1) * QB)) for i in range(own // QB)], (pull, norms))
    sums = lambda ref, j: jnp.sum(ref[8 * j : 8 * j + 8, :], axis=0, keepdims=True)
    loss = jnp.sum(sums(small_two, 1), axis=1, keepdims=True) * scale_ref[4:5, 0:1]
    vectors = jnp.concatenate(
        [sums(small_ref, 0), sums(small_ref, 1), sums(small_two, 4), sums(small_two, 2), sums(small_two, 3),
         sums(small_two, 0), jnp.zeros((2, D), F32)],
        axis=0,
    )
    high = loss.astype(BF16).astype(F32)
    row, lane = lax.broadcasted_iota(jnp.int32, (EXTRA, 128), 0), lane_of((EXTRA, 128))

    def grads(s, carry):
        tp = lax.bitwise_and(place + s, 3)
        g_own = g_ref[:, rows_of(tp * WA, WA)]
        g_halo = gh_ref[:, rows_of(tp * 2 * COLS, 2 * COLS)]
        total = dot(nto_ref[...], g_own)
        more = dot(nth_ref[...], g_halo)
        total = jnp.concatenate([total[:, 0:COLS], total[:, COLS:] + more], axis=1)
        low, sums = total[0:D].astype(BF16), total[D : D + 1]
        ups = gbup_ref[0:1, rows_of(tp * FFC, FFC)]
        mids = jnp.concatenate(
            [sums[:, 0:COLS], sums[:, 2 * COLS :]]
            + [ups[:, 128 * j : 128 * j + 128] for j in range(4)]
            + [jnp.zeros((2, 128), F32)],
            axis=0,
        ).astype(BF16)
        for r in range(8):
            dst = theirs_ref if r % 2 else mine_ref
            dst[r // 2, s, 0:ROWS, :] = low[ROWS * r : ROWS * (r + 1)]
            dst[r // 2, s, ROWS:, 128:256] = mids
        return carry

    lax.fori_loop(0, 4, grads, 0)
    for r in range(8):
        owner = lax.bitwise_xor(me, r)
        block = pltpu.roll(vectors, lax.rem(D - owner * ROWS, D), 1)[:, 0:128]
        block = jnp.where((row == 6) & (lane == 0), high, block)
        block = jnp.where((row == 6) & (lane == 1), loss - high, block).astype(BF16)
        dst = theirs_ref if r % 2 else mine_ref
        for s in range(4):
            dst[r // 2, s, ROWS:, 0:128] = block
            dst[r // 2, s, ROWS:, 256:384] = jnp.zeros((EXTRA, 128), BF16)


def own_back(x, g_near, g_more, g_own, nt_halo, nt, w, small_halo, small_two, gbup, scale):
    own = x.shape[0]
    send = jax.ShapeDtypeStruct((4, 4, ROWS + EXTRA, WA), BF16)
    return pl.pallas_call(
        own_back_kernel,
        out_shape=(jax.ShapeDtypeStruct((own, D), F32), send, send),
        scratch_shapes=[pltpu.VMEM((16, D), F32), pltpu.VMEM((HALO, 2 * D), BF16)],
        compiler_params=params(10),
        cost_estimate=SMALL,
        name="own_back",
    )(x, g_near, g_more, g_own, nt_halo, nt, w, small_halo, small_two, gbup, scale)


def close_kernel(x_ref, gn_ref, back_ref, gh_ref, vec_ref, out_ref):
    own = x_ref.shape[0]

    def block(at, extra):
        rows = rows_of(at, 128)
        xhat, rstd = normalize(x_ref[rows, :].astype(F32))
        g_n1 = gn_ref[rows, :] + extra
        out_ref[rows, :] = gh_ref[rows, :] + norm_pull(g_n1, vec_ref[0:1, :], xhat, rstd)

    def first(i, carry):
        block(i * 128, 0.0)
        return carry

    def second(i, carry):
        block(own - HALO + i * 128, back_ref[rows_of(i * 128, 128), :].astype(F32))
        return carry

    lax.fori_loop(0, (own - HALO) // 128, first, 0)
    lax.fori_loop(0, HALO // 128, second, 0)


def close(x, g_n1, back, g_h1, vec):
    return pl.pallas_call(
        close_kernel,
        out_shape=jax.ShapeDtypeStruct(x.shape, F32),
        compiler_params=params(8),
        cost_estimate=SMALL,
        name="close",
    )(x, g_n1, back, g_h1, vec)


def unpack_f_kernel(k_ref, r1, r2, r3, wo_ref, wup_ref, wdn_ref):
    total = (k_ref[0].astype(F32) + r1[...].astype(F32)) + (r2[...].astype(F32) + r3[...].astype(F32))
    wo_ref[...] = total[:, 0:COLS]
    wup_ref[...] = total[:, COLS : COLS + FFC]
    wdn_ref[...] = total[:, COLS + FFC :]


def unpack_f(k, r1, r2, r3):
    return pl.pallas_call(
        unpack_f_kernel,
        out_shape=(
            jax.ShapeDtypeStruct((ROWS, COLS), F32),
            jax.ShapeDtypeStruct((ROWS, FFC), F32),
            jax.ShapeDtypeStruct((ROWS, FFC), F32),
        ),
        compiler_params=params(6),
        name="unpack_f",
    )(k, r1, r2, r3)


def unpack_a_kernel(k_ref, r1, r2, r3, wq_ref, wk_ref, wv_ref, bq_ref, bv_ref, bup_ref, loss_ref, *vec_refs):
    me = lax.axis_index("fsdp")
    total = (k_ref[0].astype(F32) + r1[...].astype(F32)) + (r2[...].astype(F32) + r3[...].astype(F32))
    wq_ref[...] = total[0:ROWS, 0:COLS]
    wk_ref[...] = total[0:ROWS, COLS : 2 * COLS]
    wv_ref[...] = total[0:ROWS, 2 * COLS :]
    for j, ref in enumerate(vec_refs):
        ref[...] = total[ROWS + j, 0:ROWS]
    loss_ref[...] = total[ROWS + 6 : ROWS + 7, 0:1] + total[ROWS + 6 : ROWS + 7, 1:2]
    mids = pltpu.roll(total[ROWS:, 128:256], lax.rem(128 - me * 8, 128), 1)
    for i in range(2):
        bq_ref[i : i + 1, :] = mids[0:1, i * HD : i * HD + 8]
        bv_ref[i : i + 1, :] = mids[1:2, i * HD : i * HD + 8]
    for i in range(8):
        at = (i % 2) * HD
        bup_ref[i : i + 1, :] = mids[2 + i // 2 : 3 + i // 2, at : at + 8]


def unpack_a(k, r1, r2, r3):
    small = jax.ShapeDtypeStruct((ROWS, COLS), F32)
    return pl.pallas_call(
        unpack_a_kernel,
        out_shape=(
            small,
            small,
            small,
            jax.ShapeDtypeStruct((2, 8), F32),
            jax.ShapeDtypeStruct((2, 8), F32),
            jax.ShapeDtypeStruct((8, 8), F32),
            jax.ShapeDtypeStruct((1, 1), F32),
            *[jax.ShapeDtypeStruct((ROWS,), F32)] * 6,
        ),
        compiler_params=params(6),
        name="unpack_a",
    )(k, r1, r2, r3)


def to_mask(x, mask):
    return lax.ppermute(x, "fsdp", [(i, i ^ mask) for i in range(8)])


def to_step(x, step):
    return lax.ppermute(x, "tp", [(i, (i + step) % 4) for i in range(4)])


def add(a, b):
    return (a.astype(F32) + b.astype(F32)).astype(BF16)


def after(values, others):
    return lax.optimization_barrier((values, others))[0]


def local_fast(
    layer_input, segment_ids, valid_mask, teacher, cotangent, ln1_gain, ln1_bias, w_q, w_k, w_v, b_q, b_v,
    w_o, b_o, ln2_gain, ln2_bias, w_up, b_up, w_down, b_down
):
    place = lax.axis_index("tp")
    own = layer_input.shape[0]
    tokens_all = own * lax.axis_size("fsdp") * lax.axis_size("tp")

    shard_a, shard_f = pack_weights(
        (w_q, w_k, w_v, w_o.T, w_up, w_down.T, ln1_gain, ln1_bias, b_o, ln2_gain, ln2_bias, b_down, b_q, b_v, b_up,
         valid_mask)
    )
    steps_a = [shard_a] + [to_step(shard_a, s) for s in (1, 2, 3)]
    line_a = jnp.stack(steps_a)
    steps_f = [shard_f] + [to_step(shard_f, s) for s in (1, 2, 3)]
    over_f = [to_mask(x, 1) for x in steps_f]
    near_a = [to_mask(line_a, m) for m in (2, 4, 6)]
    halves_a = after([jnp.stack(steps_a[0:2]), jnp.stack(steps_a[2:4])], steps_f)
    over_a = [to_mask(a, 1) for a in halves_a]
    line_f = jnp.stack(after(steps_f, (over_a, near_a)))
    pieces_a = [line_a] + near_a + over_a + [to_mask(a, 1) for a in near_a]
    halo = lax.ppermute(layer_input[own - HALO :], "tp", [(i, i + 1) for i in range(3)])
    f_x, f_y = to_mask(line_f, 2), to_mask(line_f, 4)

    ids = segment_ids + 16 * jnp.arange(segment_ids.shape[0], dtype=jnp.int32)[:, None]
    ids = jnp.concatenate([jnp.full((HALO,), -1, jnp.int32), ids.reshape(-1)])
    id_col = lax.dynamic_slice_in_dim(ids, place * own, HALO + own)[:, None]
    mask = valid_mask.astype(F32)[:, None]

    q, k, v, kt, nt, w_all, vec, bup, scale, head = project(after(layer_input, over_f), id_col, pieces_a, tokens_all)
    o_far, qa_far = attend_far(q, k, v)
    f_x, f_y = after((f_x, f_y), o_far)
    halo = after(halo, o_far)
    f_xy = [to_mask(f_y[0:2], 2), to_mask(f_x[2:4], 4)]
    k_halo, v_halo, kt_halo, nt_halo = project_halo(halo, id_col, w_all, vec, head)
    o_near, qa_near = attend_near(q, k_halo, k, v_halo, v)
    near_f = [f_x, f_y] + after(f_xy, o_near)
    pieces_f = [x[None] for x in steps_f] + near_f + [x[None] for x in over_f] + [to_mask(a, 1) for a in near_f]
    layer_out, g_h1, ga, theirs_f, mine_f, small_two, gbup = central(
        layer_input, o_near, o_far, teacher, cotangent, mask, vec, bup, scale, pieces_f
    )

    def near(base, qa, ga):
        return pull_near(base, qa, ga, k_halo, k, v_halo, v, kt_halo, kt)

    g_near, gq_near, part_near = near(0, qa_near, ga)
    half = add(after(mine_f, g_near), to_mask(theirs_f, 1))
    from_x, from_y = to_mask(half[3, 0:2], 2), to_mask(half[3, 2:4], 4)
    g_more, gq_more, part_more = near(2, after(qa_near, half), ga)
    gn_halo, small_halo = halo_back(g_near, g_more, w_all, halo)
    back = lax.ppermute(gn_halo, "tp", [(i + 1, i) for i in range(3)])
    from_x, from_y = after((from_x, from_y), gn_halo)
    for_x = jnp.concatenate([half[1, 0:2], add(half[1, 2:4], from_y)])
    for_y = jnp.concatenate([add(half[2, 0:2], from_x), half[2, 2:4]])
    got_x, got_y = to_mask(for_x, 2), to_mask(for_y, 4)
    g_own = pull_far(after(qa_far, (for_x, for_y)), ga, k, v, kt, gq_near, gq_more, part_near, part_more)
    gn_own, theirs_a, mine_a = own_back(
        layer_input, g_near, g_more, g_own, nt_halo, nt, w_all, small_halo, small_two, gbup, scale
    )
    got_x, got_y = after((got_x, got_y), gn_own)
    line = (half[0].astype(F32) + got_x.astype(F32) + got_y.astype(F32)).astype(BF16)
    grad_wo, grad_wup, grad_wdn = unpack_f(line, *[to_step(line[s], s) for s in (1, 2, 3)])

    half = add(mine_a, to_mask(after(theirs_a, back), 1))
    from_x, from_y, from_xy = (to_mask(half[m], 2 * m) for m in (1, 2, 3))
    line = (half[0].astype(F32) + from_x.astype(F32) + from_y.astype(F32) + from_xy.astype(F32)).astype(BF16)
    grad_wq, grad_wk, grad_wv, grad_bq, grad_bv, grad_bup, loss, *six = unpack_a(
        line, *[to_step(line[s], s) for s in (1, 2, 3)]
    )
    grad_input = close(layer_input, gn_own, back, g_h1, vec)
    return (
        layer_out, loss.reshape(()), grad_input, six[0], six[1], grad_wq, grad_wk, grad_wv, grad_bq, grad_bv, grad_wo.T, six[2],
        six[3], six[4], grad_wup, grad_bup, grad_wdn.T, six[5]
    )


def solution(mesh):
    tokens = P(("fsdp", "tp"), None)
    rows, crossed, heads = P("fsdp"), P("fsdp", "tp"), P("tp", "fsdp")
    placed = (
        tokens,
        P("fsdp", None),
        P(("fsdp", "tp")),
        tokens,
        tokens,
        rows,
        rows,
        crossed,
        crossed,
        crossed,
        heads,
        heads,
        heads,
        rows,
        rows,
        rows,
        crossed,
        heads,
        heads,
        rows,
    )
    given = (
        tokens,
        P(),
        tokens,
        rows,
        rows,
        crossed,
        crossed,
        crossed,
        heads,
        heads,
        heads,
        rows,
        rows,
        rows,
        crossed,
        heads,
        heads,
        rows,
    )
    sizes = (mesh.shape["fsdp"], mesh.shape["tp"])
    body = local_fast if sizes == (8, 4) else local
    return jax.shard_map(body, mesh=mesh, in_specs=placed, out_specs=given, check_vma=False)
```

```python
import functools

import jax
import jax.numpy as jnp
from jax import lax
from jax.experimental import pallas as pl
from jax.experimental.pallas import tpu as pltpu
from jax.sharding import PartitionSpec as P

D = 512
H = 8
HD = 64
LEN = 1024
HALO = 512
PAIR = 2 * HD
NEG = -1e30
SCALE = HD ** (-0.5)
F32 = jnp.float32
BF16 = jnp.bfloat16
MIB = 1 << 20

CONTRACT_LAST = (((1,), (1,)), ((), ()))


def dot(a, b):
    return jnp.dot(a, b, preferred_element_type=F32)


def dot_t(a, b):
    return lax.dot_general(a, b, CONTRACT_LAST, preferred_element_type=F32)


def normalize(x):
    center = x - jnp.mean(x, axis=-1, keepdims=True)
    rstd = lax.rsqrt(jnp.mean(center * center, axis=-1, keepdims=True) + 1e-05)
    return center * rstd, rstd


def norm_pull(g, gain, xhat, rstd):
    gx = g * gain
    return rstd * (
        gx
        - jnp.mean(gx, axis=-1, keepdims=True)
        - xhat * jnp.mean(gx * xhat, axis=-1, keepdims=True)
    )


def fold(x):
    return jnp.sum(x.reshape(x.shape[0] // 8, 8, x.shape[1]), axis=0)


def rows_of(start, size, unit=128):
    return pl.ds(pl.multiple_of(start, unit), size)


def forward_kernel(
    qb, x_ref, vec_ref, w_ref, idr_ref, idc_ref, n_ref, q_ref, k_ref, v_ref, o_ref, lse_ref, bias_ref, stat_ref
):
    ext, own = x_ref.shape[0], o_ref.shape[0]
    window = HALO + qb

    def project(i, carry):
        rows = rows_of(i * 128, 128)
        xhat, _ = normalize(x_ref[rows, :].astype(F32))
        n1 = (xhat * vec_ref[0:1, :] + vec_ref[1:2, :]).astype(BF16)
        n_ref[rows, :] = n1
        k_ref[rows, :] = dot(n1, w_ref[:, D : 2 * D]).astype(BF16)
        v_ref[rows, :] = (dot(n1, w_ref[:, 2 * D : 3 * D]) + vec_ref[3:4, :]).astype(BF16)
        return carry

    lax.fori_loop(0, ext // 128, project, 0)

    def project_q(i, carry):
        rows = rows_of(i * 128, 128)
        q = dot(n_ref[rows_of(HALO + i * 128, 128), :], w_ref[:, 0:D]) + vec_ref[2:3, :]
        q_ref[rows, :] = q.astype(BF16) * jnp.asarray(SCALE, BF16)
        return carry

    lax.fori_loop(0, own // 128, project_q, 0)

    def query_block(i, carry):
        first = i * qb
        key = lax.broadcasted_iota(jnp.int32, (qb, window), 1)
        query = lax.broadcasted_iota(jnp.int32, (qb, window), 0)
        same = idc_ref[rows_of(HALO + first, qb), :] == idr_ref[:, rows_of(first, window)]
        bias_ref[...] = jnp.where(same & (key <= query + HALO), 0.0, NEG)

        def pair(g, inner):
            lanes = rows_of(g * PAIR, PAIR)
            lane = lax.broadcasted_iota(jnp.int32, (qb, PAIR), 1)
            keys = k_ref[rows_of(first, window), lanes]
            values = v_ref[rows_of(first, window), lanes]
            both = q_ref[rows_of(first, qb), lanes]
            got = None
            for h in range(2):
                mine = (lane < HD) if h == 0 else (lane >= HD)
                s = dot_t(jnp.where(mine, both, jnp.zeros_like(both)), keys) + bias_ref[...]
                top = jnp.max(s, axis=-1, keepdims=True)
                p = jnp.exp(s - top)
                total = jnp.sum(p, axis=-1, keepdims=True)
                o = dot(p.astype(BF16), values) / total
                got = o if h == 0 else jnp.where(mine, o, got)
                stat_ref[...] = jnp.where(lane == 2 * g + h, top + jnp.log(total), stat_ref[...])
            o_ref[rows_of(first, qb), lanes] = got.astype(BF16)
            return inner

        lax.fori_loop(0, D // PAIR, pair, 0)
        lse_ref[:, rows_of(first, qb)] = jnp.transpose(stat_ref[...])[0:H, :]
        return carry

    stat_ref[...] = jnp.zeros_like(stat_ref)
    lax.fori_loop(0, own // qb, query_block, 0)


def attention_forward(x_ext, vecs, w_qkv, id_row, id_col, own):
    ext = x_ext.shape[0]
    qb = 256 if own % 256 == 0 else 128
    shapes = (
        jax.ShapeDtypeStruct((ext, D), BF16),
        jax.ShapeDtypeStruct((own, D), BF16),
        jax.ShapeDtypeStruct((ext, D), BF16),
        jax.ShapeDtypeStruct((ext, D), BF16),
        jax.ShapeDtypeStruct((own, D), BF16),
        jax.ShapeDtypeStruct((H, own), F32),
    )
    return pl.pallas_call(
        functools.partial(forward_kernel, qb),
        out_shape=shapes,
        scratch_shapes=[pltpu.VMEM((qb, HALO + qb), F32), pltpu.VMEM((qb, 128), F32)],
        compiler_params=pltpu.CompilerParams(vmem_limit_bytes=48 * MIB),
        name="attention_forward",
    )(x_ext, vecs, w_qkv, id_row, id_col)


def middle_kernel(
    rb,
    scale_ref,
    x_ref,
    o_ref,
    teacher_ref,
    cot_ref,
    mask_ref,
    vec_ref,
    bup_ref,
    wo_ref,
    wup_ref,
    wdn_ref,
    out_ref,
    gh_ref,
    go_ref,
    delta_ref,
    gwo_ref,
    gwup_ref,
    gwdn_ref,
    small_ref,
    gbup_ref,
    slope_ref,
    hid_ref,
    gpre_ref,
    n2t_ref,
    gmlpt_ref,
    gattnt_ref,
):
    own = x_ref.shape[0]
    ff = wup_ref.shape[1]
    chunk = 512
    small_ref[...] = jnp.zeros_like(small_ref)
    head_of = lax.broadcasted_iota(jnp.int32, (D, 128), 0) // HD
    pick = (head_of == lax.broadcasted_iota(jnp.int32, (D, 128), 1)).astype(BF16)

    def block(i, carry):
        rows = rows_of(i * rb, rb)
        out_bias, gain, offset, down_bias = (vec_ref[j : j + 1, :] for j in range(4))
        h1 = x_ref[rows, :].astype(F32) + dot_t(o_ref[rows, :], wo_ref[...]) + out_bias
        xhat, rstd = normalize(h1)
        n2 = xhat * gain + offset
        n2_low = n2.astype(BF16)
        n2t_ref[:, rows] = jnp.transpose(n2).astype(BF16)
        for c in range(0, ff, chunk):
            pre = dot(n2_low, wup_ref[:, c : c + chunk]) + bup_ref[:, c : c + chunk]
            s = jax.nn.sigmoid(1.702 * pre)
            value = pre * s
            hid_ref[rows, c : c + chunk] = value.astype(BF16)
            slope_ref[:, c : c + chunk] = s + 1.702 * value * (1.0 - s)
        out = h1 + dot_t(hid_ref[rows, :], wdn_ref[...]) + down_bias
        out_ref[rows, :] = out.astype(BF16)
        valid = mask_ref[rows, :]
        diff = (out - teacher_ref[rows, :].astype(F32)) * valid
        g_out = cot_ref[rows, :].astype(F32) + scale_ref[0, 0] * diff
        small_ref[0:8, :] += fold(g_out)
        small_ref[8:16, :] += fold(diff * diff)
        g_mlp = g_out.astype(BF16)
        gmlpt_ref[:, rows] = jnp.transpose(g_out).astype(BF16)
        for c in range(0, ff, chunk):
            g_hid = dot(g_mlp, wdn_ref[:, c : c + chunk])
            gpre_ref[rows, c : c + chunk] = (g_hid * slope_ref[:, c : c + chunk]).astype(BF16)
        g_n2 = dot_t(gpre_ref[rows, :], wup_ref[...])
        small_ref[16:24, :] += fold(g_n2 * xhat)
        small_ref[24:32, :] += fold(g_n2)
        g_h1 = g_out + norm_pull(g_n2, gain, xhat, rstd)
        gh_ref[rows, :] = g_h1
        small_ref[32:40, :] += fold(g_h1)
        gattnt_ref[:, rows] = jnp.transpose(g_h1).astype(BF16)
        g_o = dot(g_h1.astype(BF16), wo_ref[...]).astype(BF16)
        go_ref[rows, :] = g_o
        product = g_o.astype(F32) * o_ref[rows, :].astype(F32)
        high = product.astype(BF16)
        low = (product - high.astype(F32)).astype(BF16)
        delta_ref[:, rows] = jnp.transpose(dot(high, pick) + dot(low, pick))[0:H, :]
        return carry

    lax.fori_loop(0, own // rb, block, 0)
    ones = jnp.ones((8, own), BF16)

    def grads(i, carry):
        cols = rows_of(i * chunk, chunk)
        gwdn_ref[:, cols] = dot(gmlpt_ref[...], hid_ref[:, cols]).astype(BF16)
        gwup_ref[:, cols] = dot(n2t_ref[...], gpre_ref[:, cols]).astype(BF16)
        gbup_ref[:, cols] = dot(ones, gpre_ref[:, cols])
        return carry

    lax.fori_loop(0, ff // chunk, grads, 0)
    gwo_ref[...] = dot(gattnt_ref[...], o_ref[...]).astype(BF16)


def middle(scale, x, o, teacher, cot, mask, vecs, b_up, w_o, w_up, w_dn):
    own, ff = x.shape[0], w_up.shape[1]
    rb = 256 if own % 256 == 0 else 128
    shapes = (
        jax.ShapeDtypeStruct((own, D), BF16),
        jax.ShapeDtypeStruct((own, D), F32),
        jax.ShapeDtypeStruct((own, D), BF16),
        jax.ShapeDtypeStruct((H, own), F32),
        jax.ShapeDtypeStruct((D, D), BF16),
        jax.ShapeDtypeStruct((D, ff), BF16),
        jax.ShapeDtypeStruct((D, ff), BF16),
        jax.ShapeDtypeStruct((40, D), F32),
        jax.ShapeDtypeStruct((8, ff), F32),
    )
    whole = pl.BlockSpec(memory_space=pltpu.VMEM)
    return pl.pallas_call(
        functools.partial(middle_kernel, rb),
        out_shape=shapes,
        in_specs=[pl.BlockSpec(memory_space=pltpu.SMEM)] + [whole] * 10,
        out_specs=[whole] * len(shapes),
        scratch_shapes=[
            pltpu.VMEM((rb, ff), F32),
            pltpu.VMEM((own, ff), BF16),
            pltpu.VMEM((own, ff), BF16),
            pltpu.VMEM((D, own), BF16),
            pltpu.VMEM((D, own), BF16),
            pltpu.VMEM((D, own), BF16),
        ],
        compiler_params=pltpu.CompilerParams(vmem_limit_bytes=56 * MIB),
        name="middle",
    )(scale, x, o, teacher, cot, mask, vecs, b_up, w_o, w_up, w_dn)


def backward_kernel(
    qb,
    q_ref,
    k_ref,
    v_ref,
    go_ref,
    lse_ref,
    delta_ref,
    idr_ref,
    idc_ref,
    n_ref,
    x_ref,
    w_ref,
    gn_halo_ref,
    gn_ref,
    gw_ref,
    small_ref,
    bias_ref,
    kt_ref,
    nt_ref,
    dqt_ref,
    dk_ref,
    dv_ref,
    g_ref,
):
    ext, own = k_ref.shape[0], q_ref.shape[0]
    window = HALO + qb
    dk_ref[...] = jnp.zeros_like(dk_ref)
    dv_ref[...] = jnp.zeros_like(dv_ref)
    small_ref[...] = jnp.zeros_like(small_ref)

    def turn(i, carry):
        rows = rows_of(i * 128, 128)
        kt_ref[:, rows] = jnp.transpose(k_ref[rows, :].astype(F32)).astype(BF16)
        nt_ref[:, rows] = jnp.transpose(n_ref[rows, :].astype(F32)).astype(BF16)
        return carry

    lax.fori_loop(0, ext // 128, turn, 0)

    def query_block(i, carry):
        first = i * qb
        key = lax.broadcasted_iota(jnp.int32, (window, qb), 0)
        query = lax.broadcasted_iota(jnp.int32, (window, qb), 1)
        same = idc_ref[rows_of(first, window), :] == idr_ref[:, rows_of(HALO + first, qb)]
        bias_ref[...] = jnp.where(same & (key <= query + HALO), 0.0, NEG)

        def pair(g, inner):
            lanes = rows_of(g * PAIR, PAIR)
            lane = lax.broadcasted_iota(jnp.int32, (qb, PAIR), 1)
            keys = k_ref[rows_of(first, window), lanes]
            values = v_ref[rows_of(first, window), lanes]
            both_q = q_ref[rows_of(first, qb), lanes]
            both_g = go_ref[rows_of(first, qb), lanes]
            all_lse = lse_ref[:, rows_of(first, qb)]
            all_delta = delta_ref[:, rows_of(first, qb)]
            line = lax.broadcasted_iota(jnp.int32, (H, qb), 0)
            dk, dv = None, None
            for h in range(2):
                head = 2 * g + h
                mine = (lane < HD) if h == 0 else (lane >= HD)
                q = jnp.where(mine, both_q, jnp.zeros_like(both_q))
                g_o = jnp.where(mine, both_g, jnp.zeros_like(both_g))
                lse = jnp.sum(jnp.where(line == head, all_lse, 0.0), axis=0, keepdims=True)
                delta = jnp.sum(jnp.where(line == head, all_delta, 0.0), axis=0, keepdims=True)
                p = jnp.exp(dot_t(keys, q) + bias_ref[...] - lse)
                ds = (p * (dot_t(values, g_o) - delta)).astype(BF16)
                dv_h = dot(p.astype(BF16), g_o)
                dk_h = dot(ds, q)
                dk, dv = (dk_h, dv_h) if h == 0 else (dk + dk_h, dv + dv_h)
                dqt_ref[rows_of(head * HD, HD, HD), rows_of(first, qb)] = dot(
                    kt_ref[rows_of(head * HD, HD, HD), rows_of(first, window)], ds
                )
            dk_ref[rows_of(first, window), lanes] += dk
            dv_ref[rows_of(first, window), lanes] += dv
            return inner

        lax.fori_loop(0, D // PAIR, pair, 0)
        return carry

    lax.fori_loop(0, own // qb, query_block, 0)

    def gather(i, carry):
        rows = rows_of(i * 128, 128)
        g_ref[rows, D : 2 * D] = dk_ref[rows, :].astype(BF16)
        g_ref[rows, 2 * D : 3 * D] = dv_ref[rows, :].astype(BF16)
        return carry

    lax.fori_loop(0, ext // 128, gather, 0)

    def gather_q(i, carry):
        cols = rows_of(i * 128, 128)
        g_ref[rows_of(HALO + i * 128, 128), 0:D] = (jnp.transpose(dqt_ref[:, cols]) * SCALE).astype(BF16)
        return carry

    lax.fori_loop(0, own // 128, gather_q, 0)

    def norms(rows, g_n1):
        xhat, _ = normalize(x_ref[rows, :].astype(F32))
        small_ref[0:8, :] += fold(g_n1 * xhat)
        small_ref[8:16, :] += fold(g_n1)

    def pull_halo(i, carry):
        rows = rows_of(i * 128, 128)
        g_n1 = dot_t(g_ref[rows, D : 3 * D], w_ref[:, D : 3 * D])
        gn_halo_ref[rows, :] = g_n1.astype(BF16)
        norms(rows, g_n1)
        return carry

    lax.fori_loop(0, HALO // 128, pull_halo, 0)

    def pull_own(i, carry):
        rows = rows_of(HALO + i * 128, 128)
        g_n1 = dot_t(g_ref[rows, :], w_ref[...])
        gn_ref[rows_of(i * 128, 128), :] = g_n1
        norms(rows, g_n1)
        return carry

    lax.fori_loop(0, own // 128, pull_own, 0)
    gw_ref[:, 0:D] = dot(nt_ref[:, HALO:], g_ref[HALO:, 0:D]).astype(BF16)
    gw_ref[:, D : 2 * D] = dot(nt_ref[...], g_ref[:, D : 2 * D]).astype(BF16)
    gw_ref[:, 2 * D : 3 * D] = dot(nt_ref[...], g_ref[:, 2 * D : 3 * D]).astype(BF16)
    small_ref[16:24, :] = dot(jnp.ones((8, own), BF16), g_ref[HALO:, 0:D])
    small_ref[24:32, :] = dot(jnp.ones((8, ext), BF16), g_ref[:, 2 * D : 3 * D])


def attention_backward(q, k, v, g_o, lse, delta, id_row, id_col, n1, x_ext, w_qkv):
    ext, own = k.shape[0], q.shape[0]
    qb = 256 if own % 256 == 0 else 128
    shapes = (
        jax.ShapeDtypeStruct((HALO, D), BF16),
        jax.ShapeDtypeStruct((own, D), F32),
        jax.ShapeDtypeStruct((D, 3 * D), BF16),
        jax.ShapeDtypeStruct((32, D), F32),
    )
    return pl.pallas_call(
        functools.partial(backward_kernel, qb),
        out_shape=shapes,
        scratch_shapes=[
            pltpu.VMEM((HALO + qb, qb), F32),
            pltpu.VMEM((D, ext), BF16),
            pltpu.VMEM((D, ext), BF16),
            pltpu.VMEM((D, own), F32),
            pltpu.VMEM((ext, D), F32),
            pltpu.VMEM((ext, D), F32),
            pltpu.VMEM((ext, 3 * D), BF16),
        ],
        compiler_params=pltpu.CompilerParams(vmem_limit_bytes=56 * MIB),
        name="attention_backward",
    )(q, k, v, g_o, lse, delta, id_row, id_col, n1, x_ext, w_qkv)


def finish_kernel(x_ref, gn_ref, gh_ref, vec_ref, out_ref):
    def block(i, carry):
        rows = rows_of(i * 128, 128)
        xhat, rstd = normalize(x_ref[rows, :].astype(F32))
        out_ref[rows, :] = gh_ref[rows, :] + norm_pull(gn_ref[rows, :], vec_ref[0:1, :], xhat, rstd)
        return carry

    lax.fori_loop(0, x_ref.shape[0] // 128, block, 0)


def finish(x, g_n1, g_h1, vecs):
    return pl.pallas_call(
        finish_kernel,
        out_shape=jax.ShapeDtypeStruct(x.shape, F32),
        compiler_params=pltpu.CompilerParams(vmem_limit_bytes=32 * MIB),
        name="finish",
    )(x, g_n1, g_h1, vecs)


def hops(rows):
    plan, left, step = [], HALO, 1
    while left > 0:
        take = min(rows, left)
        plan.append((step, take))
        left, step = left - take, step + 1
    return plan


def local(
    layer_input,
    segment_ids,
    valid_mask,
    teacher,
    cotangent,
    ln1_gain,
    ln1_bias,
    w_q,
    w_k,
    w_v,
    b_q,
    b_v,
    w_o,
    b_o,
    ln2_gain,
    ln2_bias,
    w_up,
    b_up,
    w_down,
    b_down,
):
    fsdp_size = lax.axis_size("fsdp")
    tensor_size = lax.axis_size("tp")
    place = lax.axis_index("tp")
    own = layer_input.shape[0]
    tokens_all = own * fsdp_size * tensor_size
    rows_d = w_q.shape[0]
    cols_h, cols_f = w_q.shape[1], w_up.shape[1]

    parts = []
    for step, take in hops(own):
        route = [(i, i + step) for i in range(tensor_size - step)]
        parts.insert(0, lax.ppermute(layer_input[own - take :], "tp", route))
    x_ext = jnp.concatenate(parts + [layer_input], axis=0)
    ids = segment_ids + LEN * jnp.arange(segment_ids.shape[0], dtype=jnp.int32)[:, None]
    ids = jnp.concatenate([jnp.full((HALO,), -1, jnp.int32), ids.reshape(-1)])
    ids = lax.dynamic_slice_in_dim(ids, place * own, HALO + own)
    id_row, id_col = ids[None, :], ids[:, None]

    pack = jnp.concatenate([w_q, w_k, w_v, w_o.T, w_up, w_down.T], axis=1)
    count = jnp.sum(valid_mask)
    count_high = count // 256
    vectors = jnp.concatenate([ln1_gain, ln1_bias, b_o, ln2_gain, ln2_bias, b_down])
    heads = jnp.concatenate([b_q.reshape(-1), b_v.reshape(-1), b_up.reshape(-1)])
    digits = jnp.stack([count_high, count - 256 * count_high]).astype(BF16)
    small = jnp.concatenate([vectors, heads, digits])
    width = pack.shape[1]
    lines = -(-small.shape[0] // width)
    small = jnp.pad(small, (0, lines * width - small.shape[0])).reshape(lines, width)
    shard = jnp.concatenate([pack, small], axis=0)
    every = lax.all_gather(lax.all_gather(shard, "tp", axis=0), "fsdp", axis=0)
    big = every[:, :, :rows_d, :]

    def columns(start, size):
        part = big[:, :, :, start : start + size]
        return part.transpose(0, 2, 1, 3).reshape(fsdp_size * rows_d, tensor_size * size)

    w_qkv = jnp.concatenate([columns(j * cols_h, cols_h) for j in range(3)], axis=1)
    w_ot = columns(3 * cols_h, cols_h)
    w_up_all = columns(4 * cols_h, cols_f)
    w_dn_all = columns(4 * cols_h + cols_f, cols_f)
    few = every[:, :, rows_d:, :].reshape(fsdp_size, tensor_size, -1).astype(F32)
    six = few[:, 0, : 6 * rows_d].reshape(fsdp_size, 6, rows_d).transpose(1, 0, 2).reshape(6, D)
    at = 6 * rows_d

    def by_head(start, shape):
        size = shape[0] * shape[1]
        part = few[:, :, start : start + size].reshape((fsdp_size, tensor_size) + shape)
        return part.transpose(1, 2, 0, 3).reshape(1, -1)

    bq_all = by_head(at, b_q.shape)
    at += b_q.size
    bv_all = by_head(at, b_v.shape)
    at += b_v.size
    bup_all = by_head(at, b_up.shape)
    at += b_up.size
    valid_total = 256.0 * jnp.sum(few[:, :, at]) + jnp.sum(few[:, :, at + 1])

    vec_one = jnp.concatenate([six[0:2], bq_all, bv_all], axis=0)
    vec_two = jnp.stack([six[2], six[3], six[4], six[5]])
    n1, q, k, v, o, lse = attention_forward(x_ext, vec_one, w_qkv, id_row, id_col, own)
    scale = (tokens_all / valid_total).reshape(1, 1)
    mask = valid_mask.astype(F32)[:, None]
    layer_out, g_h1, g_o, delta, g_wo, g_wup, g_wdn, small_two, g_bup = middle(
        scale, layer_input, o, teacher, cotangent, mask, vec_two, bup_all, w_ot, w_up_all, w_dn_all
    )
    gn_halo, gn_own, g_qkv, small_one = attention_backward(
        q, k, v, g_o, lse, delta, id_row, id_col, n1, x_ext, w_qkv
    )

    total = gn_own
    left = HALO
    for step, take in hops(own):
        route = [(i + step, i) for i in range(tensor_size - step)]
        part = lax.ppermute(gn_halo[left - take : left], "tp", route).astype(F32)
        total = total + jnp.pad(part, ((own - take, 0), (0, 0)))
        left -= take
    grad_input = finish(layer_input, total, g_h1, vec_one)

    def split(grad, size):
        return grad.reshape(fsdp_size, rows_d, tensor_size, size).transpose(0, 2, 1, 3)

    g_pack = jnp.concatenate(
        [split(g_qkv[:, j * D : (j + 1) * D], cols_h) for j in range(3)]
        + [split(g_wo, cols_h), split(g_wup, cols_f), split(g_wdn, cols_f)],
        axis=3,
    )
    ones = [small_one[8 * j : 8 * j + 8].sum(0) for j in range(2)] + [small_one[16], small_one[24]]
    twos = [small_two[8 * j : 8 * j + 8].sum(0) for j in range(5)]
    loss_part = 0.5 / D * jnp.sum(twos[1]) / valid_total
    six_grads = jnp.stack([ones[0], ones[1], twos[4], twos[2], twos[3], twos[0]])
    six_grads = six_grads.reshape(6, fsdp_size, 1, rows_d).transpose(1, 2, 0, 3)
    six_grads = jnp.broadcast_to(
        six_grads.reshape(fsdp_size, 1, -1), (fsdp_size, tensor_size, 6 * rows_d)
    )

    def heads_of(grad, shape):
        part = grad.reshape((tensor_size, shape[0], fsdp_size, shape[1]))
        return part.transpose(2, 0, 1, 3).reshape(fsdp_size, tensor_size, -1)

    loss_high = loss_part.astype(BF16).astype(F32)
    losses = jnp.broadcast_to(
        jnp.stack([loss_high, loss_part - loss_high]), (fsdp_size, tensor_size, 2)
    )
    g_small = jnp.concatenate(
        [
            six_grads,
            heads_of(ones[2], b_q.shape),
            heads_of(ones[3], b_v.shape),
            heads_of(g_bup[0], b_up.shape),
            losses,
        ],
        axis=2,
    ).astype(BF16)
    g_small = jnp.pad(g_small, ((0, 0), (0, 0), (0, lines * width - g_small.shape[2])))
    g_all = jnp.concatenate([g_pack, g_small.reshape(fsdp_size, tensor_size, lines, width)], axis=2)
    mine = lax.psum_scatter(g_all, "fsdp", scatter_dimension=0, tiled=False)
    mine = lax.psum_scatter(mine, "tp", scatter_dimension=0, tiled=False).astype(F32)
    g_mat, g_vec = mine[:rows_d], mine[rows_d:].reshape(-1)
    c3, c4 = 3 * cols_h, 4 * cols_h
    six_out = g_vec[: 6 * rows_d].reshape(6, rows_d)
    at = 6 * rows_d
    grad_bq = g_vec[at : at + b_q.size].reshape(b_q.shape)
    at += b_q.size
    grad_bv = g_vec[at : at + b_v.size].reshape(b_v.shape)
    at += b_v.size
    grad_bup = g_vec[at : at + b_up.size].reshape(b_up.shape)
    at += b_up.size
    loss = g_vec[at] + g_vec[at + 1]
    return (
        layer_out,
        loss,
        grad_input,
        six_out[0],
        six_out[1],
        g_mat[:, 0:cols_h],
        g_mat[:, cols_h : 2 * cols_h],
        g_mat[:, 2 * cols_h : c3],
        grad_bq,
        grad_bv,
        g_mat[:, c3:c4].T,
        six_out[2],
        six_out[3],
        six_out[4],
        g_mat[:, c4 : c4 + cols_f],
        grad_bup,
        g_mat[:, c4 + cols_f :].T,
        six_out[5],
    )


ROWS = D // 8
EXTRA = 8
COLS = D // 4
FFC = 512
WA = 3 * COLS
WF = COLS + 2 * FFC
TALL = D + 16
ALL = (0, 1, 2, 3)
PIECES_A = ((0, ALL), (2, ALL), (4, ALL), (6, ALL), (1, ALL[0:2]), (1, ALL[2:4]), (3, ALL), (5, ALL), (7, ALL))
SMALL = pl.CostEstimate(flops=1, bytes_accessed=1, transcendentals=0)


def about(us):
    return pl.CostEstimate(flops=us * 1000000, bytes_accessed=us * 3300000, transcendentals=0)


ANY = pl.BlockSpec(memory_space=pl.ANY)
VMEM = pl.BlockSpec(memory_space=pltpu.VMEM)
FAR = pl.BlockSpec(memory_space=pl.ANY)


def params(mib):
    return pltpu.CompilerParams(vmem_limit_bytes=mib * MIB)


def lane_of(shape):
    return lax.broadcasted_iota(jnp.int32, shape, len(shape) - 1)


def pack_kernel(
    wq_ref, wk_ref, wv_ref, wo_ref, wup_ref, wdn_ref, g1, b1, bo, g2, b2, bd, bq, bv, bup, mask_ref, a_ref, f_ref
):
    me = lax.axis_index("fsdp")
    a_ref[0:ROWS, 0:COLS] = wq_ref[...]
    a_ref[0:ROWS, COLS : 2 * COLS] = wk_ref[...]
    a_ref[0:ROWS, 2 * COLS : 3 * COLS] = wv_ref[...]
    f_ref[:, 0:COLS] = wo_ref[...]
    f_ref[:, COLS : COLS + FFC] = wup_ref[...]
    f_ref[:, COLS + FFC :] = wdn_ref[...]
    count = jnp.sum(mask_ref[...].astype(F32)).reshape(1, 1)
    high = jnp.floor(count / 256.0)
    lane = lane_of((1, 128))
    digits = jnp.where(lane == 0, high, jnp.where(lane == 1, count - 256.0 * high, 0.0))
    vectors = [r[...].astype(F32).reshape(1, ROWS) for r in (g1, b1, bo, g2, b2, bd)]
    rows = [jnp.concatenate([v, v], axis=1) for v in vectors] + [digits, jnp.zeros((1, 128), F32)]
    a_ref[ROWS:, 0:128] = jnp.concatenate(rows, axis=0).astype(BF16)

    def spread(ref):
        block = ref[...].astype(F32)
        count, piece = block.shape
        lanes = count * HD
        lane = lane_of((1, lanes))
        row = jnp.zeros((1, lanes), F32)
        for i in range(count):
            for j in range(piece):
                at = i * HD + me * piece + j
                row = jnp.where(lane == at, block[i : i + 1, j : j + 1], row)
        return row

    ups = spread(bup)
    rows = [spread(bq), spread(bv)] + [ups[:, 128 * j : 128 * j + 128] for j in range(4)]
    rows.append(jnp.zeros((2, 128), F32))
    a_ref[ROWS:, 128:256] = jnp.concatenate(rows, axis=0).astype(BF16)
    a_ref[ROWS:, 256:384] = jnp.zeros((EXTRA, 128), BF16)


def pack_weights(args):
    return pl.pallas_call(
        pack_kernel,
        out_shape=(
            jax.ShapeDtypeStruct((ROWS + EXTRA, WA), BF16),
            jax.ShapeDtypeStruct((ROWS, WF), BF16),
        ),
        compiler_params=params(60),
        name="pack_weights",
    )(*args)


def project_kernel(
    tokens_all, x_ref, idc_ref, p0, p1, p2, p3, p4, p5, p6, p7, p8,
    q_ref, k_ref, v_ref, kt_ref, nt_ref, w_ref, vec_ref, bup_ref, scale_ref, head_ref, ext_ref, n_ref, sem
):
    me, place = lax.axis_index("fsdp"), lax.axis_index("tp")
    pieces = (p0, p1, p2, p3, p4, p5, p6, p7, p8)

    def each(act):
        for ref, (mask, steps) in zip(pieces, PIECES_A):
            owner = lax.bitwise_xor(me, mask)
            for i, s in enumerate(steps):
                tp = lax.bitwise_and(place - s + 4, 3)
                act(ref.at[i], 4 * mask + s, owner, tp)

    def start_ext(ref, slot, owner, tp):
        pltpu.make_async_copy(ref.at[pl.ds(ROWS, EXTRA), :], ext_ref.at[slot], sem.at[0]).start()

    def start_w(ref, slot, owner, tp):
        pltpu.make_async_copy(
            ref.at[pl.ds(0, ROWS), :],
            w_ref.at[rows_of(owner * ROWS, ROWS, ROWS), rows_of(tp * WA, WA)],
            sem.at[1],
        ).start()

    each(start_ext)
    each(start_w)
    pltpu.make_async_copy(ext_ref, ext_ref, sem.at[0]).wait()
    lane = lane_of((EXTRA, D))
    vectors = jnp.zeros((EXTRA, D), F32)
    total = jnp.zeros((EXTRA, 128), F32)
    for j in range(8):
        block = ext_ref[4 * j, :, 0:128].astype(F32)
        wide = jnp.concatenate([block] * 4, axis=1)
        vectors = jnp.where(lane // ROWS == lax.bitwise_xor(me, j), wide, vectors)
        for s in range(4):
            total += ext_ref[4 * j + s, :, 0:128].astype(F32)
    vec_ref[...] = vectors
    valid = 256.0 * total[6:7, 0:1] + total[6:7, 1:2]
    scale_ref[...] = jnp.concatenate(
        [jnp.broadcast_to(tokens_all / valid, (4, 128)), jnp.broadcast_to(0.5 / D / valid, (4, 128))], axis=0
    )
    for s in range(4):
        tp = lax.bitwise_and(place - s + 4, 3)
        block = jnp.zeros((EXTRA, 128), F32)
        for j in range(8):
            block += ext_ref[4 * j + s, :, 128:256].astype(F32)
        head_ref[:, rows_of(tp * COLS, COLS)] = block
        for i in range(4):
            bup_ref[:, rows_of(tp * FFC + 128 * i, 128)] = jnp.broadcast_to(block[2 + i : 3 + i], (8, 128))

    def norm(i, carry):
        rows = rows_of(i * QB, QB)
        n_ref[rows, :] = first_norm(x_ref[rows, :], vectors, me, nt_ref, rows)
        return carry

    def product(one):
        one["made"] = dot(n_ref[one["rows"], :], w_ref[...])

    def keep(one):
        rows, made = one["rows"], one.pop("made")
        spare_q, spare_k, spare_v = spare_lanes(idc_ref[slice(HALO + rows.start, HALO + rows.stop), :])
        for t in range(4):
            lanes = slice(t * COLS, (t + 1) * COLS)
            q = (made[:, t * WA : t * WA + COLS] + head_ref[0:1, lanes]).astype(BF16)
            keep_heads(q_ref, rows, t, q * jnp.asarray(SCALE, BF16), spare_q)
            keep_keys(made[:, t * WA + COLS : (t + 1) * WA], head_ref, k_ref, v_ref, kt_ref, rows, t, spare_k, spare_v)

    blocks = [dict(rows=slice(i * QB, (i + 1) * QB)) for i in range(x_ref.shape[0] // QB)]
    lax.fori_loop(0, x_ref.shape[0] // QB, norm, 0)
    pltpu.make_async_copy(w_ref, w_ref, sem.at[1]).wait()
    staged(blocks, (product, keep))


DOCS = 48
TERMS = 3


def spare_lanes(ids):
    shape = (ids.shape[0], PAIR)
    at = lax.bitwise_and(lane_of(shape), HD - 1)
    same = at == ids
    ones = jnp.where((at >= DOCS) & (at < DOCS + TERMS), 1.0, 0.0)
    spare_q = jnp.where(same & (at < DOCS), 1.0, 0.0).astype(BF16)
    spare_k = jnp.where(at < DOCS, jnp.where(same, 0.0, NEG), ones).astype(BF16)
    return spare_q, spare_k, ones.astype(BF16)


def three_terms(x):
    high = x.astype(BF16)
    rest = x - high.astype(F32)
    middle = rest.astype(BF16)
    return high, middle, (rest - middle.astype(F32)).astype(BF16)


def keep_heads(ref, rows, pair, value, spare):
    lane = lane_of(value.shape)
    for h in range(2):
        at = (2 * pair + h) * PAIR
        mine = (lane < HD) if h == 0 else (lane >= HD)
        ref[rows, at : at + PAIR] = jnp.where(mine, value, spare)


def first_norm(x, vectors, me, nt_ref, rows):
    xhat, _ = normalize(x.astype(F32))
    n1 = xhat * vectors[0:1] + vectors[1:2]
    turned = jnp.transpose(n1).astype(BF16)
    for i in range(8):
        slot = lax.bitwise_xor(me, i)
        nt_ref[rows_of(slot * ROWS, ROWS, ROWS), rows] = turned[ROWS * i : ROWS * (i + 1)]
    nt_ref[D:, rows] = jnp.ones((TALL - D, x.shape[0]), BF16)
    return n1.astype(BF16)


def keep_keys(made, head_ref, k_ref, v_ref, kt_ref, rows, t, spare_k, spare_v):
    lanes = slice(t * COLS, (t + 1) * COLS)
    k = made[:, 0:COLS]
    keep_heads(k_ref, rows, t, k.astype(BF16), spare_k)
    kt_ref[lanes, rows] = jnp.transpose(k).astype(BF16)
    keep_heads(v_ref, rows, t, (made[:, COLS:] + head_ref[1:2, lanes]).astype(BF16), spare_v)


def project(x, id_col, pieces, tokens_all):
    own = x.shape[0]
    shapes = (
        jax.ShapeDtypeStruct((own, 2 * D), BF16),
        jax.ShapeDtypeStruct((own, 2 * D), BF16),
        jax.ShapeDtypeStruct((own, 2 * D), BF16),
        jax.ShapeDtypeStruct((D, own), BF16),
        jax.ShapeDtypeStruct((TALL, own), BF16),
        jax.ShapeDtypeStruct((D, 4 * WA), BF16),
        jax.ShapeDtypeStruct((EXTRA, D), F32),
        jax.ShapeDtypeStruct((8, 4 * FFC), F32),
        jax.ShapeDtypeStruct((8, 128), F32),
        jax.ShapeDtypeStruct((EXTRA, D), F32),
    )
    return pl.pallas_call(
        functools.partial(project_kernel, float(tokens_all)),
        out_shape=shapes,
        in_specs=[VMEM, VMEM] + [FAR] * 9,
        out_specs=[VMEM] * len(shapes),
        scratch_shapes=[pltpu.VMEM((32, EXTRA, WA), BF16), pltpu.VMEM((own, D), BF16), pltpu.SemaphoreType.DMA((2,))],
        compiler_params=params(6),
        cost_estimate=SMALL,
        name="project",
    )(x, id_col, *pieces)


def project_halo_kernel(x_ref, idc_ref, w_ref, vec_ref, head_ref, k_ref, v_ref, kt_ref, nt_ref):
    me = lax.axis_index("fsdp")

    def norm(one):
        one["n1"] = first_norm(x_ref[one["rows"], :], vec_ref[...], me, nt_ref, one["rows"])

    def product(one):
        one["made"] = [dot(one["n1"], w_ref[:, t * WA + COLS : (t + 1) * WA]) for t in range(4)]

    def keep(one):
        rows = one["rows"]
        _, spare_k, spare_v = spare_lanes(idc_ref[rows, :])
        for t, made in enumerate(one.pop("made")):
            keep_keys(made, head_ref, k_ref, v_ref, kt_ref, rows, t, spare_k, spare_v)

    staged([dict(rows=slice(i * QB, (i + 1) * QB)) for i in range(HALO // QB)], (norm, product, keep))


def project_halo(x, id_col, w, vec, head):
    shape = jax.ShapeDtypeStruct((HALO, 2 * D), BF16)
    turned, tall = (jax.ShapeDtypeStruct((size, HALO), BF16) for size in (D, TALL))
    return pl.pallas_call(
        project_halo_kernel,
        out_shape=(shape, shape, turned, tall),
        compiler_params=params(6),
        cost_estimate=SMALL,
        name="project_halo",
    )(x, id_col, w, vec, head)


QB = 256


def causal(by_rows):
    key = lax.broadcasted_iota(jnp.int32, (QB, QB), 1 if by_rows else 0)
    query = lax.broadcasted_iota(jnp.int32, (QB, QB), 0 if by_rows else 1)
    return jnp.where(key <= query, 0.0, NEG)


def staged(units, stages, lag=1, beside=()):
    steps = len(units) + lag * (len(stages) - 1)
    for n in range(steps):
        for depth, stage in enumerate(stages):
            if 0 <= n - lag * depth < len(units):
                stage(units[n - lag * depth])
        if n < len(beside):
            beside[n]()
    for extra in beside[steps:]:
        extra()


def attend_heads(heads, bias_ref):
    lane = lane_of((QB, PAIR))
    at = lax.bitwise_and(lane, HD - 1)

    def score(one):
        q = one["q"][one["rows"], one["lanes"]]
        one["s"] = []
        for keys, _, where, last in one["parts"]:
            s = dot_t(q, keys[where, one["lanes"]])
            one["s"].append(s + bias_ref[...] if last else s)

    def soften(one):
        one["top"] = functools.reduce(jnp.maximum, [jnp.max(s, axis=-1, keepdims=True) for s in one["s"]])
        one["p"] = [jnp.exp(s - one["top"]).astype(BF16) for s in one.pop("s")]

    def attend(one):
        total = None
        for p, (_, values, where, _) in zip(one.pop("p"), one["parts"]):
            part = dot(p, values[where, one["lanes"]])
            total = part if total is None else total + part
        first = (HD if one["h"] == 0 else 0) + DOCS
        weight = total[:, first : first + 1]
        mine = (lane < HD) if one["h"] == 0 else (lane >= HD)
        q = one["q"][one["rows"], one["lanes"]]
        for i, term in enumerate(three_terms(-(one["top"] + jnp.log(weight)))):
            q = jnp.where((at == DOCS + i) & ~mine, jnp.broadcast_to(term, q.shape), q)
        one["take"](one["h"], (total / weight).astype(BF16), q)

    staged(heads, (score, soften, attend), 2)


def keep_attended(o_ref, qa_ref, rows, pair):
    lane = lane_of((QB, PAIR))

    def take(h, o, q):
        lanes = rows_of(pair * PAIR, PAIR)
        qa_ref[rows, head_lanes(pair, h)] = q
        o_ref[rows, lanes] = o if h == 0 else jnp.where(lane < HD, o_ref[rows, lanes], o)

    return take


def head_lanes(pair, h):
    return rows_of((2 * pair + h) * PAIR, PAIR)


def each_two(count, act):
    def step(i, carry):
        act((2 * i, 2 * i + 1))
        return carry

    lax.fori_loop(0, count, step, 0)


def attend_far_kernel(q_ref, k_ref, v_ref, o_ref, qa_ref, bias_ref):
    bias_ref[...] = causal(True)
    parts = ((k_ref, v_ref, slice(0, HALO), False), (k_ref, v_ref, slice(HALO, HALO + QB), True))

    def two(pairs):
        heads = []
        for pair in pairs:
            take = keep_attended(o_ref, qa_ref, slice(0, QB), pair)
            for h in range(2):
                heads.append(
                    dict(q=q_ref, rows=slice(HALO, HALO + QB), lanes=head_lanes(pair, h), h=h, parts=parts, take=take)
                )
        attend_heads(heads, bias_ref)

    each_two(2, two)


def attend_far(q, k, v):
    return pl.pallas_call(
        attend_far_kernel,
        out_shape=(jax.ShapeDtypeStruct((QB, D), BF16), jax.ShapeDtypeStruct((QB, 2 * D), BF16)),
        in_specs=[VMEM] * 3,
        out_specs=[VMEM] * 2,
        scratch_shapes=[pltpu.VMEM((QB, QB), F32)],
        compiler_params=params(8),
        cost_estimate=SMALL,
        name="attend_far",
    )(q, k, v)


def near_parts(halo, own):
    return (
        ((*halo, slice(0, HALO), False), (*own, slice(0, QB), True)),
        ((*halo, slice(QB, HALO), False), (*own, slice(0, QB), False), (*own, slice(QB, HALO), True)),
    )


def attend_near_kernel(q_ref, kh_ref, ko_ref, vh_ref, vo_ref, o_ref, qa_ref, bias_ref):
    bias_ref[...] = causal(True)

    def two(pairs):
        heads = []
        for pair in pairs:
            for i, parts in enumerate(near_parts((kh_ref, vh_ref), (ko_ref, vo_ref))):
                rows = slice(i * QB, (i + 1) * QB)
                take = keep_attended(o_ref, qa_ref, rows, pair)
                for h in range(2):
                    heads.append(dict(q=q_ref, rows=rows, lanes=head_lanes(pair, h), h=h, parts=parts, take=take))
        attend_heads(heads, bias_ref)

    each_two(2, two)


def attend_near(q, k_halo, k, v_halo, v):
    return pl.pallas_call(
        attend_near_kernel,
        out_shape=(jax.ShapeDtypeStruct((HALO, D), BF16), jax.ShapeDtypeStruct((HALO, 2 * D), BF16)),
        in_specs=[VMEM] * 5,
        out_specs=[VMEM] * 2,
        scratch_shapes=[pltpu.VMEM((QB, QB), F32)],
        compiler_params=params(8),
        cost_estimate=SMALL,
        name="attend_near",
    )(q, k_halo, k, v_halo, v)


PIECES_F = ((0, ALL), (2, ALL), (4, ALL), (6, ALL[0:2]), (6, ALL[2:4]))


def central_kernel(
    rb, x_ref, oa_ref, oc_ref, teacher_ref, cot_ref, mask_ref, vec_ref, bup_ref, scale_ref,
    *rest
):
    pieces = rest[:10]
    (
    out_ref, gh_ref, ga_ref, theirs_ref, mine_ref, small_ref, gbup_ref,
    wo_ref, wup_ref, wdn_ref, slope_ref, hid_ref, gpre_ref, n2t_ref, gmlpt_ref, gattnt_ref, place_ref, o_ref,
    h1_ref, xhat_ref, n2_ref, gmlp_ref, sem
    ) = rest[10:]
    me, place = lax.axis_index("fsdp"), lax.axis_index("tp")
    own, ff = x_ref.shape[0], 4 * FFC
    parts = ((wo_ref, 0, COLS), (wup_ref, COLS, FFC), (wdn_ref, COLS + FFC, FFC))
    for n, (dst, start, size) in enumerate(parts):
        for j, ref in enumerate(pieces):
            mask, steps = PIECES_F[j % 5]
            owner = lax.bitwise_xor(me, mask + j // 5)
            for i, s in enumerate(steps):
                tp = lax.bitwise_and(place - s + 4, 3)
                pltpu.make_async_copy(
                    ref.at[i, :, pl.ds(start, size)],
                    dst.at[rows_of(owner * ROWS, ROWS, ROWS), rows_of(tp * size, size)],
                    sem.at[n],
                ).start()
    small_ref[...] = jnp.zeros_like(small_ref)
    head_of = lax.broadcasted_iota(jnp.int32, (D, 128), 0) // HD
    pick = (head_of == lax.broadcasted_iota(jnp.int32, (D, 128), 1)).astype(BF16)
    out_bias, gain, offset, down_bias = (vec_ref[j : j + 1, :] for j in range(2, 6))
    n2t_ref[D:, :] = jnp.ones((TALL - D, own), BF16)
    source = lax.broadcasted_iota(jnp.int32, (TERMS * 128, H * PAIR), 0)
    target = lax.broadcasted_iota(jnp.int32, (TERMS * 128, H * PAIR), 1)
    head, term = target // PAIR, lax.bitwise_and(target, HD - 1) - DOCS
    outside = (lax.bitwise_and(target, PAIR - 1) >= HD) == (lax.bitwise_and(head, 1) == 0)
    placed = outside & (lax.bitwise_and(source, 127) == head) & (source // 128 == term)
    place_ref[...] = jnp.where(placed, 1.0, 0.0).astype(BF16)
    o_ref[0:HALO, :] = oa_ref[...]
    o_ref[HALO:, :] = oc_ref[...]

    def turn(dst, rows, value):
        turned = jnp.transpose(value).astype(BF16)
        for i in range(8):
            slot = lax.bitwise_xor(me, i)
            dst[rows_of(slot * ROWS, ROWS, ROWS), rows] = turned[ROWS * i : ROWS * (i + 1)]

    def arrived(n):
        pltpu.make_async_copy(parts[n][0], parts[n][0], sem.at[n]).wait()

    blocks = [dict(rows=slice(i * rb, (i + 1) * rb)) for i in range(own // rb)]

    def attention_out(one):
        one["attn"] = dot_t(o_ref[one["rows"], :], wo_ref[...])

    def second_norm(one):
        rows = one["rows"]
        h1 = x_ref[rows, :].astype(F32) + one.pop("attn") + out_bias
        xhat, rstd = normalize(h1)
        n2 = xhat * gain + offset
        h1_ref[rows, :] = h1
        xhat_ref[rows, :] = xhat
        one["rstd"] = rstd
        n2_ref[rows, :] = n2.astype(BF16)
        turn(n2t_ref, rows, n2)

    arrived(0)
    staged(blocks, (attention_out, second_norm))
    arrived(1)

    def by_columns(stages):
        def step(c, carry):
            cols = rows_of(c * FFC, FFC)
            staged([dict(rows=one["rows"], cols=cols) for one in blocks], stages)
            return carry

        lax.fori_loop(0, 4, step, 0)

    def up(one):
        one["pre"] = dot(n2_ref[one["rows"], :], wup_ref[:, one["cols"]]) + bup_ref[0:1, one["cols"]]

    def gelu(one):
        pre = one.pop("pre")
        s = jax.nn.sigmoid(1.702 * pre)
        value = pre * s
        hid_ref[one["rows"], one["cols"]] = value.astype(BF16)
        slope_ref[one["rows"], one["cols"]] = s * (1.702 * (pre - value) + 1.0)

    by_columns((up, gelu))
    arrived(2)

    def down(one):
        one["mlp"] = dot_t(hid_ref[one["rows"], :], wdn_ref[...])

    def output(one):
        rows = one["rows"]
        out = h1_ref[rows, :] + one.pop("mlp") + down_bias
        out_ref[rows, :] = out.astype(BF16)
        diff = (out - teacher_ref[rows, :].astype(F32)) * mask_ref[rows, :]
        g_out = cot_ref[rows, :].astype(F32) + scale_ref[0:1, 0:1] * diff
        gh_ref[rows, :] = g_out
        small_ref[0:8, :] += fold(g_out)
        small_ref[8:16, :] += fold(diff * diff)
        gmlp_ref[rows, :] = g_out.astype(BF16)
        turn(gmlpt_ref, rows, g_out)

    staged(blocks, (down, output))

    def hidden(one):
        one["g"] = dot(gmlp_ref[one["rows"], :], wdn_ref[:, one["cols"]])

    def slope(one):
        g_pre = one.pop("g") * slope_ref[one["rows"], one["cols"]]
        gpre_ref[one["rows"], one["cols"]] = g_pre.astype(BF16)

    by_columns((hidden, slope))

    def into_norm(one):
        one["g"] = dot_t(gpre_ref[one["rows"], :], wup_ref[...])

    def pull_norm(one):
        rows, g_n2, xhat = one["rows"], one.pop("g"), xhat_ref[one["rows"], :]
        small_ref[16:24, :] += fold(g_n2 * xhat)
        small_ref[24:32, :] += fold(g_n2)
        g_h1 = gh_ref[rows, :] + norm_pull(g_n2, gain, xhat, one.pop("rstd"))
        gh_ref[rows, :] = g_h1
        small_ref[32:40, :] += fold(g_h1)
        turn(gattnt_ref, rows, g_h1)
        one["go"] = dot(g_h1.astype(BF16), wo_ref[...]).astype(BF16)

    def pull_out(one):
        rows, g_o = one["rows"], one.pop("go")
        product = g_o.astype(F32) * o_ref[rows, :].astype(F32)
        high = product.astype(BF16)
        low = (product - high.astype(F32)).astype(BF16)
        terms = jnp.concatenate(three_terms(-(dot(high, pick) + dot(low, pick))), axis=1)
        spare = dot(terms, place_ref[...]).astype(BF16)
        lane = lane_of((rb, PAIR))
        for n in range(H):
            mine = (lane < HD) if n % 2 == 0 else (lane >= HD)
            pair = g_o[:, (n // 2) * PAIR : (n // 2 + 1) * PAIR]
            ga_ref[rows, n * PAIR : (n + 1) * PAIR] = jnp.where(mine, pair, spare[:, n * PAIR : (n + 1) * PAIR])

    def keep(grad, s, start, size):
        low = grad.astype(BF16)
        for r in range(8):
            dst = theirs_ref if r % 2 else mine_ref
            dst[r // 2, s, :, start : start + size] = low[ROWS * r : ROWS * (r + 1)]

    def their(s, size):
        return rows_of(lax.bitwise_and(place + s, 3) * size, size)

    def by_down(s):
        keep(dot(gmlpt_ref[...], hid_ref[:, their(s, FFC)]), s, COLS + FFC, FFC)

    staged(
        blocks, (into_norm, pull_norm, pull_out), beside=[functools.partial(by_down, s) for s in range(4)]
    )
    for s in range(4):
        total = dot(n2t_ref[...], gpre_ref[:, their(s, FFC)])
        gbup_ref[:, their(s, FFC)] = total[D : D + 8]
        keep(total, s, COLS, FFC)
        keep(dot(gattnt_ref[...], o_ref[:, their(s, COLS)]), s, 0, COLS)


def central(x, o_near, o_far, teacher, cot, mask, vec, bup, scale, pieces):
    own = x.shape[0]
    rb = 256
    shapes = (
        jax.ShapeDtypeStruct((own, D), BF16),
        jax.ShapeDtypeStruct((own, D), F32),
        jax.ShapeDtypeStruct((own, 2 * D), BF16),
        jax.ShapeDtypeStruct((4, 4, ROWS, WF), BF16),
        jax.ShapeDtypeStruct((4, 4, ROWS, WF), BF16),
        jax.ShapeDtypeStruct((40, D), F32),
        jax.ShapeDtypeStruct((8, 4 * FFC), F32),
    )
    return pl.pallas_call(
        functools.partial(central_kernel, rb),
        out_shape=shapes,
        in_specs=[VMEM] * 9 + [FAR] * 10,
        out_specs=[VMEM] * len(shapes),
        scratch_shapes=[
            pltpu.VMEM((D, D), BF16),
            pltpu.VMEM((D, 4 * FFC), BF16),
            pltpu.VMEM((D, 4 * FFC), BF16),
            pltpu.VMEM((own, 4 * FFC), F32),
            pltpu.VMEM((own, 4 * FFC), BF16),
            pltpu.VMEM((own, 4 * FFC), BF16),
            pltpu.VMEM((TALL, own), BF16),
            pltpu.VMEM((D, own), BF16),
            pltpu.VMEM((D, own), BF16),
            pltpu.VMEM((TERMS * 128, H * PAIR), BF16),
            pltpu.VMEM((own, D), BF16),
            pltpu.VMEM((own, D), F32),
            pltpu.VMEM((own, D), F32),
            pltpu.VMEM((own, D), BF16),
            pltpu.VMEM((own, D), BF16),
            pltpu.SemaphoreType.DMA((3,)),
        ],
        compiler_params=params(30),
        cost_estimate=SMALL,
        name="central",
    )(x, o_near, o_far, teacher, cot, mask, vec, bup, scale, *pieces)


def pull_units(units, bias_ref):
    lane = lane_of((QB, PAIR))

    def mask(x, h):
        return jnp.where((lane < HD) if h == 0 else (lane >= HD), x, jnp.zeros_like(x))

    def score(one):
        keys, values, _, where, _ = one["part"]
        one["s"] = dot_t(keys[where, one["lanes"]], one["q"][one["rows"], one["qlanes"]])
        one["d"] = dot_t(values[where, one["lanes"]], one["g"][one["grows"], one["lanes"]])

    def soften(one):
        s = one.pop("s")
        p = jnp.exp(s + bias_ref[...] if one["part"][4] else s)
        one["p"], one["ds"] = p.astype(BF16), (p * one.pop("d")).astype(BF16)

    def finish(one):
        _, _, keys_t, where, last = one["part"]
        h, sums = one["h"], one["sums"]
        part = dot(keys_t[one["tlanes"], where], one["ds"])
        sums[h] = part if h not in sums else sums[h] + part
        if h == 0:
            sums["before"] = one
            return
        two = (sums.pop("before"), one)
        q = jnp.concatenate([mask(u["q"][u["rows"], u["qlanes"]], u["h"]) for u in two], axis=0)
        g = jnp.concatenate([mask(u["g"][u["grows"], u["lanes"]], u["h"]) for u in two], axis=0)
        dk = dot(jnp.concatenate([u.pop("ds") for u in two], axis=1), q)
        dv = dot(jnp.concatenate([u.pop("p") for u in two], axis=1), g)
        one["take"](dk, dv)
        if last:
            both = jnp.concatenate([sums[0], sums[1]], axis=0)
            one["take_q"]((jnp.transpose(both) * SCALE).astype(BF16))

    staged(units, (score, soften, finish), 2)


def block_units(q_ref, rows, q_pair, g_ref, grows, pair, parts, takes, take_q):
    sums, units = {}, []
    for part, take in zip(parts, takes):
        for h in range(2):
            units.append(
                dict(
                    q=q_ref, rows=rows, qlanes=head_lanes(q_pair, h), g=g_ref, grows=grows, lanes=head_lanes(pair, h), h=h,
                    part=part, tlanes=rows_of((2 * pair + h) * HD, HD, HD), take=take, take_q=take_q, sums=sums,
                )
            )
    return units


def pull_near_kernel(base, q_ref, g_ref, kh_ref, ko_ref, vh_ref, vo_ref, kth_ref, kto_ref, gh_ref, gq_ref, part_ref, bias_ref, late_ref):
    bias_ref[...] = causal(False)
    halo, own = (kh_ref, vh_ref, kth_ref), (ko_ref, vo_ref, kto_ref)

    def one(pair, carry):
        lanes = (rows_of(2 * pair * PAIR, PAIR), rows_of((2 * pair + 1) * PAIR, PAIR))

        def halo_first(*grads):
            for at, d in zip(lanes, grads):
                gh_ref[0:QB, at] = d[0:QB].astype(BF16)
                late_ref[:, at] = d[QB:]

        def halo_second(*grads):
            for at, d in zip(lanes, grads):
                gh_ref[QB:, at] = (late_ref[:, at] + d).astype(BF16)

        def own_first(*grads):
            for at, d in zip(lanes, grads):
                part_ref[0:QB, at] = d

        def own_more(*grads):
            for at, d in zip(lanes, grads):
                part_ref[0:QB, at] += d

        def own_last(*grads):
            for at, d in zip(lanes, grads):
                part_ref[QB:, at] = d

        units, takes = [], ((halo_first, own_first), (halo_second, own_more, own_last))
        for i, parts in enumerate(near_parts(halo, own)):
            rows = slice(i * QB, (i + 1) * QB)

            def take_q(dq, rows=rows):
                gq_ref[rows, rows_of(pair * PAIR, PAIR)] = dq

            units += block_units(q_ref, rows, base + pair, g_ref, rows, base + pair, parts, takes[i], take_q)
        pull_units(units, bias_ref)
        return carry

    lax.fori_loop(0, 2, one, 0)


def pull_near(base, qa, ga, k_halo, k, v_halo, v, kt_halo, kt):
    return pl.pallas_call(
        functools.partial(pull_near_kernel, base),
        out_shape=(
            jax.ShapeDtypeStruct((HALO, D), BF16),
            jax.ShapeDtypeStruct((HALO, D // 2), BF16),
            jax.ShapeDtypeStruct((HALO, D), F32),
        ),
        in_specs=[VMEM] * 8,
        out_specs=[VMEM] * 3,
        scratch_shapes=[pltpu.VMEM((QB, QB), F32), pltpu.VMEM((QB, D), F32)],
        compiler_params=params(10),
        cost_estimate=SMALL,
        name="pull_near",
    )(qa, ga, k_halo, k, v_halo, v, kt_halo, kt)


def pull_far_kernel(q_ref, go_ref, k_ref, v_ref, kt_ref, qa_ref, qb_ref, pa_ref, pb_ref, g_ref, bias_ref):
    bias_ref[...] = causal(False)
    refs = (k_ref, v_ref, kt_ref)
    parts = ((*refs, slice(0, HALO), False), (*refs, slice(HALO, HALO + QB), True))

    def two(inside, carry):
        units = []
        for half, near_q, near_part in ((0, qa_ref, pa_ref), (1, qb_ref, pb_ref)):
            pair = 2 * half + inside
            lanes = tuple(rows_of(pair * WA + n * COLS, COLS) for n in range(3))
            within = tuple(rows_of((2 * inside + n) * PAIR, PAIR) for n in range(2))
            g_ref[0:HALO, lanes[0]] = near_q[:, rows_of(inside * PAIR, PAIR)]

            def older(*grads, lanes=lanes, within=within, near_part=near_part):
                for n, d in enumerate(grads):
                    g_ref[0:HALO, lanes[n + 1]] = (near_part[:, within[n]] + d).astype(BF16)

            def newest(*grads, lanes=lanes):
                for n, d in enumerate(grads):
                    g_ref[HALO:, lanes[n + 1]] = d.astype(BF16)

            def take_q(dq, lanes=lanes):
                g_ref[HALO:, lanes[0]] = dq

            own = slice(HALO, HALO + QB)
            units += block_units(q_ref, slice(0, QB), pair, go_ref, own, pair, parts, (older, newest), take_q)
        pull_units(units, bias_ref)
        return carry

    lax.fori_loop(0, 2, two, 0)


def pull_far(qa, ga, k, v, kt, gq_near, gq_more, part_near, part_more):
    own = k.shape[0]
    return pl.pallas_call(
        pull_far_kernel,
        out_shape=jax.ShapeDtypeStruct((own, 4 * WA), BF16),
        in_specs=[VMEM] * 9,
        out_specs=VMEM,
        scratch_shapes=[pltpu.VMEM((QB, QB), F32)],
        compiler_params=params(10),
        cost_estimate=SMALL,
        name="pull_far",
    )(qa, ga, k, v, kt, gq_near, gq_more, part_near, part_more)


def norm_sums(small_ref, x, g_n1):
    xhat, _ = normalize(x.astype(F32))
    small_ref[0:8, :] += fold(g_n1 * xhat)
    small_ref[8:16, :] += fold(g_n1)


def halo_back_kernel(ga_ref, gb_ref, w_ref, x_ref, out_ref, small_ref):
    small_ref[...] = jnp.zeros_like(small_ref)

    def pull(one):
        total = None
        for t in range(4):
            g = (ga_ref, gb_ref)[t // 2][one["rows"], (t % 2) * 2 * COLS : (t % 2 + 1) * 2 * COLS]
            part = dot_t(g, w_ref[:, t * WA + COLS : (t + 1) * WA])
            total = part if total is None else total + part
        one["g"] = total

    def norms(one):
        g_n1 = one.pop("g")
        out_ref[one["rows"], :] = g_n1.astype(BF16)
        norm_sums(small_ref, x_ref[one["rows"], :], g_n1)

    staged([dict(rows=slice(i * QB, (i + 1) * QB)) for i in range(HALO // QB)], (pull, norms))


def halo_back(g_near, g_more, w, halo):
    return pl.pallas_call(
        halo_back_kernel,
        out_shape=(jax.ShapeDtypeStruct((HALO, D), BF16), jax.ShapeDtypeStruct((16, D), F32)),
        compiler_params=params(6),
        cost_estimate=SMALL,
        name="halo_back",
    )(g_near, g_more, w, halo)


def own_back_kernel(
    x_ref, ga_ref, gb_ref, g_ref, nth_ref, nto_ref, w_ref, small_halo, small_two, gbup_ref, scale_ref,
    gn_ref, theirs_ref, mine_ref, small_ref, gh_ref
):
    me, place = lax.axis_index("fsdp"), lax.axis_index("tp")
    own = x_ref.shape[0]
    small_ref[...] = small_halo[...]
    gh_ref[:, 0:D] = ga_ref[...]
    gh_ref[:, D:] = gb_ref[...]

    def pull(one):
        one["g"] = dot_t(g_ref[one["rows"], :], w_ref[...])

    def norms(one):
        g_n1 = one.pop("g")
        gn_ref[one["rows"], :] = g_n1
        norm_sums(small_ref, x_ref[one["rows"], :], g_n1)

    staged([dict(rows=slice(i * QB, (i + 1) * QB)) for i in range(own // QB)], (pull, norms))
    sums = lambda ref, j: jnp.sum(ref[8 * j : 8 * j + 8, :], axis=0, keepdims=True)
    loss = jnp.sum(sums(small_two, 1), axis=1, keepdims=True) * scale_ref[4:5, 0:1]
    vectors = jnp.concatenate(
        [sums(small_ref, 0), sums(small_ref, 1), sums(small_two, 4), sums(small_two, 2), sums(small_two, 3),
         sums(small_two, 0), jnp.zeros((2, D), F32)],
        axis=0,
    )
    high = loss.astype(BF16).astype(F32)
    row, lane = lax.broadcasted_iota(jnp.int32, (EXTRA, 128), 0), lane_of((EXTRA, 128))

    def grads(s, carry):
        tp = lax.bitwise_and(place + s, 3)
        g_own = g_ref[:, rows_of(tp * WA, WA)]
        g_halo = gh_ref[:, rows_of(tp * 2 * COLS, 2 * COLS)]
        total = dot(nto_ref[...], g_own)
        more = dot(nth_ref[...], g_halo)
        total = jnp.concatenate([total[:, 0:COLS], total[:, COLS:] + more], axis=1)
        low, sums = total[0:D].astype(BF16), total[D : D + 1]
        ups = gbup_ref[0:1, rows_of(tp * FFC, FFC)]
        mids = jnp.concatenate(
            [sums[:, 0:COLS], sums[:, 2 * COLS :]]
            + [ups[:, 128 * j : 128 * j + 128] for j in range(4)]
            + [jnp.zeros((2, 128), F32)],
            axis=0,
        ).astype(BF16)
        for r in range(8):
            dst = theirs_ref if r % 2 else mine_ref
            dst[r // 2, s, 0:ROWS, :] = low[ROWS * r : ROWS * (r + 1)]
            dst[r // 2, s, ROWS:, 128:256] = mids
        return carry

    lax.fori_loop(0, 4, grads, 0)
    for r in range(8):
        owner = lax.bitwise_xor(me, r)
        block = pltpu.roll(vectors, lax.rem(D - owner * ROWS, D), 1)[:, 0:128]
        block = jnp.where((row == 6) & (lane == 0), high, block)
        block = jnp.where((row == 6) & (lane == 1), loss - high, block).astype(BF16)
        dst = theirs_ref if r % 2 else mine_ref
        for s in range(4):
            dst[r // 2, s, ROWS:, 0:128] = block
            dst[r // 2, s, ROWS:, 256:384] = jnp.zeros((EXTRA, 128), BF16)


def own_back(x, g_near, g_more, g_own, nt_halo, nt, w, small_halo, small_two, gbup, scale):
    own = x.shape[0]
    send = jax.ShapeDtypeStruct((4, 4, ROWS + EXTRA, WA), BF16)
    return pl.pallas_call(
        own_back_kernel,
        out_shape=(jax.ShapeDtypeStruct((own, D), F32), send, send),
        scratch_shapes=[pltpu.VMEM((16, D), F32), pltpu.VMEM((HALO, 2 * D), BF16)],
        compiler_params=params(10),
        cost_estimate=SMALL,
        name="own_back",
    )(x, g_near, g_more, g_own, nt_halo, nt, w, small_halo, small_two, gbup, scale)


def close_kernel(x_ref, gn_ref, back_ref, gh_ref, vec_ref, out_ref):
    own = x_ref.shape[0]

    def block(at, extra):
        rows = rows_of(at, 128)
        xhat, rstd = normalize(x_ref[rows, :].astype(F32))
        g_n1 = gn_ref[rows, :] + extra
        out_ref[rows, :] = gh_ref[rows, :] + norm_pull(g_n1, vec_ref[0:1, :], xhat, rstd)

    def first(i, carry):
        block(i * 128, 0.0)
        return carry

    def second(i, carry):
        block(own - HALO + i * 128, back_ref[rows_of(i * 128, 128), :].astype(F32))
        return carry

    lax.fori_loop(0, (own - HALO) // 128, first, 0)
    lax.fori_loop(0, HALO // 128, second, 0)


def close(x, g_n1, back, g_h1, vec):
    return pl.pallas_call(
        close_kernel,
        out_shape=jax.ShapeDtypeStruct(x.shape, F32),
        compiler_params=params(8),
        cost_estimate=SMALL,
        name="close",
    )(x, g_n1, back, g_h1, vec)


def unpack_f_kernel(k_ref, r1, r2, r3, wo_ref, wup_ref, wdn_ref):
    total = (k_ref[0].astype(F32) + r1[...].astype(F32)) + (r2[...].astype(F32) + r3[...].astype(F32))
    wo_ref[...] = total[:, 0:COLS]
    wup_ref[...] = total[:, COLS : COLS + FFC]
    wdn_ref[...] = total[:, COLS + FFC :]


def unpack_f(k, r1, r2, r3):
    return pl.pallas_call(
        unpack_f_kernel,
        out_shape=(
            jax.ShapeDtypeStruct((ROWS, COLS), F32),
            jax.ShapeDtypeStruct((ROWS, FFC), F32),
            jax.ShapeDtypeStruct((ROWS, FFC), F32),
        ),
        compiler_params=params(6),
        name="unpack_f",
    )(k, r1, r2, r3)


def unpack_a_kernel(k_ref, r1, r2, r3, wq_ref, wk_ref, wv_ref, bq_ref, bv_ref, bup_ref, loss_ref, *vec_refs):
    me = lax.axis_index("fsdp")
    total = (k_ref[0].astype(F32) + r1[...].astype(F32)) + (r2[...].astype(F32) + r3[...].astype(F32))
    wq_ref[...] = total[0:ROWS, 0:COLS]
    wk_ref[...] = total[0:ROWS, COLS : 2 * COLS]
    wv_ref[...] = total[0:ROWS, 2 * COLS :]
    for j, ref in enumerate(vec_refs):
        ref[...] = total[ROWS + j, 0:ROWS]
    loss_ref[...] = total[ROWS + 6 : ROWS + 7, 0:1] + total[ROWS + 6 : ROWS + 7, 1:2]
    mids = pltpu.roll(total[ROWS:, 128:256], lax.rem(128 - me * 8, 128), 1)
    for i in range(2):
        bq_ref[i : i + 1, :] = mids[0:1, i * HD : i * HD + 8]
        bv_ref[i : i + 1, :] = mids[1:2, i * HD : i * HD + 8]
    for i in range(8):
        at = (i % 2) * HD
        bup_ref[i : i + 1, :] = mids[2 + i // 2 : 3 + i // 2, at : at + 8]


def unpack_a(k, r1, r2, r3):
    small = jax.ShapeDtypeStruct((ROWS, COLS), F32)
    return pl.pallas_call(
        unpack_a_kernel,
        out_shape=(
            small,
            small,
            small,
            jax.ShapeDtypeStruct((2, 8), F32),
            jax.ShapeDtypeStruct((2, 8), F32),
            jax.ShapeDtypeStruct((8, 8), F32),
            jax.ShapeDtypeStruct((1, 1), F32),
            *[jax.ShapeDtypeStruct((ROWS,), F32)] * 6,
        ),
        compiler_params=params(6),
        name="unpack_a",
    )(k, r1, r2, r3)


def to_mask(x, mask):
    return lax.ppermute(x, "fsdp", [(i, i ^ mask) for i in range(8)])


def to_step(x, step):
    return lax.ppermute(x, "tp", [(i, (i + step) % 4) for i in range(4)])


def add(a, b):
    return (a.astype(F32) + b.astype(F32)).astype(BF16)


def after(values, others):
    return lax.optimization_barrier((values, others))[0]


def local_fast(
    layer_input, segment_ids, valid_mask, teacher, cotangent, ln1_gain, ln1_bias, w_q, w_k, w_v, b_q, b_v,
    w_o, b_o, ln2_gain, ln2_bias, w_up, b_up, w_down, b_down
):
    place = lax.axis_index("tp")
    own = layer_input.shape[0]
    tokens_all = own * lax.axis_size("fsdp") * lax.axis_size("tp")

    shard_a, shard_f = pack_weights(
        (w_q, w_k, w_v, w_o.T, w_up, w_down.T, ln1_gain, ln1_bias, b_o, ln2_gain, ln2_bias, b_down, b_q, b_v, b_up,
         valid_mask)
    )
    steps_a = [shard_a] + [to_step(shard_a, s) for s in (1, 2, 3)]
    line_a = jnp.stack(steps_a)
    steps_f = [shard_f] + [to_step(shard_f, s) for s in (1, 2, 3)]
    near_a = [to_mask(line_a, m) for m in (2, 4, 6)]
    last_rows = layer_input[own - HALO :]
    halves_a, last_rows = after(([jnp.stack(steps_a[0:2]), jnp.stack(steps_a[2:4])], last_rows), steps_f)
    over_a = [to_mask(a, 1) for a in halves_a]
    line_f = jnp.stack(after(steps_f, (over_a, near_a)))
    over_f = to_mask(line_f, 1)
    pieces_a = [line_a] + near_a + over_a + [to_mask(a, 1) for a in near_a]
    halo = lax.ppermute(last_rows, "tp", [(i, i + 1) for i in range(3)])
    f_x, f_y = to_mask(line_f, 2), to_mask(line_f, 4)

    ids = segment_ids + 16 * jnp.arange(segment_ids.shape[0], dtype=jnp.int32)[:, None]
    ids = jnp.concatenate([jnp.full((HALO,), -1, jnp.int32), ids.reshape(-1)])
    id_col = lax.dynamic_slice_in_dim(ids, place * own, HALO + own)[:, None]
    mask = valid_mask.astype(F32)[:, None]

    q, k, v, kt, nt, w_all, vec, bup, scale, head = project(after(layer_input, over_f), id_col, pieces_a, tokens_all)
    o_far, qa_far = attend_far(q, k, v)
    f_x, f_y = after((f_x, f_y), o_far)
    halo = after(halo, o_far)
    f_xy = [to_mask(f_y[0:2], 2), to_mask(f_x[2:4], 4)]
    k_halo, v_halo, kt_halo, nt_halo = project_halo(halo, id_col, w_all, vec, head)
    o_near, qa_near = attend_near(q, k_halo, k, v_halo, v)
    near_f = [f_x, f_y] + after(f_xy, o_near)
    pieces_f = [line_f] + near_f + [over_f] + [to_mask(a, 1) for a in near_f]
    layer_out, g_h1, ga, theirs_f, mine_f, small_two, gbup = central(
        layer_input, o_near, o_far, teacher, cotangent, mask, vec, bup, scale, pieces_f
    )

    def near(base, qa, ga):
        return pull_near(base, qa, ga, k_halo, k, v_halo, v, kt_halo, kt)

    g_near, gq_near, part_near = near(0, qa_near, ga)
    half = add(after(mine_f, g_near), to_mask(theirs_f, 1))
    from_x, from_y = to_mask(half[3, 0:2], 2), to_mask(half[3, 2:4], 4)
    g_more, gq_more, part_more = near(2, after(qa_near, half), ga)
    gn_halo, small_halo = halo_back(g_near, g_more, w_all, halo)
    back = lax.ppermute(gn_halo, "tp", [(i + 1, i) for i in range(3)])
    from_x, from_y = after((from_x, from_y), gn_halo)
    for_x = jnp.concatenate([half[1, 0:2], add(half[1, 2:4], from_y)])
    for_y = jnp.concatenate([add(half[2, 0:2], from_x), half[2, 2:4]])
    got_x, got_y = to_mask(for_x, 2), to_mask(for_y, 4)
    g_own = pull_far(after(qa_far, (for_x, for_y)), ga, k, v, kt, gq_near, gq_more, part_near, part_more)
    gn_own, theirs_a, mine_a = own_back(
        layer_input, g_near, g_more, g_own, nt_halo, nt, w_all, small_halo, small_two, gbup, scale
    )
    got_x, got_y = after((got_x, got_y), gn_own)
    line = (half[0].astype(F32) + got_x.astype(F32) + got_y.astype(F32)).astype(BF16)
    grad_wo, grad_wup, grad_wdn = unpack_f(line, *[to_step(line[s], s) for s in (1, 2, 3)])

    half = add(mine_a, to_mask(after(theirs_a, back), 1))
    from_x, from_y, from_xy = (to_mask(half[m], 2 * m) for m in (1, 2, 3))
    line = (half[0].astype(F32) + from_x.astype(F32) + from_y.astype(F32) + from_xy.astype(F32)).astype(BF16)
    grad_wq, grad_wk, grad_wv, grad_bq, grad_bv, grad_bup, loss, *six = unpack_a(
        line, *[to_step(line[s], s) for s in (1, 2, 3)]
    )
    grad_input = close(layer_input, gn_own, back, g_h1, vec)
    return (
        layer_out, loss.reshape(()), grad_input, six[0], six[1], grad_wq, grad_wk, grad_wv, grad_bq, grad_bv, grad_wo.T, six[2],
        six[3], six[4], grad_wup, grad_bup, grad_wdn.T, six[5]
    )


def solution(mesh):
    tokens = P(("fsdp", "tp"), None)
    rows, crossed, heads = P("fsdp"), P("fsdp", "tp"), P("tp", "fsdp")
    placed = (
        tokens,
        P("fsdp", None),
        P(("fsdp", "tp")),
        tokens,
        tokens,
        rows,
        rows,
        crossed,
        crossed,
        crossed,
        heads,
        heads,
        heads,
        rows,
        rows,
        rows,
        crossed,
        heads,
        heads,
        rows,
    )
    given = (
        tokens,
        P(),
        tokens,
        rows,
        rows,
        crossed,
        crossed,
        crossed,
        heads,
        heads,
        heads,
        rows,
        rows,
        rows,
        crossed,
        heads,
        heads,
        rows,
    )
    sizes = (mesh.shape["fsdp"], mesh.shape["tp"])
    body = local_fast if sizes == (8, 4) else local
    return jax.shard_map(body, mesh=mesh, in_specs=placed, out_specs=given, check_vma=False)
```

```python
import functools

import jax
import jax.numpy as jnp
from jax import lax
from jax.experimental import pallas as pl
from jax.experimental.pallas import tpu as pltpu
from jax.sharding import PartitionSpec as P

D = 512
H = 8
HD = 64
LEN = 1024
HALO = 512
PAIR = 2 * HD
NEG = -1e30
SCALE = HD ** (-0.5)
F32 = jnp.float32
BF16 = jnp.bfloat16
MIB = 1 << 20

CONTRACT_LAST = (((1,), (1,)), ((), ()))


def dot(a, b):
    return jnp.dot(a, b, preferred_element_type=F32)


def dot_t(a, b):
    return lax.dot_general(a, b, CONTRACT_LAST, preferred_element_type=F32)


def normalize(x):
    center = x - jnp.mean(x, axis=-1, keepdims=True)
    rstd = lax.rsqrt(jnp.mean(center * center, axis=-1, keepdims=True) + 1e-05)
    return center * rstd, rstd


def norm_pull(g, gain, xhat, rstd):
    gx = g * gain
    return rstd * (
        gx
        - jnp.mean(gx, axis=-1, keepdims=True)
        - xhat * jnp.mean(gx * xhat, axis=-1, keepdims=True)
    )


def fold(x):
    return jnp.sum(x.reshape(x.shape[0] // 8, 8, x.shape[1]), axis=0)


def rows_of(start, size, unit=128):
    return pl.ds(pl.multiple_of(start, unit), size)


def forward_kernel(
    qb, x_ref, vec_ref, w_ref, idr_ref, idc_ref, n_ref, q_ref, k_ref, v_ref, o_ref, lse_ref, bias_ref, stat_ref
):
    ext, own = x_ref.shape[0], o_ref.shape[0]
    window = HALO + qb

    def project(i, carry):
        rows = rows_of(i * 128, 128)
        xhat, _ = normalize(x_ref[rows, :].astype(F32))
        n1 = (xhat * vec_ref[0:1, :] + vec_ref[1:2, :]).astype(BF16)
        n_ref[rows, :] = n1
        k_ref[rows, :] = dot(n1, w_ref[:, D : 2 * D]).astype(BF16)
        v_ref[rows, :] = (dot(n1, w_ref[:, 2 * D : 3 * D]) + vec_ref[3:4, :]).astype(BF16)
        return carry

    lax.fori_loop(0, ext // 128, project, 0)

    def project_q(i, carry):
        rows = rows_of(i * 128, 128)
        q = dot(n_ref[rows_of(HALO + i * 128, 128), :], w_ref[:, 0:D]) + vec_ref[2:3, :]
        q_ref[rows, :] = q.astype(BF16) * jnp.asarray(SCALE, BF16)
        return carry

    lax.fori_loop(0, own // 128, project_q, 0)

    def query_block(i, carry):
        first = i * qb
        key = lax.broadcasted_iota(jnp.int32, (qb, window), 1)
        query = lax.broadcasted_iota(jnp.int32, (qb, window), 0)
        same = idc_ref[rows_of(HALO + first, qb), :] == idr_ref[:, rows_of(first, window)]
        bias_ref[...] = jnp.where(same & (key <= query + HALO), 0.0, NEG)

        def pair(g, inner):
            lanes = rows_of(g * PAIR, PAIR)
            lane = lax.broadcasted_iota(jnp.int32, (qb, PAIR), 1)
            keys = k_ref[rows_of(first, window), lanes]
            values = v_ref[rows_of(first, window), lanes]
            both = q_ref[rows_of(first, qb), lanes]
            got = None
            for h in range(2):
                mine = (lane < HD) if h == 0 else (lane >= HD)
                s = dot_t(jnp.where(mine, both, jnp.zeros_like(both)), keys) + bias_ref[...]
                top = jnp.max(s, axis=-1, keepdims=True)
                p = jnp.exp(s - top)
                total = jnp.sum(p, axis=-1, keepdims=True)
                o = dot(p.astype(BF16), values) / total
                got = o if h == 0 else jnp.where(mine, o, got)
                stat_ref[...] = jnp.where(lane == 2 * g + h, top + jnp.log(total), stat_ref[...])
            o_ref[rows_of(first, qb), lanes] = got.astype(BF16)
            return inner

        lax.fori_loop(0, D // PAIR, pair, 0)
        lse_ref[:, rows_of(first, qb)] = jnp.transpose(stat_ref[...])[0:H, :]
        return carry

    stat_ref[...] = jnp.zeros_like(stat_ref)
    lax.fori_loop(0, own // qb, query_block, 0)


def attention_forward(x_ext, vecs, w_qkv, id_row, id_col, own):
    ext = x_ext.shape[0]
    qb = 256 if own % 256 == 0 else 128
    shapes = (
        jax.ShapeDtypeStruct((ext, D), BF16),
        jax.ShapeDtypeStruct((own, D), BF16),
        jax.ShapeDtypeStruct((ext, D), BF16),
        jax.ShapeDtypeStruct((ext, D), BF16),
        jax.ShapeDtypeStruct((own, D), BF16),
        jax.ShapeDtypeStruct((H, own), F32),
    )
    return pl.pallas_call(
        functools.partial(forward_kernel, qb),
        out_shape=shapes,
        scratch_shapes=[pltpu.VMEM((qb, HALO + qb), F32), pltpu.VMEM((qb, 128), F32)],
        compiler_params=pltpu.CompilerParams(vmem_limit_bytes=48 * MIB),
        name="attention_forward",
    )(x_ext, vecs, w_qkv, id_row, id_col)


def middle_kernel(
    rb,
    scale_ref,
    x_ref,
    o_ref,
    teacher_ref,
    cot_ref,
    mask_ref,
    vec_ref,
    bup_ref,
    wo_ref,
    wup_ref,
    wdn_ref,
    out_ref,
    gh_ref,
    go_ref,
    delta_ref,
    gwo_ref,
    gwup_ref,
    gwdn_ref,
    small_ref,
    gbup_ref,
    slope_ref,
    hid_ref,
    gpre_ref,
    n2t_ref,
    gmlpt_ref,
    gattnt_ref,
):
    own = x_ref.shape[0]
    ff = wup_ref.shape[1]
    chunk = 512
    small_ref[...] = jnp.zeros_like(small_ref)
    head_of = lax.broadcasted_iota(jnp.int32, (D, 128), 0) // HD
    pick = (head_of == lax.broadcasted_iota(jnp.int32, (D, 128), 1)).astype(BF16)

    def block(i, carry):
        rows = rows_of(i * rb, rb)
        out_bias, gain, offset, down_bias = (vec_ref[j : j + 1, :] for j in range(4))
        h1 = x_ref[rows, :].astype(F32) + dot_t(o_ref[rows, :], wo_ref[...]) + out_bias
        xhat, rstd = normalize(h1)
        n2 = xhat * gain + offset
        n2_low = n2.astype(BF16)
        n2t_ref[:, rows] = jnp.transpose(n2).astype(BF16)
        for c in range(0, ff, chunk):
            pre = dot(n2_low, wup_ref[:, c : c + chunk]) + bup_ref[:, c : c + chunk]
            s = jax.nn.sigmoid(1.702 * pre)
            value = pre * s
            hid_ref[rows, c : c + chunk] = value.astype(BF16)
            slope_ref[:, c : c + chunk] = s + 1.702 * value * (1.0 - s)
        out = h1 + dot_t(hid_ref[rows, :], wdn_ref[...]) + down_bias
        out_ref[rows, :] = out.astype(BF16)
        valid = mask_ref[rows, :]
        diff = (out - teacher_ref[rows, :].astype(F32)) * valid
        g_out = cot_ref[rows, :].astype(F32) + scale_ref[0, 0] * diff
        small_ref[0:8, :] += fold(g_out)
        small_ref[8:16, :] += fold(diff * diff)
        g_mlp = g_out.astype(BF16)
        gmlpt_ref[:, rows] = jnp.transpose(g_out).astype(BF16)
        for c in range(0, ff, chunk):
            g_hid = dot(g_mlp, wdn_ref[:, c : c + chunk])
            gpre_ref[rows, c : c + chunk] = (g_hid * slope_ref[:, c : c + chunk]).astype(BF16)
        g_n2 = dot_t(gpre_ref[rows, :], wup_ref[...])
        small_ref[16:24, :] += fold(g_n2 * xhat)
        small_ref[24:32, :] += fold(g_n2)
        g_h1 = g_out + norm_pull(g_n2, gain, xhat, rstd)
        gh_ref[rows, :] = g_h1
        small_ref[32:40, :] += fold(g_h1)
        gattnt_ref[:, rows] = jnp.transpose(g_h1).astype(BF16)
        g_o = dot(g_h1.astype(BF16), wo_ref[...]).astype(BF16)
        go_ref[rows, :] = g_o
        product = g_o.astype(F32) * o_ref[rows, :].astype(F32)
        high = product.astype(BF16)
        low = (product - high.astype(F32)).astype(BF16)
        delta_ref[:, rows] = jnp.transpose(dot(high, pick) + dot(low, pick))[0:H, :]
        return carry

    lax.fori_loop(0, own // rb, block, 0)
    ones = jnp.ones((8, own), BF16)

    def grads(i, carry):
        cols = rows_of(i * chunk, chunk)
        gwdn_ref[:, cols] = dot(gmlpt_ref[...], hid_ref[:, cols]).astype(BF16)
        gwup_ref[:, cols] = dot(n2t_ref[...], gpre_ref[:, cols]).astype(BF16)
        gbup_ref[:, cols] = dot(ones, gpre_ref[:, cols])
        return carry

    lax.fori_loop(0, ff // chunk, grads, 0)
    gwo_ref[...] = dot(gattnt_ref[...], o_ref[...]).astype(BF16)


def middle(scale, x, o, teacher, cot, mask, vecs, b_up, w_o, w_up, w_dn):
    own, ff = x.shape[0], w_up.shape[1]
    rb = 256 if own % 256 == 0 else 128
    shapes = (
        jax.ShapeDtypeStruct((own, D), BF16),
        jax.ShapeDtypeStruct((own, D), F32),
        jax.ShapeDtypeStruct((own, D), BF16),
        jax.ShapeDtypeStruct((H, own), F32),
        jax.ShapeDtypeStruct((D, D), BF16),
        jax.ShapeDtypeStruct((D, ff), BF16),
        jax.ShapeDtypeStruct((D, ff), BF16),
        jax.ShapeDtypeStruct((40, D), F32),
        jax.ShapeDtypeStruct((8, ff), F32),
    )
    whole = pl.BlockSpec(memory_space=pltpu.VMEM)
    return pl.pallas_call(
        functools.partial(middle_kernel, rb),
        out_shape=shapes,
        in_specs=[pl.BlockSpec(memory_space=pltpu.SMEM)] + [whole] * 10,
        out_specs=[whole] * len(shapes),
        scratch_shapes=[
            pltpu.VMEM((rb, ff), F32),
            pltpu.VMEM((own, ff), BF16),
            pltpu.VMEM((own, ff), BF16),
            pltpu.VMEM((D, own), BF16),
            pltpu.VMEM((D, own), BF16),
            pltpu.VMEM((D, own), BF16),
        ],
        compiler_params=pltpu.CompilerParams(vmem_limit_bytes=56 * MIB),
        name="middle",
    )(scale, x, o, teacher, cot, mask, vecs, b_up, w_o, w_up, w_dn)


def backward_kernel(
    qb,
    q_ref,
    k_ref,
    v_ref,
    go_ref,
    lse_ref,
    delta_ref,
    idr_ref,
    idc_ref,
    n_ref,
    x_ref,
    w_ref,
    gn_halo_ref,
    gn_ref,
    gw_ref,
    small_ref,
    bias_ref,
    kt_ref,
    nt_ref,
    dqt_ref,
    dk_ref,
    dv_ref,
    g_ref,
):
    ext, own = k_ref.shape[0], q_ref.shape[0]
    window = HALO + qb
    dk_ref[...] = jnp.zeros_like(dk_ref)
    dv_ref[...] = jnp.zeros_like(dv_ref)
    small_ref[...] = jnp.zeros_like(small_ref)

    def turn(i, carry):
        rows = rows_of(i * 128, 128)
        kt_ref[:, rows] = jnp.transpose(k_ref[rows, :].astype(F32)).astype(BF16)
        nt_ref[:, rows] = jnp.transpose(n_ref[rows, :].astype(F32)).astype(BF16)
        return carry

    lax.fori_loop(0, ext // 128, turn, 0)

    def query_block(i, carry):
        first = i * qb
        key = lax.broadcasted_iota(jnp.int32, (window, qb), 0)
        query = lax.broadcasted_iota(jnp.int32, (window, qb), 1)
        same = idc_ref[rows_of(first, window), :] == idr_ref[:, rows_of(HALO + first, qb)]
        bias_ref[...] = jnp.where(same & (key <= query + HALO), 0.0, NEG)

        def pair(g, inner):
            lanes = rows_of(g * PAIR, PAIR)
            lane = lax.broadcasted_iota(jnp.int32, (qb, PAIR), 1)
            keys = k_ref[rows_of(first, window), lanes]
            values = v_ref[rows_of(first, window), lanes]
            both_q = q_ref[rows_of(first, qb), lanes]
            both_g = go_ref[rows_of(first, qb), lanes]
            all_lse = lse_ref[:, rows_of(first, qb)]
            all_delta = delta_ref[:, rows_of(first, qb)]
            line = lax.broadcasted_iota(jnp.int32, (H, qb), 0)
            dk, dv = None, None
            for h in range(2):
                head = 2 * g + h
                mine = (lane < HD) if h == 0 else (lane >= HD)
                q = jnp.where(mine, both_q, jnp.zeros_like(both_q))
                g_o = jnp.where(mine, both_g, jnp.zeros_like(both_g))
                lse = jnp.sum(jnp.where(line == head, all_lse, 0.0), axis=0, keepdims=True)
                delta = jnp.sum(jnp.where(line == head, all_delta, 0.0), axis=0, keepdims=True)
                p = jnp.exp(dot_t(keys, q) + bias_ref[...] - lse)
                ds = (p * (dot_t(values, g_o) - delta)).astype(BF16)
                dv_h = dot(p.astype(BF16), g_o)
                dk_h = dot(ds, q)
                dk, dv = (dk_h, dv_h) if h == 0 else (dk + dk_h, dv + dv_h)
                dqt_ref[rows_of(head * HD, HD, HD), rows_of(first, qb)] = dot(
                    kt_ref[rows_of(head * HD, HD, HD), rows_of(first, window)], ds
                )
            dk_ref[rows_of(first, window), lanes] += dk
            dv_ref[rows_of(first, window), lanes] += dv
            return inner

        lax.fori_loop(0, D // PAIR, pair, 0)
        return carry

    lax.fori_loop(0, own // qb, query_block, 0)

    def gather(i, carry):
        rows = rows_of(i * 128, 128)
        g_ref[rows, D : 2 * D] = dk_ref[rows, :].astype(BF16)
        g_ref[rows, 2 * D : 3 * D] = dv_ref[rows, :].astype(BF16)
        return carry

    lax.fori_loop(0, ext // 128, gather, 0)

    def gather_q(i, carry):
        cols = rows_of(i * 128, 128)
        g_ref[rows_of(HALO + i * 128, 128), 0:D] = (jnp.transpose(dqt_ref[:, cols]) * SCALE).astype(BF16)
        return carry

    lax.fori_loop(0, own // 128, gather_q, 0)

    def norms(rows, g_n1):
        xhat, _ = normalize(x_ref[rows, :].astype(F32))
        small_ref[0:8, :] += fold(g_n1 * xhat)
        small_ref[8:16, :] += fold(g_n1)

    def pull_halo(i, carry):
        rows = rows_of(i * 128, 128)
        g_n1 = dot_t(g_ref[rows, D : 3 * D], w_ref[:, D : 3 * D])
        gn_halo_ref[rows, :] = g_n1.astype(BF16)
        norms(rows, g_n1)
        return carry

    lax.fori_loop(0, HALO // 128, pull_halo, 0)

    def pull_own(i, carry):
        rows = rows_of(HALO + i * 128, 128)
        g_n1 = dot_t(g_ref[rows, :], w_ref[...])
        gn_ref[rows_of(i * 128, 128), :] = g_n1
        norms(rows, g_n1)
        return carry

    lax.fori_loop(0, own // 128, pull_own, 0)
    gw_ref[:, 0:D] = dot(nt_ref[:, HALO:], g_ref[HALO:, 0:D]).astype(BF16)
    gw_ref[:, D : 2 * D] = dot(nt_ref[...], g_ref[:, D : 2 * D]).astype(BF16)
    gw_ref[:, 2 * D : 3 * D] = dot(nt_ref[...], g_ref[:, 2 * D : 3 * D]).astype(BF16)
    small_ref[16:24, :] = dot(jnp.ones((8, own), BF16), g_ref[HALO:, 0:D])
    small_ref[24:32, :] = dot(jnp.ones((8, ext), BF16), g_ref[:, 2 * D : 3 * D])


def attention_backward(q, k, v, g_o, lse, delta, id_row, id_col, n1, x_ext, w_qkv):
    ext, own = k.shape[0], q.shape[0]
    qb = 256 if own % 256 == 0 else 128
    shapes = (
        jax.ShapeDtypeStruct((HALO, D), BF16),
        jax.ShapeDtypeStruct((own, D), F32),
        jax.ShapeDtypeStruct((D, 3 * D), BF16),
        jax.ShapeDtypeStruct((32, D), F32),
    )
    return pl.pallas_call(
        functools.partial(backward_kernel, qb),
        out_shape=shapes,
        scratch_shapes=[
            pltpu.VMEM((HALO + qb, qb), F32),
            pltpu.VMEM((D, ext), BF16),
            pltpu.VMEM((D, ext), BF16),
            pltpu.VMEM((D, own), F32),
            pltpu.VMEM((ext, D), F32),
            pltpu.VMEM((ext, D), F32),
            pltpu.VMEM((ext, 3 * D), BF16),
        ],
        compiler_params=pltpu.CompilerParams(vmem_limit_bytes=56 * MIB),
        name="attention_backward",
    )(q, k, v, g_o, lse, delta, id_row, id_col, n1, x_ext, w_qkv)


def finish_kernel(x_ref, gn_ref, gh_ref, vec_ref, out_ref):
    def block(i, carry):
        rows = rows_of(i * 128, 128)
        xhat, rstd = normalize(x_ref[rows, :].astype(F32))
        out_ref[rows, :] = gh_ref[rows, :] + norm_pull(gn_ref[rows, :], vec_ref[0:1, :], xhat, rstd)
        return carry

    lax.fori_loop(0, x_ref.shape[0] // 128, block, 0)


def finish(x, g_n1, g_h1, vecs):
    return pl.pallas_call(
        finish_kernel,
        out_shape=jax.ShapeDtypeStruct(x.shape, F32),
        compiler_params=pltpu.CompilerParams(vmem_limit_bytes=32 * MIB),
        name="finish",
    )(x, g_n1, g_h1, vecs)


def hops(rows):
    plan, left, step = [], HALO, 1
    while left > 0:
        take = min(rows, left)
        plan.append((step, take))
        left, step = left - take, step + 1
    return plan


def local(
    layer_input,
    segment_ids,
    valid_mask,
    teacher,
    cotangent,
    ln1_gain,
    ln1_bias,
    w_q,
    w_k,
    w_v,
    b_q,
    b_v,
    w_o,
    b_o,
    ln2_gain,
    ln2_bias,
    w_up,
    b_up,
    w_down,
    b_down,
):
    fsdp_size = lax.axis_size("fsdp")
    tensor_size = lax.axis_size("tp")
    place = lax.axis_index("tp")
    own = layer_input.shape[0]
    tokens_all = own * fsdp_size * tensor_size
    rows_d = w_q.shape[0]
    cols_h, cols_f = w_q.shape[1], w_up.shape[1]

    parts = []
    for step, take in hops(own):
        route = [(i, i + step) for i in range(tensor_size - step)]
        parts.insert(0, lax.ppermute(layer_input[own - take :], "tp", route))
    x_ext = jnp.concatenate(parts + [layer_input], axis=0)
    ids = segment_ids + LEN * jnp.arange(segment_ids.shape[0], dtype=jnp.int32)[:, None]
    ids = jnp.concatenate([jnp.full((HALO,), -1, jnp.int32), ids.reshape(-1)])
    ids = lax.dynamic_slice_in_dim(ids, place * own, HALO + own)
    id_row, id_col = ids[None, :], ids[:, None]

    pack = jnp.concatenate([w_q, w_k, w_v, w_o.T, w_up, w_down.T], axis=1)
    count = jnp.sum(valid_mask)
    count_high = count // 256
    vectors = jnp.concatenate([ln1_gain, ln1_bias, b_o, ln2_gain, ln2_bias, b_down])
    heads = jnp.concatenate([b_q.reshape(-1), b_v.reshape(-1), b_up.reshape(-1)])
    digits = jnp.stack([count_high, count - 256 * count_high]).astype(BF16)
    small = jnp.concatenate([vectors, heads, digits])
    width = pack.shape[1]
    lines = -(-small.shape[0] // width)
    small = jnp.pad(small, (0, lines * width - small.shape[0])).reshape(lines, width)
    shard = jnp.concatenate([pack, small], axis=0)
    every = lax.all_gather(lax.all_gather(shard, "tp", axis=0), "fsdp", axis=0)
    big = every[:, :, :rows_d, :]

    def columns(start, size):
        part = big[:, :, :, start : start + size]
        return part.transpose(0, 2, 1, 3).reshape(fsdp_size * rows_d, tensor_size * size)

    w_qkv = jnp.concatenate([columns(j * cols_h, cols_h) for j in range(3)], axis=1)
    w_ot = columns(3 * cols_h, cols_h)
    w_up_all = columns(4 * cols_h, cols_f)
    w_dn_all = columns(4 * cols_h + cols_f, cols_f)
    few = every[:, :, rows_d:, :].reshape(fsdp_size, tensor_size, -1).astype(F32)
    six = few[:, 0, : 6 * rows_d].reshape(fsdp_size, 6, rows_d).transpose(1, 0, 2).reshape(6, D)
    at = 6 * rows_d

    def by_head(start, shape):
        size = shape[0] * shape[1]
        part = few[:, :, start : start + size].reshape((fsdp_size, tensor_size) + shape)
        return part.transpose(1, 2, 0, 3).reshape(1, -1)

    bq_all = by_head(at, b_q.shape)
    at += b_q.size
    bv_all = by_head(at, b_v.shape)
    at += b_v.size
    bup_all = by_head(at, b_up.shape)
    at += b_up.size
    valid_total = 256.0 * jnp.sum(few[:, :, at]) + jnp.sum(few[:, :, at + 1])

    vec_one = jnp.concatenate([six[0:2], bq_all, bv_all], axis=0)
    vec_two = jnp.stack([six[2], six[3], six[4], six[5]])
    n1, q, k, v, o, lse = attention_forward(x_ext, vec_one, w_qkv, id_row, id_col, own)
    scale = (tokens_all / valid_total).reshape(1, 1)
    mask = valid_mask.astype(F32)[:, None]
    layer_out, g_h1, g_o, delta, g_wo, g_wup, g_wdn, small_two, g_bup = middle(
        scale, layer_input, o, teacher, cotangent, mask, vec_two, bup_all, w_ot, w_up_all, w_dn_all
    )
    gn_halo, gn_own, g_qkv, small_one = attention_backward(
        q, k, v, g_o, lse, delta, id_row, id_col, n1, x_ext, w_qkv
    )

    total = gn_own
    left = HALO
    for step, take in hops(own):
        route = [(i + step, i) for i in range(tensor_size - step)]
        part = lax.ppermute(gn_halo[left - take : left], "tp", route).astype(F32)
        total = total + jnp.pad(part, ((own - take, 0), (0, 0)))
        left -= take
    grad_input = finish(layer_input, total, g_h1, vec_one)

    def split(grad, size):
        return grad.reshape(fsdp_size, rows_d, tensor_size, size).transpose(0, 2, 1, 3)

    g_pack = jnp.concatenate(
        [split(g_qkv[:, j * D : (j + 1) * D], cols_h) for j in range(3)]
        + [split(g_wo, cols_h), split(g_wup, cols_f), split(g_wdn, cols_f)],
        axis=3,
    )
    ones = [small_one[8 * j : 8 * j + 8].sum(0) for j in range(2)] + [small_one[16], small_one[24]]
    twos = [small_two[8 * j : 8 * j + 8].sum(0) for j in range(5)]
    loss_part = 0.5 / D * jnp.sum(twos[1]) / valid_total
    six_grads = jnp.stack([ones[0], ones[1], twos[4], twos[2], twos[3], twos[0]])
    six_grads = six_grads.reshape(6, fsdp_size, 1, rows_d).transpose(1, 2, 0, 3)
    six_grads = jnp.broadcast_to(
        six_grads.reshape(fsdp_size, 1, -1), (fsdp_size, tensor_size, 6 * rows_d)
    )

    def heads_of(grad, shape):
        part = grad.reshape((tensor_size, shape[0], fsdp_size, shape[1]))
        return part.transpose(2, 0, 1, 3).reshape(fsdp_size, tensor_size, -1)

    loss_high = loss_part.astype(BF16).astype(F32)
    losses = jnp.broadcast_to(
        jnp.stack([loss_high, loss_part - loss_high]), (fsdp_size, tensor_size, 2)
    )
    g_small = jnp.concatenate(
        [
            six_grads,
            heads_of(ones[2], b_q.shape),
            heads_of(ones[3], b_v.shape),
            heads_of(g_bup[0], b_up.shape),
            losses,
        ],
        axis=2,
    ).astype(BF16)
    g_small = jnp.pad(g_small, ((0, 0), (0, 0), (0, lines * width - g_small.shape[2])))
    g_all = jnp.concatenate([g_pack, g_small.reshape(fsdp_size, tensor_size, lines, width)], axis=2)
    mine = lax.psum_scatter(g_all, "fsdp", scatter_dimension=0, tiled=False)
    mine = lax.psum_scatter(mine, "tp", scatter_dimension=0, tiled=False).astype(F32)
    g_mat, g_vec = mine[:rows_d], mine[rows_d:].reshape(-1)
    c3, c4 = 3 * cols_h, 4 * cols_h
    six_out = g_vec[: 6 * rows_d].reshape(6, rows_d)
    at = 6 * rows_d
    grad_bq = g_vec[at : at + b_q.size].reshape(b_q.shape)
    at += b_q.size
    grad_bv = g_vec[at : at + b_v.size].reshape(b_v.shape)
    at += b_v.size
    grad_bup = g_vec[at : at + b_up.size].reshape(b_up.shape)
    at += b_up.size
    loss = g_vec[at] + g_vec[at + 1]
    return (
        layer_out,
        loss,
        grad_input,
        six_out[0],
        six_out[1],
        g_mat[:, 0:cols_h],
        g_mat[:, cols_h : 2 * cols_h],
        g_mat[:, 2 * cols_h : c3],
        grad_bq,
        grad_bv,
        g_mat[:, c3:c4].T,
        six_out[2],
        six_out[3],
        six_out[4],
        g_mat[:, c4 : c4 + cols_f],
        grad_bup,
        g_mat[:, c4 + cols_f :].T,
        six_out[5],
    )


ROWS = D // 8
EXTRA = 8
COLS = D // 4
FFC = 512
WA = 3 * COLS
WF = COLS + 2 * FFC
TALL = D + 16
ALL = (0, 1, 2, 3)
PIECES_A = ((0, ALL), (2, ALL), (4, ALL), (6, ALL), (1, ALL), (3, ALL), (5, ALL), (7, ALL))
SMALL = pl.CostEstimate(flops=1, bytes_accessed=1, transcendentals=0)


def about(us):
    return pl.CostEstimate(flops=us * 1000000, bytes_accessed=us * 3300000, transcendentals=0)


ANY = pl.BlockSpec(memory_space=pl.ANY)
VMEM = pl.BlockSpec(memory_space=pltpu.VMEM)
FAR = pl.BlockSpec(memory_space=pl.ANY)


def params(mib):
    return pltpu.CompilerParams(vmem_limit_bytes=mib * MIB)


def lane_of(shape):
    return lax.broadcasted_iota(jnp.int32, shape, len(shape) - 1)


def pack_kernel(
    wq_ref, wk_ref, wv_ref, wo_ref, wup_ref, wdn_ref, g1, b1, bo, g2, b2, bd, bq, bv, bup, mask_ref, a_ref, f_ref
):
    me = lax.axis_index("fsdp")
    a_ref[0:ROWS, 0:COLS] = wq_ref[...]
    a_ref[0:ROWS, COLS : 2 * COLS] = wk_ref[...]
    a_ref[0:ROWS, 2 * COLS : 3 * COLS] = wv_ref[...]
    f_ref[:, 0:COLS] = wo_ref[...]
    f_ref[:, COLS : COLS + FFC] = wup_ref[...]
    f_ref[:, COLS + FFC :] = wdn_ref[...]
    count = jnp.sum(mask_ref[...].astype(F32)).reshape(1, 1)
    high = jnp.floor(count / 256.0)
    lane = lane_of((1, 128))
    digits = jnp.where(lane == 0, high, jnp.where(lane == 1, count - 256.0 * high, 0.0))
    vectors = [r[...].astype(F32).reshape(1, ROWS) for r in (g1, b1, bo, g2, b2, bd)]
    rows = [jnp.concatenate([v, v], axis=1) for v in vectors] + [digits, jnp.zeros((1, 128), F32)]
    a_ref[ROWS:, 0:128] = jnp.concatenate(rows, axis=0).astype(BF16)

    def spread(ref):
        block = ref[...].astype(F32)
        count, piece = block.shape
        lanes = count * HD
        lane = lane_of((1, lanes))
        row = jnp.zeros((1, lanes), F32)
        for i in range(count):
            for j in range(piece):
                at = i * HD + me * piece + j
                row = jnp.where(lane == at, block[i : i + 1, j : j + 1], row)
        return row

    ups = spread(bup)
    rows = [spread(bq), spread(bv)] + [ups[:, 128 * j : 128 * j + 128] for j in range(4)]
    rows.append(jnp.zeros((2, 128), F32))
    a_ref[ROWS:, 128:256] = jnp.concatenate(rows, axis=0).astype(BF16)
    a_ref[ROWS:, 256:384] = jnp.zeros((EXTRA, 128), BF16)


def pack_weights(args):
    return pl.pallas_call(
        pack_kernel,
        out_shape=(
            jax.ShapeDtypeStruct((ROWS + EXTRA, WA), BF16),
            jax.ShapeDtypeStruct((ROWS, WF), BF16),
        ),
        compiler_params=params(60),
        name="pack_weights",
    )(*args)


def project_kernel(
    tokens_all, x_ref, idc_ref, p0, p1, p2, p3, p4,
    q_ref, k_ref, v_ref, kt_ref, nt_ref, w_ref, vec_ref, bup_ref, scale_ref, head_ref, ext_ref, n_ref, sem
):
    me, place = lax.axis_index("fsdp"), lax.axis_index("tp")
    pieces = (p0, p1, p2, p3) + tuple(p4.at[4 * i : 4 * i + 4] for i in range(4))

    def each(act):
        for ref, (mask, steps) in zip(pieces, PIECES_A):
            owner = lax.bitwise_xor(me, mask)
            for i, s in enumerate(steps):
                tp = lax.bitwise_and(place - s + 4, 3)
                act(ref.at[i], 4 * mask + s, owner, tp)

    def start_ext(ref, slot, owner, tp):
        pltpu.make_async_copy(ref.at[pl.ds(ROWS, EXTRA), :], ext_ref.at[slot], sem.at[0]).start()

    def start_w(ref, slot, owner, tp):
        pltpu.make_async_copy(
            ref.at[pl.ds(0, ROWS), :],
            w_ref.at[rows_of(owner * ROWS, ROWS, ROWS), rows_of(tp * WA, WA)],
            sem.at[1],
        ).start()

    each(start_ext)
    each(start_w)
    pltpu.make_async_copy(ext_ref, ext_ref, sem.at[0]).wait()
    lane = lane_of((EXTRA, D))
    vectors = jnp.zeros((EXTRA, D), F32)
    total = jnp.zeros((EXTRA, 128), F32)
    for j in range(8):
        block = ext_ref[4 * j, :, 0:128].astype(F32)
        wide = jnp.concatenate([block] * 4, axis=1)
        vectors = jnp.where(lane // ROWS == lax.bitwise_xor(me, j), wide, vectors)
        for s in range(4):
            total += ext_ref[4 * j + s, :, 0:128].astype(F32)
    vec_ref[...] = vectors
    valid = 256.0 * total[6:7, 0:1] + total[6:7, 1:2]
    scale_ref[...] = jnp.concatenate(
        [jnp.broadcast_to(tokens_all / valid, (4, 128)), jnp.broadcast_to(0.5 / D / valid, (4, 128))], axis=0
    )
    for s in range(4):
        tp = lax.bitwise_and(place - s + 4, 3)
        block = jnp.zeros((EXTRA, 128), F32)
        for j in range(8):
            block += ext_ref[4 * j + s, :, 128:256].astype(F32)
        head_ref[:, rows_of(tp * COLS, COLS)] = block
        for i in range(4):
            bup_ref[:, rows_of(tp * FFC + 128 * i, 128)] = jnp.broadcast_to(block[2 + i : 3 + i], (8, 128))

    def norm(i, carry):
        rows = rows_of(i * QB, QB)
        n_ref[rows, :] = first_norm(x_ref[rows, :], vectors, me, nt_ref, rows)
        return carry

    def product(one):
        one["made"] = dot(n_ref[one["rows"], :], w_ref[...])

    def keep(one):
        rows, made = one["rows"], one.pop("made")
        spare_q, spare_k, spare_v = spare_lanes(idc_ref[slice(HALO + rows.start, HALO + rows.stop), :])
        for t in range(4):
            lanes = slice(t * COLS, (t + 1) * COLS)
            q = (made[:, t * WA : t * WA + COLS] + head_ref[0:1, lanes]).astype(BF16)
            keep_heads(q_ref, rows, t, q * jnp.asarray(SCALE, BF16), spare_q)
            keep_keys(made[:, t * WA + COLS : (t + 1) * WA], head_ref, k_ref, v_ref, kt_ref, rows, t, spare_k, spare_v)

    blocks = [dict(rows=slice(i * QB, (i + 1) * QB)) for i in range(x_ref.shape[0] // QB)]
    lax.fori_loop(0, x_ref.shape[0] // QB, norm, 0)
    pltpu.make_async_copy(w_ref, w_ref, sem.at[1]).wait()
    staged(blocks, (product, keep))


DOCS = 48
TERMS = 3


def spare_lanes(ids):
    shape = (ids.shape[0], PAIR)
    at = lax.bitwise_and(lane_of(shape), HD - 1)
    same = at == ids
    ones = jnp.where((at >= DOCS) & (at < DOCS + TERMS), 1.0, 0.0)
    spare_q = jnp.where(same & (at < DOCS), 1.0, 0.0).astype(BF16)
    spare_k = jnp.where(at < DOCS, jnp.where(same, 0.0, NEG), ones).astype(BF16)
    return spare_q, spare_k, ones.astype(BF16)


def three_terms(x):
    high = x.astype(BF16)
    rest = x - high.astype(F32)
    middle = rest.astype(BF16)
    return high, middle, (rest - middle.astype(F32)).astype(BF16)


def keep_heads(ref, rows, pair, value, spare):
    lane = lane_of(value.shape)
    for h in range(2):
        at = (2 * pair + h) * PAIR
        mine = (lane < HD) if h == 0 else (lane >= HD)
        ref[rows, at : at + PAIR] = jnp.where(mine, value, spare)


def first_norm(x, vectors, me, nt_ref, rows):
    xhat, _ = normalize(x.astype(F32))
    n1 = xhat * vectors[0:1] + vectors[1:2]
    turned = jnp.transpose(n1).astype(BF16)
    for i in range(8):
        slot = lax.bitwise_xor(me, i)
        nt_ref[rows_of(slot * ROWS, ROWS, ROWS), rows] = turned[ROWS * i : ROWS * (i + 1)]
    nt_ref[D:, rows] = jnp.ones((TALL - D, x.shape[0]), BF16)
    return n1.astype(BF16)


def keep_keys(made, head_ref, k_ref, v_ref, kt_ref, rows, t, spare_k, spare_v):
    lanes = slice(t * COLS, (t + 1) * COLS)
    k = made[:, 0:COLS]
    keep_heads(k_ref, rows, t, k.astype(BF16), spare_k)
    kt_ref[lanes, rows] = jnp.transpose(k).astype(BF16)
    keep_heads(v_ref, rows, t, (made[:, COLS:] + head_ref[1:2, lanes]).astype(BF16), spare_v)


def project(x, id_col, pieces, tokens_all):
    own = x.shape[0]
    shapes = (
        jax.ShapeDtypeStruct((own, 2 * D), BF16),
        jax.ShapeDtypeStruct((own, 2 * D), BF16),
        jax.ShapeDtypeStruct((own, 2 * D), BF16),
        jax.ShapeDtypeStruct((D, own), BF16),
        jax.ShapeDtypeStruct((TALL, own), BF16),
        jax.ShapeDtypeStruct((D, 4 * WA), BF16),
        jax.ShapeDtypeStruct((EXTRA, D), F32),
        jax.ShapeDtypeStruct((8, 4 * FFC), F32),
        jax.ShapeDtypeStruct((8, 128), F32),
        jax.ShapeDtypeStruct((EXTRA, D), F32),
    )
    return pl.pallas_call(
        functools.partial(project_kernel, float(tokens_all)),
        out_shape=shapes,
        in_specs=[VMEM, VMEM] + [FAR] * 5,
        out_specs=[VMEM] * len(shapes),
        scratch_shapes=[pltpu.VMEM((32, EXTRA, WA), BF16), pltpu.VMEM((own, D), BF16), pltpu.SemaphoreType.DMA((2,))],
        compiler_params=params(6),
        cost_estimate=SMALL,
        name="project",
    )(x, id_col, *pieces)


def project_halo_kernel(x_ref, idc_ref, w_ref, vec_ref, head_ref, k_ref, v_ref, kt_ref, nt_ref):
    me = lax.axis_index("fsdp")

    def norm(one):
        one["n1"] = first_norm(x_ref[one["rows"], :], vec_ref[...], me, nt_ref, one["rows"])

    def product(one):
        one["made"] = [dot(one["n1"], w_ref[:, t * WA + COLS : (t + 1) * WA]) for t in range(4)]

    def keep(one):
        rows = one["rows"]
        _, spare_k, spare_v = spare_lanes(idc_ref[rows, :])
        for t, made in enumerate(one.pop("made")):
            keep_keys(made, head_ref, k_ref, v_ref, kt_ref, rows, t, spare_k, spare_v)

    staged([dict(rows=slice(i * QB, (i + 1) * QB)) for i in range(HALO // QB)], (norm, product, keep))


def project_halo(x, id_col, w, vec, head):
    shape = jax.ShapeDtypeStruct((HALO, 2 * D), BF16)
    turned, tall = (jax.ShapeDtypeStruct((size, HALO), BF16) for size in (D, TALL))
    return pl.pallas_call(
        project_halo_kernel,
        out_shape=(shape, shape, turned, tall),
        compiler_params=params(6),
        cost_estimate=SMALL,
        name="project_halo",
    )(x, id_col, w, vec, head)


QB = 256


def causal(by_rows):
    key = lax.broadcasted_iota(jnp.int32, (QB, QB), 1 if by_rows else 0)
    query = lax.broadcasted_iota(jnp.int32, (QB, QB), 0 if by_rows else 1)
    return jnp.where(key <= query, 0.0, NEG)


def staged(units, stages, lag=1, beside=()):
    steps = len(units) + lag * (len(stages) - 1)
    for n in range(steps):
        for depth, stage in enumerate(stages):
            if 0 <= n - lag * depth < len(units):
                stage(units[n - lag * depth])
        if n < len(beside):
            beside[n]()
    for extra in beside[steps:]:
        extra()


def attend_heads(heads, bias_ref):
    lane = lane_of((QB, PAIR))
    at = lax.bitwise_and(lane, HD - 1)

    def score(one):
        q = one["q"][one["rows"], one["lanes"]]
        one["s"] = []
        for keys, _, where, last in one["parts"]:
            s = dot_t(q, keys[where, one["lanes"]])
            one["s"].append(s + bias_ref[...] if last else s)

    def soften(one):
        one["top"] = functools.reduce(jnp.maximum, [jnp.max(s, axis=-1, keepdims=True) for s in one["s"]])
        one["p"] = [jnp.exp(s - one["top"]).astype(BF16) for s in one.pop("s")]

    def attend(one):
        total = None
        for p, (_, values, where, _) in zip(one.pop("p"), one["parts"]):
            part = dot(p, values[where, one["lanes"]])
            total = part if total is None else total + part
        first = (HD if one["h"] == 0 else 0) + DOCS
        weight = total[:, first : first + 1]
        mine = (lane < HD) if one["h"] == 0 else (lane >= HD)
        q = one["q"][one["rows"], one["lanes"]]
        for i, term in enumerate(three_terms(-(one["top"] + jnp.log(weight)))):
            q = jnp.where((at == DOCS + i) & ~mine, jnp.broadcast_to(term, q.shape), q)
        one["take"](one["h"], (total / weight).astype(BF16), q)

    staged(heads, (score, soften, attend), 3)


def keep_attended(o_ref, qa_ref, rows, pair):
    lane = lane_of((QB, PAIR))

    def take(h, o, q):
        lanes = rows_of(pair * PAIR, PAIR)
        qa_ref[rows, head_lanes(pair, h)] = q
        o_ref[rows, lanes] = o if h == 0 else jnp.where(lane < HD, o_ref[rows, lanes], o)

    return take


def head_lanes(pair, h):
    return rows_of((2 * pair + h) * PAIR, PAIR)


def each_two(count, act):
    def step(i, carry):
        act((2 * i, 2 * i + 1))
        return carry

    lax.fori_loop(0, count, step, 0)


def attend_far_kernel(q_ref, k_ref, v_ref, o_ref, qa_ref, bias_ref):
    bias_ref[...] = causal(True)
    parts = ((k_ref, v_ref, slice(0, HALO), False), (k_ref, v_ref, slice(HALO, HALO + QB), True))

    def two(pairs):
        heads = []
        for pair in pairs:
            take = keep_attended(o_ref, qa_ref, slice(0, QB), pair)
            for h in range(2):
                heads.append(
                    dict(q=q_ref, rows=slice(HALO, HALO + QB), lanes=head_lanes(pair, h), h=h, parts=parts, take=take)
                )
        attend_heads(heads, bias_ref)

    each_two(2, two)


def attend_far(q, k, v):
    return pl.pallas_call(
        attend_far_kernel,
        out_shape=(jax.ShapeDtypeStruct((QB, D), BF16), jax.ShapeDtypeStruct((QB, 2 * D), BF16)),
        in_specs=[VMEM] * 3,
        out_specs=[VMEM] * 2,
        scratch_shapes=[pltpu.VMEM((QB, QB), F32)],
        compiler_params=params(8),
        cost_estimate=SMALL,
        name="attend_far",
    )(q, k, v)


def near_parts(halo, own):
    return (
        ((*halo, slice(0, HALO), False), (*own, slice(0, QB), True)),
        ((*halo, slice(QB, HALO), False), (*own, slice(0, QB), False), (*own, slice(QB, HALO), True)),
    )


def attend_near_kernel(q_ref, kh_ref, ko_ref, vh_ref, vo_ref, o_ref, qa_ref, bias_ref):
    bias_ref[...] = causal(True)

    def two(pairs):
        heads = []
        for pair in pairs:
            for i, parts in enumerate(near_parts((kh_ref, vh_ref), (ko_ref, vo_ref))):
                rows = slice(i * QB, (i + 1) * QB)
                take = keep_attended(o_ref, qa_ref, rows, pair)
                for h in range(2):
                    heads.append(dict(q=q_ref, rows=rows, lanes=head_lanes(pair, h), h=h, parts=parts, take=take))
        attend_heads(heads, bias_ref)

    each_two(2, two)


def attend_near(q, k_halo, k, v_halo, v):
    return pl.pallas_call(
        attend_near_kernel,
        out_shape=(jax.ShapeDtypeStruct((HALO, D), BF16), jax.ShapeDtypeStruct((HALO, 2 * D), BF16)),
        in_specs=[VMEM] * 5,
        out_specs=[VMEM] * 2,
        scratch_shapes=[pltpu.VMEM((QB, QB), F32)],
        compiler_params=params(8),
        cost_estimate=SMALL,
        name="attend_near",
    )(q, k_halo, k, v_halo, v)


PIECES_F = ((0, ALL), (2, ALL), (4, ALL), (6, ALL[0:2]), (6, ALL[2:4]))


def central_kernel(
    rb, x_ref, oa_ref, oc_ref, teacher_ref, cot_ref, mask_ref, vec_ref, bup_ref, scale_ref,
    *rest
):
    pieces = rest[:10]
    (
    out_ref, gh_ref, ga_ref, theirs_ref, mine_ref, small_ref, gbup_ref,
    wo_ref, wup_ref, wdn_ref, slope_ref, hid_ref, gpre_ref, n2t_ref, gmlpt_ref, gattnt_ref, place_ref, o_ref,
    h1_ref, xhat_ref, n2_ref, gmlp_ref, sem
    ) = rest[10:]
    me, place = lax.axis_index("fsdp"), lax.axis_index("tp")
    own, ff = x_ref.shape[0], 4 * FFC
    parts = ((wo_ref, 0, COLS), (wup_ref, COLS, FFC), (wdn_ref, COLS + FFC, FFC))
    for n, (dst, start, size) in enumerate(parts):
        for j, ref in enumerate(pieces):
            mask, steps = PIECES_F[j % 5]
            owner = lax.bitwise_xor(me, mask + j // 5)
            for i, s in enumerate(steps):
                tp = lax.bitwise_and(place - s + 4, 3)
                pltpu.make_async_copy(
                    ref.at[i, :, pl.ds(start, size)],
                    dst.at[rows_of(owner * ROWS, ROWS, ROWS), rows_of(tp * size, size)],
                    sem.at[n],
                ).start()
    small_ref[...] = jnp.zeros_like(small_ref)
    head_of = lax.broadcasted_iota(jnp.int32, (D, 128), 0) // HD
    pick = (head_of == lax.broadcasted_iota(jnp.int32, (D, 128), 1)).astype(BF16)
    out_bias, gain, offset, down_bias = (vec_ref[j : j + 1, :] for j in range(2, 6))
    n2t_ref[D:, :] = jnp.ones((TALL - D, own), BF16)
    source = lax.broadcasted_iota(jnp.int32, (TERMS * 128, H * PAIR), 0)
    target = lax.broadcasted_iota(jnp.int32, (TERMS * 128, H * PAIR), 1)
    head, term = target // PAIR, lax.bitwise_and(target, HD - 1) - DOCS
    outside = (lax.bitwise_and(target, PAIR - 1) >= HD) == (lax.bitwise_and(head, 1) == 0)
    placed = outside & (lax.bitwise_and(source, 127) == head) & (source // 128 == term)
    place_ref[...] = jnp.where(placed, 1.0, 0.0).astype(BF16)
    o_ref[0:HALO, :] = oa_ref[...]
    o_ref[HALO:, :] = oc_ref[...]

    def turn(dst, rows, value):
        turned = jnp.transpose(value).astype(BF16)
        for i in range(8):
            slot = lax.bitwise_xor(me, i)
            dst[rows_of(slot * ROWS, ROWS, ROWS), rows] = turned[ROWS * i : ROWS * (i + 1)]

    def arrived(n):
        pltpu.make_async_copy(parts[n][0], parts[n][0], sem.at[n]).wait()

    blocks = [dict(rows=slice(i * rb, (i + 1) * rb)) for i in range(own // rb)]

    def attention_out(one):
        one["attn"] = dot_t(o_ref[one["rows"], :], wo_ref[...])

    def second_norm(one):
        rows = one["rows"]
        h1 = x_ref[rows, :].astype(F32) + one.pop("attn") + out_bias
        xhat, rstd = normalize(h1)
        n2 = xhat * gain + offset
        h1_ref[rows, :] = h1
        xhat_ref[rows, :] = xhat
        one["rstd"] = rstd
        n2_ref[rows, :] = n2.astype(BF16)
        turn(n2t_ref, rows, n2)

    arrived(0)
    staged(blocks, (attention_out, second_norm))
    arrived(1)

    def by_columns(stages):
        def step(c, carry):
            cols = rows_of(c * FFC, FFC)
            staged([dict(rows=one["rows"], cols=cols) for one in blocks], stages)
            return carry

        lax.fori_loop(0, 4, step, 0)

    def up(one):
        one["pre"] = dot(n2_ref[one["rows"], :], wup_ref[:, one["cols"]]) + bup_ref[0:1, one["cols"]]

    def gelu(one):
        pre = one.pop("pre")
        s = jax.nn.sigmoid(1.702 * pre)
        value = pre * s
        hid_ref[one["rows"], one["cols"]] = value.astype(BF16)
        slope_ref[one["rows"], one["cols"]] = s * (1.702 * (pre - value) + 1.0)

    by_columns((up, gelu))
    arrived(2)

    def down(one):
        one["mlp"] = dot_t(hid_ref[one["rows"], :], wdn_ref[...])

    def output(one):
        rows = one["rows"]
        out = h1_ref[rows, :] + one.pop("mlp") + down_bias
        out_ref[rows, :] = out.astype(BF16)
        diff = (out - teacher_ref[rows, :].astype(F32)) * mask_ref[rows, :]
        g_out = cot_ref[rows, :].astype(F32) + scale_ref[0:1, 0:1] * diff
        gh_ref[rows, :] = g_out
        small_ref[0:8, :] += fold(g_out)
        small_ref[8:16, :] += fold(diff * diff)
        gmlp_ref[rows, :] = g_out.astype(BF16)
        turn(gmlpt_ref, rows, g_out)

    staged(blocks, (down, output))

    def hidden(one):
        one["g"] = dot(gmlp_ref[one["rows"], :], wdn_ref[:, one["cols"]])

    def slope(one):
        g_pre = one.pop("g") * slope_ref[one["rows"], one["cols"]]
        gpre_ref[one["rows"], one["cols"]] = g_pre.astype(BF16)

    by_columns((hidden, slope))

    def into_norm(one):
        one["g"] = dot_t(gpre_ref[one["rows"], :], wup_ref[...])

    def pull_norm(one):
        rows, g_n2, xhat = one["rows"], one.pop("g"), xhat_ref[one["rows"], :]
        small_ref[16:24, :] += fold(g_n2 * xhat)
        small_ref[24:32, :] += fold(g_n2)
        g_h1 = gh_ref[rows, :] + norm_pull(g_n2, gain, xhat, one.pop("rstd"))
        gh_ref[rows, :] = g_h1
        small_ref[32:40, :] += fold(g_h1)
        turn(gattnt_ref, rows, g_h1)
        one["go"] = dot(g_h1.astype(BF16), wo_ref[...]).astype(BF16)

    def pull_out(one):
        rows, g_o = one["rows"], one.pop("go")
        product = g_o.astype(F32) * o_ref[rows, :].astype(F32)
        high = product.astype(BF16)
        low = (product - high.astype(F32)).astype(BF16)
        terms = jnp.concatenate(three_terms(-(dot(high, pick) + dot(low, pick))), axis=1)
        spare = dot(terms, place_ref[...]).astype(BF16)
        lane = lane_of((rb, PAIR))
        for n in range(H):
            mine = (lane < HD) if n % 2 == 0 else (lane >= HD)
            pair = g_o[:, (n // 2) * PAIR : (n // 2 + 1) * PAIR]
            ga_ref[rows, n * PAIR : (n + 1) * PAIR] = jnp.where(mine, pair, spare[:, n * PAIR : (n + 1) * PAIR])

    def keep(grad, s, start, size):
        low = grad.astype(BF16)
        for r in range(8):
            dst = theirs_ref if r % 2 else mine_ref
            dst[r // 2, s, :, start : start + size] = low[ROWS * r : ROWS * (r + 1)]

    def their(s, size):
        return rows_of(lax.bitwise_and(place + s, 3) * size, size)

    def by_down(s):
        keep(dot(gmlpt_ref[...], hid_ref[:, their(s, FFC)]), s, COLS + FFC, FFC)

    staged(
        blocks, (into_norm, pull_norm, pull_out), beside=[functools.partial(by_down, s) for s in range(4)]
    )
    for s in range(4):
        total = dot(n2t_ref[...], gpre_ref[:, their(s, FFC)])
        gbup_ref[:, their(s, FFC)] = total[D : D + 8]
        keep(total, s, COLS, FFC)
        keep(dot(gattnt_ref[...], o_ref[:, their(s, COLS)]), s, 0, COLS)


def central(x, o_near, o_far, teacher, cot, mask, vec, bup, scale, pieces):
    own = x.shape[0]
    rb = 256
    shapes = (
        jax.ShapeDtypeStruct((own, D), BF16),
        jax.ShapeDtypeStruct((own, D), F32),
        jax.ShapeDtypeStruct((own, 2 * D), BF16),
        jax.ShapeDtypeStruct((4, 4, ROWS, WF), BF16),
        jax.ShapeDtypeStruct((4, 4, ROWS, WF), BF16),
        jax.ShapeDtypeStruct((40, D), F32),
        jax.ShapeDtypeStruct((8, 4 * FFC), F32),
    )
    return pl.pallas_call(
        functools.partial(central_kernel, rb),
        out_shape=shapes,
        in_specs=[VMEM] * 9 + [FAR] * 10,
        out_specs=[VMEM] * len(shapes),
        scratch_shapes=[
            pltpu.VMEM((D, D), BF16),
            pltpu.VMEM((D, 4 * FFC), BF16),
            pltpu.VMEM((D, 4 * FFC), BF16),
            pltpu.VMEM((own, 4 * FFC), F32),
            pltpu.VMEM((own, 4 * FFC), BF16),
            pltpu.VMEM((own, 4 * FFC), BF16),
            pltpu.VMEM((TALL, own), BF16),
            pltpu.VMEM((D, own), BF16),
            pltpu.VMEM((D, own), BF16),
            pltpu.VMEM((TERMS * 128, H * PAIR), BF16),
            pltpu.VMEM((own, D), BF16),
            pltpu.VMEM((own, D), F32),
            pltpu.VMEM((own, D), F32),
            pltpu.VMEM((own, D), BF16),
            pltpu.VMEM((own, D), BF16),
            pltpu.SemaphoreType.DMA((3,)),
        ],
        compiler_params=params(30),
        cost_estimate=SMALL,
        name="central",
    )(x, o_near, o_far, teacher, cot, mask, vec, bup, scale, *pieces)


def pull_units(units, bias_ref):
    lane = lane_of((QB, PAIR))

    def mask(x, h):
        return jnp.where((lane < HD) if h == 0 else (lane >= HD), x, jnp.zeros_like(x))

    def score(one):
        keys, values, _, where, _ = one["part"]
        one["s"] = dot_t(keys[where, one["lanes"]], one["q"][one["rows"], one["qlanes"]])
        one["d"] = dot_t(values[where, one["lanes"]], one["g"][one["grows"], one["lanes"]])

    def soften(one):
        s = one.pop("s")
        p = jnp.exp(s + bias_ref[...] if one["part"][4] else s)
        one["p"], one["ds"] = p.astype(BF16), (p * one.pop("d")).astype(BF16)

    def finish(one):
        _, _, keys_t, where, last = one["part"]
        h, sums = one["h"], one["sums"]
        part = dot(keys_t[one["tlanes"], where], one["ds"])
        sums[h] = part if h not in sums else sums[h] + part
        if h == 0:
            sums["before"] = one
            return
        two = (sums.pop("before"), one)
        q = jnp.concatenate([mask(u["q"][u["rows"], u["qlanes"]], u["h"]) for u in two], axis=0)
        g = jnp.concatenate([mask(u["g"][u["grows"], u["lanes"]], u["h"]) for u in two], axis=0)
        dk = dot(jnp.concatenate([u.pop("ds") for u in two], axis=1), q)
        dv = dot(jnp.concatenate([u.pop("p") for u in two], axis=1), g)
        one["take"](dk, dv)
        if last:
            both = jnp.concatenate([sums[0], sums[1]], axis=0)
            one["take_q"]((jnp.transpose(both) * SCALE).astype(BF16))

    staged(units, (score, soften, finish), 2)


def block_units(q_ref, rows, q_pair, g_ref, grows, pair, parts, takes, take_q):
    sums, units = {}, []
    for part, take in zip(parts, takes):
        for h in range(2):
            units.append(
                dict(
                    q=q_ref, rows=rows, qlanes=head_lanes(q_pair, h), g=g_ref, grows=grows, lanes=head_lanes(pair, h), h=h,
                    part=part, tlanes=rows_of((2 * pair + h) * HD, HD, HD), take=take, take_q=take_q, sums=sums,
                )
            )
    return units


def pull_near_kernel(base, q_ref, g_ref, kh_ref, ko_ref, vh_ref, vo_ref, kth_ref, kto_ref, gh_ref, gq_ref, part_ref, bias_ref, late_ref):
    bias_ref[...] = causal(False)
    halo, own = (kh_ref, vh_ref, kth_ref), (ko_ref, vo_ref, kto_ref)

    def one(pair, carry):
        lanes = (rows_of(2 * pair * PAIR, PAIR), rows_of((2 * pair + 1) * PAIR, PAIR))

        def halo_first(*grads):
            for at, d in zip(lanes, grads):
                gh_ref[0:QB, at] = d[0:QB].astype(BF16)
                late_ref[:, at] = d[QB:]

        def halo_second(*grads):
            for at, d in zip(lanes, grads):
                gh_ref[QB:, at] = (late_ref[:, at] + d).astype(BF16)

        def own_first(*grads):
            for at, d in zip(lanes, grads):
                part_ref[0:QB, at] = d

        def own_more(*grads):
            for at, d in zip(lanes, grads):
                part_ref[0:QB, at] += d

        def own_last(*grads):
            for at, d in zip(lanes, grads):
                part_ref[QB:, at] = d

        units, takes = [], ((halo_first, own_first), (halo_second, own_more, own_last))
        for i, parts in enumerate(near_parts(halo, own)):
            rows = slice(i * QB, (i + 1) * QB)

            def take_q(dq, rows=rows):
                gq_ref[rows, rows_of(pair * PAIR, PAIR)] = dq

            units += block_units(q_ref, rows, base + pair, g_ref, rows, base + pair, parts, takes[i], take_q)
        pull_units(units, bias_ref)
        return carry

    lax.fori_loop(0, 2, one, 0)


def pull_near(base, qa, ga, k_halo, k, v_halo, v, kt_halo, kt):
    return pl.pallas_call(
        functools.partial(pull_near_kernel, base),
        out_shape=(
            jax.ShapeDtypeStruct((HALO, D), BF16),
            jax.ShapeDtypeStruct((HALO, D // 2), BF16),
            jax.ShapeDtypeStruct((HALO, D), F32),
        ),
        in_specs=[VMEM] * 8,
        out_specs=[VMEM] * 3,
        scratch_shapes=[pltpu.VMEM((QB, QB), F32), pltpu.VMEM((QB, D), F32)],
        compiler_params=params(10),
        cost_estimate=SMALL,
        name="pull_near",
    )(qa, ga, k_halo, k, v_halo, v, kt_halo, kt)


def pull_far_kernel(q_ref, go_ref, k_ref, v_ref, kt_ref, qa_ref, qb_ref, pa_ref, pb_ref, g_ref, bias_ref):
    bias_ref[...] = causal(False)
    refs = (k_ref, v_ref, kt_ref)
    parts = ((*refs, slice(0, HALO), False), (*refs, slice(HALO, HALO + QB), True))

    def two(inside, carry):
        units = []
        for half, near_q, near_part in ((0, qa_ref, pa_ref), (1, qb_ref, pb_ref)):
            pair = 2 * half + inside
            lanes = tuple(rows_of(pair * WA + n * COLS, COLS) for n in range(3))
            within = tuple(rows_of((2 * inside + n) * PAIR, PAIR) for n in range(2))
            g_ref[0:HALO, lanes[0]] = near_q[:, rows_of(inside * PAIR, PAIR)]

            def older(*grads, lanes=lanes, within=within, near_part=near_part):
                for n, d in enumerate(grads):
                    g_ref[0:HALO, lanes[n + 1]] = (near_part[:, within[n]] + d).astype(BF16)

            def newest(*grads, lanes=lanes):
                for n, d in enumerate(grads):
                    g_ref[HALO:, lanes[n + 1]] = d.astype(BF16)

            def take_q(dq, lanes=lanes):
                g_ref[HALO:, lanes[0]] = dq

            own = slice(HALO, HALO + QB)
            units += block_units(q_ref, slice(0, QB), pair, go_ref, own, pair, parts, (older, newest), take_q)
        pull_units(units, bias_ref)
        return carry

    lax.fori_loop(0, 2, two, 0)


def pull_far(qa, ga, k, v, kt, gq_near, gq_more, part_near, part_more):
    own = k.shape[0]
    return pl.pallas_call(
        pull_far_kernel,
        out_shape=jax.ShapeDtypeStruct((own, 4 * WA), BF16),
        in_specs=[VMEM] * 9,
        out_specs=VMEM,
        scratch_shapes=[pltpu.VMEM((QB, QB), F32)],
        compiler_params=params(10),
        cost_estimate=SMALL,
        name="pull_far",
    )(qa, ga, k, v, kt, gq_near, gq_more, part_near, part_more)


def norm_sums(small_ref, x, g_n1):
    xhat, _ = normalize(x.astype(F32))
    small_ref[0:8, :] += fold(g_n1 * xhat)
    small_ref[8:16, :] += fold(g_n1)


def halo_back_kernel(ga_ref, gb_ref, w_ref, x_ref, out_ref, small_ref):
    small_ref[...] = jnp.zeros_like(small_ref)

    def pull(one):
        total = None
        for t in range(4):
            g = (ga_ref, gb_ref)[t // 2][one["rows"], (t % 2) * 2 * COLS : (t % 2 + 1) * 2 * COLS]
            part = dot_t(g, w_ref[:, t * WA + COLS : (t + 1) * WA])
            total = part if total is None else total + part
        one["g"] = total

    def norms(one):
        g_n1 = one.pop("g")
        out_ref[one["rows"], :] = g_n1.astype(BF16)
        norm_sums(small_ref, x_ref[one["rows"], :], g_n1)

    staged([dict(rows=slice(i * QB, (i + 1) * QB)) for i in range(HALO // QB)], (pull, norms))


def halo_back(g_near, g_more, w, halo):
    return pl.pallas_call(
        halo_back_kernel,
        out_shape=(jax.ShapeDtypeStruct((HALO, D), BF16), jax.ShapeDtypeStruct((16, D), F32)),
        compiler_params=params(6),
        cost_estimate=SMALL,
        name="halo_back",
    )(g_near, g_more, w, halo)


def own_back_kernel(
    x_ref, ga_ref, gb_ref, g_ref, nth_ref, nto_ref, w_ref, small_halo, small_two, gbup_ref, scale_ref,
    gn_ref, theirs_ref, mine_ref, small_ref, gh_ref
):
    me, place = lax.axis_index("fsdp"), lax.axis_index("tp")
    own = x_ref.shape[0]
    small_ref[...] = small_halo[...]
    gh_ref[:, 0:D] = ga_ref[...]
    gh_ref[:, D:] = gb_ref[...]

    def pull(one):
        one["g"] = dot_t(g_ref[one["rows"], :], w_ref[...])

    def norms(one):
        g_n1 = one.pop("g")
        gn_ref[one["rows"], :] = g_n1
        norm_sums(small_ref, x_ref[one["rows"], :], g_n1)

    staged([dict(rows=slice(i * QB, (i + 1) * QB)) for i in range(own // QB)], (pull, norms))
    sums = lambda ref, j: jnp.sum(ref[8 * j : 8 * j + 8, :], axis=0, keepdims=True)
    loss = jnp.sum(sums(small_two, 1), axis=1, keepdims=True) * scale_ref[4:5, 0:1]
    vectors = jnp.concatenate(
        [sums(small_ref, 0), sums(small_ref, 1), sums(small_two, 4), sums(small_two, 2), sums(small_two, 3),
         sums(small_two, 0), jnp.zeros((2, D), F32)],
        axis=0,
    )
    high = loss.astype(BF16).astype(F32)
    row, lane = lax.broadcasted_iota(jnp.int32, (EXTRA, 128), 0), lane_of((EXTRA, 128))

    def grads(s, carry):
        tp = lax.bitwise_and(place + s, 3)
        g_own = g_ref[:, rows_of(tp * WA, WA)]
        g_halo = gh_ref[:, rows_of(tp * 2 * COLS, 2 * COLS)]
        total = dot(nto_ref[...], g_own)
        more = dot(nth_ref[...], g_halo)
        total = jnp.concatenate([total[:, 0:COLS], total[:, COLS:] + more], axis=1)
        low, sums = total[0:D].astype(BF16), total[D : D + 1]
        ups = gbup_ref[0:1, rows_of(tp * FFC, FFC)]
        mids = jnp.concatenate(
            [sums[:, 0:COLS], sums[:, 2 * COLS :]]
            + [ups[:, 128 * j : 128 * j + 128] for j in range(4)]
            + [jnp.zeros((2, 128), F32)],
            axis=0,
        ).astype(BF16)
        for r in range(8):
            dst = theirs_ref if r % 2 else mine_ref
            dst[r // 2, s, 0:ROWS, :] = low[ROWS * r : ROWS * (r + 1)]
            dst[r // 2, s, ROWS:, 128:256] = mids
        return carry

    lax.fori_loop(0, 4, grads, 0)
    for r in range(8):
        owner = lax.bitwise_xor(me, r)
        block = pltpu.roll(vectors, lax.rem(D - owner * ROWS, D), 1)[:, 0:128]
        block = jnp.where((row == 6) & (lane == 0), high, block)
        block = jnp.where((row == 6) & (lane == 1), loss - high, block).astype(BF16)
        dst = theirs_ref if r % 2 else mine_ref
        for s in range(4):
            dst[r // 2, s, ROWS:, 0:128] = block
            dst[r // 2, s, ROWS:, 256:384] = jnp.zeros((EXTRA, 128), BF16)


def own_back(x, g_near, g_more, g_own, nt_halo, nt, w, small_halo, small_two, gbup, scale):
    own = x.shape[0]
    send = jax.ShapeDtypeStruct((4, 4, ROWS + EXTRA, WA), BF16)
    return pl.pallas_call(
        own_back_kernel,
        out_shape=(jax.ShapeDtypeStruct((own, D), F32), send, send),
        scratch_shapes=[pltpu.VMEM((16, D), F32), pltpu.VMEM((HALO, 2 * D), BF16)],
        compiler_params=params(10),
        cost_estimate=SMALL,
        name="own_back",
    )(x, g_near, g_more, g_own, nt_halo, nt, w, small_halo, small_two, gbup, scale)


def close_kernel(x_ref, gn_ref, back_ref, gh_ref, vec_ref, out_ref):
    own = x_ref.shape[0]

    def block(at, extra):
        rows = rows_of(at, 128)
        xhat, rstd = normalize(x_ref[rows, :].astype(F32))
        g_n1 = gn_ref[rows, :] + extra
        out_ref[rows, :] = gh_ref[rows, :] + norm_pull(g_n1, vec_ref[0:1, :], xhat, rstd)

    def first(i, carry):
        block(i * 128, 0.0)
        return carry

    def second(i, carry):
        block(own - HALO + i * 128, back_ref[rows_of(i * 128, 128), :].astype(F32))
        return carry

    lax.fori_loop(0, (own - HALO) // 128, first, 0)
    lax.fori_loop(0, HALO // 128, second, 0)


def close(x, g_n1, back, g_h1, vec):
    return pl.pallas_call(
        close_kernel,
        out_shape=jax.ShapeDtypeStruct(x.shape, F32),
        compiler_params=params(8),
        cost_estimate=SMALL,
        name="close",
    )(x, g_n1, back, g_h1, vec)


def unpack_f_kernel(k_ref, r1, r2, r3, wo_ref, wup_ref, wdn_ref):
    total = (k_ref[0].astype(F32) + r1[...].astype(F32)) + (r2[...].astype(F32) + r3[...].astype(F32))
    wo_ref[...] = total[:, 0:COLS]
    wup_ref[...] = total[:, COLS : COLS + FFC]
    wdn_ref[...] = total[:, COLS + FFC :]


def unpack_f(k, r1, r2, r3):
    return pl.pallas_call(
        unpack_f_kernel,
        out_shape=(
            jax.ShapeDtypeStruct((ROWS, COLS), F32),
            jax.ShapeDtypeStruct((ROWS, FFC), F32),
            jax.ShapeDtypeStruct((ROWS, FFC), F32),
        ),
        compiler_params=params(6),
        name="unpack_f",
    )(k, r1, r2, r3)


def unpack_a_kernel(k_ref, r1, r2, r3, wq_ref, wk_ref, wv_ref, bq_ref, bv_ref, bup_ref, loss_ref, *vec_refs):
    me = lax.axis_index("fsdp")
    total = (k_ref[0].astype(F32) + r1[...].astype(F32)) + (r2[...].astype(F32) + r3[...].astype(F32))
    wq_ref[...] = total[0:ROWS, 0:COLS]
    wk_ref[...] = total[0:ROWS, COLS : 2 * COLS]
    wv_ref[...] = total[0:ROWS, 2 * COLS :]
    for j, ref in enumerate(vec_refs):
        ref[...] = total[ROWS + j, 0:ROWS]
    loss_ref[...] = total[ROWS + 6 : ROWS + 7, 0:1] + total[ROWS + 6 : ROWS + 7, 1:2]
    mids = pltpu.roll(total[ROWS:, 128:256], lax.rem(128 - me * 8, 128), 1)
    for i in range(2):
        bq_ref[i : i + 1, :] = mids[0:1, i * HD : i * HD + 8]
        bv_ref[i : i + 1, :] = mids[1:2, i * HD : i * HD + 8]
    for i in range(8):
        at = (i % 2) * HD
        bup_ref[i : i + 1, :] = mids[2 + i // 2 : 3 + i // 2, at : at + 8]


def unpack_a(k, r1, r2, r3):
    small = jax.ShapeDtypeStruct((ROWS, COLS), F32)
    return pl.pallas_call(
        unpack_a_kernel,
        out_shape=(
            small,
            small,
            small,
            jax.ShapeDtypeStruct((2, 8), F32),
            jax.ShapeDtypeStruct((2, 8), F32),
            jax.ShapeDtypeStruct((8, 8), F32),
            jax.ShapeDtypeStruct((1, 1), F32),
            *[jax.ShapeDtypeStruct((ROWS,), F32)] * 6,
        ),
        compiler_params=params(6),
        name="unpack_a",
    )(k, r1, r2, r3)


def to_mask(x, mask):
    return lax.ppermute(x, "fsdp", [(i, i ^ mask) for i in range(8)])


def to_step(x, step):
    return lax.ppermute(x, "tp", [(i, (i + step) % 4) for i in range(4)])


def add(a, b):
    return (a.astype(F32) + b.astype(F32)).astype(BF16)


def after(values, others):
    return lax.optimization_barrier((values, others))[0]


def local_fast(
    layer_input, segment_ids, valid_mask, teacher, cotangent, ln1_gain, ln1_bias, w_q, w_k, w_v, b_q, b_v,
    w_o, b_o, ln2_gain, ln2_bias, w_up, b_up, w_down, b_down
):
    place = lax.axis_index("tp")
    own = layer_input.shape[0]
    tokens_all = own * lax.axis_size("fsdp") * lax.axis_size("tp")

    shard_a, shard_f = pack_weights(
        (w_q, w_k, w_v, w_o.T, w_up, w_down.T, ln1_gain, ln1_bias, b_o, ln2_gain, ln2_bias, b_down, b_q, b_v, b_up,
         valid_mask)
    )
    steps_a = [shard_a] + [to_step(shard_a, s) for s in (1, 2, 3)]
    line_a = jnp.stack(steps_a)
    steps_f = [shard_f] + [to_step(shard_f, s) for s in (1, 2, 3)]
    near_a = [to_mask(line_a, m) for m in (2, 4, 6)]
    last_rows = layer_input[own - HALO :]
    halves_a, last_rows = after(([jnp.stack(steps_a[0:2]), jnp.stack(steps_a[2:4])], last_rows), steps_f)
    over_a = [to_mask(a, 1) for a in halves_a]
    line_f = jnp.stack(after(steps_f, (over_a, near_a)))
    over_f = to_mask(line_f, 1)
    pieces_a = [line_a] + near_a + [jnp.concatenate(over_a + [to_mask(a, 1) for a in near_a])]
    halo = lax.ppermute(last_rows, "tp", [(i, i + 1) for i in range(3)])
    f_x, f_y = to_mask(line_f, 2), to_mask(line_f, 4)

    ids = segment_ids + 16 * jnp.arange(segment_ids.shape[0], dtype=jnp.int32)[:, None]
    ids = jnp.concatenate([jnp.full((HALO,), -1, jnp.int32), ids.reshape(-1)])
    id_col = lax.dynamic_slice_in_dim(ids, place * own, HALO + own)[:, None]
    mask = valid_mask.astype(F32)[:, None]

    q, k, v, kt, nt, w_all, vec, bup, scale, head = project(after(layer_input, over_f), id_col, pieces_a, tokens_all)
    o_far, qa_far = attend_far(q, k, v)
    f_x, f_y = after((f_x, f_y), o_far)
    halo = after(halo, o_far)
    f_xy = [to_mask(f_y[0:2], 2), to_mask(f_x[2:4], 4)]
    k_halo, v_halo, kt_halo, nt_halo = project_halo(halo, id_col, w_all, vec, head)
    o_near, qa_near = attend_near(q, k_halo, k, v_halo, v)
    near_f = [f_x, f_y] + after(f_xy, o_near)
    pieces_f = [line_f] + near_f + [over_f] + [to_mask(a, 1) for a in near_f]
    layer_out, g_h1, ga, theirs_f, mine_f, small_two, gbup = central(
        layer_input, o_near, o_far, teacher, cotangent, mask, vec, bup, scale, pieces_f
    )

    def near(base, qa, ga):
        return pull_near(base, qa, ga, k_halo, k, v_halo, v, kt_halo, kt)

    g_near, gq_near, part_near = near(0, qa_near, ga)
    half = add(after(mine_f, g_near), to_mask(theirs_f, 1))
    from_x, from_y = to_mask(half[3, 0:2], 2), to_mask(half[3, 2:4], 4)
    g_more, gq_more, part_more = near(2, after(qa_near, half), ga)
    gn_halo, small_halo = halo_back(g_near, g_more, w_all, halo)
    back = lax.ppermute(gn_halo, "tp", [(i + 1, i) for i in range(3)])
    from_x, from_y = after((from_x, from_y), gn_halo)
    for_x = jnp.concatenate([half[1, 0:2], add(half[1, 2:4], from_y)])
    for_y = jnp.concatenate([add(half[2, 0:2], from_x), half[2, 2:4]])
    got_x, got_y = to_mask(for_x, 2), to_mask(for_y, 4)
    g_own = pull_far(after(qa_far, (for_x, for_y)), ga, k, v, kt, gq_near, gq_more, part_near, part_more)
    gn_own, theirs_a, mine_a = own_back(
        layer_input, g_near, g_more, g_own, nt_halo, nt, w_all, small_halo, small_two, gbup, scale
    )
    got_x, got_y = after((got_x, got_y), gn_own)
    line = (half[0].astype(F32) + got_x.astype(F32) + got_y.astype(F32)).astype(BF16)
    grad_wo, grad_wup, grad_wdn = unpack_f(line, *[to_step(line[s], s) for s in (1, 2, 3)])

    half = add(mine_a, to_mask(after(theirs_a, back), 1))
    from_x, from_y, from_xy = (to_mask(half[m], 2 * m) for m in (1, 2, 3))
    line = (half[0].astype(F32) + from_x.astype(F32) + from_y.astype(F32) + from_xy.astype(F32)).astype(BF16)
    grad_wq, grad_wk, grad_wv, grad_bq, grad_bv, grad_bup, loss, *six = unpack_a(
        line, *[to_step(line[s], s) for s in (1, 2, 3)]
    )
    grad_input = close(layer_input, gn_own, back, g_h1, vec)
    return (
        layer_out, loss.reshape(()), grad_input, six[0], six[1], grad_wq, grad_wk, grad_wv, grad_bq, grad_bv, grad_wo.T, six[2],
        six[3], six[4], grad_wup, grad_bup, grad_wdn.T, six[5]
    )


def solution(mesh):
    tokens = P(("fsdp", "tp"), None)
    rows, crossed, heads = P("fsdp"), P("fsdp", "tp"), P("tp", "fsdp")
    placed = (
        tokens,
        P("fsdp", None),
        P(("fsdp", "tp")),
        tokens,
        tokens,
        rows,
        rows,
        crossed,
        crossed,
        crossed,
        heads,
        heads,
        heads,
        rows,
        rows,
        rows,
        crossed,
        heads,
        heads,
        rows,
    )
    given = (
        tokens,
        P(),
        tokens,
        rows,
        rows,
        crossed,
        crossed,
        crossed,
        heads,
        heads,
        heads,
        rows,
        rows,
        rows,
        crossed,
        heads,
        heads,
        rows,
    )
    sizes = (mesh.shape["fsdp"], mesh.shape["tp"])

    def body(*args):
        x, ids, w_q, w_up = args[0], args[1], args[7], args[16]
        fits = x.shape[0] == HALO + QB and 16 * ids.shape[0] <= DOCS
        fits = fits and w_q.shape == (ROWS, COLS) and w_up.shape == (ROWS, FFC)
        return (local_fast if fits and sizes == (8, 4) else local)(*args)

    return jax.shard_map(body, mesh=mesh, in_specs=placed, out_specs=given, check_vma=False)
```
